32 devices in a mesh: dp: 4 (over z), ctx: 8 (over y, x, core).
Axes of the slice: x: 2, y: 2, z: 4, core: 2. Of those that a mesh axis runs over, the one named last changes fastest.
Arguments:
- tokens: bfloat16 [2, 32, 1024, 512], P(None, 'dp', 'ctx'), may hold values from -8 to 8
- prefix: int32 [2, 32], P(None, 'dp'), may hold values from 102 to 512
- w_qkv: bfloat16 [512, 1536], P('dp', 'ctx'), may hold values from -0.25 to 0.25
- w_out: bfloat16 [512, 512], P('dp', 'ctx'), may hold values from -0.75 to 0.75
- w_up: bfloat16 [512, 2048], P('dp', 'ctx'), may hold values from -0.25 to 0.25
- w_down: bfloat16 [2048, 512], P('dp', 'ctx'), may hold values from -0.125 to 0.125
- gain_one: bfloat16 [512], P('ctx'), may hold values from 0.25 to 1.75
- gain_two: bfloat16 [512], P('ctx'), may hold values from 0.25 to 1.75
- cotangent: bfloat16 [2, 32, 1024, 512], P(None, 'dp', 'ctx'), may hold values from -6 to 6
Outputs:
- output: bfloat16 [2, 32, 1024, 512], P(None, 'dp', 'ctx')
- input_grad: bfloat16 [2, 32, 1024, 512], P(None, 'dp', 'ctx')
- grad_qkv: float32 [512, 1536], P('dp', 'ctx')
- grad_out: float32 [512, 512], P('dp', 'ctx')
- grad_up: float32 [512, 2048], P('dp', 'ctx')
- grad_down: float32 [2048, 512], P('dp', 'ctx')
- grad_gain_one: float32 [512], P('ctx')
- grad_gain_two: float32 [512], P('ctx')
The draws below stay inside these ranges and needn't reach their ends.
Inputs may be any that keep to these rules, and one draw needn't show every extreme that they name: `prefix`: each sequence's number of leading positions that attend both ways.
All inputs are finite; a program needn't handle non-finite values.
Results may differ from the reference program's by a relative error of at most 0.017.
Values may be sent and summed in bfloat16 or wider, within the bound.
A program may use at most 192 MiB of HBM per device.

```python
import math
import jax
import jax.numpy as jnp
from jax import lax

D = 512
HEADS = 8
FF = 2048
SPAN_POSITIONS = 128
MB = 2
LENGTH = 1024
SEQS_MB = 32


def draw_tokens(key, part):
    first_key, second_key = jax.random.split(jax.random.fold_in(key, 11))
    block_count = LENGTH // SPAN_POSITIONS
    noise = jnp.clip(jax.random.normal(first_key, (MB, SEQS_MB, block_count, SPAN_POSITIONS, D), jnp.float32), -4.0, 4.0)
    offset = 0.8 * jnp.clip(jax.random.normal(second_key, (MB, SEQS_MB, block_count, 1, D), jnp.float32), -3.0, 3.0)
    combined = noise + offset
    return combined.reshape(MB, SEQS_MB, LENGTH, D).astype(jnp.bfloat16)


def set_ends(values, key, least, high):
    longest = values.shape.index(max(values.shape))
    spots = []
    for shift in (0, 1):
        where = [jax.random.randint(jax.random.fold_in(key, axis), (), 0, length) for axis, length in enumerate(values.shape)]
        where[longest] = (where[longest] + shift) % values.shape[longest]
        spots.append(tuple(where))
    return values.at[spots[0]].set(least).at[spots[1]].set(high)


def raised(values, stream_key, source, target, shards_of, factor):
    owner, partner = [(jnp.arange(values.shape[dim]) // (values.shape[dim] // shards_of)).reshape([-1 if axis == dim else 1 for axis in range(values.ndim)]) for dim in (source, target)]
    chosen = jax.random.permutation(stream_key, shards_of)[partner]
    strong = (owner == chosen) | (owner == (partner + shards_of // 2) % shards_of)
    return jnp.where(strong, factor * values, values)


def shard_levels(stream_key, dims, cuts, least, high):
    level = 1.0
    for dim, parts in cuts:
        steps = jax.random.uniform(jax.random.fold_in(jax.random.fold_in(stream_key, 6), dim), (parts,), jnp.float32, least / len(cuts), high / len(cuts))
        level = level * jnp.repeat(jnp.exp(steps), dims[dim] // parts).reshape((-1,) + (1,) * (len(dims) - 1 - dim))
    return level


def gaussian(rng, dims, scale, most, pieces=(), held_as=jnp.bfloat16):
    values = jax.random.normal(rng, dims, jnp.float32) * scale
    if len(pieces) > 0:
        values = shard_levels(rng, dims, pieces, -0.22, 0.18) * values
    return jnp.clip(values, min=-most, max=most).astype(held_as)


def bell_draw_with(own_key, extent, spread, most, cuts, heavy, kind=jnp.bfloat16):
    array = spread * jax.random.normal(own_key, extent, jnp.float32)
    if cuts:
        array = array * shard_levels(own_key, extent, cuts, -0.22, 0.18)
    return jnp.clip(raised(array, jax.random.fold_in(own_key, 3), *heavy), -most, most).astype(kind)


def setup_inputs(seed: int = 0) -> dict:
    splits = jax.random.split(jax.random.key(seed), 10)
    return {
        "tokens": draw_tokens(jax.random.fold_in(splits[9], 71), 0),
        "prefix": set_ends(jax.random.randint(splits[1], (MB, SEQS_MB), LENGTH // 10, LENGTH // 2 + 1), jax.random.fold_in(splits[1], 1), LENGTH // 10, (LENGTH // 2 + 1) - 1).astype(jnp.int32),
        "w_qkv": gaussian(splits[2], (D, 3 * D), D ** -0.5, 0.25, ((0, 4), (1, 8))),
        "w_out": gaussian(splits[3], (D, D), (D // 8) ** -0.5, 0.75, ((0, 4), (1, 8))),
        "w_up": gaussian(splits[4], (D, FF), D ** -0.5, 0.25, ((0, 4), (1, 8))),
        "w_down": gaussian(splits[5], (FF, D), FF ** -0.5, 0.125, ((0, 4), (1, 8))),
        "gain_one": jnp.clip(1.0 + 0.15 * jax.random.normal(splits[6], (D,), jnp.float32), 0.25, 1.75).astype(jnp.bfloat16),
        "gain_two": jnp.clip(1.0 + 0.15 * jax.random.normal(splits[7], (D,), jnp.float32), 0.25, 1.75).astype(jnp.bfloat16),
        "cotangent": bell_draw_with(splits[8], (MB, SEQS_MB, LENGTH, D), 1.0, 6.0, ((1, 4), (2, 8)), (2, 3, 8, 2.0)),
    }


@jax.custom_vjp
def low(v):
    return lax.optimization_barrier(v.astype(jnp.bfloat16)).astype(jnp.float32)

@jax.custom_vjp
def lower_backward(v):
    return v

def low_keep(v):
    return (low(v), None)

def low_pass(kept, grad):
    return (grad,)

def back_keep(v):
    return (v, None)

def back_low(kept, grad):
    return (low(grad),)
low.defvjp(low_keep, low_pass)
lower_backward.defvjp(back_keep, back_low)
EPSILON = 1e-05
HIGHEST = lax.Precision.HIGHEST

def layer_norm(values, gain):
    row_mean = lax.optimization_barrier(jnp.mean(values, axis=-1, keepdims=True))
    centred = values - row_mean
    variance = lax.optimization_barrier(jnp.mean(centred * centred, axis=-1, keepdims=True))
    return centred * lax.rsqrt(variance + EPSILON) * gain

def gelu_exact(values):
    return 0.5 * values * (1.0 + lax.erf(values * 0.7071067811865476))

def visible_units(block_ids, prefix_len, span_length, block_count):
    query_pos = jnp.arange(span_length)[:, None]
    unit_positions = jnp.arange(2 * span_length + block_count)[None, :]
    start_pos = block_ids * span_length
    query_abs = start_pos + query_pos
    prev_ok = (unit_positions < span_length) & (block_ids >= 1)
    own_pos = unit_positions - span_length
    own_ok = (unit_positions >= span_length) & (unit_positions < 2 * span_length) & ((own_pos <= query_pos) | (start_pos + own_pos < prefix_len))
    summary_id = unit_positions - 2 * span_length
    far_ok = (summary_id <= block_ids - 1) | (query_abs < prefix_len) & (summary_id >= block_ids + 1) & ((summary_id + 1) * span_length <= prefix_len)
    summary_ok = (unit_positions >= 2 * span_length) & far_ok
    return prev_ok | own_ok | summary_ok

def layer(seq_tokens, prefix_len, w_qkv, w_out, w_up, w_down, gain_one, gain_two):
    model_width = seq_tokens.shape[1]
    block_count = seq_tokens.shape[0] // SPAN_POSITIONS
    head_features = model_width // HEADS
    normed_one = low(layer_norm(seq_tokens, gain_one))
    projected = low(lower_backward(jnp.dot(normed_one, w_qkv, precision=HIGHEST)))
    query_rows = projected[:, :model_width].reshape(block_count, SPAN_POSITIONS, HEADS, head_features)
    key_rows = projected[:, model_width:2 * model_width].reshape(block_count, SPAN_POSITIONS, model_width)
    value_rows = projected[:, 2 * model_width:].reshape(block_count, SPAN_POSITIONS, model_width)
    key_summary = low(lax.optimization_barrier(jnp.mean(key_rows, axis=1)))
    value_summary = low(lax.optimization_barrier(jnp.mean(value_rows, axis=1)))
    empty_block = jnp.zeros((1, SPAN_POSITIONS, model_width), seq_tokens.dtype)
    key_prev = jnp.concatenate([empty_block, key_rows[:-1]], axis=0)
    value_prev = jnp.concatenate([empty_block, value_rows[:-1]], axis=0)
    key_far = jnp.broadcast_to(key_summary[None], (block_count, block_count, model_width))
    value_far = jnp.broadcast_to(value_summary[None], (block_count, block_count, model_width))
    key_units = jnp.concatenate([key_prev, key_rows, key_far], axis=1).reshape(block_count, -1, HEADS, head_features)
    value_units = jnp.concatenate([value_prev, value_rows, value_far], axis=1).reshape(block_count, -1, HEADS, head_features)
    units_number = key_units.shape[1]
    plain_score = jnp.einsum('bqhd,bkhd->bhqk', query_rows, key_units, precision=HIGHEST)
    summary_extra_bias = jnp.where(jnp.arange(units_number) >= 2 * SPAN_POSITIONS, math.log(SPAN_POSITIONS), 0.0)
    score_matrix = lower_backward(plain_score * head_features ** (-0.5) + summary_extra_bias)
    block_ids = jnp.arange(block_count)[:, None, None]
    permitted_mask = visible_units(block_ids, prefix_len, SPAN_POSITIONS, block_count)[:, None]
    masked = jnp.where(permitted_mask, score_matrix, -1e+30)
    highest = lax.optimization_barrier(jnp.max(masked, axis=-1, keepdims=True))
    expanded = jnp.exp(masked - highest)
    prob_grid = low(expanded / lax.optimization_barrier(jnp.sum(expanded, axis=-1, keepdims=True)))
    attended = jnp.einsum('bhqk,bkhd->bqhd', prob_grid, value_units, precision=HIGHEST)
    mixed = low(lower_backward(attended)).reshape(-1, model_width)
    branch = lower_backward(jnp.dot(mixed, w_out, precision=HIGHEST))
    resid = seq_tokens + branch
    normed_two = low(layer_norm(resid, gain_two))
    upper = lower_backward(jnp.dot(normed_two, w_up, precision=HIGHEST))
    hidden = low(gelu_exact(upper))
    return resid + jnp.dot(hidden, w_down, precision=HIGHEST)

def reference(tokens, prefix, w_qkv, w_out, w_up, w_down, gain_one, gain_two, cotangent):
    weights = tuple((weight.astype(jnp.float32) for weight in (w_qkv, w_out, w_up, w_down, gain_one, gain_two)))
    seq_total = tokens.shape[0] * tokens.shape[1]
    flat_tokens = tokens.reshape(seq_total, tokens.shape[2], tokens.shape[3])
    flat_grads = cotangent.reshape(seq_total, tokens.shape[2], tokens.shape[3])
    flat_prefix = prefix.reshape(seq_total)

    def one_sequence(running, packed):
        seq_tokens, prefix_len, seq_grad = packed

        def forward(inputs, *params):
            return layer(inputs, prefix_len, *params)
        result, pull_back = jax.vjp(forward, seq_tokens.astype(jnp.float32), *weights)
        grad_list = pull_back(seq_grad.astype(jnp.float32))
        running = tuple((summed + addend for summed, addend in zip(running, grad_list[1:])))
        return (running, (result.astype(jnp.bfloat16), grad_list[0].astype(jnp.bfloat16)))
    initial = tuple((jnp.zeros_like(weight) for weight in weights))
    running, (outputs, input_grads) = lax.scan(one_sequence, initial, (flat_tokens, flat_prefix, flat_grads))
    return (outputs.reshape(tokens.shape), input_grads.reshape(tokens.shape), running[0], running[1], running[2], running[3], running[4], running[5])
```

```python
import functools
import math

import jax
import jax.numpy as jnp
from jax import lax
from jax.experimental import pallas as pl
from jax.experimental.pallas import tpu as pltpu
from jax.sharding import PartitionSpec as P

HEADS = 8
EPSILON = 1e-05
MASKED = -1e30
F32 = jnp.float32
BF16 = jnp.bfloat16
TILE_SEQS = 2
FF_CHUNK = 512
VMEM_MOST = 60 * 1024 * 1024


def dot(a, b):
    return jnp.dot(a, b, preferred_element_type=F32)


def dot_t(a, b):
    return lax.dot_general(a, b, (((1,), (1,)), ((), ())), preferred_element_type=F32)


def standardize(values):
    row_mean = jnp.mean(values, axis=-1, keepdims=True)
    centred = values - row_mean
    variance = jnp.mean(centred * centred, axis=-1, keepdims=True)
    inv_std = lax.rsqrt(variance + EPSILON)
    return (centred * inv_std, inv_std)


def norm_back(grad_in, unit_rows, inv_std, gain):
    scaled = grad_in * gain
    row_mean = jnp.mean(scaled, axis=-1, keepdims=True)
    cross_mean = jnp.mean(scaled * unit_rows, axis=-1, keepdims=True)
    return inv_std * (scaled - row_mean - unit_rows * cross_mean)


def fold_rows(values):
    return jnp.sum(values.reshape(-1, 8, values.shape[-1]), axis=0)


def gelu_parts(upper):
    cdf = 0.5 * (1.0 + lax.erf(upper * 0.7071067811865476))
    slope = cdf + upper * jnp.exp(-0.5 * upper * upper) * 0.3989422804014327
    return (upper * cdf, slope)


def pair_halves(rows):
    lanes = lax.broadcasted_iota(jnp.int32, rows.shape, 1)
    half = rows.shape[1] // 2
    zero = jnp.zeros_like(rows)
    return jnp.concatenate(
        [jnp.where(lanes < half, rows, zero), jnp.where(lanes >= half, rows, zero)], axis=0
    )


def head_select(count, width):
    head_of_row = lax.broadcasted_iota(jnp.int32, (HEADS * count, width), 0) // count
    head_of_lane = lax.broadcasted_iota(jnp.int32, (HEADS * count, width), 1) // (width // HEADS)
    return head_of_row == head_of_lane


def per_head(rows, select):
    tiled = jnp.concatenate([rows.astype(F32)] * HEADS, axis=0)
    return jnp.where(select, tiled, 0.0).astype(BF16)


def project_kernel(x_ref, xp_ref, w_ref, gain_ref, q_ref, k_ref, v_ref, kp_ref, vp_ref, n_ref, np_ref, sum_ref):
    width = x_ref.shape[1]
    gain = gain_ref[...]
    normed = (standardize(x_ref[...].astype(F32))[0] * gain).astype(BF16)
    n_ref[...] = normed
    scale = (width // HEADS) ** -0.5
    q_ref[...] = (dot(normed, w_ref[:, :width]).astype(BF16).astype(F32) * scale).astype(BF16)
    for part, out in ((1, k_ref), (2, v_ref)):
        rows = dot(normed, w_ref[:, part * width : (part + 1) * width]).astype(BF16)
        out[...] = rows
        means = jnp.mean(rows.astype(F32).reshape(TILE_SEQS, -1, width), axis=1)
        sum_ref[0, :, (part - 1) * width : part * width] = means.astype(BF16)
    normed_prev = (standardize(xp_ref[...].astype(F32))[0] * gain).astype(BF16)
    np_ref[...] = normed_prev
    kp_ref[...] = dot(normed_prev, w_ref[:, width : 2 * width]).astype(BF16)
    vp_ref[...] = dot(normed_prev, w_ref[:, 2 * width :]).astype(BF16)


def row_spec(rows, width):
    return pl.BlockSpec((rows, width), lambda i: (i, 0))


def whole_spec(shape):
    return pl.BlockSpec(shape, lambda i: (0,) * len(shape))


def params():
    return pltpu.CompilerParams(vmem_limit_bytes=VMEM_MOST)


def project(x, x_prev, w_qkv, gain, span):
    rows, width = x.shape
    tile = TILE_SEQS * span
    low = jax.ShapeDtypeStruct((rows, width), BF16)
    return pl.pallas_call(
        project_kernel,
        grid=(rows // tile,),
        in_specs=[row_spec(tile, width)] * 2 + [whole_spec(w_qkv.shape), whole_spec(gain.shape)],
        out_specs=[row_spec(tile, width)] * 7
        + [pl.BlockSpec((1, TILE_SEQS, 2 * width), lambda i: (i, 0, 0))],
        out_shape=[low] * 7 + [jax.ShapeDtypeStruct((rows // tile, TILE_SEQS, 2 * width), BF16)],
        compiler_params=params(),
        name="project",
    )(x, x_prev, w_qkv, gain)


def attend_kernel(
    span, prefix_ref, block_ref, q_ref, k_ref, v_ref, kp_ref, vp_ref, sums_ref, mixed_ref, prob_ref, psum_ref
):
    width = q_ref.shape[1]
    pair = 2 * width // HEADS
    half = pair // 2
    count = sums_ref.shape[1]
    tile = pl.program_id(0)
    block = block_ref[0]
    select = head_select(count, width)
    unit_pos = lax.broadcasted_iota(jnp.int32, (span, span), 0)
    query_pos = lax.broadcasted_iota(jnp.int32, (span, span), 1)
    sum_id = lax.broadcasted_iota(jnp.int32, (count, span), 0)
    sum_query = lax.broadcasted_iota(jnp.int32, (count, span), 1)
    bias_prev = jnp.where(block >= 1, 0.0, MASKED).astype(F32)
    for s in range(TILE_SEQS):
        prefix = prefix_ref[tile * TILE_SEQS + s]
        start = block * span
        rows = slice(s * span, (s + 1) * span)
        own_ok = (unit_pos <= query_pos) | (start + unit_pos < prefix)
        bias_own = jnp.where(own_ok, 0.0, MASKED)
        sum_ok = (sum_id <= block - 1) | (
            (start + sum_query < prefix) & (sum_id >= block + 1) & ((sum_id + 1) * span <= prefix)
        )
        bias_sum = jnp.where(sum_ok, math.log(span), MASKED)
        queries = q_ref[rows, :]
        keys = jnp.concatenate([kp_ref[rows, :], k_ref[rows, :]], axis=0)
        values_t = jnp.concatenate([vp_ref[rows, :], v_ref[rows, :]], axis=0).T
        sum_keys = per_head(sums_ref[s, :, :width], select)
        sum_values_t = per_head(sums_ref[s, :, width:], select).T
        sum_scores = dot_t(sum_keys, queries)
        mixed_parts = []
        sum_probs = []
        for p in range(HEADS // 2):
            lanes = slice(p * pair, (p + 1) * pair)
            scores = dot_t(keys[:, lanes], pair_halves(queries[:, lanes]))
            probs = []
            for e in range(2):
                h = 2 * p + e
                cols = slice(e * span, (e + 1) * span)
                s_prev = scores[:span, cols]
                s_own = scores[span:, cols] + bias_own
                s_sum = sum_scores[h * count : (h + 1) * count] + bias_sum
                most = jnp.maximum(
                    jnp.maximum(
                        jnp.max(s_prev, axis=0, keepdims=True) + bias_prev,
                        jnp.max(s_own, axis=0, keepdims=True),
                    ),
                    jnp.max(s_sum, axis=0, keepdims=True),
                )
                e_prev = jnp.exp(s_prev + (bias_prev - most))
                e_own = jnp.exp(s_own - most)
                e_sum = jnp.exp(s_sum - most)
                total = (
                    jnp.sum(e_prev, axis=0, keepdims=True)
                    + jnp.sum(e_own, axis=0, keepdims=True)
                    + jnp.sum(e_sum, axis=0, keepdims=True)
                )
                inverse = 1.0 / total
                probs.append(
                    jnp.concatenate([e_prev * inverse, e_own * inverse], axis=0).astype(BF16)
                )
                sum_probs.append(e_sum * inverse)
            both = jnp.concatenate(probs, axis=1)
            prob_ref[s, p] = both
            crossed = dot(values_t[lanes, :], both)
            mixed_parts.append(crossed[:half, :span])
            mixed_parts.append(crossed[half:, span:])
        all_sums = jnp.concatenate(sum_probs, axis=0).astype(BF16)
        psum_ref[s] = all_sums
        mixed_t = jnp.concatenate(mixed_parts, axis=0) + dot(sum_values_t, all_sums)
        mixed_ref[rows, :] = mixed_t.T.astype(BF16)


def attend(prefix, block, q, k, v, kp, vp, sums, span):
    rows, width = q.shape
    tile = TILE_SEQS * span
    seqs, count = sums.shape[0], sums.shape[1]
    pairs = HEADS // 2
    return pl.pallas_call(
        functools.partial(attend_kernel, span),
        grid=(rows // tile,),
        in_specs=[pl.BlockSpec(memory_space=pltpu.SMEM)] * 2
        + [row_spec(tile, width)] * 5
        + [pl.BlockSpec((TILE_SEQS, count, 2 * width), lambda i: (i, 0, 0))],
        out_specs=[
            row_spec(tile, width),
            pl.BlockSpec((TILE_SEQS, pairs, 2 * span, 2 * span), lambda i: (i, 0, 0, 0)),
            pl.BlockSpec((TILE_SEQS, HEADS * count, span), lambda i: (i, 0, 0)),
        ],
        out_shape=[
            jax.ShapeDtypeStruct((rows, width), BF16),
            jax.ShapeDtypeStruct((seqs, pairs, 2 * span, 2 * span), BF16),
            jax.ShapeDtypeStruct((seqs, HEADS * count, span), BF16),
        ],
        compiler_params=params(),
        name="attend",
    )(prefix, block, q, k, v, kp, vp, sums)


def feed_kernel(
    x_ref, mixed_ref, g_ref, wo_ref, wu_ref, wd_ref, gain_ref,
    out_ref, gm_ref, gr_ref, gout_ref, gup_ref, gdown_ref, ggain_ref,
    acc_out, acc_up, acc_down, acc_gain,
):
    step = pl.program_id(0)

    @pl.when(step == 0)
    def _():
        acc_out[...] = jnp.zeros_like(acc_out)
        acc_up[...] = jnp.zeros_like(acc_up)
        acc_down[...] = jnp.zeros_like(acc_down)
        acc_gain[...] = jnp.zeros_like(acc_gain)

    gain = gain_ref[...]
    mixed = mixed_ref[...]
    resid = x_ref[...].astype(F32) + dot(mixed, wo_ref[...])
    unit, inv = standardize(resid)
    normed = (unit * gain).astype(BF16)
    normed_t = normed.T
    grad = g_ref[...]
    grad_t = grad.T
    hidden_width = wu_ref.shape[1]
    result = resid
    grad_norm = None
    for c in range(hidden_width // FF_CHUNK):
        cols = slice(c * FF_CHUNK, (c + 1) * FF_CHUNK)
        upper = dot(normed, wu_ref[:, cols])
        grad_hidden = dot_t(grad, wd_ref[cols, :])
        activated, slope = gelu_parts(upper)
        hidden = activated.astype(BF16)
        grad_upper = (grad_hidden * slope).astype(BF16)
        result = result + dot(hidden, wd_ref[cols, :])
        back = dot_t(grad_upper, wu_ref[:, cols])
        grad_norm = back if grad_norm is None else grad_norm + back
        acc_down[:, cols] += dot(grad_t, hidden)
        acc_up[:, cols] += dot(normed_t, grad_upper)
    out_ref[...] = result.astype(BF16)
    acc_gain[...] += fold_rows(grad_norm * unit)
    grad_resid = grad.astype(F32) + norm_back(grad_norm, unit, inv, gain)
    gr_ref[...] = grad_resid
    grad_branch = grad_resid.astype(BF16)
    acc_out[...] += dot(mixed.T, grad_branch)
    gm_ref[...] = dot_t(grad_branch, wo_ref[...]).astype(BF16)

    @pl.when(step == pl.num_programs(0) - 1)
    def _():
        gout_ref[...] = acc_out[...].astype(BF16)
        gup_ref[...] = acc_up[...].astype(BF16)
        gdown_ref[...] = acc_down[...].astype(BF16)
        ggain_ref[...] = acc_gain[...]


def feed(x, mixed, grad, w_out, w_up, w_down, gain, tile):
    rows, width = x.shape
    hidden = w_up.shape[1]
    wide = (width, hidden)
    square = (width, width)
    return pl.pallas_call(
        feed_kernel,
        grid=(rows // tile,),
        in_specs=[row_spec(tile, width)] * 3
        + [whole_spec(w_out.shape), whole_spec(w_up.shape), whole_spec(w_down.shape), whole_spec(gain.shape)],
        out_specs=[row_spec(tile, width)] * 3
        + [whole_spec(square), whole_spec(wide), whole_spec(wide), whole_spec((8, width))],
        out_shape=[
            jax.ShapeDtypeStruct((rows, width), BF16),
            jax.ShapeDtypeStruct((rows, width), BF16),
            jax.ShapeDtypeStruct((rows, width), F32),
            jax.ShapeDtypeStruct(square, BF16),
            jax.ShapeDtypeStruct(wide, BF16),
            jax.ShapeDtypeStruct(wide, BF16),
            jax.ShapeDtypeStruct((8, width), F32),
        ],
        scratch_shapes=[
            pltpu.VMEM(square, F32),
            pltpu.VMEM(wide, F32),
            pltpu.VMEM(wide, F32),
            pltpu.VMEM((8, width), F32),
        ],
        compiler_params=params(),
        name="feed",
    )(x, mixed, grad, w_out, w_up, w_down, gain)


def return_kernel(
    span, q_ref, k_ref, v_ref, kp_ref, vp_ref, sums_ref, gm_ref, prob_ref, psum_ref, n_ref, np_ref, nsum_ref, w_ref,
    gn_ref, gp_ref, gs_ref, gqkv_ref, acc,
):
    width = q_ref.shape[1]
    pair = 2 * width // HEADS
    half = pair // 2
    count = sums_ref.shape[1]
    scale = half ** -0.5
    step = pl.program_id(0)
    select = head_select(count, width)

    @pl.when(step == 0)
    def _():
        acc[...] = jnp.zeros_like(acc)

    own = []
    before = []
    shared = []
    for s in range(TILE_SEQS):
        rows = slice(s * span, (s + 1) * span)
        queries = q_ref[rows, :]
        grad_mixed = gm_ref[rows, :]
        keys_t = jnp.concatenate([kp_ref[rows, :], k_ref[rows, :]], axis=0).T
        values = jnp.concatenate([vp_ref[rows, :], v_ref[rows, :]], axis=0)
        sum_keys_t = per_head(sums_ref[s, :, :width], select).T
        sum_values = per_head(sums_ref[s, :, width:], select)
        sum_low = psum_ref[s]
        sum_prob = sum_low.astype(F32)
        sum_moved = sum_prob * dot_t(sum_values, grad_mixed)
        grad_q_parts = []
        grad_k_parts = []
        grad_v_parts = []
        sum_grads = []
        for p in range(HEADS // 2):
            lanes = slice(p * pair, (p + 1) * pair)
            grads2 = pair_halves(grad_mixed[:, lanes])
            grad_prob = dot_t(values[:, lanes], grads2)
            low = prob_ref[s, p]
            prob = low.astype(F32)
            moved = prob * grad_prob
            deltas = jnp.sum(moved, axis=0, keepdims=True)
            sums = []
            for e in range(2):
                h = 2 * p + e
                part = slice(h * count, (h + 1) * count)
                delta = deltas[:, e * span : (e + 1) * span] + jnp.sum(
                    sum_moved[part], axis=0, keepdims=True
                )
                sums.append(delta)
                sum_grads.append(sum_moved[part] - sum_prob[part] * delta)
            grad_scores = (moved - prob * jnp.concatenate(sums, axis=1)).astype(BF16)
            grad_k_parts.append(dot(grad_scores, pair_halves(queries[:, lanes])))
            grad_v_parts.append(dot(low, grads2))
            crossed = dot(keys_t[lanes, :], grad_scores)
            grad_q_parts.append(crossed[:half, :span])
            grad_q_parts.append(crossed[half:, span:])
        sum_scores_grad = jnp.concatenate(sum_grads, axis=0).astype(BF16)
        grad_q = jnp.concatenate(grad_q_parts, axis=0) + dot(sum_keys_t, sum_scores_grad)
        grad_q = (grad_q.T * scale).astype(BF16)
        grad_k = jnp.concatenate(grad_k_parts, axis=1).astype(BF16)
        grad_v = jnp.concatenate(grad_v_parts, axis=1).astype(BF16)
        own.append(jnp.concatenate([grad_q, grad_k[span:], grad_v[span:]], axis=1))
        before.append(jnp.concatenate([grad_k[:span], grad_v[:span]], axis=1))
        wide_k = jnp.where(select, dot(sum_scores_grad, queries), 0.0)
        wide_v = jnp.where(select, dot(sum_low, grad_mixed), 0.0)
        folded_k = jnp.sum(wide_k.reshape(HEADS, count, width), axis=0)
        folded_v = jnp.sum(wide_v.reshape(HEADS, count, width), axis=0)
        shared.append(jnp.concatenate([folded_k, folded_v], axis=1) * (1.0 / span))
    grad_own = jnp.concatenate(own, axis=0)
    grad_before = jnp.concatenate(before, axis=0)
    grad_shared = jnp.concatenate(shared, axis=0).astype(BF16)
    gn_ref[...] = dot_t(grad_own, w_ref[...])
    gp_ref[...] = dot_t(grad_before, w_ref[:, width:]).astype(BF16)
    gs_ref[...] = dot_t(grad_shared, w_ref[:, width:]).reshape(gs_ref.shape).astype(BF16)
    normed_t = n_ref[...].T
    normed_prev_t = np_ref[...].T
    normed_sum_t = nsum_ref[...].reshape(-1, width).T
    acc[:, :width] += dot(normed_t, grad_own[:, :width])
    acc[:, width:] += (
        dot(normed_t, grad_own[:, width:]) + dot(normed_prev_t, grad_before) + dot(normed_sum_t, grad_shared)
    )

    @pl.when(step == pl.num_programs(0) - 1)
    def _():
        gqkv_ref[...] = acc[...].astype(BF16)


def give_back(q, k, v, kp, vp, sums, gm, prob, psum, n, n_prev, n_sum, w_qkv, span):
    rows, width = q.shape
    tile = TILE_SEQS * span
    seqs, count = sums.shape[0], sums.shape[1]
    pairs = HEADS // 2
    return pl.pallas_call(
        functools.partial(return_kernel, span),
        grid=(rows // tile,),
        in_specs=[row_spec(tile, width)] * 5
        + [
            pl.BlockSpec((TILE_SEQS, count, 2 * width), lambda i: (i, 0, 0)),
            row_spec(tile, width),
            pl.BlockSpec((TILE_SEQS, pairs, 2 * span, 2 * span), lambda i: (i, 0, 0, 0)),
            pl.BlockSpec((TILE_SEQS, HEADS * count, span), lambda i: (i, 0, 0)),
            row_spec(tile, width),
            row_spec(tile, width),
            pl.BlockSpec((TILE_SEQS, count, width), lambda i: (i, 0, 0)),
            whole_spec(w_qkv.shape),
        ],
        out_specs=[
            row_spec(tile, width),
            row_spec(tile, width),
            pl.BlockSpec((TILE_SEQS, count, width), lambda i: (i, 0, 0)),
            whole_spec(w_qkv.shape),
        ],
        out_shape=[
            jax.ShapeDtypeStruct((rows, width), F32),
            jax.ShapeDtypeStruct((rows, width), BF16),
            jax.ShapeDtypeStruct((seqs, count, width), BF16),
            jax.ShapeDtypeStruct(w_qkv.shape, BF16),
        ],
        scratch_shapes=[pltpu.VMEM(w_qkv.shape, F32)],
        compiler_params=params(),
        name="give_back",
    )(q, k, v, kp, vp, sums, gm, prob, psum, n, n_prev, n_sum, w_qkv)


def close_kernel(span, x_ref, gn_ref, gb_ref, gs_ref, gr_ref, gain_ref, out_ref, ggain_ref, acc):
    step = pl.program_id(0)
    width = x_ref.shape[1]

    @pl.when(step == 0)
    def _():
        acc[...] = jnp.zeros_like(acc)

    unit, inv = standardize(x_ref[...].astype(F32))
    grad_norm = gn_ref[...] + gb_ref[...].astype(F32)
    lifted = [
        grad_norm[s * span : (s + 1) * span] + gs_ref[s].astype(F32) for s in range(TILE_SEQS)
    ]
    grad_norm = jnp.concatenate(lifted, axis=0)
    acc[...] += fold_rows(grad_norm * unit)
    part = norm_back(grad_norm, unit, inv, gain_ref[...])
    out_ref[...] = (gr_ref[...] + part).astype(BF16)

    @pl.when(step == pl.num_programs(0) - 1)
    def _():
        ggain_ref[...] = acc[...]


def close(x, gn, gb, gs, gr, gain, span):
    rows, width = x.shape
    tile = TILE_SEQS * span
    return pl.pallas_call(
        functools.partial(close_kernel, span),
        grid=(rows // tile,),
        in_specs=[row_spec(tile, width)] * 3
        + [pl.BlockSpec((TILE_SEQS, 1, width), lambda i: (i, 0, 0)), row_spec(tile, width), whole_spec(gain.shape)],
        out_specs=[row_spec(tile, width), whole_spec((8, width))],
        out_shape=[jax.ShapeDtypeStruct((rows, width), BF16), jax.ShapeDtypeStruct((8, width), F32)],
        scratch_shapes=[pltpu.VMEM((8, width), F32)],
        compiler_params=params(),
        name="close",
    )(x, gn, gb, gs, gr, gain)


def fetch(shard):
    return lax.all_gather(lax.all_gather(shard, "ctx", axis=1, tiled=True), "dp", axis=0, tiled=True)


def reduce_weight(partial, row_axis):
    columns = lax.psum_scatter(partial, "ctx", scatter_dimension=1 - row_axis, tiled=True)
    return lax.psum_scatter(columns, "dp", scatter_dimension=row_axis, tiled=True).astype(F32)


def shards(tokens, prefix, w_qkv, w_out, w_up, w_down, gain_one, gain_two, cotangent):
    span, width = tokens.shape[2], tokens.shape[3]
    count = lax.axis_size("ctx")
    x = tokens.reshape(-1, width)
    grad = cotangent.reshape(-1, width)
    tile = TILE_SEQS * span
    block = lax.axis_index("ctx").reshape(1).astype(jnp.int32)
    x_prev = lax.ppermute(x, "ctx", [(i, i + 1) for i in range(count - 1)])
    gain1 = lax.all_gather(gain_one, "ctx", axis=0, tiled=True).astype(F32).reshape(1, width)
    gain2 = lax.all_gather(gain_two, "ctx", axis=0, tiled=True).astype(F32).reshape(1, width)
    wq, wo, wu, wd = (fetch(w) for w in (w_qkv, w_out, w_up, w_down))
    q, k, v, kp, vp, n, n_prev, own_sums = project(x, x_prev, wq, gain1, span)
    own_sums = own_sums.reshape(-1, 2 * width)
    n_sum = jnp.sum(n.reshape(-1, span, width).astype(F32), axis=1).astype(BF16)
    everything = lax.all_gather(jnp.concatenate([own_sums, n_sum], axis=1), "ctx", axis=0, tiled=False)
    everything = jnp.transpose(everything, (1, 0, 2))
    sums, n_sums = everything[:, :, : 2 * width], everything[:, :, 2 * width :]
    mixed, prob, psum = attend(prefix.reshape(-1), block, q, k, v, kp, vp, sums, span)
    out, gm, gr, gout, gup, gdown, ggain2 = feed(x, mixed, grad, wo, wu, wd, gain2, tile)
    gn, gp, gs, gqkv = give_back(q, k, v, kp, vp, sums, gm, prob, psum, n, n_prev, n_sums, wq, span)
    gb = lax.ppermute(gp, "ctx", [(i, i - 1) for i in range(1, count)])
    gs_own = lax.psum_scatter(gs, "ctx", scatter_dimension=1, tiled=True)
    input_grad, ggain1 = close(x, gn, gb, gs_own, gr, gain1, span)
    gains = jnp.concatenate([jnp.sum(ggain1, axis=0), jnp.sum(ggain2, axis=0)]).reshape(2, width)
    gains = lax.psum(gains, "dp")
    gains = lax.psum_scatter(gains, "ctx", scatter_dimension=1, tiled=True)
    return (
        out.reshape(tokens.shape),
        input_grad.reshape(tokens.shape),
        reduce_weight(gqkv, 0),
        reduce_weight(gout, 0),
        reduce_weight(gup, 0),
        reduce_weight(gdown, 1).T,
        gains[0],
        gains[1],
    )


def solution(mesh):
    rows = P(None, "dp", "ctx", None)
    both = P("dp", "ctx")
    return jax.shard_map(
        shards,
        mesh=mesh,
        in_specs=(rows, P(None, "dp"), both, both, both, both, P("ctx"), P("ctx"), rows),
        out_specs=(rows, rows, both, both, both, both, P("ctx"), P("ctx")),
        check_vma=False,
    )
```

```python
import functools
import math

import jax
import jax.numpy as jnp
from jax import lax
from jax.experimental import pallas as pl
from jax.experimental.pallas import tpu as pltpu
from jax.sharding import PartitionSpec as P

HEADS = 8
EPSILON = 1e-05
MASKED = -1e30
F32 = jnp.float32
BF16 = jnp.bfloat16
TILE_SEQS = 2
FF_CHUNK = 512
VMEM_MOST = 60 * 1024 * 1024

MESH = pl.DeviceIdType.MESH
FLIPS = 8


def place():
    depth, spot = lax.axis_index("dp"), lax.axis_index("ctx")
    return depth, spot, (spot % 2, (spot // 2) % 2, spot // 4)


def flipped(bits, flip):
    out = 0
    for i, bit in enumerate(bits):
        out = out + ((1 - bit) if (flip >> i) & 1 else bit) * (1 << i)
    return out


def spot_of(depths, turn, flip):
    depth, _, bits = place()
    return lax.rem(depth + turn, depths), flipped(bits, flip)


def greet(depths):
    barrier = pltpu.get_barrier_semaphore()
    peers = [(turn, 0) for turn in range(1, depths)] + [(0, 1), (0, 2), (0, 4)]
    for turn, flip in peers:
        pl.semaphore_signal(barrier, inc=1, device_id=spot_of(depths, turn, flip), device_id_type=MESH)
    pl.semaphore_wait(barrier, len(peers))


class Gather:
    def __init__(self, depths, own, full, send, recv):
        self.depths, self.own, self.full, self.send, self.recv = depths, own, full, send, recv
        self.sent = []

    def block(self, turn, flip):
        return self.full.at[spot_of(self.depths, turn, flip)]

    def push(self, turn, flip, to_turn, to_flip):
        there = ((turn - to_turn) % self.depths) * FLIPS + (flip ^ to_flip)
        source = self.own if (turn, flip) == (0, 0) else self.block(turn, flip)
        copy = pltpu.make_async_remote_copy(
            src_ref=source,
            dst_ref=self.block(turn, flip),
            send_sem=self.send.at[len(self.sent)],
            recv_sem=self.recv.at[there],
            device_id=spot_of(self.depths, to_turn, to_flip),
            device_id_type=MESH,
        )
        copy.start()
        self.sent.append(copy)

    def arrive(self, turn, flip):
        pltpu.make_async_remote_copy(
            src_ref=self.block(turn, flip),
            dst_ref=self.block(turn, flip),
            send_sem=self.send.at[0],
            recv_sem=self.recv.at[turn * FLIPS + flip],
            device_id=spot_of(self.depths, 0, 1),
            device_id_type=MESH,
        ).wait_recv()

    def begin(self, keep):
        self.keep = pltpu.make_async_copy(self.own, self.block(0, 0), keep)
        self.keep.start()
        for turn in range(1, self.depths):
            self.push(0, 0, turn, 0)
        for flip in (2, 4, 1):
            self.push(0, 0, 0, flip)

    def spread(self):
        for turn in range(1, self.depths):
            self.arrive(turn, 0)
            for flip in (2, 4, 1):
                self.push(turn, 0, 0, flip)

    def cross(self):
        for turn in range(self.depths):
            self.arrive(turn, 2)
            if turn < self.depths // 2:
                self.push(turn, 2, 0, 4)
            self.push(turn, 2, 0, 1)
            self.arrive(turn, 4)
            if turn >= self.depths // 2:
                self.push(turn, 4, 0, 2)
            self.push(turn, 4, 0, 1)

    def hand_over(self):
        for turn in range(self.depths):
            self.arrive(turn, 6)
            self.push(turn, 6, 0, 1)

    def complete(self):
        for turn in range(self.depths):
            for flip in (1, 3, 5, 7):
                self.arrive(turn, flip)
        for copy in self.sent:
            copy.wait_send()
        self.keep.wait()


def gather_kernel(depths, *refs):
    count = len(refs) // 2 - 1
    owns, fulls = refs[:count], refs[count : 2 * count]
    send, recv, keep = refs[2 * count :]
    greet(depths)
    moves = [Gather(depths, owns[a], fulls[a], send.at[a], recv.at[a]) for a in range(count)]
    for a, move in enumerate(moves):
        move.begin(keep.at[a])
    for move in moves:
        move.spread()
    for move in moves:
        move.cross()
    for move in moves:
        move.hand_over()
    for move in moves:
        move.complete()


def gather_blocks(blocks, depths):
    total = depths * FLIPS
    return pl.pallas_call(
        functools.partial(gather_kernel, depths),
        in_specs=[pl.BlockSpec(memory_space=pltpu.VMEM)] * len(blocks),
        out_specs=[pl.BlockSpec(memory_space=pl.ANY)] * len(blocks),
        out_shape=[jax.ShapeDtypeStruct((depths, FLIPS) + b.shape, b.dtype) for b in blocks],
        scratch_shapes=[
            pltpu.SemaphoreType.DMA((len(blocks), total)),
            pltpu.SemaphoreType.DMA((len(blocks), total)),
            pltpu.SemaphoreType.DMA((len(blocks),)),
        ],
        compiler_params=pltpu.CompilerParams(collective_id=0, has_side_effects=True, vmem_limit_bytes=VMEM_MOST),
        name="gather",
    )(*blocks)


class Scatter:
    def __init__(self, depths, part, mate, total, near, far, send, recv):
        self.depths, self.part, self.mate, self.total = depths, part, mate, total
        self.near, self.far, self.send, self.recv = near, far, send, recv
        self.sent = []

    def block(self, turn, flip):
        return self.part.at[spot_of(self.depths, turn, flip)]

    def push(self, source, target, slot, to_turn, to_flip):
        copy = pltpu.make_async_remote_copy(
            src_ref=source,
            dst_ref=target,
            send_sem=self.send.at[len(self.sent)],
            recv_sem=self.recv.at[slot],
            device_id=spot_of(self.depths, to_turn, to_flip),
            device_id_type=MESH,
        )
        copy.start()
        self.sent.append(copy)

    def arrive(self, target, slot):
        pltpu.make_async_remote_copy(
            src_ref=target,
            dst_ref=target,
            send_sem=self.send.at[0],
            recv_sem=self.recv.at[slot],
            device_id=spot_of(self.depths, 0, 1),
            device_id_type=MESH,
        ).wait_recv()

    def begin(self):
        for flip in (6, 2, 4, 0):
            for turn in range(self.depths):
                at = (flip // 2, turn)
                self.push(self.block(turn, flip ^ 1), self.mate.at[at], flip // 2 * self.depths + turn, 0, 1)

    def fold(self, turn, flip):
        self.arrive(self.mate.at[flip // 2, turn], flip // 2 * self.depths + turn)
        mine = self.block(turn, flip)[...].astype(F32)
        self.total[flip // 2, turn] = (mine + self.mate[flip // 2, turn].astype(F32)).astype(BF16)

    def cross(self):
        base = 4 * self.depths
        for turn in range(self.depths):
            self.fold(turn, 6)
            by = 2 if turn < self.depths // 2 else 4
            self.push(self.total.at[3, turn], self.near.at[turn], base + turn, 0, by)

    def spread(self):
        base = 4 * self.depths
        late = 5 * self.depths
        for turn in range(self.depths):
            self.fold(turn, 2)
            self.fold(turn, 4)
            via = 2 if turn < self.depths // 2 else 1
            self.arrive(self.near.at[turn], base + turn)
            self.total[via, turn] = (self.total[via, turn].astype(F32) + self.near[turn].astype(F32)).astype(BF16)
            self.push(self.total.at[1, turn], self.far.at[0, turn], late + turn, 0, 2)
            self.push(self.total.at[2, turn], self.far.at[1, turn], late + self.depths + turn, 0, 4)

    def climb(self):
        late = 5 * self.depths
        last = 7 * self.depths
        for turn in [*range(1, self.depths), 0]:
            self.fold(turn, 0)
            self.arrive(self.far.at[0, turn], late + turn)
            self.arrive(self.far.at[1, turn], late + self.depths + turn)
            self.total[0, turn] = (
                self.total[0, turn].astype(F32) + self.far[0, turn].astype(F32) + self.far[1, turn].astype(F32)
            ).astype(BF16)
            if turn:
                back = self.depths - turn
                self.push(self.total.at[0, turn], self.far.at[2, back], last + back, turn, 0)

    def finish(self):
        last = 7 * self.depths
        out = self.total[0, 0].astype(F32)
        for turn in range(1, self.depths):
            self.arrive(self.far.at[2, turn], last + turn)
            out = out + self.far[2, turn].astype(F32)
        for copy in self.sent:
            copy.wait_send()
        return out


def scatter_scratch(block, depths):
    return [
        pltpu.VMEM((4, depths) + block, BF16),
        pltpu.VMEM((4, depths) + block, BF16),
        pltpu.VMEM((depths,) + block, BF16),
        pltpu.VMEM((3, depths) + block, BF16),
    ]


def scatter_kernel(depths, count, *refs):
    parts, outs = refs[:count], refs[count : 2 * count]
    send, recv = refs[-2:]
    greet(depths)
    moves = []
    for a in range(count):
        mate, total, near, far = refs[2 * count + 4 * a : 2 * count + 4 * a + 4]
        moves.append(Scatter(depths, parts[a], mate, total, near, far, send.at[a], recv.at[a]))
    for move in moves:
        move.begin()
    for move in moves:
        move.cross()
    for move in moves:
        move.spread()
    for move in moves:
        move.climb()
    for a, move in enumerate(moves):
        outs[a][...] = move.finish()


def scatter_blocks(parts, depths):
    count = len(parts)
    scratch = []
    for part in parts:
        scratch += scatter_scratch(part.shape[2:], depths)
    return pl.pallas_call(
        functools.partial(scatter_kernel, depths, count),
        in_specs=[pl.BlockSpec(memory_space=pltpu.VMEM)] * count,
        out_specs=[pl.BlockSpec(memory_space=pltpu.VMEM)] * count,
        out_shape=[jax.ShapeDtypeStruct(p.shape[2:], F32) for p in parts],
        scratch_shapes=scratch
        + [pltpu.SemaphoreType.DMA((count, 8 * depths)), pltpu.SemaphoreType.DMA((count, 8 * depths))],
        compiler_params=pltpu.CompilerParams(collective_id=1, has_side_effects=True, vmem_limit_bytes=VMEM_MOST),
        name="scatter",
    )(*parts)


def dot(a, b):
    return jnp.dot(a, b, preferred_element_type=F32)


def dot_t(a, b):
    return lax.dot_general(a, b, (((1,), (1,)), ((), ())), preferred_element_type=F32)


def standardize(values):
    row_mean = jnp.mean(values, axis=-1, keepdims=True)
    centred = values - row_mean
    variance = jnp.mean(centred * centred, axis=-1, keepdims=True)
    inv_std = lax.rsqrt(variance + EPSILON)
    return (centred * inv_std, inv_std)


def norm_back(grad_in, unit_rows, inv_std, gain):
    scaled = grad_in * gain
    row_mean = jnp.mean(scaled, axis=-1, keepdims=True)
    cross_mean = jnp.mean(scaled * unit_rows, axis=-1, keepdims=True)
    return inv_std * (scaled - row_mean - unit_rows * cross_mean)


def fold_rows(values):
    return jnp.sum(values.reshape(-1, 8, values.shape[-1]), axis=0)


def gelu_parts(upper):
    cdf = 0.5 * (1.0 + lax.erf(upper * 0.7071067811865476))
    slope = cdf + upper * jnp.exp(-0.5 * upper * upper) * 0.3989422804014327
    return (upper * cdf, slope)


def pair_halves(rows):
    lanes = lax.broadcasted_iota(jnp.int32, rows.shape, 1)
    half = rows.shape[1] // 2
    zero = jnp.zeros_like(rows)
    return jnp.concatenate(
        [jnp.where(lanes < half, rows, zero), jnp.where(lanes >= half, rows, zero)], axis=0
    )


def head_select(count, width):
    head_of_row = lax.broadcasted_iota(jnp.int32, (HEADS * count, width), 0) // count
    head_of_lane = lax.broadcasted_iota(jnp.int32, (HEADS * count, width), 1) // (width // HEADS)
    return head_of_row == head_of_lane


def per_head(rows, select):
    tiled = jnp.concatenate([rows.astype(F32)] * HEADS, axis=0)
    return jnp.where(select, tiled, 0.0).astype(BF16)


def rows_of(ref):
    depths, lanes = ref.shape[0], ref.shape[3]
    return jnp.concatenate([ref[d].reshape(-1, lanes) for d in range(depths)], axis=1)


def lanes_of(ref, chunk, along):
    lanes = ref.shape[3]
    take = (lambda i: ref[i]) if along == 0 else (lambda i: ref[:, i])
    if lanes >= FF_CHUNK:
        per = lanes // FF_CHUNK
        cut = slice(chunk % per * FF_CHUNK, (chunk % per + 1) * FF_CHUNK)
        return take(chunk // per).reshape(-1, lanes)[:, cut]
    per = FF_CHUNK // lanes
    return jnp.concatenate([take(i).reshape(-1, lanes) for i in range(chunk * per, (chunk + 1) * per)], axis=1)


def put_blocks(ref, values, rows_along):
    depths, spots, rows, lanes = ref.shape
    for d in range(depths):
        for c in range(spots):
            r, l = (c, d) if rows_along == 1 else (d, c)
            ref[d, c] = values[r * rows : (r + 1) * rows, l * lanes : (l + 1) * lanes].astype(ref.dtype)


def project_kernel(x_ref, xp_ref, w_ref, gain_ref, q_ref, k_ref, v_ref, kp_ref, vp_ref, n_ref, np_ref, sum_ref):
    width = x_ref.shape[1]
    gain = gain_ref[...]
    weight = rows_of(w_ref)
    normed = (standardize(x_ref[...].astype(F32))[0] * gain).astype(BF16)
    n_ref[...] = normed
    scale = (width // HEADS) ** -0.5
    q_ref[...] = (dot_t(normed, weight[:width]).astype(BF16).astype(F32) * scale).astype(BF16)
    for part, out in ((1, k_ref), (2, v_ref)):
        rows = dot_t(normed, weight[part * width : (part + 1) * width]).astype(BF16)
        out[...] = rows
        means = jnp.mean(rows.astype(F32).reshape(TILE_SEQS, -1, width), axis=1)
        sum_ref[0, :, (part - 1) * width : part * width] = means.astype(BF16)
    normed_prev = (standardize(xp_ref[...].astype(F32))[0] * gain).astype(BF16)
    np_ref[...] = normed_prev
    kp_ref[...] = dot_t(normed_prev, weight[width : 2 * width]).astype(BF16)
    vp_ref[...] = dot_t(normed_prev, weight[2 * width :]).astype(BF16)


def row_spec(rows, width):
    return pl.BlockSpec((rows, width), lambda i: (i, 0))


def whole_spec(shape):
    return pl.BlockSpec(shape, lambda i: (0,) * len(shape))


def params():
    return pltpu.CompilerParams(vmem_limit_bytes=VMEM_MOST)


def project(x, x_prev, w_qkv, gain, span):
    rows, width = x.shape
    tile = TILE_SEQS * span
    low = jax.ShapeDtypeStruct((rows, width), BF16)
    return pl.pallas_call(
        project_kernel,
        grid=(rows // tile,),
        in_specs=[row_spec(tile, width)] * 2 + [whole_spec(w_qkv.shape), whole_spec(gain.shape)],
        out_specs=[row_spec(tile, width)] * 7
        + [pl.BlockSpec((1, TILE_SEQS, 2 * width), lambda i: (i, 0, 0))],
        out_shape=[low] * 7 + [jax.ShapeDtypeStruct((rows // tile, TILE_SEQS, 2 * width), BF16)],
        compiler_params=params(),
        name="project",
    )(x, x_prev, w_qkv, gain)


def attend_kernel(
    span, prefix_ref, block_ref, q_ref, k_ref, v_ref, kp_ref, vp_ref, sums_ref, mixed_ref, prob_ref, psum_ref
):
    width = q_ref.shape[1]
    pair = 2 * width // HEADS
    half = pair // 2
    count = sums_ref.shape[1]
    tile = pl.program_id(0)
    block = block_ref[0]
    select = head_select(count, width)
    unit_pos = lax.broadcasted_iota(jnp.int32, (span, span), 0)
    query_pos = lax.broadcasted_iota(jnp.int32, (span, span), 1)
    sum_id = lax.broadcasted_iota(jnp.int32, (count, span), 0)
    sum_query = lax.broadcasted_iota(jnp.int32, (count, span), 1)
    bias_prev = jnp.where(block >= 1, 0.0, MASKED).astype(F32)
    for s in range(TILE_SEQS):
        prefix = prefix_ref[tile * TILE_SEQS + s]
        start = block * span
        rows = slice(s * span, (s + 1) * span)
        own_ok = (unit_pos <= query_pos) | (start + unit_pos < prefix)
        bias_own = jnp.where(own_ok, 0.0, MASKED)
        sum_ok = (sum_id <= block - 1) | (
            (start + sum_query < prefix) & (sum_id >= block + 1) & ((sum_id + 1) * span <= prefix)
        )
        bias_sum = jnp.where(sum_ok, math.log(span), MASKED)
        queries = q_ref[rows, :]
        keys = jnp.concatenate([kp_ref[rows, :], k_ref[rows, :]], axis=0)
        values_t = jnp.concatenate([vp_ref[rows, :], v_ref[rows, :]], axis=0).T
        sum_keys = per_head(sums_ref[s, :, :width], select)
        sum_values_t = per_head(sums_ref[s, :, width:], select).T
        sum_scores = dot_t(sum_keys, queries)
        mixed_parts = []
        sum_probs = []
        for p in range(HEADS // 2):
            lanes = slice(p * pair, (p + 1) * pair)
            scores = dot_t(keys[:, lanes], pair_halves(queries[:, lanes]))
            probs = []
            for e in range(2):
                h = 2 * p + e
                cols = slice(e * span, (e + 1) * span)
                s_prev = scores[:span, cols]
                s_own = scores[span:, cols] + bias_own
                s_sum = sum_scores[h * count : (h + 1) * count] + bias_sum
                most = jnp.maximum(
                    jnp.maximum(
                        jnp.max(s_prev, axis=0, keepdims=True) + bias_prev,
                        jnp.max(s_own, axis=0, keepdims=True),
                    ),
                    jnp.max(s_sum, axis=0, keepdims=True),
                )
                e_prev = jnp.exp(s_prev + (bias_prev - most))
                e_own = jnp.exp(s_own - most)
                e_sum = jnp.exp(s_sum - most)
                total = (
                    jnp.sum(e_prev, axis=0, keepdims=True)
                    + jnp.sum(e_own, axis=0, keepdims=True)
                    + jnp.sum(e_sum, axis=0, keepdims=True)
                )
                inverse = 1.0 / total
                probs.append(
                    jnp.concatenate([e_prev * inverse, e_own * inverse], axis=0).astype(BF16)
                )
                sum_probs.append(e_sum * inverse)
            both = jnp.concatenate(probs, axis=1)
            prob_ref[s, p] = both
            crossed = dot(values_t[lanes, :], both)
            mixed_parts.append(crossed[:half, :span])
            mixed_parts.append(crossed[half:, span:])
        all_sums = jnp.concatenate(sum_probs, axis=0).astype(BF16)
        psum_ref[s] = all_sums
        mixed_t = jnp.concatenate(mixed_parts, axis=0) + dot(sum_values_t, all_sums)
        mixed_ref[rows, :] = mixed_t.T.astype(BF16)


def attend(prefix, block, q, k, v, kp, vp, sums, span):
    rows, width = q.shape
    tile = TILE_SEQS * span
    seqs, count = sums.shape[0], sums.shape[1]
    pairs = HEADS // 2
    return pl.pallas_call(
        functools.partial(attend_kernel, span),
        grid=(rows // tile,),
        in_specs=[pl.BlockSpec(memory_space=pltpu.SMEM)] * 2
        + [row_spec(tile, width)] * 5
        + [pl.BlockSpec((TILE_SEQS, count, 2 * width), lambda i: (i, 0, 0))],
        out_specs=[
            row_spec(tile, width),
            pl.BlockSpec((TILE_SEQS, pairs, 2 * span, 2 * span), lambda i: (i, 0, 0, 0)),
            pl.BlockSpec((TILE_SEQS, HEADS * count, span), lambda i: (i, 0, 0)),
        ],
        out_shape=[
            jax.ShapeDtypeStruct((rows, width), BF16),
            jax.ShapeDtypeStruct((seqs, pairs, 2 * span, 2 * span), BF16),
            jax.ShapeDtypeStruct((seqs, HEADS * count, span), BF16),
        ],
        compiler_params=params(),
        name="attend",
    )(prefix, block, q, k, v, kp, vp, sums)


def feed_kernel(
    x_ref, mixed_ref, g_ref, wo_ref, wu_ref, wd_ref, gain_ref,
    out_ref, gm_ref, gr_ref, gout_ref, gup_ref, gdown_ref, ggain_ref,
    acc_out, acc_up, acc_down, acc_gain,
):
    step = pl.program_id(0)

    @pl.when(step == 0)
    def _():
        acc_out[...] = jnp.zeros_like(acc_out)
        acc_up[...] = jnp.zeros_like(acc_up)
        acc_down[...] = jnp.zeros_like(acc_down)
        acc_gain[...] = jnp.zeros_like(acc_gain)

    gain = gain_ref[...]
    mixed = mixed_ref[...]
    w_out = rows_of(wo_ref)
    resid = x_ref[...].astype(F32) + dot_t(mixed, w_out)
    unit, inv = standardize(resid)
    normed = (unit * gain).astype(BF16)
    normed_t = normed.T
    grad = g_ref[...]
    grad_t = grad.T
    hidden_width = acc_up.shape[1]
    result = resid
    grad_norm = None
    for c in range(hidden_width // FF_CHUNK):
        cols = slice(c * FF_CHUNK, (c + 1) * FF_CHUNK)
        w_up = lanes_of(wu_ref, c, 1)
        w_down = lanes_of(wd_ref, c, 0)
        upper = dot(normed, w_up)
        grad_hidden = dot(grad, w_down)
        activated, slope = gelu_parts(upper)
        hidden = activated.astype(BF16)
        grad_upper = (grad_hidden * slope).astype(BF16)
        result = result + dot_t(hidden, w_down)
        back = dot_t(grad_upper, w_up)
        grad_norm = back if grad_norm is None else grad_norm + back
        acc_down[:, cols] += dot(grad_t, hidden)
        acc_up[:, cols] += dot(normed_t, grad_upper)
    out_ref[...] = result.astype(BF16)
    acc_gain[...] += fold_rows(grad_norm * unit)
    grad_resid = grad.astype(F32) + norm_back(grad_norm, unit, inv, gain)
    gr_ref[...] = grad_resid
    grad_branch = grad_resid.astype(BF16)
    acc_out[...] += dot(grad_branch.T, mixed)
    gm_ref[...] = dot(grad_branch, w_out).astype(BF16)

    @pl.when(step == pl.num_programs(0) - 1)
    def _():
        put_blocks(gout_ref, acc_out, 1)
        put_blocks(gup_ref, acc_up, 0)
        put_blocks(gdown_ref, acc_down, 1)
        ggain_ref[...] = acc_gain[...]


def feed(x, mixed, grad, w_out, w_up, w_down, gain, tile):
    rows, width = x.shape
    hidden = w_up.shape[1] * w_up.shape[3]
    wide = (width, hidden)
    square = (width, width)
    return pl.pallas_call(
        feed_kernel,
        grid=(rows // tile,),
        in_specs=[row_spec(tile, width)] * 3
        + [whole_spec(w_out.shape), whole_spec(w_up.shape), whole_spec(w_down.shape), whole_spec(gain.shape)],
        out_specs=[row_spec(tile, width)] * 3
        + [whole_spec(w_out.shape), whole_spec(w_up.shape), whole_spec(w_down.shape), whole_spec((8, width))],
        out_shape=[
            jax.ShapeDtypeStruct((rows, width), BF16),
            jax.ShapeDtypeStruct((rows, width), BF16),
            jax.ShapeDtypeStruct((rows, width), F32),
            jax.ShapeDtypeStruct(w_out.shape, BF16),
            jax.ShapeDtypeStruct(w_up.shape, BF16),
            jax.ShapeDtypeStruct(w_down.shape, BF16),
            jax.ShapeDtypeStruct((8, width), F32),
        ],
        scratch_shapes=[
            pltpu.VMEM(square, F32),
            pltpu.VMEM(wide, F32),
            pltpu.VMEM(wide, F32),
            pltpu.VMEM((8, width), F32),
        ],
        compiler_params=params(),
        name="feed",
    )(x, mixed, grad, w_out, w_up, w_down, gain)


def return_kernel(
    span, q_ref, k_ref, v_ref, kp_ref, vp_ref, sums_ref, gm_ref, prob_ref, psum_ref, n_ref, np_ref, nsum_ref, w_ref,
    gn_ref, gp_ref, gs_ref, gqkv_ref, acc,
):
    width = q_ref.shape[1]
    pair = 2 * width // HEADS
    half = pair // 2
    count = sums_ref.shape[1]
    scale = half ** -0.5
    step = pl.program_id(0)
    select = head_select(count, width)

    @pl.when(step == 0)
    def _():
        acc[...] = jnp.zeros_like(acc)

    own = []
    before = []
    shared = []
    for s in range(TILE_SEQS):
        rows = slice(s * span, (s + 1) * span)
        queries = q_ref[rows, :]
        grad_mixed = gm_ref[rows, :]
        keys_t = jnp.concatenate([kp_ref[rows, :], k_ref[rows, :]], axis=0).T
        values = jnp.concatenate([vp_ref[rows, :], v_ref[rows, :]], axis=0)
        sum_keys_t = per_head(sums_ref[s, :, :width], select).T
        sum_values = per_head(sums_ref[s, :, width:], select)
        sum_low = psum_ref[s]
        sum_prob = sum_low.astype(F32)
        sum_moved = sum_prob * dot_t(sum_values, grad_mixed)
        grad_q_parts = []
        grad_k_parts = []
        grad_v_parts = []
        sum_grads = []
        for p in range(HEADS // 2):
            lanes = slice(p * pair, (p + 1) * pair)
            grads2 = pair_halves(grad_mixed[:, lanes])
            grad_prob = dot_t(values[:, lanes], grads2)
            low = prob_ref[s, p]
            prob = low.astype(F32)
            moved = prob * grad_prob
            deltas = jnp.sum(moved, axis=0, keepdims=True)
            sums = []
            for e in range(2):
                h = 2 * p + e
                part = slice(h * count, (h + 1) * count)
                delta = deltas[:, e * span : (e + 1) * span] + jnp.sum(
                    sum_moved[part], axis=0, keepdims=True
                )
                sums.append(delta)
                sum_grads.append(sum_moved[part] - sum_prob[part] * delta)
            grad_scores = (moved - prob * jnp.concatenate(sums, axis=1)).astype(BF16)
            grad_k_parts.append(dot(grad_scores, pair_halves(queries[:, lanes])))
            grad_v_parts.append(dot(low, grads2))
            crossed = dot(keys_t[lanes, :], grad_scores)
            grad_q_parts.append(crossed[:half, :span])
            grad_q_parts.append(crossed[half:, span:])
        sum_scores_grad = jnp.concatenate(sum_grads, axis=0).astype(BF16)
        grad_q = jnp.concatenate(grad_q_parts, axis=0) + dot(sum_keys_t, sum_scores_grad)
        grad_q = (grad_q.T * scale).astype(BF16)
        grad_k = jnp.concatenate(grad_k_parts, axis=1).astype(BF16)
        grad_v = jnp.concatenate(grad_v_parts, axis=1).astype(BF16)
        own.append(jnp.concatenate([grad_q, grad_k[span:], grad_v[span:]], axis=1))
        before.append(jnp.concatenate([grad_k[:span], grad_v[:span]], axis=1))
        wide_k = jnp.where(select, dot(sum_scores_grad, queries), 0.0)
        wide_v = jnp.where(select, dot(sum_low, grad_mixed), 0.0)
        folded_k = jnp.sum(wide_k.reshape(HEADS, count, width), axis=0)
        folded_v = jnp.sum(wide_v.reshape(HEADS, count, width), axis=0)
        shared.append(jnp.concatenate([folded_k, folded_v], axis=1) * (1.0 / span))
    grad_own = jnp.concatenate(own, axis=0)
    grad_before = jnp.concatenate(before, axis=0)
    grad_shared = jnp.concatenate(shared, axis=0).astype(BF16)
    weight = rows_of(w_ref)
    gn_ref[...] = dot(grad_own, weight)
    gp_ref[...] = dot(grad_before, weight[width:]).astype(BF16)
    gs_ref[...] = dot(grad_shared, weight[width:]).reshape(gs_ref.shape).astype(BF16)
    normed_t = n_ref[...].T
    normed_prev_t = np_ref[...].T
    normed_sum_t = nsum_ref[...].reshape(-1, width).T
    acc[:, :width] += dot(normed_t, grad_own[:, :width])
    acc[:, width:] += (
        dot(normed_t, grad_own[:, width:]) + dot(normed_prev_t, grad_before) + dot(normed_sum_t, grad_shared)
    )

    @pl.when(step == pl.num_programs(0) - 1)
    def _():
        put_blocks(gqkv_ref, acc[...].astype(BF16).T, 1)


def give_back(q, k, v, kp, vp, sums, gm, prob, psum, n, n_prev, n_sum, w_qkv, span):
    rows, width = q.shape
    tile = TILE_SEQS * span
    seqs, count = sums.shape[0], sums.shape[1]
    pairs = HEADS // 2
    return pl.pallas_call(
        functools.partial(return_kernel, span),
        grid=(rows // tile,),
        in_specs=[row_spec(tile, width)] * 5
        + [
            pl.BlockSpec((TILE_SEQS, count, 2 * width), lambda i: (i, 0, 0)),
            row_spec(tile, width),
            pl.BlockSpec((TILE_SEQS, pairs, 2 * span, 2 * span), lambda i: (i, 0, 0, 0)),
            pl.BlockSpec((TILE_SEQS, HEADS * count, span), lambda i: (i, 0, 0)),
            row_spec(tile, width),
            row_spec(tile, width),
            pl.BlockSpec((TILE_SEQS, count, width), lambda i: (i, 0, 0)),
            whole_spec(w_qkv.shape),
        ],
        out_specs=[
            row_spec(tile, width),
            row_spec(tile, width),
            pl.BlockSpec((TILE_SEQS, count, width), lambda i: (i, 0, 0)),
            whole_spec(w_qkv.shape),
        ],
        out_shape=[
            jax.ShapeDtypeStruct((rows, width), F32),
            jax.ShapeDtypeStruct((rows, width), BF16),
            jax.ShapeDtypeStruct((seqs, count, width), BF16),
            jax.ShapeDtypeStruct(w_qkv.shape, BF16),
        ],
        scratch_shapes=[pltpu.VMEM((width, 3 * width), F32)],
        compiler_params=params(),
        name="give_back",
    )(q, k, v, kp, vp, sums, gm, prob, psum, n, n_prev, n_sum, w_qkv)


def close_kernel(span, x_ref, gn_ref, gb_ref, gs_ref, gr_ref, gain_ref, out_ref, ggain_ref, acc):
    step = pl.program_id(0)
    width = x_ref.shape[1]

    @pl.when(step == 0)
    def _():
        acc[...] = jnp.zeros_like(acc)

    unit, inv = standardize(x_ref[...].astype(F32))
    grad_norm = gn_ref[...] + gb_ref[...].astype(F32)
    lifted = [
        grad_norm[s * span : (s + 1) * span] + gs_ref[s].astype(F32) for s in range(TILE_SEQS)
    ]
    grad_norm = jnp.concatenate(lifted, axis=0)
    acc[...] += fold_rows(grad_norm * unit)
    part = norm_back(grad_norm, unit, inv, gain_ref[...])
    out_ref[...] = (gr_ref[...] + part).astype(BF16)

    @pl.when(step == pl.num_programs(0) - 1)
    def _():
        ggain_ref[...] = acc[...]


def close(x, gn, gb, gs, gr, gain, span):
    rows, width = x.shape
    tile = TILE_SEQS * span
    return pl.pallas_call(
        functools.partial(close_kernel, span),
        grid=(rows // tile,),
        in_specs=[row_spec(tile, width)] * 3
        + [pl.BlockSpec((TILE_SEQS, 1, width), lambda i: (i, 0, 0)), row_spec(tile, width), whole_spec(gain.shape)],
        out_specs=[row_spec(tile, width), whole_spec((8, width))],
        out_shape=[jax.ShapeDtypeStruct((rows, width), BF16), jax.ShapeDtypeStruct((8, width), F32)],
        scratch_shapes=[pltpu.VMEM((8, width), F32)],
        compiler_params=params(),
        name="close",
    )(x, gn, gb, gs, gr, gain)


def fetch(block, rows_along):
    spot, depth = (0, 1) if rows_along == 1 else (1, 0)
    whole = lax.all_gather(lax.all_gather(block, "ctx", axis=spot, tiled=True), "dp", axis=depth, tiled=True)
    return whole[None, None]


def reduce_weight(partial, rows_along):
    spot, depth = (0, 1) if rows_along == 1 else (1, 0)
    columns = lax.psum_scatter(partial[0, 0], "ctx", scatter_dimension=spot, tiled=True)
    return lax.psum_scatter(columns, "dp", scatter_dimension=depth, tiled=True).astype(F32)


def shards(tokens, prefix, w_qkv, w_out, w_up, w_down, gain_one, gain_two, cotangent):
    span, width = tokens.shape[2], tokens.shape[3]
    count = lax.axis_size("ctx")
    x = tokens.reshape(-1, width)
    grad = cotangent.reshape(-1, width)
    tile = TILE_SEQS * span
    block = lax.axis_index("ctx").reshape(1).astype(jnp.int32)
    x_prev = lax.ppermute(x, "ctx", [(i, i + 1) for i in range(count - 1)])
    gain1 = lax.all_gather(gain_one, "ctx", axis=0, tiled=True).astype(F32).reshape(1, width)
    gain2 = lax.all_gather(gain_two, "ctx", axis=0, tiled=True).astype(F32).reshape(1, width)
    depths = lax.axis_size("dp")
    blocks = (w_qkv.T, w_out.T, w_up, w_down.T)
    along = (1, 1, 0, 1)
    direct = count == FLIPS and all(b.shape[0] % 16 == 0 and b.shape[1] % 128 == 0 for b in blocks)
    if direct:
        wq, wo, wu, wd = gather_blocks(blocks, depths)
    else:
        wq, wo, wu, wd = (fetch(b, r) for b, r in zip(blocks, along))
    q, k, v, kp, vp, n, n_prev, own_sums = project(x, x_prev, wq, gain1, span)
    own_sums = own_sums.reshape(-1, 2 * width)
    n_sum = jnp.sum(n.reshape(-1, span, width).astype(F32), axis=1).astype(BF16)
    everything = lax.all_gather(jnp.concatenate([own_sums, n_sum], axis=1), "ctx", axis=0, tiled=False)
    everything = jnp.transpose(everything, (1, 0, 2))
    sums, n_sums = everything[:, :, : 2 * width], everything[:, :, 2 * width :]
    mixed, prob, psum = attend(prefix.reshape(-1), block, q, k, v, kp, vp, sums, span)
    out, gm, gr, gout, gup, gdown, ggain2 = feed(x, mixed, grad, wo, wu, wd, gain2, tile)
    gn, gp, gs, gqkv = give_back(q, k, v, kp, vp, sums, gm, prob, psum, n, n_prev, n_sums, wq, span)
    gb = lax.ppermute(gp, "ctx", [(i, i - 1) for i in range(1, count)])
    gs_own = lax.psum_scatter(gs, "ctx", scatter_dimension=1, tiled=True)
    input_grad, ggain1 = close(x, gn, gb, gs_own, gr, gain1, span)
    gains = jnp.concatenate([jnp.sum(ggain1, axis=0), jnp.sum(ggain2, axis=0)]).reshape(2, width)
    gains = lax.psum(gains, "dp")
    gains = lax.psum_scatter(gains, "ctx", scatter_dimension=1, tiled=True)
    partials = (gqkv, gout, gup, gdown)
    if direct:
        sums_w = scatter_blocks(partials, depths)
    else:
        sums_w = [reduce_weight(p, r) for p, r in zip(partials, along)]
    return (
        out.reshape(tokens.shape),
        input_grad.reshape(tokens.shape),
        sums_w[0].T,
        sums_w[1].T,
        sums_w[2],
        sums_w[3].T,
        gains[0],
        gains[1],
    )


def solution(mesh):
    rows = P(None, "dp", "ctx", None)
    both = P("dp", "ctx")
    return jax.shard_map(
        shards,
        mesh=mesh,
        in_specs=(rows, P(None, "dp"), both, both, both, both, P("ctx"), P("ctx"), rows),
        out_specs=(rows, rows, both, both, both, both, P("ctx"), P("ctx")),
        check_vma=False,
    )
```

```python
import functools
import math

import jax
import jax.numpy as jnp
from jax import lax
from jax.experimental import pallas as pl
from jax.experimental.pallas import tpu as pltpu
from jax.sharding import PartitionSpec as P

HEADS = 8
EPSILON = 1e-05
MASKED = -1e30
F32 = jnp.float32
BF16 = jnp.bfloat16
TILE_SEQS = 2
FF_CHUNK = 512
VMEM_MOST = 60 * 1024 * 1024

MESH = pl.DeviceIdType.MESH
FLIPS = 8


def place():
    depth, spot = lax.axis_index("dp"), lax.axis_index("ctx")
    return depth, spot, (spot % 2, (spot // 2) % 2, spot // 4)


def flipped(bits, flip):
    out = 0
    for i, bit in enumerate(bits):
        out = out + ((1 - bit) if (flip >> i) & 1 else bit) * (1 << i)
    return out


def spot_of(depths, turn, flip):
    depth, _, bits = place()
    return lax.rem(depth + turn, depths), flipped(bits, flip)


def greet(depths):
    barrier = pltpu.get_barrier_semaphore()
    peers = [(turn, 0) for turn in range(1, depths)] + [(0, flip) for flip in range(1, FLIPS)]
    for turn, flip in peers:
        pl.semaphore_signal(barrier, inc=1, device_id=spot_of(depths, turn, flip), device_id_type=MESH)
    pl.semaphore_wait(barrier, len(peers))


class Moves:
    def __init__(self, depths, send, recv):
        self.depths, self.send, self.recv, self.sent = depths, send, recv, 0

    def copy(self, source, target, number, slot, to_turn, to_flip):
        return pltpu.make_async_remote_copy(
            src_ref=source,
            dst_ref=target,
            send_sem=self.send.at[number],
            recv_sem=self.recv.at[slot],
            device_id=spot_of(self.depths, to_turn, to_flip),
            device_id_type=MESH,
        )

    def start(self, source, target, slot, to_turn, to_flip):
        self.copy(source, target, self.sent, slot, to_turn, to_flip).start()
        self.sent += 1

    def landed(self, target, slot):
        self.copy(target, target, 0, slot, 0, 1).wait_recv()

    def drain(self, like):
        for number in range(self.sent):
            self.copy(like, like, number, 0, 0, 1).wait_send()


class Gather(Moves):
    def __init__(self, depths, own, full, send, recv, keep):
        super().__init__(depths, send, recv)
        self.own, self.full, self.keep = own, full, keep

    def block(self, turn, flip):
        return self.full.at[spot_of(self.depths, turn, flip)]

    def push(self, turn, flip, to_turn, to_flip):
        there = ((turn - to_turn) % self.depths) * FLIPS + (flip ^ to_flip)
        source = self.own if (turn, flip) == (0, 0) else self.block(turn, flip)
        self.start(source, self.block(turn, flip), there, to_turn, to_flip)

    def arrive(self, turn, flip):
        self.landed(self.block(turn, flip), turn * FLIPS + flip)

    def begin(self):
        for turn in range(1, self.depths):
            self.push(0, 0, turn, 0)
        for flip in (2, 4, 1):
            self.push(0, 0, 0, flip)
        pltpu.make_async_copy(self.own, self.block(0, 0), self.keep).start()

    def spread(self):
        for turn in range(1, self.depths):
            self.arrive(turn, 0)
            for flip in (2, 4, 1):
                self.push(turn, 0, 0, flip)

    def cross(self):
        for turn in range(self.depths):
            self.arrive(turn, 2)
            if turn < self.depths // 2:
                self.push(turn, 2, 0, 4)
            self.push(turn, 2, 0, 1)
            self.arrive(turn, 4)
            if turn >= self.depths // 2:
                self.push(turn, 4, 0, 2)
            self.push(turn, 4, 0, 1)

    def hand_over(self):
        for turn in range(self.depths):
            self.arrive(turn, 6)
            self.push(turn, 6, 0, 1)

    def complete(self):
        for turn in range(self.depths):
            for flip in (1, 3, 5, 7):
                self.arrive(turn, flip)
        pltpu.make_async_copy(self.own, self.block(0, 0), self.keep).wait()

    def close(self):
        self.drain(self.own)


class Share(Moves):
    def __init__(self, depths, slots, send, recv):
        super().__init__(depths, send, recv)
        self.slots = slots

    def block(self, flip):
        return self.slots.at[spot_of(self.depths, 0, flip)[1]]

    def begin(self):
        for flip in (2, 4, 6, 1):
            self.start(self.block(0), self.block(0), flip, 0, flip)

    def forward(self):
        for flip in (2, 4, 6):
            self.landed(self.block(flip), flip)
            self.start(self.block(flip), self.block(flip), flip ^ 1, 0, 1)

    def complete(self):
        for flip in (1, 3, 5, 7):
            self.landed(self.block(flip), flip)

    def close(self):
        self.drain(self.block(0))


class Scatter(Moves):
    def __init__(self, depths, part, mate, total, near, far, send, recv):
        super().__init__(depths, send, recv)
        self.part, self.mate, self.total, self.near, self.far = part, mate, total, near, far

    def block(self, turn, flip):
        return self.part.at[spot_of(self.depths, turn, flip)]

    push = Moves.start
    arrive = Moves.landed

    def begin(self):
        for flip in (6, 2, 4, 0):
            for turn in range(self.depths):
                at = (flip // 2, turn)
                self.push(self.block(turn, flip ^ 1), self.mate.at[at], flip // 2 * self.depths + turn, 0, 1)

    def fold(self, turn, flip):
        self.arrive(self.mate.at[flip // 2, turn], flip // 2 * self.depths + turn)
        mine = self.block(turn, flip)[...].astype(F32)
        self.total[flip // 2, turn] = (mine + self.mate[flip // 2, turn].astype(F32)).astype(BF16)

    def cross(self):
        base = 4 * self.depths
        for turn in range(self.depths):
            self.fold(turn, 6)
            by = 2 if turn < self.depths // 2 else 4
            self.push(self.total.at[3, turn], self.near.at[turn], base + turn, 0, by)

    def spread(self):
        base = 4 * self.depths
        late = 5 * self.depths
        for turn in range(self.depths):
            self.fold(turn, 2)
            self.fold(turn, 4)
            via = 2 if turn < self.depths // 2 else 1
            self.arrive(self.near.at[turn], base + turn)
            self.total[via, turn] = (self.total[via, turn].astype(F32) + self.near[turn].astype(F32)).astype(BF16)
            self.push(self.total.at[1, turn], self.far.at[0, turn], late + turn, 0, 2)
            self.push(self.total.at[2, turn], self.far.at[1, turn], late + self.depths + turn, 0, 4)

    def climb(self):
        late = 5 * self.depths
        last = 7 * self.depths
        for turn in [*range(1, self.depths), 0]:
            self.fold(turn, 0)
            self.arrive(self.far.at[0, turn], late + turn)
            self.arrive(self.far.at[1, turn], late + self.depths + turn)
            self.total[0, turn] = (
                self.total[0, turn].astype(F32) + self.far[0, turn].astype(F32) + self.far[1, turn].astype(F32)
            ).astype(BF16)
            if turn:
                back = self.depths - turn
                self.push(self.total.at[0, turn], self.far.at[2, back], last + back, turn, 0)

    def finish(self):
        last = 7 * self.depths
        out = self.total[0, 0].astype(F32)
        for turn in range(1, self.depths):
            self.arrive(self.far.at[2, turn], last + turn)
            out = out + self.far[2, turn].astype(F32)
        return out

    def close(self):
        self.drain(self.near.at[0])


def scatter_scratch(block, depths):
    return [
        pltpu.VMEM((4, depths) + block, BF16),
        pltpu.VMEM((4, depths) + block, BF16),
        pltpu.VMEM((depths,) + block, BF16),
        pltpu.VMEM((3, depths) + block, BF16),
    ]


def dot(a, b):
    return jnp.dot(a, b, preferred_element_type=F32)


def dot_t(a, b):
    return lax.dot_general(a, b, (((1,), (1,)), ((), ())), preferred_element_type=F32)


def standardize(values):
    row_mean = jnp.mean(values, axis=-1, keepdims=True)
    centred = values - row_mean
    variance = jnp.mean(centred * centred, axis=-1, keepdims=True)
    inv_std = lax.rsqrt(variance + EPSILON)
    return (centred * inv_std, inv_std)


def norm_back(grad_in, unit_rows, inv_std, gain):
    scaled = grad_in * gain
    row_mean = jnp.mean(scaled, axis=-1, keepdims=True)
    cross_mean = jnp.mean(scaled * unit_rows, axis=-1, keepdims=True)
    return inv_std * (scaled - row_mean - unit_rows * cross_mean)


def fold_rows(values):
    return jnp.sum(values.reshape(-1, 8, values.shape[-1]), axis=0)


def gelu_parts(upper):
    cdf = 0.5 * (1.0 + lax.erf(upper * 0.7071067811865476))
    slope = cdf + upper * jnp.exp(-0.5 * upper * upper) * 0.3989422804014327
    return (upper * cdf, slope)


def pair_halves(rows):
    lanes = lax.broadcasted_iota(jnp.int32, rows.shape, 1)
    half = rows.shape[1] // 2
    zero = jnp.zeros_like(rows)
    return jnp.concatenate(
        [jnp.where(lanes < half, rows, zero), jnp.where(lanes >= half, rows, zero)], axis=0
    )


def head_select(count, width):
    head_of_row = lax.broadcasted_iota(jnp.int32, (HEADS * count, width), 0) // count
    head_of_lane = lax.broadcasted_iota(jnp.int32, (HEADS * count, width), 1) // (width // HEADS)
    return head_of_row == head_of_lane


def per_head(rows, select):
    tiled = jnp.concatenate([rows.astype(F32)] * HEADS, axis=0)
    return jnp.where(select, tiled, 0.0).astype(BF16)


def rows_of(ref):
    depths, lanes = ref.shape[0], ref.shape[3]
    return jnp.concatenate([ref[d].reshape(-1, lanes) for d in range(depths)], axis=1)


def lanes_of(ref, chunk, along):
    lanes = ref.shape[3]
    take = (lambda i: ref[i]) if along == 0 else (lambda i: ref[:, i])
    if lanes >= FF_CHUNK:
        per = lanes // FF_CHUNK
        cut = slice(chunk % per * FF_CHUNK, (chunk % per + 1) * FF_CHUNK)
        return take(chunk // per).reshape(-1, lanes)[:, cut]
    per = FF_CHUNK // lanes
    return jnp.concatenate([take(i).reshape(-1, lanes) for i in range(chunk * per, (chunk + 1) * per)], axis=1)


def put_blocks(ref, values, rows_along):
    depths, spots, rows, lanes = ref.shape
    for d in range(depths):
        for c in range(spots):
            r, l = (c, d) if rows_along == 1 else (d, c)
            ref[d, c] = values[r * rows : (r + 1) * rows, l * lanes : (l + 1) * lanes].astype(ref.dtype)


def project_kernel(x_ref, xp_ref, w_ref, gain_ref, q_ref, k_ref, v_ref, kp_ref, vp_ref, n_ref, np_ref, sum_ref):
    width = x_ref.shape[1]
    gain = gain_ref[...]
    weight = rows_of(w_ref)
    normed = (standardize(x_ref[...].astype(F32))[0] * gain).astype(BF16)
    n_ref[...] = normed
    scale = (width // HEADS) ** -0.5
    q_ref[...] = (dot_t(normed, weight[:width]).astype(BF16).astype(F32) * scale).astype(BF16)
    for part, out in ((1, k_ref), (2, v_ref)):
        rows = dot_t(normed, weight[part * width : (part + 1) * width]).astype(BF16)
        out[...] = rows
        means = jnp.mean(rows.astype(F32).reshape(TILE_SEQS, -1, width), axis=1)
        sum_ref[0, :, (part - 1) * width : part * width] = means.astype(BF16)
    normed_prev = (standardize(xp_ref[...].astype(F32))[0] * gain).astype(BF16)
    np_ref[...] = normed_prev
    kp_ref[...] = dot_t(normed_prev, weight[width : 2 * width]).astype(BF16)
    vp_ref[...] = dot_t(normed_prev, weight[2 * width :]).astype(BF16)


def row_spec(rows, width):
    return pl.BlockSpec((rows, width), lambda i: (i, 0))


def whole_spec(shape):
    return pl.BlockSpec(shape, lambda i: (0,) * len(shape))


def params():
    return pltpu.CompilerParams(vmem_limit_bytes=VMEM_MOST)


def project(x, x_prev, w_qkv, gain, span):
    rows, width = x.shape
    tile = TILE_SEQS * span
    low = jax.ShapeDtypeStruct((rows, width), BF16)
    return pl.pallas_call(
        project_kernel,
        grid=(rows // tile,),
        in_specs=[row_spec(tile, width)] * 2 + [whole_spec(w_qkv.shape), whole_spec(gain.shape)],
        out_specs=[row_spec(tile, width)] * 7
        + [pl.BlockSpec((1, TILE_SEQS, 2 * width), lambda i: (i, 0, 0))],
        out_shape=[low] * 7 + [jax.ShapeDtypeStruct((rows // tile, TILE_SEQS, 2 * width), BF16)],
        compiler_params=params(),
        name="project",
    )(x, x_prev, w_qkv, gain)


def attend_one(span, block, prefix, queries, keys, values, sums, keep_prob):
    width = queries.shape[1]
    pair = 2 * width // HEADS
    half = pair // 2
    count = sums.shape[0]
    select = head_select(count, width)
    unit_pos = lax.broadcasted_iota(jnp.int32, (span, span), 0)
    query_pos = lax.broadcasted_iota(jnp.int32, (span, span), 1)
    sum_id = lax.broadcasted_iota(jnp.int32, (count, span), 0)
    sum_query = lax.broadcasted_iota(jnp.int32, (count, span), 1)
    bias_prev = jnp.where(block >= 1, 0.0, MASKED).astype(F32)
    start = block * span
    own_ok = (unit_pos <= query_pos) | (start + unit_pos < prefix)
    bias_own = jnp.where(own_ok, 0.0, MASKED)
    sum_ok = (sum_id <= block - 1) | (
        (start + sum_query < prefix) & (sum_id >= block + 1) & ((sum_id + 1) * span <= prefix)
    )
    bias_sum = jnp.where(sum_ok, math.log(span), MASKED)
    values_t = values.T
    sum_keys = per_head(sums[:, :width], select)
    sum_values_t = per_head(sums[:, width : 2 * width], select).T
    sum_scores = dot_t(sum_keys, queries)
    mixed_parts = []
    sum_probs = []
    for p in range(HEADS // 2):
        lanes = slice(p * pair, (p + 1) * pair)
        scores = dot_t(keys[:, lanes], pair_halves(queries[:, lanes]))
        probs = []
        for e in range(2):
            h = 2 * p + e
            cols = slice(e * span, (e + 1) * span)
            s_prev = scores[:span, cols]
            s_own = scores[span:, cols] + bias_own
            s_sum = sum_scores[h * count : (h + 1) * count] + bias_sum
            most = jnp.maximum(
                jnp.maximum(
                    jnp.max(s_prev, axis=0, keepdims=True) + bias_prev,
                    jnp.max(s_own, axis=0, keepdims=True),
                ),
                jnp.max(s_sum, axis=0, keepdims=True),
            )
            e_prev = jnp.exp(s_prev + (bias_prev - most))
            e_own = jnp.exp(s_own - most)
            e_sum = jnp.exp(s_sum - most)
            total = (
                jnp.sum(e_prev, axis=0, keepdims=True)
                + jnp.sum(e_own, axis=0, keepdims=True)
                + jnp.sum(e_sum, axis=0, keepdims=True)
            )
            inverse = 1.0 / total
            probs.append(jnp.concatenate([e_prev * inverse, e_own * inverse], axis=0).astype(BF16))
            sum_probs.append(e_sum * inverse)
        both = jnp.concatenate(probs, axis=1)
        keep_prob(p, both)
        crossed = dot(values_t[lanes, :], both)
        mixed_parts.append(crossed[:half, :span])
        mixed_parts.append(crossed[half:, span:])
    all_sums = jnp.concatenate(sum_probs, axis=0).astype(BF16)
    mixed_t = jnp.concatenate(mixed_parts, axis=0) + dot(sum_values_t, all_sums)
    return mixed_t.T.astype(BF16), all_sums


def attend_kernel(
    span, prefix_ref, block_ref, q_ref, k_ref, v_ref, kp_ref, vp_ref, sums_ref, mixed_ref, prob_ref, psum_ref
):
    for s in range(TILE_SEQS):
        rows = slice(s * span, (s + 1) * span)

        def keep_prob(p, both, s=s):
            prob_ref[s, p] = both

        mixed, all_sums = attend_one(
            span,
            block_ref[0],
            prefix_ref[pl.program_id(0) * TILE_SEQS + s],
            q_ref[rows, :],
            jnp.concatenate([kp_ref[rows, :], k_ref[rows, :]], axis=0),
            jnp.concatenate([vp_ref[rows, :], v_ref[rows, :]], axis=0),
            sums_ref[s],
            keep_prob,
        )
        mixed_ref[rows, :] = mixed
        psum_ref[s] = all_sums


def attend(prefix, block, q, k, v, kp, vp, sums, span):
    rows, width = q.shape
    tile = TILE_SEQS * span
    seqs, count = sums.shape[0], sums.shape[1]
    pairs = HEADS // 2
    return pl.pallas_call(
        functools.partial(attend_kernel, span),
        grid=(rows // tile,),
        in_specs=[pl.BlockSpec(memory_space=pltpu.SMEM)] * 2
        + [row_spec(tile, width)] * 5
        + [pl.BlockSpec((TILE_SEQS, count, 2 * width), lambda i: (i, 0, 0))],
        out_specs=[
            row_spec(tile, width),
            pl.BlockSpec((TILE_SEQS, pairs, 2 * span, 2 * span), lambda i: (i, 0, 0, 0)),
            pl.BlockSpec((TILE_SEQS, HEADS * count, span), lambda i: (i, 0, 0)),
        ],
        out_shape=[
            jax.ShapeDtypeStruct((rows, width), BF16),
            jax.ShapeDtypeStruct((seqs, pairs, 2 * span, 2 * span), BF16),
            jax.ShapeDtypeStruct((seqs, HEADS * count, span), BF16),
        ],
        compiler_params=params(),
        name="attend",
    )(prefix, block, q, k, v, kp, vp, sums)


def feed_kernel(
    x_ref, mixed_ref, g_ref, wo_ref, wu_ref, wd_ref, gain_ref,
    out_ref, gm_ref, gr_ref, gout_ref, gup_ref, gdown_ref, ggain_ref,
    acc_out, acc_up, acc_down, acc_gain,
):
    step = pl.program_id(0)

    @pl.when(step == 0)
    def _():
        acc_out[...] = jnp.zeros_like(acc_out)
        acc_up[...] = jnp.zeros_like(acc_up)
        acc_down[...] = jnp.zeros_like(acc_down)
        acc_gain[...] = jnp.zeros_like(acc_gain)

    gain = gain_ref[...]
    mixed = mixed_ref[...]
    w_out = rows_of(wo_ref)
    resid = x_ref[...].astype(F32) + dot_t(mixed, w_out)
    unit, inv = standardize(resid)
    normed = (unit * gain).astype(BF16)
    normed_t = normed.T
    grad = g_ref[...]
    grad_t = grad.T
    hidden_width = acc_up.shape[1]
    result = resid
    grad_norm = None
    for c in range(hidden_width // FF_CHUNK):
        cols = slice(c * FF_CHUNK, (c + 1) * FF_CHUNK)
        w_up = lanes_of(wu_ref, c, 1)
        w_down = lanes_of(wd_ref, c, 0)
        upper = dot(normed, w_up)
        grad_hidden = dot(grad, w_down)
        activated, slope = gelu_parts(upper)
        hidden = activated.astype(BF16)
        grad_upper = (grad_hidden * slope).astype(BF16)
        result = result + dot_t(hidden, w_down)
        back = dot_t(grad_upper, w_up)
        grad_norm = back if grad_norm is None else grad_norm + back
        acc_down[:, cols] += dot(grad_t, hidden)
        acc_up[:, cols] += dot(normed_t, grad_upper)
    out_ref[...] = result.astype(BF16)
    acc_gain[...] += fold_rows(grad_norm * unit)
    grad_resid = grad.astype(F32) + norm_back(grad_norm, unit, inv, gain)
    gr_ref[...] = grad_resid
    grad_branch = grad_resid.astype(BF16)
    acc_out[...] += dot(grad_branch.T, mixed)
    gm_ref[...] = dot(grad_branch, w_out).astype(BF16)

    @pl.when(step == pl.num_programs(0) - 1)
    def _():
        put_blocks(gout_ref, acc_out, 1)
        put_blocks(gup_ref, acc_up, 0)
        put_blocks(gdown_ref, acc_down, 1)
        ggain_ref[...] = acc_gain[...]


def feed(x, mixed, grad, w_out, w_up, w_down, gain, tile):
    rows, width = x.shape
    hidden = w_up.shape[1] * w_up.shape[3]
    wide = (width, hidden)
    square = (width, width)
    return pl.pallas_call(
        feed_kernel,
        grid=(rows // tile,),
        in_specs=[row_spec(tile, width)] * 3
        + [whole_spec(w_out.shape), whole_spec(w_up.shape), whole_spec(w_down.shape), whole_spec(gain.shape)],
        out_specs=[row_spec(tile, width)] * 3
        + [whole_spec(w_out.shape), whole_spec(w_up.shape), whole_spec(w_down.shape), whole_spec((8, width))],
        out_shape=[
            jax.ShapeDtypeStruct((rows, width), BF16),
            jax.ShapeDtypeStruct((rows, width), BF16),
            jax.ShapeDtypeStruct((rows, width), F32),
            jax.ShapeDtypeStruct(w_out.shape, BF16),
            jax.ShapeDtypeStruct(w_up.shape, BF16),
            jax.ShapeDtypeStruct(w_down.shape, BF16),
            jax.ShapeDtypeStruct((8, width), F32),
        ],
        scratch_shapes=[
            pltpu.VMEM(square, F32),
            pltpu.VMEM(wide, F32),
            pltpu.VMEM(wide, F32),
            pltpu.VMEM((8, width), F32),
        ],
        compiler_params=params(),
        name="feed",
    )(x, mixed, grad, w_out, w_up, w_down, gain)


def return_one(span, queries, keys, values, sums, grad_mixed, prob_at, sum_low):
    width = queries.shape[1]
    pair = 2 * width // HEADS
    half = pair // 2
    count = sums.shape[0]
    scale = half ** -0.5
    select = head_select(count, width)
    keys_t = keys.T
    sum_keys_t = per_head(sums[:, :width], select).T
    sum_values = per_head(sums[:, width : 2 * width], select)
    sum_prob = sum_low.astype(F32)
    sum_moved = sum_prob * dot_t(sum_values, grad_mixed)
    grad_q_parts = []
    grad_k_parts = []
    grad_v_parts = []
    sum_grads = []
    for p in range(HEADS // 2):
        lanes = slice(p * pair, (p + 1) * pair)
        grads2 = pair_halves(grad_mixed[:, lanes])
        grad_prob = dot_t(values[:, lanes], grads2)
        low = prob_at(p)
        prob = low.astype(F32)
        moved = prob * grad_prob
        deltas = jnp.sum(moved, axis=0, keepdims=True)
        sums_of = []
        for e in range(2):
            h = 2 * p + e
            part = slice(h * count, (h + 1) * count)
            delta = deltas[:, e * span : (e + 1) * span] + jnp.sum(sum_moved[part], axis=0, keepdims=True)
            sums_of.append(delta)
            sum_grads.append(sum_moved[part] - sum_prob[part] * delta)
        grad_scores = (moved - prob * jnp.concatenate(sums_of, axis=1)).astype(BF16)
        grad_k_parts.append(dot(grad_scores, pair_halves(queries[:, lanes])))
        grad_v_parts.append(dot(low, grads2))
        crossed = dot(keys_t[lanes, :], grad_scores)
        grad_q_parts.append(crossed[:half, :span])
        grad_q_parts.append(crossed[half:, span:])
    sum_scores_grad = jnp.concatenate(sum_grads, axis=0).astype(BF16)
    grad_q = jnp.concatenate(grad_q_parts, axis=0) + dot(sum_keys_t, sum_scores_grad)
    grad_q = (grad_q.T * scale).astype(BF16)
    grad_k = jnp.concatenate(grad_k_parts, axis=1).astype(BF16)
    grad_v = jnp.concatenate(grad_v_parts, axis=1).astype(BF16)
    wide_k = jnp.where(select, dot(sum_scores_grad, queries), 0.0)
    wide_v = jnp.where(select, dot(sum_low, grad_mixed), 0.0)
    folded_k = jnp.sum(wide_k.reshape(HEADS, count, width), axis=0)
    folded_v = jnp.sum(wide_v.reshape(HEADS, count, width), axis=0)
    return (
        jnp.concatenate([grad_q, grad_k[span:], grad_v[span:]], axis=1),
        jnp.concatenate([grad_k[:span], grad_v[:span]], axis=1),
        jnp.concatenate([folded_k, folded_v], axis=1) * (1.0 / span),
    )


def return_tile(weight, own, before, shared, normed, normed_prev, normed_sum, acc):
    width = normed.shape[1]
    grad_own = jnp.concatenate(own, axis=0)
    grad_before = jnp.concatenate(before, axis=0)
    grad_shared = jnp.concatenate(shared, axis=0).astype(BF16)
    normed_t = normed.T
    acc[:, :width] += dot(normed_t, grad_own[:, :width])
    acc[:, width:] += (
        dot(normed_t, grad_own[:, width:]) + dot(normed_prev.T, grad_before) + dot(normed_sum.T, grad_shared)
    )
    return dot(grad_own, weight), dot(grad_before, weight[width:]), dot(grad_shared, weight[width:])


def return_kernel(
    span, q_ref, k_ref, v_ref, kp_ref, vp_ref, sums_ref, gm_ref, prob_ref, psum_ref, n_ref, np_ref, nsum_ref, w_ref,
    gn_ref, gp_ref, gs_ref, gqkv_ref, acc,
):
    step = pl.program_id(0)

    @pl.when(step == 0)
    def _():
        acc[...] = jnp.zeros_like(acc)

    parts = []
    for s in range(TILE_SEQS):
        rows = slice(s * span, (s + 1) * span)
        parts.append(
            return_one(
                span,
                q_ref[rows, :],
                jnp.concatenate([kp_ref[rows, :], k_ref[rows, :]], axis=0),
                jnp.concatenate([vp_ref[rows, :], v_ref[rows, :]], axis=0),
                sums_ref[s],
                gm_ref[rows, :],
                lambda p, s=s: prob_ref[s, p],
                psum_ref[s],
            )
        )
    normed_sum = nsum_ref[...].reshape(-1, nsum_ref.shape[2])
    gn, gp, gs = return_tile(rows_of(w_ref), *zip(*parts), n_ref[...], np_ref[...], normed_sum, acc)
    gn_ref[...] = gn
    gp_ref[...] = gp.astype(BF16)
    gs_ref[...] = gs.reshape(gs_ref.shape).astype(BF16)

    @pl.when(step == pl.num_programs(0) - 1)
    def _():
        put_blocks(gqkv_ref, acc[...].astype(BF16).T, 1)


def give_back(q, k, v, kp, vp, sums, gm, prob, psum, n, n_prev, n_sum, w_qkv, span):
    rows, width = q.shape
    tile = TILE_SEQS * span
    seqs, count = sums.shape[0], sums.shape[1]
    pairs = HEADS // 2
    return pl.pallas_call(
        functools.partial(return_kernel, span),
        grid=(rows // tile,),
        in_specs=[row_spec(tile, width)] * 5
        + [
            pl.BlockSpec((TILE_SEQS, count, 2 * width), lambda i: (i, 0, 0)),
            row_spec(tile, width),
            pl.BlockSpec((TILE_SEQS, pairs, 2 * span, 2 * span), lambda i: (i, 0, 0, 0)),
            pl.BlockSpec((TILE_SEQS, HEADS * count, span), lambda i: (i, 0, 0)),
            row_spec(tile, width),
            row_spec(tile, width),
            pl.BlockSpec((TILE_SEQS, count, width), lambda i: (i, 0, 0)),
            whole_spec(w_qkv.shape),
        ],
        out_specs=[
            row_spec(tile, width),
            row_spec(tile, width),
            pl.BlockSpec((TILE_SEQS, count, width), lambda i: (i, 0, 0)),
            whole_spec(w_qkv.shape),
        ],
        out_shape=[
            jax.ShapeDtypeStruct((rows, width), F32),
            jax.ShapeDtypeStruct((rows, width), BF16),
            jax.ShapeDtypeStruct((seqs, count, width), BF16),
            jax.ShapeDtypeStruct(w_qkv.shape, BF16),
        ],
        scratch_shapes=[pltpu.VMEM((width, 3 * width), F32)],
        compiler_params=params(),
        name="give_back",
    )(q, k, v, kp, vp, sums, gm, prob, psum, n, n_prev, n_sum, w_qkv)


def close_kernel(span, x_ref, gn_ref, gb_ref, gs_ref, gr_ref, gain_ref, out_ref, ggain_ref, acc):
    step = pl.program_id(0)
    width = x_ref.shape[1]

    @pl.when(step == 0)
    def _():
        acc[...] = jnp.zeros_like(acc)

    unit, inv = standardize(x_ref[...].astype(F32))
    grad_norm = gn_ref[...] + gb_ref[...].astype(F32)
    lifted = [
        grad_norm[s * span : (s + 1) * span] + gs_ref[s].astype(F32) for s in range(TILE_SEQS)
    ]
    grad_norm = jnp.concatenate(lifted, axis=0)
    acc[...] += fold_rows(grad_norm * unit)
    part = norm_back(grad_norm, unit, inv, gain_ref[...])
    out_ref[...] = (gr_ref[...] + part).astype(BF16)

    @pl.when(step == pl.num_programs(0) - 1)
    def _():
        ggain_ref[...] = acc[...]


def close(x, gn, gb, gs, gr, gain, span):
    rows, width = x.shape
    tile = TILE_SEQS * span
    return pl.pallas_call(
        functools.partial(close_kernel, span),
        grid=(rows // tile,),
        in_specs=[row_spec(tile, width)] * 3
        + [pl.BlockSpec((TILE_SEQS, 1, width), lambda i: (i, 0, 0)), row_spec(tile, width), whole_spec(gain.shape)],
        out_specs=[row_spec(tile, width), whole_spec((8, width))],
        out_shape=[jax.ShapeDtypeStruct((rows, width), BF16), jax.ShapeDtypeStruct((8, width), F32)],
        scratch_shapes=[pltpu.VMEM((8, width), F32)],
        compiler_params=params(),
        name="close",
    )(x, gn, gb, gs, gr, gain)


def in_order(count, seqs):
    row = lax.broadcasted_iota(jnp.int32, (count * seqs, count * seqs), 0)
    col = lax.broadcasted_iota(jnp.int32, (count * seqs, count * seqs), 1)
    return ((col % seqs == row // count) & (col // seqs == row % count)).astype(BF16)


def neighbour(by):
    depth, spot = lax.axis_index("dp"), lax.axis_index("ctx")
    return depth, lax.rem(spot + by + FLIPS, FLIPS)


ENTER_RELAYS = {
    0: ((1, "spread"),),
    1: ((2, "spread"), (3, "spread")),
    2: ((1, "cross"),),
    3: ((2, "cross"),),
    4: ((1, "hand_over"), (3, "cross")),
    5: ((2, "hand_over"),),
    6: ((3, "hand_over"),),
}


def enter_kernel(
    depths, span,
    x_ref, prefix_ref, bq_ref, bo_ref, bu_ref, bd_ref, gain_ref,
    wq_out, wo_out, wu_out, wd_out, gain_out, q_out, k_out, v_out, kp_out, vp_out, n_out, np_out, mixed_out, prob_out,
    sums_out, psum_out,
    xp, wq, gains, q, k, v, kp, vp, n, n_prev, mixed, prob, slots,
    send, recv, keep, gain_send, gain_recv, sum_send, sum_recv, tok_send, tok_recv, out_sem, prob_sem, wq_sem,
):
    rows, width = x_ref.shape
    tile = TILE_SEQS * span
    tiles = rows // tile
    seqs = rows // span
    spot = lax.axis_index("ctx")
    scale = (width // HEADS) ** -0.5
    gathers = [
        Gather(depths, own, full, send.at[a], recv.at[a], keep.at[a])
        for a, (own, full) in enumerate(((bq_ref, wq), (bo_ref, wo_out), (bu_ref, wu_out), (bd_ref, wd_out)))
    ]
    gain_share = Share(depths, gains, gain_send, gain_recv)
    sum_share = Share(depths, slots, sum_send, sum_recv)
    gains[spot] = gain_ref[...]

    @pl.when(spot == 0)
    def _():
        xp[...] = jnp.zeros_like(xp)

    greet(depths)
    gathers[0].begin()
    gain_share.begin()
    gathers[0].spread()
    gain_share.forward()
    gain_share.complete()
    gain = gains[0]
    for c in range(1, FLIPS):
        gain = gain + gains[c]
    gain_out[...] = gain

    def at(i):
        return pl.ds(pl.multiple_of(i * tile, tile), tile)

    def token_copy(i):
        return pltpu.make_async_remote_copy(
            src_ref=x_ref.at[at(i)],
            dst_ref=xp.at[at(i)],
            send_sem=tok_send.at[i],
            recv_sem=tok_recv.at[i],
            device_id=neighbour(1),
            device_id_type=MESH,
        )

    def out_copy(a, i):
        pairs = ((q, q_out), (k, k_out), (v, v_out), (n, n_out), (kp, kp_out), (vp, vp_out), (n_prev, np_out), (mixed, mixed_out))
        return pltpu.make_async_copy(pairs[a][0].at[at(i)], pairs[a][1].at[at(i)], out_sem.at[a, i])

    def prob_copy(i):
        part = pl.ds(i * TILE_SEQS, TILE_SEQS)
        return pltpu.make_async_copy(prob.at[part], prob_out.at[part], prob_sem.at[i])

    @pl.loop(0, tiles)
    def _(i):
        n[at(i), :] = (standardize(x_ref[at(i), :].astype(F32))[0] * gain[0:1]).astype(BF16)

    gathers[0].cross()
    gathers[0].hand_over()

    @pl.when(spot < FLIPS - 1)
    def _():
        for i in range(tiles):
            token_copy(i).start()

    for gather in gathers[1:]:
        gather.begin()
    gathers[0].complete()
    wq_copy = pltpu.make_async_copy(wq, wq_out, wq_sem.at[0])
    wq_copy.start()

    @pl.loop(0, tiles)
    def _(i):
        weight = rows_of(wq)
        normed = n[at(i), :]
        q[at(i), :] = (dot_t(normed, weight[:width]).astype(BF16).astype(F32) * scale).astype(BF16)
        k[at(i), :] = dot_t(normed, weight[width : 2 * width]).astype(BF16)
        v[at(i), :] = dot_t(normed, weight[2 * width :]).astype(BF16)
        for a in range(4):
            out_copy(a, i).start()

    for part, (ref, weigh) in enumerate(((k, 1.0 / span), (v, 1.0 / span), (n, 1.0))):
        means = [
            jnp.sum(ref[s * span : (s + 1) * span, :].astype(F32), axis=0, keepdims=True) * weigh for s in range(seqs)
        ]
        slots[spot, :, part * width : (part + 1) * width] = jnp.concatenate(means, axis=0).astype(BF16)
    sum_share.begin()

    def project_prev(i):
        @pl.when(spot > 0)
        def _():
            token_copy(i).wait_recv()

        weight = rows_of(wq)
        normed = (standardize(xp[at(i), :].astype(F32))[0] * gain[0:1]).astype(BF16)
        n_prev[at(i), :] = normed
        kp[at(i), :] = dot_t(normed, weight[width : 2 * width]).astype(BF16)
        vp[at(i), :] = dot_t(normed, weight[2 * width :]).astype(BF16)
        for a in range(4, 7):
            out_copy(a, i).start()

    project_prev(0)
    sum_share.forward()
    sum_share.complete()
    ordered = dot(in_order(FLIPS, seqs), slots[...].reshape(FLIPS * seqs, 3 * width)).astype(BF16)
    sums_out[...] = ordered.reshape(sums_out.shape)

    @pl.loop(0, tiles)
    def _(i):
        @pl.when(i + 1 < tiles)
        def _():
            project_prev(i + 1)

        for s in range(TILE_SEQS):
            here = pl.ds(pl.multiple_of(i * tile + s * span, span), span)
            seq = i * TILE_SEQS + s

            def keep_prob(p, both, seq=seq):
                prob[seq, p] = both

            rows_mixed, all_sums = attend_one(
                span,
                spot,
                prefix_ref[seq],
                q[here, :],
                jnp.concatenate([kp[here, :], k[here, :]], axis=0),
                jnp.concatenate([vp[here, :], v[here, :]], axis=0),
                sums_out[seq],
                keep_prob,
            )
            mixed[here, :] = rows_mixed
            psum_out[seq] = all_sums
        out_copy(7, i).start()
        prob_copy(i).start()
        for when, relays in ENTER_RELAYS.items():

            @pl.when(i == when)
            def _(relays=relays):
                for a, name in relays:
                    getattr(gathers[a], name)()

    for gather in gathers[1:]:
        gather.complete()
    for move in (*gathers, gain_share, sum_share):
        move.close()

    @pl.when(spot < FLIPS - 1)
    def _():
        for i in range(tiles):
            token_copy(i).wait_send()

    wq_copy.wait()

    @pl.loop(0, tiles)
    def _(i):
        for a in range(8):
            out_copy(a, i).wait()
        prob_copy(i).wait()


def enter(x, prefix, blocks, gains, span, depths):
    rows, width = x.shape
    tile = TILE_SEQS * span
    tiles, seqs = rows // tile, rows // span
    low = jax.ShapeDtypeStruct((rows, width), BF16)
    fulls = [jax.ShapeDtypeStruct((depths, FLIPS) + b.shape, BF16) for b in blocks]
    prob_shape = (seqs, HEADS // 2, 2 * span, 2 * span)
    vmem = pl.BlockSpec(memory_space=pltpu.VMEM)
    far = pl.BlockSpec(memory_space=pl.ANY)
    sems = pltpu.SemaphoreType.DMA
    held = pltpu.VMEM((rows, width), BF16)
    return pl.pallas_call(
        functools.partial(enter_kernel, depths, span),
        in_specs=[vmem, pl.BlockSpec(memory_space=pltpu.SMEM)] + [vmem] * 5,
        out_specs=[far] * 4 + [vmem] + [far] * 9 + [vmem] * 2,
        out_shape=fulls
        + [jax.ShapeDtypeStruct(gains.shape, F32)]
        + [low] * 8
        + [
            jax.ShapeDtypeStruct(prob_shape, BF16),
            jax.ShapeDtypeStruct((seqs, FLIPS, 3 * width), BF16),
            jax.ShapeDtypeStruct((seqs, HEADS * FLIPS, span), BF16),
        ],
        scratch_shapes=[
            held,
            pltpu.VMEM(fulls[0].shape, BF16),
            pltpu.VMEM((FLIPS,) + gains.shape, F32),
        ]
        + [held] * 8
        + [pltpu.VMEM(prob_shape, BF16), pltpu.VMEM((FLIPS, seqs, 3 * width), BF16)]
        + [
            sems((4, depths * FLIPS)), sems((4, depths * FLIPS)), sems((4,)),
            sems((FLIPS,)), sems((FLIPS,)), sems((FLIPS,)), sems((FLIPS,)),
            sems((tiles,)), sems((tiles,)), sems((8, tiles)), sems((tiles,)), sems((1,)),
        ],
        compiler_params=pltpu.CompilerParams(collective_id=0, has_side_effects=True, vmem_limit_bytes=VMEM_MOST),
        name="enter",
    )(x, prefix, *blocks, gains)


LEAVE_RELAYS = {
    1: ((0, "cross"),),
    2: ((1, "cross"), (0, "spread")),
    3: ((2, "cross"), (0, "climb")),
    4: ((1, "spread"),),
    5: ((2, "spread"), (1, "climb")),
    6: ((2, "climb"),),
}


def leave_kernel(
    depths, span,
    q_in, k_in, v_in, kp_in, vp_in, gm_in, n_in, np_in, prob_in, gr_in, x_in,
    psum_ref, sums_ref, wq_ref, gout_ref, gup_ref, gdown_ref, gain_ref, ggain_ref,
    ig_out, dqkv_out, dout_out, dup_out, ddown_out, dgain_out,
    held, prob, gn, gp, gb, gr, x, ig, acc, part, gs, gs_send_buf, gs_slots, gain_slots, gain_deep,
    *rest,
):
    moves_refs, sems = rest[:16], rest[16:]
    send, recv, gs_send, gs_recv, gain_send, gain_recv, deep_send, deep_recv, gb_send, gb_recv, in_sem, late_sem, ig_sem = sems
    rows, width = gn.shape
    tile = TILE_SEQS * span
    tiles = rows // tile
    seqs = rows // span
    spot = lax.axis_index("ctx")
    depth = lax.axis_index("dp")
    parts = (gout_ref, gup_ref, gdown_ref, part)
    scatters = [
        Scatter(depths, parts[a], *moves_refs[4 * a : 4 * a + 4], send.at[a], recv.at[a]) for a in range(4)
    ]
    gain_share = Share(depths, gain_slots, gain_send, gain_recv)
    gs_moves = Moves(depths, gs_send, gs_recv)
    deep_moves = Moves(depths, deep_send, deep_recv)

    def at(i):
        return pl.ds(pl.multiple_of(i * tile, tile), tile)

    def loads(i, slot):
        arrays = (q_in, k_in, v_in, kp_in, vp_in, gm_in, n_in, np_in)
        copies = [pltpu.make_async_copy(ref.at[at(i)], held.at[slot, a], in_sem.at[slot, a]) for a, ref in enumerate(arrays)]
        of_tile = pl.ds(i * TILE_SEQS, TILE_SEQS)
        return copies + [pltpu.make_async_copy(prob_in.at[of_tile], prob.at[slot], in_sem.at[slot, len(arrays)])]

    def gb_copy(i):
        return pltpu.make_async_remote_copy(
            src_ref=gp.at[at(i)],
            dst_ref=gb.at[at(i)],
            send_sem=gb_send.at[i],
            recv_sem=gb_recv.at[i],
            device_id=neighbour(-1),
            device_id_type=MESH,
        )

    for copy in loads(0, 0):
        copy.start()
    late = [pltpu.make_async_copy(gr_in, gr, late_sem.at[0]), pltpu.make_async_copy(x_in, x, late_sem.at[1])]

    @pl.when(spot == FLIPS - 1)
    def _():
        gb[...] = jnp.zeros_like(gb)

    greet(depths)
    for scatter in scatters[:3]:
        scatter.begin()
    acc[...] = jnp.zeros_like(acc)

    def tile_step(i, gain_sum):
        slot = lax.rem(i, 2)
        for copy in loads(i, slot):
            copy.wait()

        @pl.when(i + 1 < tiles)
        def _():
            for copy in loads(i + 1, 1 - slot):
                copy.start()

        pieces = []
        for s in range(TILE_SEQS):
            here = slice(s * span, (s + 1) * span)
            seq = i * TILE_SEQS + s
            pieces.append(
                return_one(
                    span,
                    held[slot, 0, here],
                    jnp.concatenate([held[slot, 3, here], held[slot, 1, here]], axis=0),
                    jnp.concatenate([held[slot, 4, here], held[slot, 2, here]], axis=0),
                    sums_ref[seq],
                    held[slot, 5, here],
                    lambda p, s=s: prob[slot, s, p],
                    psum_ref[seq],
                )
            )
        of_tile = pl.ds(i * TILE_SEQS, TILE_SEQS)
        normed, normed_prev = held[slot, 6], held[slot, 7]
        normed_sum = sums_ref[of_tile, :, 2 * width :].reshape(-1, width)
        to_own, to_prev, to_sums = return_tile(rows_of(wq_ref), *zip(*pieces), normed, normed_prev, normed_sum, acc)
        gn[at(i), :] = to_own
        gp[at(i), :] = to_prev.astype(BF16)
        gs[i] = to_sums.astype(BF16)

        @pl.when(spot > 0)
        def _():
            gb_copy(i).start()

        for when, relays in LEAVE_RELAYS.items():

            @pl.when(i == when)
            def _(relays=relays):
                for a, name in relays:
                    getattr(scatters[a], name)()

        @pl.when(i == tiles - 3)
        def _():
            for copy in late:
                copy.start()

        return (
            gain_sum
            + fold_rows(to_own * normed.astype(F32))
            + fold_rows(to_prev * normed_prev.astype(F32))
            + fold_rows(to_sums * normed_sum.astype(F32))
        )

    gain_sum = lax.fori_loop(0, tiles, tile_step, jnp.zeros((8, width), F32))

    by_spot = lax.dot_general(
        in_order(FLIPS, seqs), gs[...].reshape(seqs * FLIPS, width), (((0,), (0,)), ((), ())), preferred_element_type=F32
    )
    gs_send_buf[...] = by_spot.astype(BF16).reshape(gs_send_buf.shape)
    for flip in (6, 7, 2, 4, 3, 5, 1):
        gs_moves.start(gs_send_buf.at[spot_of(depths, 0, flip)[1]], gs_slots.at[flip], flip, 0, flip)
    total_one = jnp.sum(gain_sum, axis=0, keepdims=True) / gain_ref[0:1]
    total_two = jnp.sum(ggain_ref[...], axis=0, keepdims=True)
    gain_slots[spot] = jnp.concatenate([total_one, total_two], axis=0)
    gain_share.begin()
    put_blocks(part, acc[...].astype(BF16).T, 1)
    scatters[3].begin()
    dout_out[...] = scatters[0].finish()
    gain_share.forward()
    scatters[3].cross()
    dup_out[...] = scatters[1].finish()
    ddown_out[...] = scatters[2].finish()
    for copy in late:
        copy.wait()
    for flip in range(1, FLIPS):
        gs_moves.landed(gs_slots.at[flip], flip)
    shared = gs_send_buf[spot].astype(F32)
    for flip in range(1, FLIPS):
        shared = shared + gs_slots[flip].astype(F32)
    gain = gain_ref[0:1]

    def close_tile(i):
        @pl.when(spot < FLIPS - 1)
        def _():
            gb_copy(i).wait_recv()

        unit, inv = standardize(x[at(i), :].astype(F32))
        grad_norm = gn[at(i), :] + gb[at(i), :].astype(F32)
        lifted = [
            grad_norm[s * span : (s + 1) * span] + shared[i * TILE_SEQS + s : i * TILE_SEQS + s + 1]
            for s in range(TILE_SEQS)
        ]
        grad_norm = jnp.concatenate(lifted, axis=0)
        ig[at(i), :] = (gr[at(i), :] + norm_back(grad_norm, unit, inv, gain)).astype(BF16)
        pltpu.make_async_copy(ig.at[at(i)], ig_out.at[at(i)], ig_sem.at[i]).start()

    cut = tiles // 3
    for i in range(cut):
        close_tile(i)
    scatters[3].spread()
    gain_share.complete()
    over_ctx = gain_slots[0]
    for c in range(1, FLIPS):
        over_ctx = over_ctx + gain_slots[c]
    gain_deep[0] = over_ctx
    for turn in range(1, depths):
        deep_moves.start(gain_deep.at[0], gain_deep.at[depths - turn], depths - turn, turn, 0)
    for i in range(cut, 2 * cut):
        close_tile(i)
    scatters[3].climb()
    for i in range(2 * cut, tiles):
        close_tile(i)
    for turn in range(1, depths):
        deep_moves.landed(gain_deep.at[turn], turn)
    over_all = gain_deep[0]
    for turn in range(1, depths):
        over_all = over_all + gain_deep[turn]
    lanes = width // FLIPS
    mine = jnp.zeros((2, lanes), F32)
    for c in range(FLIPS):
        mine = jnp.where(spot == c, over_all[:, c * lanes : (c + 1) * lanes], mine)
    dgain_out[...] = mine
    dqkv_out[...] = scatters[3].finish()
    for scatter in scatters:
        scatter.close()
    gain_share.close()
    gs_moves.drain(gs_slots.at[0])
    deep_moves.drain(gain_deep.at[0])

    @pl.when(spot > 0)
    def _():
        for i in range(tiles):
            gb_copy(i).wait_send()

    for i in range(tiles):
        pltpu.make_async_copy(ig.at[at(i)], ig_out.at[at(i)], ig_sem.at[i]).wait()


def leave(arrays, psum, sums, wq, partials, gains, ggain, span, depths):
    rows, width = arrays[0].shape
    tile = TILE_SEQS * span
    tiles, seqs = rows // tile, rows // span
    vmem = pl.BlockSpec(memory_space=pltpu.VMEM)
    far = pl.BlockSpec(memory_space=pl.ANY)
    sems = pltpu.SemaphoreType.DMA
    low = pltpu.VMEM((rows, width), BF16)
    high = pltpu.VMEM((rows, width), F32)
    shapes = [p.shape[2:] for p in (*partials, wq)]
    scratch = [
        pltpu.VMEM((2, 8, tile, width), BF16),
        pltpu.VMEM((2, TILE_SEQS, HEADS // 2, 2 * span, 2 * span), BF16),
        high, low, low, high, low, low,
        pltpu.VMEM((width, 3 * width), F32),
        pltpu.VMEM(wq.shape, BF16),
        pltpu.VMEM((tiles, TILE_SEQS * FLIPS, width), BF16),
        pltpu.VMEM((FLIPS, seqs, width), BF16),
        pltpu.VMEM((FLIPS, seqs, width), BF16),
        pltpu.VMEM((FLIPS, 2, width), F32),
        pltpu.VMEM((depths, 2, width), F32),
    ]
    for shape in shapes:
        scratch += scatter_scratch(shape, depths)
    scratch += [
        sems((4, 8 * depths)), sems((4, 8 * depths)), sems((FLIPS,)), sems((FLIPS,)), sems((FLIPS,)), sems((FLIPS,)),
        sems((depths,)), sems((depths,)), sems((tiles,)), sems((tiles,)), sems((2, 9)), sems((2,)), sems((tiles,)),
    ]
    outs = [jax.ShapeDtypeStruct(shape, F32) for shape in (shapes[3], *shapes[:3])]
    return pl.pallas_call(
        functools.partial(leave_kernel, depths, span),
        in_specs=[far] * 11 + [vmem] * 8,
        out_specs=[far] + [vmem] * 5,
        out_shape=[jax.ShapeDtypeStruct((rows, width), BF16), *outs, jax.ShapeDtypeStruct((2, width // FLIPS), F32)],
        scratch_shapes=scratch,
        compiler_params=pltpu.CompilerParams(collective_id=1, has_side_effects=True, vmem_limit_bytes=VMEM_MOST),
        name="leave",
    )(*arrays, psum, sums, wq, *partials, gains, ggain)


def direct_shards(tokens, prefix, blocks, gain_one, gain_two, cotangent):
    span, width = tokens.shape[2], tokens.shape[3]
    depths = lax.axis_size("dp")
    x = tokens.reshape(-1, width)
    grad = cotangent.reshape(-1, width)
    shard = jnp.stack([gain_one, gain_two]).astype(F32)
    lane_owner = lax.broadcasted_iota(jnp.int32, (2, width), 1) // shard.shape[1]
    gains = jnp.where(lane_owner == lax.axis_index("ctx"), jnp.tile(shard, (1, FLIPS)), 0.0)
    (wq, wo, wu, wd, gains, q, k, v, kp, vp, n, n_prev, mixed, prob, sums, psum) = enter(
        x, prefix.reshape(-1), blocks, gains, span, depths
    )
    out, gm, gr, gout, gup, gdown, ggain = feed(x, mixed, grad, wo, wu, wd, gains[1:2], TILE_SEQS * span)
    arrays = (q, k, v, kp, vp, gm, n, n_prev, prob, gr, x)
    ig, dqkv, dout, dup, ddown, dgain = leave(arrays, psum, sums, wq, (gout, gup, gdown), gains, ggain, span, depths)
    return (
        out.reshape(tokens.shape),
        ig.reshape(tokens.shape),
        dqkv.T,
        dout.T,
        dup,
        ddown.T,
        dgain[0],
        dgain[1],
    )


def fetch(block, rows_along):
    spot, depth = (0, 1) if rows_along == 1 else (1, 0)
    whole = lax.all_gather(lax.all_gather(block, "ctx", axis=spot, tiled=True), "dp", axis=depth, tiled=True)
    return whole[None, None]


def reduce_weight(partial, rows_along):
    spot, depth = (0, 1) if rows_along == 1 else (1, 0)
    columns = lax.psum_scatter(partial[0, 0], "ctx", scatter_dimension=spot, tiled=True)
    return lax.psum_scatter(columns, "dp", scatter_dimension=depth, tiled=True).astype(F32)


def shards(tokens, prefix, w_qkv, w_out, w_up, w_down, gain_one, gain_two, cotangent):
    span, width = tokens.shape[2], tokens.shape[3]
    count = lax.axis_size("ctx")
    blocks = (w_qkv.T, w_out.T, w_up, w_down.T)
    if count == FLIPS and all(b.shape[0] % 16 == 0 and b.shape[1] % 128 == 0 for b in blocks):
        return direct_shards(tokens, prefix, blocks, gain_one, gain_two, cotangent)
    along = (1, 1, 0, 1)
    x = tokens.reshape(-1, width)
    grad = cotangent.reshape(-1, width)
    tile = TILE_SEQS * span
    block = lax.axis_index("ctx").reshape(1).astype(jnp.int32)
    x_prev = lax.ppermute(x, "ctx", [(i, i + 1) for i in range(count - 1)])
    gain1 = lax.all_gather(gain_one, "ctx", axis=0, tiled=True).astype(F32).reshape(1, width)
    gain2 = lax.all_gather(gain_two, "ctx", axis=0, tiled=True).astype(F32).reshape(1, width)
    wq, wo, wu, wd = (fetch(b, r) for b, r in zip(blocks, along))
    q, k, v, kp, vp, n, n_prev, own_sums = project(x, x_prev, wq, gain1, span)
    own_sums = own_sums.reshape(-1, 2 * width)
    n_sum = jnp.sum(n.reshape(-1, span, width).astype(F32), axis=1).astype(BF16)
    everything = lax.all_gather(jnp.concatenate([own_sums, n_sum], axis=1), "ctx", axis=0, tiled=False)
    everything = jnp.transpose(everything, (1, 0, 2))
    sums, n_sums = everything[:, :, : 2 * width], everything[:, :, 2 * width :]
    mixed, prob, psum = attend(prefix.reshape(-1), block, q, k, v, kp, vp, sums, span)
    out, gm, gr, gout, gup, gdown, ggain2 = feed(x, mixed, grad, wo, wu, wd, gain2, tile)
    gn, gp, gs, gqkv = give_back(q, k, v, kp, vp, sums, gm, prob, psum, n, n_prev, n_sums, wq, span)
    gb = lax.ppermute(gp, "ctx", [(i, i - 1) for i in range(1, count)])
    gs_own = lax.psum_scatter(gs, "ctx", scatter_dimension=1, tiled=True)
    input_grad, ggain1 = close(x, gn, gb, gs_own, gr, gain1, span)
    gains = jnp.concatenate([jnp.sum(ggain1, axis=0), jnp.sum(ggain2, axis=0)]).reshape(2, width)
    gains = lax.psum(gains, "dp")
    gains = lax.psum_scatter(gains, "ctx", scatter_dimension=1, tiled=True)
    sums_w = [reduce_weight(p, r) for p, r in zip((gqkv, gout, gup, gdown), along)]
    return (
        out.reshape(tokens.shape),
        input_grad.reshape(tokens.shape),
        sums_w[0].T,
        sums_w[1].T,
        sums_w[2],
        sums_w[3].T,
        gains[0],
        gains[1],
    )


def solution(mesh):
    rows = P(None, "dp", "ctx", None)
    both = P("dp", "ctx")
    return jax.shard_map(
        shards,
        mesh=mesh,
        in_specs=(rows, P(None, "dp"), both, both, both, both, P("ctx"), P("ctx"), rows),
        out_specs=(rows, rows, both, both, both, both, P("ctx"), P("ctx")),
        check_vma=False,
    )
```

```python
import functools
import math

import jax
import jax.numpy as jnp
from jax import lax
from jax.experimental import pallas as pl
from jax.experimental.pallas import tpu as pltpu
from jax.sharding import PartitionSpec as P

HEADS = 8
EPSILON = 1e-05
MASKED = -1e30
F32 = jnp.float32
BF16 = jnp.bfloat16
TILE_SEQS = 2
CHUNK_TILES = 2
FF_CHUNK = 512
VMEM_MOST = 60 * 1024 * 1024

MESH = pl.DeviceIdType.MESH
FLIPS = 8


def place():
    depth, spot = lax.axis_index("dp"), lax.axis_index("ctx")
    return depth, spot, (spot % 2, (spot // 2) % 2, spot // 4)


def flipped(bits, flip):
    out = 0
    for i, bit in enumerate(bits):
        out = out + ((1 - bit) if (flip >> i) & 1 else bit) * (1 << i)
    return out


def spot_of(depths, turn, flip):
    depth, _, bits = place()
    return lax.rem(depth + turn, depths), flipped(bits, flip)


def greet(depths):
    barrier = pltpu.get_barrier_semaphore()
    peers = [(turn, 0) for turn in range(1, depths)] + [(0, flip) for flip in range(1, FLIPS)]
    for turn, flip in peers:
        pl.semaphore_signal(barrier, inc=1, device_id=spot_of(depths, turn, flip), device_id_type=MESH)
    pl.semaphore_wait(barrier, len(peers))


class Moves:
    def __init__(self, depths, send, recv):
        self.depths, self.send, self.recv, self.sent = depths, send, recv, 0

    def copy(self, source, target, number, slot, to_turn, to_flip):
        return pltpu.make_async_remote_copy(
            src_ref=source,
            dst_ref=target,
            send_sem=self.send.at[number],
            recv_sem=self.recv.at[slot],
            device_id=spot_of(self.depths, to_turn, to_flip),
            device_id_type=MESH,
        )

    def start(self, source, target, slot, to_turn, to_flip):
        self.copy(source, target, self.sent, slot, to_turn, to_flip).start()
        self.sent += 1

    def landed(self, target, slot):
        self.copy(target, target, 0, slot, 0, 1).wait_recv()

    def drain(self, like):
        for number in range(self.sent):
            self.copy(like, like, number, 0, 0, 1).wait_send()


class Gather(Moves):
    def __init__(self, depths, own, full, send, recv, keep):
        super().__init__(depths, send, recv)
        self.own, self.full, self.keep = own, full, keep

    def block(self, turn, flip):
        return self.full.at[spot_of(self.depths, turn, flip)]

    def push(self, turn, flip, to_turn, to_flip):
        there = ((turn - to_turn) % self.depths) * FLIPS + (flip ^ to_flip)
        source = self.own if (turn, flip) == (0, 0) else self.block(turn, flip)
        self.start(source, self.block(turn, flip), there, to_turn, to_flip)

    def arrive(self, turn, flip):
        self.landed(self.block(turn, flip), turn * FLIPS + flip)

    def begin(self):
        for turn in range(1, self.depths):
            self.push(0, 0, turn, 0)
        for flip in (2, 4, 1):
            self.push(0, 0, 0, flip)
        pltpu.make_async_copy(self.own, self.block(0, 0), self.keep).start()

    def spread(self):
        for turn in range(1, self.depths):
            self.arrive(turn, 0)
            for flip in (2, 4, 1):
                self.push(turn, 0, 0, flip)

    def cross(self):
        for turn in range(self.depths):
            self.arrive(turn, 2)
            if turn < self.depths // 2:
                self.push(turn, 2, 0, 4)
            self.push(turn, 2, 0, 1)
            self.arrive(turn, 4)
            if turn >= self.depths // 2:
                self.push(turn, 4, 0, 2)
            self.push(turn, 4, 0, 1)

    def hand_over(self):
        for turn in range(self.depths):
            self.arrive(turn, 6)
            self.push(turn, 6, 0, 1)

    def complete(self):
        for turn in range(self.depths):
            for flip in (1, 3, 5, 7):
                self.arrive(turn, flip)
        pltpu.make_async_copy(self.own, self.block(0, 0), self.keep).wait()

    def close(self):
        self.drain(self.own)


class Share(Moves):
    def __init__(self, depths, slots, send, recv):
        super().__init__(depths, send, recv)
        self.slots = slots

    def block(self, flip):
        return self.slots.at[spot_of(self.depths, 0, flip)[1]]

    def begin(self):
        for flip in (2, 4, 6, 1):
            self.start(self.block(0), self.block(0), flip, 0, flip)

    def forward(self):
        for flip in (2, 4, 6):
            self.landed(self.block(flip), flip)
            self.start(self.block(flip), self.block(flip), flip ^ 1, 0, 1)

    def complete(self):
        for flip in (1, 3, 5, 7):
            self.landed(self.block(flip), flip)

    def close(self):
        self.drain(self.block(0))


class Scatter(Moves):
    def __init__(self, depths, part, mate, total, near, far, send, recv):
        super().__init__(depths, send, recv)
        self.part, self.mate, self.total, self.near, self.far = part, mate, total, near, far

    def block(self, turn, flip):
        return self.part.at[spot_of(self.depths, turn, flip)]

    push = Moves.start
    arrive = Moves.landed

    def begin(self):
        for flip in (6, 2, 4, 0):
            for turn in range(self.depths):
                at = (flip // 2, turn)
                self.push(self.block(turn, flip ^ 1), self.mate.at[at], flip // 2 * self.depths + turn, 0, 1)

    def fold(self, turn, flip):
        self.arrive(self.mate.at[flip // 2, turn], flip // 2 * self.depths + turn)
        mine = self.block(turn, flip)[...].astype(F32)
        self.total[flip // 2, turn] = (mine + self.mate[flip // 2, turn].astype(F32)).astype(BF16)

    def cross(self):
        base = 4 * self.depths
        for turn in range(self.depths):
            self.fold(turn, 6)
            by = 2 if turn < self.depths // 2 else 4
            self.push(self.total.at[3, turn], self.near.at[turn], base + turn, 0, by)

    def spread(self):
        base = 4 * self.depths
        late = 5 * self.depths
        for turn in range(self.depths):
            self.fold(turn, 2)
            self.fold(turn, 4)
            via = 2 if turn < self.depths // 2 else 1
            self.arrive(self.near.at[turn], base + turn)
            self.total[via, turn] = (self.total[via, turn].astype(F32) + self.near[turn].astype(F32)).astype(BF16)
            self.push(self.total.at[1, turn], self.far.at[0, turn], late + turn, 0, 2)
            self.push(self.total.at[2, turn], self.far.at[1, turn], late + self.depths + turn, 0, 4)

    def climb(self):
        late = 5 * self.depths
        last = 7 * self.depths
        for turn in [*range(1, self.depths), 0]:
            self.fold(turn, 0)
            self.arrive(self.far.at[0, turn], late + turn)
            self.arrive(self.far.at[1, turn], late + self.depths + turn)
            self.total[0, turn] = (
                self.total[0, turn].astype(F32) + self.far[0, turn].astype(F32) + self.far[1, turn].astype(F32)
            ).astype(BF16)
            if turn:
                back = self.depths - turn
                self.push(self.total.at[0, turn], self.far.at[2, back], last + back, turn, 0)

    def finish(self):
        last = 7 * self.depths
        out = self.total[0, 0].astype(F32)
        for turn in range(1, self.depths):
            self.arrive(self.far.at[2, turn], last + turn)
            out = out + self.far[2, turn].astype(F32)
        return out

    def close(self):
        self.drain(self.near.at[0])


def scatter_scratch(block, depths):
    return [
        pltpu.VMEM((4, depths) + block, BF16),
        pltpu.VMEM((4, depths) + block, BF16),
        pltpu.VMEM((depths,) + block, BF16),
        pltpu.VMEM((3, depths) + block, BF16),
    ]


def dot(a, b):
    return jnp.dot(a, b, preferred_element_type=F32)


def dot_t(a, b):
    return lax.dot_general(a, b, (((1,), (1,)), ((), ())), preferred_element_type=F32)


def standardize(values):
    row_mean = jnp.mean(values, axis=-1, keepdims=True)
    centred = values - row_mean
    variance = jnp.mean(centred * centred, axis=-1, keepdims=True)
    inv_std = lax.rsqrt(variance + EPSILON)
    return (centred * inv_std, inv_std)


def norm_back(grad_in, unit_rows, inv_std, gain):
    scaled = grad_in * gain
    row_mean = jnp.mean(scaled, axis=-1, keepdims=True)
    cross_mean = jnp.mean(scaled * unit_rows, axis=-1, keepdims=True)
    return inv_std * (scaled - row_mean - unit_rows * cross_mean)


def fold_rows(values):
    return jnp.sum(values.reshape(-1, 8, values.shape[-1]), axis=0)


def gelu_parts(upper):
    cdf = 0.5 * (1.0 + lax.erf(upper * 0.7071067811865476))
    slope = cdf + upper * jnp.exp(-0.5 * upper * upper) * 0.3989422804014327
    return (upper * cdf, slope)


def pair_halves(rows):
    lanes = lax.broadcasted_iota(jnp.int32, rows.shape, 1)
    half = rows.shape[1] // 2
    zero = jnp.zeros_like(rows)
    return jnp.concatenate(
        [jnp.where(lanes < half, rows, zero), jnp.where(lanes >= half, rows, zero)], axis=0
    )


def head_select(count, width):
    head_of_row = lax.broadcasted_iota(jnp.int32, (HEADS * count, width), 0) // count
    head_of_lane = lax.broadcasted_iota(jnp.int32, (HEADS * count, width), 1) // (width // HEADS)
    return head_of_row == head_of_lane


def per_head(rows, select):
    tiled = jnp.concatenate([rows.astype(F32)] * HEADS, axis=0)
    return jnp.where(select, tiled, 0.0).astype(BF16)


def rows_of(ref):
    depths, lanes = ref.shape[0], ref.shape[3]
    return jnp.concatenate([ref[d].reshape(-1, lanes) for d in range(depths)], axis=1)


def lanes_of(ref, chunk, along):
    lanes = ref.shape[3]
    take = (lambda i: ref[i]) if along == 0 else (lambda i: ref[:, i])
    if lanes >= FF_CHUNK:
        per = lanes // FF_CHUNK
        cut = slice(chunk % per * FF_CHUNK, (chunk % per + 1) * FF_CHUNK)
        return take(chunk // per).reshape(-1, lanes)[:, cut]
    per = FF_CHUNK // lanes
    return jnp.concatenate([take(i).reshape(-1, lanes) for i in range(chunk * per, (chunk + 1) * per)], axis=1)


def put_blocks(ref, values, rows_along):
    depths, spots, rows, lanes = ref.shape
    for d in range(depths):
        for c in range(spots):
            r, l = (c, d) if rows_along == 1 else (d, c)
            ref[d, c] = values[r * rows : (r + 1) * rows, l * lanes : (l + 1) * lanes].astype(ref.dtype)


def project_kernel(x_ref, xp_ref, w_ref, gain_ref, q_ref, k_ref, v_ref, kp_ref, vp_ref, n_ref, np_ref, sum_ref):
    width = x_ref.shape[1]
    gain = gain_ref[...]
    weight = rows_of(w_ref)
    normed = (standardize(x_ref[...].astype(F32))[0] * gain).astype(BF16)
    n_ref[...] = normed
    scale = (width // HEADS) ** -0.5
    q_ref[...] = (dot_t(normed, weight[:width]).astype(BF16).astype(F32) * scale).astype(BF16)
    for part, out in ((1, k_ref), (2, v_ref)):
        rows = dot_t(normed, weight[part * width : (part + 1) * width]).astype(BF16)
        out[...] = rows
        means = jnp.mean(rows.astype(F32).reshape(TILE_SEQS, -1, width), axis=1)
        sum_ref[0, :, (part - 1) * width : part * width] = means.astype(BF16)
    normed_prev = (standardize(xp_ref[...].astype(F32))[0] * gain).astype(BF16)
    np_ref[...] = normed_prev
    kp_ref[...] = dot_t(normed_prev, weight[width : 2 * width]).astype(BF16)
    vp_ref[...] = dot_t(normed_prev, weight[2 * width :]).astype(BF16)


def row_spec(rows, width):
    return pl.BlockSpec((rows, width), lambda i: (i, 0))


def whole_spec(shape):
    return pl.BlockSpec(shape, lambda i: (0,) * len(shape))


def params():
    return pltpu.CompilerParams(vmem_limit_bytes=VMEM_MOST)


def project(x, x_prev, w_qkv, gain, span):
    rows, width = x.shape
    tile = TILE_SEQS * span
    low = jax.ShapeDtypeStruct((rows, width), BF16)
    return pl.pallas_call(
        project_kernel,
        grid=(rows // tile,),
        in_specs=[row_spec(tile, width)] * 2 + [whole_spec(w_qkv.shape), whole_spec(gain.shape)],
        out_specs=[row_spec(tile, width)] * 7
        + [pl.BlockSpec((1, TILE_SEQS, 2 * width), lambda i: (i, 0, 0))],
        out_shape=[low] * 7 + [jax.ShapeDtypeStruct((rows // tile, TILE_SEQS, 2 * width), BF16)],
        compiler_params=params(),
        name="project",
    )(x, x_prev, w_qkv, gain)


def attend_one(span, block, prefix, queries, keys, values, sums, keep_prob):
    width = queries.shape[1]
    pair = 2 * width // HEADS
    half = pair // 2
    count = sums.shape[0]
    select = head_select(count, width)
    unit_pos = lax.broadcasted_iota(jnp.int32, (span, span), 0)
    query_pos = lax.broadcasted_iota(jnp.int32, (span, span), 1)
    sum_id = lax.broadcasted_iota(jnp.int32, (count, span), 0)
    sum_query = lax.broadcasted_iota(jnp.int32, (count, span), 1)
    bias_prev = jnp.where(block >= 1, 0.0, MASKED).astype(F32)
    start = block * span
    own_ok = (unit_pos <= query_pos) | (start + unit_pos < prefix)
    bias_own = jnp.where(own_ok, 0.0, MASKED)
    sum_ok = (sum_id <= block - 1) | (
        (start + sum_query < prefix) & (sum_id >= block + 1) & ((sum_id + 1) * span <= prefix)
    )
    bias_sum = jnp.where(sum_ok, math.log(span), MASKED)
    values_t = values.T
    sum_keys = per_head(sums[:, :width], select)
    sum_values_t = per_head(sums[:, width : 2 * width], select).T
    sum_scores = dot_t(sum_keys, queries)
    mixed_parts = []
    sum_probs = []
    for p in range(HEADS // 2):
        lanes = slice(p * pair, (p + 1) * pair)
        scores = dot_t(keys[:, lanes], pair_halves(queries[:, lanes]))
        probs = []
        for e in range(2):
            h = 2 * p + e
            cols = slice(e * span, (e + 1) * span)
            s_prev = scores[:span, cols]
            s_own = scores[span:, cols] + bias_own
            s_sum = sum_scores[h * count : (h + 1) * count] + bias_sum
            most = jnp.maximum(
                jnp.maximum(
                    jnp.max(s_prev, axis=0, keepdims=True) + bias_prev,
                    jnp.max(s_own, axis=0, keepdims=True),
                ),
                jnp.max(s_sum, axis=0, keepdims=True),
            )
            e_prev = jnp.exp(s_prev + (bias_prev - most))
            e_own = jnp.exp(s_own - most)
            e_sum = jnp.exp(s_sum - most)
            total = (
                jnp.sum(e_prev, axis=0, keepdims=True)
                + jnp.sum(e_own, axis=0, keepdims=True)
                + jnp.sum(e_sum, axis=0, keepdims=True)
            )
            inverse = 1.0 / total
            probs.append(jnp.concatenate([e_prev * inverse, e_own * inverse], axis=0).astype(BF16))
            sum_probs.append(e_sum * inverse)
        both = jnp.concatenate(probs, axis=1)
        keep_prob(p, both)
        crossed = dot(values_t[lanes, :], both)
        mixed_parts.append(crossed[:half, :span])
        mixed_parts.append(crossed[half:, span:])
    all_sums = jnp.concatenate(sum_probs, axis=0).astype(BF16)
    mixed_t = jnp.concatenate(mixed_parts, axis=0) + dot(sum_values_t, all_sums)
    return mixed_t.T.astype(BF16), all_sums


def attend_kernel(
    span, prefix_ref, block_ref, q_ref, k_ref, v_ref, kp_ref, vp_ref, sums_ref, mixed_ref, prob_ref, psum_ref
):
    for s in range(TILE_SEQS):
        rows = slice(s * span, (s + 1) * span)

        def keep_prob(p, both, s=s):
            prob_ref[s, p] = both

        mixed, all_sums = attend_one(
            span,
            block_ref[0],
            prefix_ref[pl.program_id(0) * TILE_SEQS + s],
            q_ref[rows, :],
            jnp.concatenate([kp_ref[rows, :], k_ref[rows, :]], axis=0),
            jnp.concatenate([vp_ref[rows, :], v_ref[rows, :]], axis=0),
            sums_ref[s],
            keep_prob,
        )
        mixed_ref[rows, :] = mixed
        psum_ref[s] = all_sums


def attend(prefix, block, q, k, v, kp, vp, sums, span):
    rows, width = q.shape
    tile = TILE_SEQS * span
    seqs, count = sums.shape[0], sums.shape[1]
    pairs = HEADS // 2
    return pl.pallas_call(
        functools.partial(attend_kernel, span),
        grid=(rows // tile,),
        in_specs=[pl.BlockSpec(memory_space=pltpu.SMEM)] * 2
        + [row_spec(tile, width)] * 5
        + [pl.BlockSpec((TILE_SEQS, count, 2 * width), lambda i: (i, 0, 0))],
        out_specs=[
            row_spec(tile, width),
            pl.BlockSpec((TILE_SEQS, pairs, 2 * span, 2 * span), lambda i: (i, 0, 0, 0)),
            pl.BlockSpec((TILE_SEQS, HEADS * count, span), lambda i: (i, 0, 0)),
        ],
        out_shape=[
            jax.ShapeDtypeStruct((rows, width), BF16),
            jax.ShapeDtypeStruct((seqs, pairs, 2 * span, 2 * span), BF16),
            jax.ShapeDtypeStruct((seqs, HEADS * count, span), BF16),
        ],
        compiler_params=params(),
        name="attend",
    )(prefix, block, q, k, v, kp, vp, sums)


def feed_kernel(
    x_ref, mixed_ref, g_ref, wo_ref, wu_ref, wd_ref, gain_ref,
    out_ref, gm_ref, gr_ref, gout_ref, gup_ref, gdown_ref, ggain_ref,
    acc_out, acc_up, acc_down, acc_gain,
):
    step = pl.program_id(0)

    @pl.when(step == 0)
    def _():
        acc_out[...] = jnp.zeros_like(acc_out)
        acc_up[...] = jnp.zeros_like(acc_up)
        acc_down[...] = jnp.zeros_like(acc_down)
        acc_gain[...] = jnp.zeros_like(acc_gain)

    gain = gain_ref[gain_ref.shape[0] - 1 :, :]
    mixed = mixed_ref[...]
    w_out = rows_of(wo_ref)
    resid = x_ref[...].astype(F32) + dot_t(mixed, w_out)
    unit, inv = standardize(resid)
    normed = (unit * gain).astype(BF16)
    normed_t = normed.T
    grad = g_ref[...]
    grad_t = grad.T
    hidden_width = acc_up.shape[1]
    result = resid
    grad_norm = None
    for c in range(hidden_width // FF_CHUNK):
        cols = slice(c * FF_CHUNK, (c + 1) * FF_CHUNK)
        w_up = lanes_of(wu_ref, c, 1)
        w_down = lanes_of(wd_ref, c, 0)
        upper = dot(normed, w_up)
        grad_hidden = dot(grad, w_down)
        activated, slope = gelu_parts(upper)
        hidden = activated.astype(BF16)
        grad_upper = (grad_hidden * slope).astype(BF16)
        result = result + dot_t(hidden, w_down)
        back = dot_t(grad_upper, w_up)
        grad_norm = back if grad_norm is None else grad_norm + back
        acc_down[:, cols] += dot(grad_t, hidden)
        acc_up[:, cols] += dot(normed_t, grad_upper)
    out_ref[...] = result.astype(BF16)
    acc_gain[...] += fold_rows(grad_norm * unit)
    grad_resid = grad.astype(F32) + norm_back(grad_norm, unit, inv, gain)
    gr_ref[...] = grad_resid
    grad_branch = grad_resid.astype(BF16)
    acc_out[...] += dot(grad_branch.T, mixed)
    gm_ref[...] = dot(grad_branch, w_out).astype(BF16)

    @pl.when(step == pl.num_programs(0) - 1)
    def _():
        put_blocks(gout_ref, acc_out, 1)
        put_blocks(gup_ref, acc_up, 0)
        put_blocks(gdown_ref, acc_down, 1)
        ggain_ref[...] = acc_gain[...]


def feed(x, mixed, grad, w_out, w_up, w_down, gain, tile):
    rows, width = x.shape
    hidden = w_up.shape[1] * w_up.shape[3]
    wide = (width, hidden)
    square = (width, width)
    return pl.pallas_call(
        feed_kernel,
        grid=(rows // tile,),
        in_specs=[row_spec(tile, width)] * 3
        + [whole_spec(w_out.shape), whole_spec(w_up.shape), whole_spec(w_down.shape), whole_spec(gain.shape)],
        out_specs=[row_spec(tile, width)] * 3
        + [whole_spec(w_out.shape), whole_spec(w_up.shape), whole_spec(w_down.shape), whole_spec((8, width))],
        out_shape=[
            jax.ShapeDtypeStruct((rows, width), BF16),
            jax.ShapeDtypeStruct((rows, width), BF16),
            jax.ShapeDtypeStruct((rows, width), F32),
            jax.ShapeDtypeStruct(w_out.shape, BF16),
            jax.ShapeDtypeStruct(w_up.shape, BF16),
            jax.ShapeDtypeStruct(w_down.shape, BF16),
            jax.ShapeDtypeStruct((8, width), F32),
        ],
        scratch_shapes=[
            pltpu.VMEM(square, F32),
            pltpu.VMEM(wide, F32),
            pltpu.VMEM(wide, F32),
            pltpu.VMEM((8, width), F32),
        ],
        compiler_params=params(),
        name="feed",
    )(x, mixed, grad, w_out, w_up, w_down, gain)


def return_one(span, queries, keys, values, sums, grad_mixed, prob_at, sum_low):
    width = queries.shape[1]
    pair = 2 * width // HEADS
    half = pair // 2
    count = sums.shape[0]
    scale = half ** -0.5
    select = head_select(count, width)
    keys_t = keys.T
    sum_keys_t = per_head(sums[:, :width], select).T
    sum_values = per_head(sums[:, width : 2 * width], select)
    sum_prob = sum_low.astype(F32)
    sum_moved = sum_prob * dot_t(sum_values, grad_mixed)
    grad_q_parts = []
    grad_k_parts = []
    grad_v_parts = []
    sum_grads = []
    for p in range(HEADS // 2):
        lanes = slice(p * pair, (p + 1) * pair)
        grads2 = pair_halves(grad_mixed[:, lanes])
        grad_prob = dot_t(values[:, lanes], grads2)
        low = prob_at(p)
        prob = low.astype(F32)
        moved = prob * grad_prob
        deltas = jnp.sum(moved, axis=0, keepdims=True)
        sums_of = []
        for e in range(2):
            h = 2 * p + e
            part = slice(h * count, (h + 1) * count)
            delta = deltas[:, e * span : (e + 1) * span] + jnp.sum(sum_moved[part], axis=0, keepdims=True)
            sums_of.append(delta)
            sum_grads.append(sum_moved[part] - sum_prob[part] * delta)
        grad_scores = (moved - prob * jnp.concatenate(sums_of, axis=1)).astype(BF16)
        grad_k_parts.append(dot(grad_scores, pair_halves(queries[:, lanes])))
        grad_v_parts.append(dot(low, grads2))
        crossed = dot(keys_t[lanes, :], grad_scores)
        grad_q_parts.append(crossed[:half, :span])
        grad_q_parts.append(crossed[half:, span:])
    sum_scores_grad = jnp.concatenate(sum_grads, axis=0).astype(BF16)
    grad_q = jnp.concatenate(grad_q_parts, axis=0) + dot(sum_keys_t, sum_scores_grad)
    grad_q = (grad_q.T * scale).astype(BF16)
    grad_k = jnp.concatenate(grad_k_parts, axis=1).astype(BF16)
    grad_v = jnp.concatenate(grad_v_parts, axis=1).astype(BF16)
    wide_k = jnp.where(select, dot(sum_scores_grad, queries), 0.0)
    wide_v = jnp.where(select, dot(sum_low, grad_mixed), 0.0)
    folded_k = jnp.sum(wide_k.reshape(HEADS, count, width), axis=0)
    folded_v = jnp.sum(wide_v.reshape(HEADS, count, width), axis=0)
    return (
        jnp.concatenate([grad_q, grad_k[span:], grad_v[span:]], axis=1),
        jnp.concatenate([grad_k[:span], grad_v[:span]], axis=1),
        jnp.concatenate([folded_k, folded_v], axis=1) * (1.0 / span),
    )


def return_tile(weight, own, before, shared, normed, normed_prev, normed_sum, acc):
    width = normed.shape[1]
    grad_own = jnp.concatenate(own, axis=0)
    grad_before = jnp.concatenate(before, axis=0)
    grad_shared = jnp.concatenate(shared, axis=0).astype(BF16)
    normed_t = normed.T
    acc[:, :width] += dot(normed_t, grad_own[:, :width])
    acc[:, width:] += (
        dot(normed_t, grad_own[:, width:]) + dot(normed_prev.T, grad_before) + dot(normed_sum.T, grad_shared)
    )
    return dot(grad_own, weight), dot(grad_before, weight[width:]), dot(grad_shared, weight[width:])


def return_kernel(
    span, q_ref, k_ref, v_ref, kp_ref, vp_ref, sums_ref, gm_ref, prob_ref, psum_ref, n_ref, np_ref, nsum_ref, w_ref,
    gn_ref, gp_ref, gs_ref, gqkv_ref, acc,
):
    step = pl.program_id(0)

    @pl.when(step == 0)
    def _():
        acc[...] = jnp.zeros_like(acc)

    parts = []
    for s in range(TILE_SEQS):
        rows = slice(s * span, (s + 1) * span)
        parts.append(
            return_one(
                span,
                q_ref[rows, :],
                jnp.concatenate([kp_ref[rows, :], k_ref[rows, :]], axis=0),
                jnp.concatenate([vp_ref[rows, :], v_ref[rows, :]], axis=0),
                sums_ref[s],
                gm_ref[rows, :],
                lambda p, s=s: prob_ref[s, p],
                psum_ref[s],
            )
        )
    normed_sum = nsum_ref[...].reshape(-1, nsum_ref.shape[2])
    gn, gp, gs = return_tile(rows_of(w_ref), *zip(*parts), n_ref[...], np_ref[...], normed_sum, acc)
    gn_ref[...] = gn
    gp_ref[...] = gp.astype(BF16)
    gs_ref[...] = gs.reshape(gs_ref.shape).astype(BF16)

    @pl.when(step == pl.num_programs(0) - 1)
    def _():
        put_blocks(gqkv_ref, acc[...].astype(BF16).T, 1)


def give_back(q, k, v, kp, vp, sums, gm, prob, psum, n, n_prev, n_sum, w_qkv, span):
    rows, width = q.shape
    tile = TILE_SEQS * span
    seqs, count = sums.shape[0], sums.shape[1]
    pairs = HEADS // 2
    return pl.pallas_call(
        functools.partial(return_kernel, span),
        grid=(rows // tile,),
        in_specs=[row_spec(tile, width)] * 5
        + [
            pl.BlockSpec((TILE_SEQS, count, 2 * width), lambda i: (i, 0, 0)),
            row_spec(tile, width),
            pl.BlockSpec((TILE_SEQS, pairs, 2 * span, 2 * span), lambda i: (i, 0, 0, 0)),
            pl.BlockSpec((TILE_SEQS, HEADS * count, span), lambda i: (i, 0, 0)),
            row_spec(tile, width),
            row_spec(tile, width),
            pl.BlockSpec((TILE_SEQS, count, width), lambda i: (i, 0, 0)),
            whole_spec(w_qkv.shape),
        ],
        out_specs=[
            row_spec(tile, width),
            row_spec(tile, width),
            pl.BlockSpec((TILE_SEQS, count, width), lambda i: (i, 0, 0)),
            whole_spec(w_qkv.shape),
        ],
        out_shape=[
            jax.ShapeDtypeStruct((rows, width), F32),
            jax.ShapeDtypeStruct((rows, width), BF16),
            jax.ShapeDtypeStruct((seqs, count, width), BF16),
            jax.ShapeDtypeStruct(w_qkv.shape, BF16),
        ],
        scratch_shapes=[pltpu.VMEM((width, 3 * width), F32)],
        compiler_params=params(),
        name="give_back",
    )(q, k, v, kp, vp, sums, gm, prob, psum, n, n_prev, n_sum, w_qkv)


def close_kernel(span, x_ref, gn_ref, gb_ref, gs_ref, gr_ref, gain_ref, out_ref, ggain_ref, acc):
    step = pl.program_id(0)
    width = x_ref.shape[1]

    @pl.when(step == 0)
    def _():
        acc[...] = jnp.zeros_like(acc)

    unit, inv = standardize(x_ref[...].astype(F32))
    grad_norm = gn_ref[...] + gb_ref[...].astype(F32)
    lifted = [
        grad_norm[s * span : (s + 1) * span] + gs_ref[s].astype(F32) for s in range(TILE_SEQS)
    ]
    grad_norm = jnp.concatenate(lifted, axis=0)
    acc[...] += fold_rows(grad_norm * unit)
    part = norm_back(grad_norm, unit, inv, gain_ref[...])
    out_ref[...] = (gr_ref[...] + part).astype(BF16)

    @pl.when(step == pl.num_programs(0) - 1)
    def _():
        ggain_ref[...] = acc[...]


def close(x, gn, gb, gs, gr, gain, span):
    rows, width = x.shape
    tile = TILE_SEQS * span
    return pl.pallas_call(
        functools.partial(close_kernel, span),
        grid=(rows // tile,),
        in_specs=[row_spec(tile, width)] * 3
        + [pl.BlockSpec((TILE_SEQS, 1, width), lambda i: (i, 0, 0)), row_spec(tile, width), whole_spec(gain.shape)],
        out_specs=[row_spec(tile, width), whole_spec((8, width))],
        out_shape=[jax.ShapeDtypeStruct((rows, width), BF16), jax.ShapeDtypeStruct((8, width), F32)],
        scratch_shapes=[pltpu.VMEM((8, width), F32)],
        compiler_params=params(),
        name="close",
    )(x, gn, gb, gs, gr, gain)


def in_order(count, seqs):
    row = lax.broadcasted_iota(jnp.int32, (count * seqs, count * seqs), 0)
    col = lax.broadcasted_iota(jnp.int32, (count * seqs, count * seqs), 1)
    return ((col % seqs == row // count) & (col // seqs == row % count)).astype(BF16)


def neighbour(by):
    depth, spot = lax.axis_index("dp"), lax.axis_index("ctx")
    return depth, lax.rem(spot + by + FLIPS, FLIPS)


ENTER_RELAYS = {
    0: ((1, "spread"), (2, "spread"), (3, "spread")),
    3: ((1, "cross"),),
    4: ((2, "cross"),),
    5: ((3, "cross"),),
    6: ((1, "hand_over"), (2, "hand_over")),
    7: ((3, "hand_over"),),
}


def enter_kernel(
    depths, span,
    x_ref, prefix_ref, bq_ref, bo_ref, bu_ref, bd_ref, one_ref, two_ref,
    wq_out, wo_out, wu_out, wd_out, gain_out, q_out, k_out, v_out, kp_out, vp_out, n_out, np_out, mixed_out, prob_out,
    sums_out, psum_out,
    xp, wq, gains, q, k, v, kp, vp, n, n_prev, mixed, prob, slots,
    send, recv, keep, gain_send, gain_recv, sum_send, sum_recv, tok_send, tok_recv, out_sem, prob_sem, wq_sem,
):
    rows, width = x_ref.shape
    tile = TILE_SEQS * span
    tiles = rows // tile
    chunks = tiles // CHUNK_TILES
    seqs = rows // span
    spot = lax.axis_index("ctx")
    scale = (width // HEADS) ** -0.5
    gathers = [
        Gather(depths, own, full, send.at[a], recv.at[a], keep.at[a])
        for a, (own, full) in enumerate(((bq_ref, wq), (bo_ref, wo_out), (bu_ref, wu_out), (bd_ref, wd_out)))
    ]
    gain_share = Share(depths, gains, gain_send, gain_recv)
    sum_share = Share(depths, slots, sum_send, sum_recv)
    shard = jnp.concatenate([one_ref[...].reshape(1, -1), two_ref[...].reshape(1, -1)], axis=0).astype(F32)
    owner = lax.broadcasted_iota(jnp.int32, (2, width), 1) // shard.shape[1]
    gains[spot] = jnp.where(owner == spot, jnp.concatenate([shard] * FLIPS, axis=1), 0.0)

    @pl.when(spot == 0)
    def _():
        xp[...] = jnp.zeros_like(xp)

    def at(i):
        return pl.ds(pl.multiple_of(i * tile, tile), tile)

    def chunk_at(c):
        return pl.ds(pl.multiple_of(c * CHUNK_TILES * tile, CHUNK_TILES * tile), CHUNK_TILES * tile)

    def token_copy(i):
        return pltpu.make_async_remote_copy(
            src_ref=x_ref.at[at(i)],
            dst_ref=xp.at[at(i)],
            send_sem=tok_send.at[i],
            recv_sem=tok_recv.at[i],
            device_id=neighbour(1),
            device_id_type=MESH,
        )

    def out_copy(a, i):
        pairs = ((q, q_out), (k, k_out), (v, v_out), (n, n_out), (kp, kp_out), (vp, vp_out), (n_prev, np_out), (mixed, mixed_out))
        return pltpu.make_async_copy(pairs[a][0].at[at(i)], pairs[a][1].at[at(i)], out_sem.at[a, i])

    def prob_copy(i):
        part = pl.ds(i * TILE_SEQS, TILE_SEQS)
        return pltpu.make_async_copy(prob.at[part], prob_out.at[part], prob_sem.at[i])

    def send_tokens(first, last):
        @pl.when(spot < FLIPS - 1)
        def _():
            for i in range(first, last):
                token_copy(i).start()

    greet(depths)
    gathers[0].begin()
    gain_share.begin()
    send_tokens(0, 2)
    gain_share.forward()
    gain_share.complete()
    gain = gains[0]
    for c in range(1, FLIPS):
        gain = gain + gains[c]
    gain_out[...] = gain

    def normalize(c):
        n[chunk_at(c), :] = (standardize(x_ref[chunk_at(c), :].astype(F32))[0] * gain[0:1]).astype(BF16)

    def keep_mean(part, ref, weigh):
        means = [
            jnp.sum(ref[s * span : (s + 1) * span, :].astype(F32), axis=0, keepdims=True) * weigh for s in range(seqs)
        ]
        slots[spot, :, part * width : (part + 1) * width] = jnp.concatenate(means, axis=0).astype(BF16)

    pl.loop(0, chunks // 2)(normalize)
    gathers[0].spread()
    pl.loop(chunks // 2, chunks)(normalize)
    gathers[0].cross()
    keep_mean(2, n, 1.0)
    gathers[0].hand_over()
    for gather in gathers[1:]:
        gather.begin()
    send_tokens(2, 5)
    gathers[0].complete()
    wq_copy = pltpu.make_async_copy(wq, wq_out, wq_sem.at[0])
    wq_copy.start()

    def send_out(a, c):
        for t in range(CHUNK_TILES):
            out_copy(a, c * CHUNK_TILES + t).start()

    @pl.loop(0, chunks)
    def _(c):
        weight = rows_of(wq)
        normed = n[chunk_at(c), :]
        k[chunk_at(c), :] = dot_t(normed, weight[width : 2 * width]).astype(BF16)
        v[chunk_at(c), :] = dot_t(normed, weight[2 * width :]).astype(BF16)
        for a in (1, 2, 3):
            send_out(a, c)

    keep_mean(0, k, 1.0 / span)
    keep_mean(1, v, 1.0 / span)
    sum_share.begin()
    send_tokens(5, tiles)

    @pl.loop(0, chunks)
    def _(c):
        weight = rows_of(wq)
        rows_q = dot_t(n[chunk_at(c), :], weight[:width]).astype(BF16)
        q[chunk_at(c), :] = (rows_q.astype(F32) * scale).astype(BF16)
        send_out(0, c)

    sum_share.forward()

    def project_prev(c):
        @pl.when(spot > 0)
        def _():
            for t in range(CHUNK_TILES):
                token_copy(c * CHUNK_TILES + t).wait_recv()

        weight = rows_of(wq)
        normed = (standardize(xp[chunk_at(c), :].astype(F32))[0] * gain[0:1]).astype(BF16)
        n_prev[chunk_at(c), :] = normed
        kp[chunk_at(c), :] = dot_t(normed, weight[width : 2 * width]).astype(BF16)
        vp[chunk_at(c), :] = dot_t(normed, weight[2 * width :]).astype(BF16)
        for a in (4, 5, 6):
            send_out(a, c)

    pl.loop(0, 2)(project_prev)
    sum_share.complete()
    ordered = dot(in_order(FLIPS, seqs), slots[...].reshape(FLIPS * seqs, 3 * width)).astype(BF16)
    sums_out[...] = ordered.reshape(sums_out.shape)

    @pl.loop(0, tiles)
    def _(i):
        @pl.when((lax.rem(i, CHUNK_TILES) == 0) & (i >= 2 * CHUNK_TILES))
        def _():
            project_prev(i // CHUNK_TILES)

        for s in range(TILE_SEQS):
            here = pl.ds(pl.multiple_of(i * tile + s * span, span), span)
            seq = i * TILE_SEQS + s

            def keep_prob(p, both, seq=seq):
                prob[seq, p] = both

            rows_mixed, all_sums = attend_one(
                span,
                spot,
                prefix_ref[seq // prefix_ref.shape[1], lax.rem(seq, prefix_ref.shape[1])],
                q[here, :],
                jnp.concatenate([kp[here, :], k[here, :]], axis=0),
                jnp.concatenate([vp[here, :], v[here, :]], axis=0),
                sums_out[seq],
                keep_prob,
            )
            mixed[here, :] = rows_mixed
            psum_out[seq] = all_sums
        out_copy(7, i).start()
        prob_copy(i).start()
        for when, relays in ENTER_RELAYS.items():

            @pl.when(i == when)
            def _(relays=relays):
                for a, name in relays:
                    getattr(gathers[a], name)()

    for gather in gathers[1:]:
        gather.complete()
    for move in (*gathers, gain_share, sum_share):
        move.close()

    @pl.when(spot < FLIPS - 1)
    def _():
        for i in range(tiles):
            token_copy(i).wait_send()

    wq_copy.wait()

    @pl.loop(0, tiles)
    def _(i):
        for a in range(8):
            out_copy(a, i).wait()
        prob_copy(i).wait()


def enter(x, prefix, blocks, gain_one, gain_two, span, depths):
    rows, width = x.shape
    tile = TILE_SEQS * span
    tiles, seqs = rows // tile, rows // span
    low = jax.ShapeDtypeStruct((rows, width), BF16)
    fulls = [jax.ShapeDtypeStruct((depths, FLIPS) + b.shape, BF16) for b in blocks]
    prob_shape = (seqs, HEADS // 2, 2 * span, 2 * span)
    vmem = pl.BlockSpec(memory_space=pltpu.VMEM)
    far = pl.BlockSpec(memory_space=pl.ANY)
    sems = pltpu.SemaphoreType.DMA
    held = pltpu.VMEM((rows, width), BF16)
    return pl.pallas_call(
        functools.partial(enter_kernel, depths, span),
        in_specs=[vmem, pl.BlockSpec(memory_space=pltpu.SMEM)] + [vmem] * 6,
        out_specs=[far] * 4 + [vmem] + [far] * 9 + [vmem] * 2,
        out_shape=fulls
        + [jax.ShapeDtypeStruct((2, width), F32)]
        + [low] * 8
        + [
            jax.ShapeDtypeStruct(prob_shape, BF16),
            jax.ShapeDtypeStruct((seqs, FLIPS, 3 * width), BF16),
            jax.ShapeDtypeStruct((seqs, HEADS * FLIPS, span), BF16),
        ],
        scratch_shapes=[
            held,
            pltpu.VMEM(fulls[0].shape, BF16),
            pltpu.VMEM((FLIPS, 2, width), F32),
        ]
        + [held] * 8
        + [pltpu.VMEM(prob_shape, BF16), pltpu.VMEM((FLIPS, seqs, 3 * width), BF16)]
        + [
            sems((4, depths * FLIPS)), sems((4, depths * FLIPS)), sems((4,)),
            sems((FLIPS,)), sems((FLIPS,)), sems((FLIPS,)), sems((FLIPS,)),
            sems((tiles,)), sems((tiles,)), sems((8, tiles)), sems((tiles,)), sems((1,)),
        ],
        compiler_params=pltpu.CompilerParams(collective_id=0, has_side_effects=True, vmem_limit_bytes=VMEM_MOST),
        name="enter",
    )(x, prefix, *blocks, gain_one, gain_two)


LEAVE_RELAYS = {
    1: ((0, "cross"),),
    2: ((1, "cross"), (0, "spread")),
    3: ((2, "cross"), (0, "climb")),
    4: ((1, "spread"),),
    5: ((2, "spread"), (1, "climb")),
    6: ((2, "climb"),),
}


def leave_kernel(
    depths, span,
    q_in, k_in, v_in, kp_in, vp_in, gm_in, n_in, np_in, prob_in, gr_in, x_in,
    psum_ref, sums_ref, wq_ref, gout_ref, gup_ref, gdown_ref, gain_ref, ggain_ref,
    ig_out, dqkv_out, dout_out, dup_out, ddown_out, dgain_out,
    held, prob, gn, gp, gb, gr, x, ig, acc, part, gs, gs_send_buf, gs_slots, gain_slots, gain_deep,
    *rest,
):
    moves_refs, sems = rest[:16], rest[16:]
    send, recv, gs_send, gs_recv, gain_send, gain_recv, deep_send, deep_recv, gb_send, gb_recv, in_sem, late_sem, ig_sem = sems
    rows, width = gn.shape
    tile = TILE_SEQS * span
    tiles = rows // tile
    seqs = rows // span
    spot = lax.axis_index("ctx")
    depth = lax.axis_index("dp")
    parts = (gout_ref, gup_ref, gdown_ref, part)
    scatters = [
        Scatter(depths, parts[a], *moves_refs[4 * a : 4 * a + 4], send.at[a], recv.at[a]) for a in range(4)
    ]
    gain_share = Share(depths, gain_slots, gain_send, gain_recv)
    gs_moves = Moves(depths, gs_send, gs_recv)
    deep_moves = Moves(depths, deep_send, deep_recv)

    def at(i):
        return pl.ds(pl.multiple_of(i * tile, tile), tile)

    def loads(i, slot):
        arrays = (q_in, k_in, v_in, kp_in, vp_in, gm_in, n_in, np_in)
        copies = [pltpu.make_async_copy(ref.at[at(i)], held.at[slot, a], in_sem.at[slot, a]) for a, ref in enumerate(arrays)]
        of_tile = pl.ds(i * TILE_SEQS, TILE_SEQS)
        return copies + [pltpu.make_async_copy(prob_in.at[of_tile], prob.at[slot], in_sem.at[slot, len(arrays)])]

    def gb_copy(i):
        return pltpu.make_async_remote_copy(
            src_ref=gp.at[at(i)],
            dst_ref=gb.at[at(i)],
            send_sem=gb_send.at[i],
            recv_sem=gb_recv.at[i],
            device_id=neighbour(-1),
            device_id_type=MESH,
        )

    for copy in loads(0, 0):
        copy.start()
    late = [pltpu.make_async_copy(gr_in, gr, late_sem.at[0]), pltpu.make_async_copy(x_in, x, late_sem.at[1])]

    @pl.when(spot == FLIPS - 1)
    def _():
        gb[...] = jnp.zeros_like(gb)

    greet(depths)
    for scatter in scatters[:3]:
        scatter.begin()
    acc[...] = jnp.zeros_like(acc)

    def tile_step(i, gain_sum):
        slot = lax.rem(i, 2)
        for copy in loads(i, slot):
            copy.wait()

        @pl.when(i + 1 < tiles)
        def _():
            for copy in loads(i + 1, 1 - slot):
                copy.start()

        pieces = []
        for s in range(TILE_SEQS):
            here = slice(s * span, (s + 1) * span)
            seq = i * TILE_SEQS + s
            pieces.append(
                return_one(
                    span,
                    held[slot, 0, here],
                    jnp.concatenate([held[slot, 3, here], held[slot, 1, here]], axis=0),
                    jnp.concatenate([held[slot, 4, here], held[slot, 2, here]], axis=0),
                    sums_ref[seq],
                    held[slot, 5, here],
                    lambda p, s=s: prob[slot, s, p],
                    psum_ref[seq],
                )
            )
        of_tile = pl.ds(i * TILE_SEQS, TILE_SEQS)
        normed, normed_prev = held[slot, 6], held[slot, 7]
        normed_sum = sums_ref[of_tile, :, 2 * width :].reshape(-1, width)
        to_own, to_prev, to_sums = return_tile(rows_of(wq_ref), *zip(*pieces), normed, normed_prev, normed_sum, acc)
        gn[at(i), :] = to_own
        gp[at(i), :] = to_prev.astype(BF16)
        gs[i] = to_sums.astype(BF16)

        @pl.when(spot > 0)
        def _():
            gb_copy(i).start()

        for when, relays in LEAVE_RELAYS.items():

            @pl.when(i == when)
            def _(relays=relays):
                for a, name in relays:
                    getattr(scatters[a], name)()

        @pl.when(i == tiles - 3)
        def _():
            for copy in late:
                copy.start()

        return (
            gain_sum
            + fold_rows(to_own * normed.astype(F32))
            + fold_rows(to_prev * normed_prev.astype(F32))
            + fold_rows(to_sums * normed_sum.astype(F32))
        )

    gain_sum = lax.fori_loop(0, tiles, tile_step, jnp.zeros((8, width), F32))

    by_spot = lax.dot_general(
        in_order(FLIPS, seqs), gs[...].reshape(seqs * FLIPS, width), (((0,), (0,)), ((), ())), preferred_element_type=F32
    )
    gs_send_buf[...] = by_spot.astype(BF16).reshape(gs_send_buf.shape)
    for flip in (6, 7, 2, 4, 3, 5, 1):
        gs_moves.start(gs_send_buf.at[spot_of(depths, 0, flip)[1]], gs_slots.at[flip], flip, 0, flip)
    total_one = jnp.sum(gain_sum, axis=0, keepdims=True) / gain_ref[0:1]
    total_two = jnp.sum(ggain_ref[...], axis=0, keepdims=True)
    gain_slots[spot] = jnp.concatenate([total_one, total_two], axis=0)
    gain_share.begin()
    put_blocks(part, acc[...].astype(BF16).T, 1)
    scatters[3].begin()
    dout_out[...] = scatters[0].finish()
    gain_share.forward()
    scatters[3].cross()
    dup_out[...] = scatters[1].finish()
    ddown_out[...] = scatters[2].finish()
    for copy in late:
        copy.wait()
    for flip in range(1, FLIPS):
        gs_moves.landed(gs_slots.at[flip], flip)
    shared = gs_send_buf[spot].astype(F32)
    for flip in range(1, FLIPS):
        shared = shared + gs_slots[flip].astype(F32)
    gain = gain_ref[0:1]

    def close_tile(i):
        @pl.when(spot < FLIPS - 1)
        def _():
            gb_copy(i).wait_recv()

        unit, inv = standardize(x[at(i), :].astype(F32))
        grad_norm = gn[at(i), :] + gb[at(i), :].astype(F32)
        lifted = [
            grad_norm[s * span : (s + 1) * span] + shared[i * TILE_SEQS + s : i * TILE_SEQS + s + 1]
            for s in range(TILE_SEQS)
        ]
        grad_norm = jnp.concatenate(lifted, axis=0)
        ig[at(i), :] = (gr[at(i), :] + norm_back(grad_norm, unit, inv, gain)).astype(BF16)
        pltpu.make_async_copy(ig.at[at(i)], ig_out.at[at(i)], ig_sem.at[i]).start()

    cut = tiles // 3
    for i in range(cut):
        close_tile(i)
    scatters[3].spread()
    gain_share.complete()
    over_ctx = gain_slots[0]
    for c in range(1, FLIPS):
        over_ctx = over_ctx + gain_slots[c]
    gain_deep[0] = over_ctx
    for turn in range(1, depths):
        deep_moves.start(gain_deep.at[0], gain_deep.at[depths - turn], depths - turn, turn, 0)
    for i in range(cut, 2 * cut):
        close_tile(i)
    scatters[3].climb()
    for i in range(2 * cut, tiles):
        close_tile(i)
    for turn in range(1, depths):
        deep_moves.landed(gain_deep.at[turn], turn)
    over_all = gain_deep[0]
    for turn in range(1, depths):
        over_all = over_all + gain_deep[turn]
    lanes = width // FLIPS
    mine = jnp.zeros((2, lanes), F32)
    for c in range(FLIPS):
        mine = jnp.where(spot == c, over_all[:, c * lanes : (c + 1) * lanes], mine)
    dgain_out[...] = mine
    dqkv_out[...] = scatters[3].finish()
    for scatter in scatters:
        scatter.close()
    gain_share.close()
    gs_moves.drain(gs_slots.at[0])
    deep_moves.drain(gain_deep.at[0])

    @pl.when(spot > 0)
    def _():
        for i in range(tiles):
            gb_copy(i).wait_send()

    for i in range(tiles):
        pltpu.make_async_copy(ig.at[at(i)], ig_out.at[at(i)], ig_sem.at[i]).wait()


def leave(arrays, psum, sums, wq, partials, gains, ggain, span, depths):
    rows, width = arrays[0].shape
    tile = TILE_SEQS * span
    tiles, seqs = rows // tile, rows // span
    vmem = pl.BlockSpec(memory_space=pltpu.VMEM)
    far = pl.BlockSpec(memory_space=pl.ANY)
    sems = pltpu.SemaphoreType.DMA
    low = pltpu.VMEM((rows, width), BF16)
    high = pltpu.VMEM((rows, width), F32)
    shapes = [p.shape[2:] for p in (*partials, wq)]
    scratch = [
        pltpu.VMEM((2, 8, tile, width), BF16),
        pltpu.VMEM((2, TILE_SEQS, HEADS // 2, 2 * span, 2 * span), BF16),
        high, low, low, high, low, low,
        pltpu.VMEM((width, 3 * width), F32),
        pltpu.VMEM(wq.shape, BF16),
        pltpu.VMEM((tiles, TILE_SEQS * FLIPS, width), BF16),
        pltpu.VMEM((FLIPS, seqs, width), BF16),
        pltpu.VMEM((FLIPS, seqs, width), BF16),
        pltpu.VMEM((FLIPS, 2, width), F32),
        pltpu.VMEM((depths, 2, width), F32),
    ]
    for shape in shapes:
        scratch += scatter_scratch(shape, depths)
    scratch += [
        sems((4, 8 * depths)), sems((4, 8 * depths)), sems((FLIPS,)), sems((FLIPS,)), sems((FLIPS,)), sems((FLIPS,)),
        sems((depths,)), sems((depths,)), sems((tiles,)), sems((tiles,)), sems((2, 9)), sems((2,)), sems((tiles,)),
    ]
    outs = [jax.ShapeDtypeStruct(shape, F32) for shape in (shapes[3], *shapes[:3])]
    return pl.pallas_call(
        functools.partial(leave_kernel, depths, span),
        in_specs=[far] * 11 + [vmem] * 8,
        out_specs=[far] + [vmem] * 5,
        out_shape=[jax.ShapeDtypeStruct((rows, width), BF16), *outs, jax.ShapeDtypeStruct((2, width // FLIPS), F32)],
        scratch_shapes=scratch,
        compiler_params=pltpu.CompilerParams(collective_id=1, has_side_effects=True, vmem_limit_bytes=VMEM_MOST),
        name="leave",
    )(*arrays, psum, sums, wq, *partials, gains, ggain)


def direct_shards(tokens, prefix, blocks, gain_one, gain_two, cotangent):
    span, width = tokens.shape[2], tokens.shape[3]
    depths = lax.axis_size("dp")
    x = tokens.reshape(-1, width)
    grad = cotangent.reshape(-1, width)
    (wq, wo, wu, wd, gains, q, k, v, kp, vp, n, n_prev, mixed, prob, sums, psum) = enter(
        x, prefix, blocks, gain_one, gain_two, span, depths
    )
    out, gm, gr, gout, gup, gdown, ggain = feed(x, mixed, grad, wo, wu, wd, gains, TILE_SEQS * span)
    arrays = (q, k, v, kp, vp, gm, n, n_prev, prob, gr, x)
    ig, dqkv, dout, dup, ddown, dgain = leave(arrays, psum, sums, wq, (gout, gup, gdown), gains, ggain, span, depths)
    return (
        out.reshape(tokens.shape),
        ig.reshape(tokens.shape),
        dqkv.T,
        dout.T,
        dup,
        ddown.T,
        dgain[0],
        dgain[1],
    )


def fetch(block, rows_along):
    spot, depth = (0, 1) if rows_along == 1 else (1, 0)
    whole = lax.all_gather(lax.all_gather(block, "ctx", axis=spot, tiled=True), "dp", axis=depth, tiled=True)
    return whole[None, None]


def reduce_weight(partial, rows_along):
    spot, depth = (0, 1) if rows_along == 1 else (1, 0)
    columns = lax.psum_scatter(partial[0, 0], "ctx", scatter_dimension=spot, tiled=True)
    return lax.psum_scatter(columns, "dp", scatter_dimension=depth, tiled=True).astype(F32)


def shards(tokens, prefix, w_qkv, w_out, w_up, w_down, gain_one, gain_two, cotangent):
    span, width = tokens.shape[2], tokens.shape[3]
    count = lax.axis_size("ctx")
    blocks = (w_qkv.T, w_out.T, w_up, w_down.T)
    if count == FLIPS and all(b.shape[0] % 16 == 0 and b.shape[1] % 128 == 0 for b in blocks):
        return direct_shards(tokens, prefix, blocks, gain_one, gain_two, cotangent)
    along = (1, 1, 0, 1)
    x = tokens.reshape(-1, width)
    grad = cotangent.reshape(-1, width)
    tile = TILE_SEQS * span
    block = lax.axis_index("ctx").reshape(1).astype(jnp.int32)
    x_prev = lax.ppermute(x, "ctx", [(i, i + 1) for i in range(count - 1)])
    gain1 = lax.all_gather(gain_one, "ctx", axis=0, tiled=True).astype(F32).reshape(1, width)
    gain2 = lax.all_gather(gain_two, "ctx", axis=0, tiled=True).astype(F32).reshape(1, width)
    wq, wo, wu, wd = (fetch(b, r) for b, r in zip(blocks, along))
    q, k, v, kp, vp, n, n_prev, own_sums = project(x, x_prev, wq, gain1, span)
    own_sums = own_sums.reshape(-1, 2 * width)
    n_sum = jnp.sum(n.reshape(-1, span, width).astype(F32), axis=1).astype(BF16)
    everything = lax.all_gather(jnp.concatenate([own_sums, n_sum], axis=1), "ctx", axis=0, tiled=False)
    everything = jnp.transpose(everything, (1, 0, 2))
    sums, n_sums = everything[:, :, : 2 * width], everything[:, :, 2 * width :]
    mixed, prob, psum = attend(prefix.reshape(-1), block, q, k, v, kp, vp, sums, span)
    out, gm, gr, gout, gup, gdown, ggain2 = feed(x, mixed, grad, wo, wu, wd, gain2, tile)
    gn, gp, gs, gqkv = give_back(q, k, v, kp, vp, sums, gm, prob, psum, n, n_prev, n_sums, wq, span)
    gb = lax.ppermute(gp, "ctx", [(i, i - 1) for i in range(1, count)])
    gs_own = lax.psum_scatter(gs, "ctx", scatter_dimension=1, tiled=True)
    input_grad, ggain1 = close(x, gn, gb, gs_own, gr, gain1, span)
    gains = jnp.concatenate([jnp.sum(ggain1, axis=0), jnp.sum(ggain2, axis=0)]).reshape(2, width)
    gains = lax.psum(gains, "dp")
    gains = lax.psum_scatter(gains, "ctx", scatter_dimension=1, tiled=True)
    sums_w = [reduce_weight(p, r) for p, r in zip((gqkv, gout, gup, gdown), along)]
    return (
        out.reshape(tokens.shape),
        input_grad.reshape(tokens.shape),
        sums_w[0].T,
        sums_w[1].T,
        sums_w[2],
        sums_w[3].T,
        gains[0],
        gains[1],
    )


def solution(mesh):
    rows = P(None, "dp", "ctx", None)
    both = P("dp", "ctx")
    return jax.shard_map(
        shards,
        mesh=mesh,
        in_specs=(rows, P(None, "dp"), both, both, both, both, P("ctx"), P("ctx"), rows),
        out_specs=(rows, rows, both, both, both, both, P("ctx"), P("ctx")),
        check_vma=False,
    )
```

```python
import functools
import math

import jax
import jax.numpy as jnp
from jax import lax
from jax.experimental import pallas as pl
from jax.experimental.pallas import tpu as pltpu
from jax.sharding import PartitionSpec as P

HEADS = 8
EPSILON = 1e-05
MASKED = -1e30
F32 = jnp.float32
BF16 = jnp.bfloat16
TILE_SEQS = 2
CHUNK_TILES = 2
FF_CHUNK = 1024
VMEM_MOST = 60 * 1024 * 1024

MESH = pl.DeviceIdType.MESH
FLIPS = 8


def place():
    depth, spot = lax.axis_index("dp"), lax.axis_index("ctx")
    return depth, spot, (spot % 2, (spot // 2) % 2, spot // 4)


def flipped(bits, flip):
    out = 0
    for i, bit in enumerate(bits):
        out = out + ((1 - bit) if (flip >> i) & 1 else bit) * (1 << i)
    return out


def spot_of(depths, turn, flip):
    depth, _, bits = place()
    return lax.rem(depth + turn, depths), flipped(bits, flip)


def greet(depths):
    barrier = pltpu.get_barrier_semaphore()
    peers = [(turn, 0) for turn in range(1, depths)] + [(0, flip) for flip in range(1, FLIPS)]
    for turn, flip in peers:
        pl.semaphore_signal(barrier, inc=1, device_id=spot_of(depths, turn, flip), device_id_type=MESH)
    pl.semaphore_wait(barrier, len(peers))


class Moves:
    def __init__(self, depths, send, recv):
        self.depths, self.send, self.recv, self.sent = depths, send, recv, 0

    def copy(self, source, target, number, slot, to_turn, to_flip):
        return pltpu.make_async_remote_copy(
            src_ref=source,
            dst_ref=target,
            send_sem=self.send.at[number],
            recv_sem=self.recv.at[slot],
            device_id=spot_of(self.depths, to_turn, to_flip),
            device_id_type=MESH,
        )

    def start(self, source, target, slot, to_turn, to_flip):
        self.copy(source, target, self.sent, slot, to_turn, to_flip).start()
        self.sent += 1

    def landed(self, target, slot):
        self.copy(target, target, 0, slot, 0, 1).wait_recv()

    def drain(self, like):
        for number in range(self.sent):
            self.copy(like, like, number, 0, 0, 1).wait_send()


class Gather(Moves):
    def __init__(self, depths, own, full, send, recv, keep):
        super().__init__(depths, send, recv)
        self.own, self.full, self.keep = own, full, keep

    def block(self, turn, flip):
        return self.full.at[spot_of(self.depths, turn, flip)]

    def push(self, turn, flip, to_turn, to_flip):
        there = ((turn - to_turn) % self.depths) * FLIPS + (flip ^ to_flip)
        source = self.own if (turn, flip) == (0, 0) else self.block(turn, flip)
        self.start(source, self.block(turn, flip), there, to_turn, to_flip)

    def arrive(self, turn, flip):
        self.landed(self.block(turn, flip), turn * FLIPS + flip)

    def begin(self):
        for turn in range(1, self.depths):
            self.push(0, 0, turn, 0)
        for flip in (2, 4, 1):
            self.push(0, 0, 0, flip)
        pltpu.make_async_copy(self.own, self.block(0, 0), self.keep).start()

    def spread(self):
        for turn in range(1, self.depths):
            self.arrive(turn, 0)
            for flip in (2, 4, 1):
                self.push(turn, 0, 0, flip)

    def cross(self):
        for turn in range(self.depths):
            self.arrive(turn, 2)
            if turn < self.depths // 2:
                self.push(turn, 2, 0, 4)
            self.push(turn, 2, 0, 1)
            self.arrive(turn, 4)
            if turn >= self.depths // 2:
                self.push(turn, 4, 0, 2)
            self.push(turn, 4, 0, 1)

    def hand_over(self):
        for turn in range(self.depths):
            self.arrive(turn, 6)
            self.push(turn, 6, 0, 1)

    def complete(self):
        for turn in range(self.depths):
            for flip in (1, 3, 5, 7):
                self.arrive(turn, flip)
        pltpu.make_async_copy(self.own, self.block(0, 0), self.keep).wait()

    def close(self):
        self.drain(self.own)


class Share(Moves):
    def __init__(self, depths, slots, send, recv):
        super().__init__(depths, send, recv)
        self.slots = slots

    def block(self, flip):
        return self.slots.at[spot_of(self.depths, 0, flip)[1]]

    def begin(self):
        for flip in (2, 4, 6, 1):
            self.start(self.block(0), self.block(0), flip, 0, flip)

    def forward(self):
        for flip in (2, 4, 6):
            self.landed(self.block(flip), flip)
            self.start(self.block(flip), self.block(flip), flip ^ 1, 0, 1)

    def complete(self):
        for flip in (1, 3, 5, 7):
            self.landed(self.block(flip), flip)

    def close(self):
        self.drain(self.block(0))


class Scatter(Moves):
    def __init__(self, depths, part, mate, total, near, far, send, recv):
        super().__init__(depths, send, recv)
        self.part, self.mate, self.total, self.near, self.far = part, mate, total, near, far

    def block(self, turn, flip):
        return self.part.at[spot_of(self.depths, turn, flip)]

    push = Moves.start
    arrive = Moves.landed

    def begin(self, turns):
        for flip in (6, 2, 4, 0):
            for turn in turns:
                at = (flip // 2, turn)
                self.push(self.block(turn, flip ^ 1), self.mate.at[at], flip // 2 * self.depths + turn, 0, 1)

    def fold(self, turn, flip):
        self.arrive(self.mate.at[flip // 2, turn], flip // 2 * self.depths + turn)
        mine = self.block(turn, flip)[...].astype(F32)
        self.total[flip // 2, turn] = (mine + self.mate[flip // 2, turn].astype(F32)).astype(BF16)

    def cross(self, turns):
        base = 4 * self.depths
        for turn in turns:
            self.fold(turn, 6)
            by = 2 if turn < self.depths // 2 else 4
            self.push(self.total.at[3, turn], self.near.at[turn], base + turn, 0, by)

    def spread(self, turns):
        base = 4 * self.depths
        late = 5 * self.depths
        for turn in turns:
            self.fold(turn, 2)
            self.fold(turn, 4)
            via = 2 if turn < self.depths // 2 else 1
            self.arrive(self.near.at[turn], base + turn)
            self.total[via, turn] = (self.total[via, turn].astype(F32) + self.near[turn].astype(F32)).astype(BF16)
            self.push(self.total.at[1, turn], self.far.at[0, turn], late + turn, 0, 2)
            self.push(self.total.at[2, turn], self.far.at[1, turn], late + self.depths + turn, 0, 4)

    def climb(self, turns):
        late = 5 * self.depths
        last = 7 * self.depths
        for turn in turns:
            self.fold(turn, 0)
            self.arrive(self.far.at[0, turn], late + turn)
            self.arrive(self.far.at[1, turn], late + self.depths + turn)
            self.total[0, turn] = (
                self.total[0, turn].astype(F32) + self.far[0, turn].astype(F32) + self.far[1, turn].astype(F32)
            ).astype(BF16)
            if turn:
                back = self.depths - turn
                self.push(self.total.at[0, turn], self.far.at[2, back], last + back, turn, 0)

    def finish(self):
        last = 7 * self.depths
        out = self.total[0, 0].astype(F32)
        for turn in range(1, self.depths):
            self.arrive(self.far.at[2, turn], last + turn)
            out = out + self.far[2, turn].astype(F32)
        return out

    def close(self):
        self.drain(self.near.at[0])


def scatter_scratch(block, depths):
    return [
        pltpu.VMEM((4, depths) + block, BF16),
        pltpu.VMEM((4, depths) + block, BF16),
        pltpu.VMEM((depths,) + block, BF16),
        pltpu.VMEM((3, depths) + block, BF16),
    ]


def dot(a, b):
    return jnp.dot(a, b, preferred_element_type=F32)


def dot_t(a, b):
    return lax.dot_general(a, b, (((1,), (1,)), ((), ())), preferred_element_type=F32)


def standardize(values):
    row_mean = jnp.mean(values, axis=-1, keepdims=True)
    centred = values - row_mean
    variance = jnp.mean(centred * centred, axis=-1, keepdims=True)
    inv_std = lax.rsqrt(variance + EPSILON)
    return (centred * inv_std, inv_std)


def norm_back(grad_in, unit_rows, inv_std, gain):
    scaled = grad_in * gain
    row_mean = jnp.mean(scaled, axis=-1, keepdims=True)
    cross_mean = jnp.mean(scaled * unit_rows, axis=-1, keepdims=True)
    return inv_std * (scaled - row_mean - unit_rows * cross_mean)


def fold_rows(values):
    return jnp.sum(values.reshape(-1, 8, values.shape[-1]), axis=0)


def gelu_parts(upper):
    cdf = 0.5 * (1.0 + lax.erf(upper * 0.7071067811865476))
    slope = cdf + upper * jnp.exp(-0.5 * upper * upper) * 0.3989422804014327
    return (upper * cdf, slope)


def pair_halves(rows):
    lanes = lax.broadcasted_iota(jnp.int32, rows.shape, 1)
    half = rows.shape[1] // 2
    zero = jnp.zeros_like(rows)
    return jnp.concatenate(
        [jnp.where(lanes < half, rows, zero), jnp.where(lanes >= half, rows, zero)], axis=0
    )


def head_select(count, width):
    head_of_row = lax.broadcasted_iota(jnp.int32, (HEADS * count, width), 0) // count
    head_of_lane = lax.broadcasted_iota(jnp.int32, (HEADS * count, width), 1) // (width // HEADS)
    return head_of_row == head_of_lane


def per_head(rows, select):
    tiled = jnp.concatenate([rows.astype(F32)] * HEADS, axis=0)
    return jnp.where(select, tiled, 0.0).astype(BF16)


def rows_of(ref):
    depths, lanes = ref.shape[0], ref.shape[3]
    return jnp.concatenate([ref[d].reshape(-1, lanes) for d in range(depths)], axis=1)


def lanes_of(ref, chunk, along):
    lanes = ref.shape[3]
    take = (lambda i: ref[i]) if along == 0 else (lambda i: ref[:, i])
    if lanes >= FF_CHUNK:
        per = lanes // FF_CHUNK
        cut = slice(chunk % per * FF_CHUNK, (chunk % per + 1) * FF_CHUNK)
        return take(chunk // per).reshape(-1, lanes)[:, cut]
    per = FF_CHUNK // lanes
    return jnp.concatenate([take(i).reshape(-1, lanes) for i in range(chunk * per, (chunk + 1) * per)], axis=1)


def put_blocks(ref, values, rows_along):
    depths, spots, rows, lanes = ref.shape
    for d in range(depths):
        for c in range(spots):
            r, l = (c, d) if rows_along == 1 else (d, c)
            ref[d, c] = values[r * rows : (r + 1) * rows, l * lanes : (l + 1) * lanes].astype(ref.dtype)


def project_kernel(x_ref, xp_ref, w_ref, gain_ref, q_ref, k_ref, v_ref, kp_ref, vp_ref, n_ref, np_ref, sum_ref):
    width = x_ref.shape[1]
    gain = gain_ref[...]
    weight = rows_of(w_ref)
    normed = (standardize(x_ref[...].astype(F32))[0] * gain).astype(BF16)
    n_ref[...] = normed
    scale = (width // HEADS) ** -0.5
    q_ref[...] = (dot_t(normed, weight[:width]).astype(BF16).astype(F32) * scale).astype(BF16)
    for part, out in ((1, k_ref), (2, v_ref)):
        rows = dot_t(normed, weight[part * width : (part + 1) * width]).astype(BF16)
        out[...] = rows
        means = jnp.mean(rows.astype(F32).reshape(TILE_SEQS, -1, width), axis=1)
        sum_ref[0, :, (part - 1) * width : part * width] = means.astype(BF16)
    normed_prev = (standardize(xp_ref[...].astype(F32))[0] * gain).astype(BF16)
    np_ref[...] = normed_prev
    kp_ref[...] = dot_t(normed_prev, weight[width : 2 * width]).astype(BF16)
    vp_ref[...] = dot_t(normed_prev, weight[2 * width :]).astype(BF16)


def row_spec(rows, width):
    return pl.BlockSpec((rows, width), lambda i: (i, 0))


def whole_spec(shape):
    return pl.BlockSpec(shape, lambda i: (0,) * len(shape))


def params():
    return pltpu.CompilerParams(vmem_limit_bytes=VMEM_MOST)


def project(x, x_prev, w_qkv, gain, span):
    rows, width = x.shape
    tile = TILE_SEQS * span
    low = jax.ShapeDtypeStruct((rows, width), BF16)
    return pl.pallas_call(
        project_kernel,
        grid=(rows // tile,),
        in_specs=[row_spec(tile, width)] * 2 + [whole_spec(w_qkv.shape), whole_spec(gain.shape)],
        out_specs=[row_spec(tile, width)] * 7
        + [pl.BlockSpec((1, TILE_SEQS, 2 * width), lambda i: (i, 0, 0))],
        out_shape=[low] * 7 + [jax.ShapeDtypeStruct((rows // tile, TILE_SEQS, 2 * width), BF16)],
        compiler_params=params(),
        name="project",
    )(x, x_prev, w_qkv, gain)


def attend_one(span, block, prefix, queries, keys, values, sums, keep_prob):
    width = queries.shape[1]
    pair = 2 * width // HEADS
    half = pair // 2
    count = sums.shape[0]
    select = head_select(count, width)
    unit_pos = lax.broadcasted_iota(jnp.int32, (span, span), 0)
    query_pos = lax.broadcasted_iota(jnp.int32, (span, span), 1)
    sum_id = lax.broadcasted_iota(jnp.int32, (count, span), 0)
    sum_query = lax.broadcasted_iota(jnp.int32, (count, span), 1)
    bias_prev = jnp.where(block >= 1, 0.0, MASKED).astype(F32)
    start = block * span
    own_ok = (unit_pos <= query_pos) | (start + unit_pos < prefix)
    bias_own = jnp.where(own_ok, 0.0, MASKED)
    sum_ok = (sum_id <= block - 1) | (
        (start + sum_query < prefix) & (sum_id >= block + 1) & ((sum_id + 1) * span <= prefix)
    )
    bias_sum = jnp.where(sum_ok, math.log(span), MASKED)
    values_t = values.T
    sum_keys = per_head(sums[:, :width], select)
    sum_values_t = per_head(sums[:, width : 2 * width], select).T
    sum_scores = dot_t(sum_keys, queries)
    mixed_parts = []
    sum_probs = []
    for p in range(HEADS // 2):
        lanes = slice(p * pair, (p + 1) * pair)
        scores = dot_t(keys[:, lanes], pair_halves(queries[:, lanes]))
        probs = []
        for e in range(2):
            h = 2 * p + e
            cols = slice(e * span, (e + 1) * span)
            s_prev = scores[:span, cols]
            s_own = scores[span:, cols] + bias_own
            s_sum = sum_scores[h * count : (h + 1) * count] + bias_sum
            most = jnp.maximum(
                jnp.maximum(
                    jnp.max(s_prev, axis=0, keepdims=True) + bias_prev,
                    jnp.max(s_own, axis=0, keepdims=True),
                ),
                jnp.max(s_sum, axis=0, keepdims=True),
            )
            e_prev = jnp.exp(s_prev + (bias_prev - most))
            e_own = jnp.exp(s_own - most)
            e_sum = jnp.exp(s_sum - most)
            total = (
                jnp.sum(e_prev, axis=0, keepdims=True)
                + jnp.sum(e_own, axis=0, keepdims=True)
                + jnp.sum(e_sum, axis=0, keepdims=True)
            )
            inverse = 1.0 / total
            probs.append(jnp.concatenate([e_prev * inverse, e_own * inverse], axis=0).astype(BF16))
            sum_probs.append(e_sum * inverse)
        both = jnp.concatenate(probs, axis=1)
        keep_prob(p, both)
        crossed = dot(values_t[lanes, :], both)
        mixed_parts.append(crossed[:half, :span])
        mixed_parts.append(crossed[half:, span:])
    all_sums = jnp.concatenate(sum_probs, axis=0).astype(BF16)
    mixed_t = jnp.concatenate(mixed_parts, axis=0) + dot(sum_values_t, all_sums)
    return mixed_t.T.astype(BF16), all_sums


def attend_kernel(
    span, prefix_ref, block_ref, q_ref, k_ref, v_ref, kp_ref, vp_ref, sums_ref, mixed_ref, prob_ref, psum_ref
):
    for s in range(TILE_SEQS):
        rows = slice(s * span, (s + 1) * span)

        def keep_prob(p, both, s=s):
            prob_ref[s, p] = both

        mixed, all_sums = attend_one(
            span,
            block_ref[0],
            prefix_ref[pl.program_id(0) * TILE_SEQS + s],
            q_ref[rows, :],
            jnp.concatenate([kp_ref[rows, :], k_ref[rows, :]], axis=0),
            jnp.concatenate([vp_ref[rows, :], v_ref[rows, :]], axis=0),
            sums_ref[s],
            keep_prob,
        )
        mixed_ref[rows, :] = mixed
        psum_ref[s] = all_sums


def attend(prefix, block, q, k, v, kp, vp, sums, span):
    rows, width = q.shape
    tile = TILE_SEQS * span
    seqs, count = sums.shape[0], sums.shape[1]
    pairs = HEADS // 2
    return pl.pallas_call(
        functools.partial(attend_kernel, span),
        grid=(rows // tile,),
        in_specs=[pl.BlockSpec(memory_space=pltpu.SMEM)] * 2
        + [row_spec(tile, width)] * 5
        + [pl.BlockSpec((TILE_SEQS, count, 2 * width), lambda i: (i, 0, 0))],
        out_specs=[
            row_spec(tile, width),
            pl.BlockSpec((TILE_SEQS, pairs, 2 * span, 2 * span), lambda i: (i, 0, 0, 0)),
            pl.BlockSpec((TILE_SEQS, HEADS * count, span), lambda i: (i, 0, 0)),
        ],
        out_shape=[
            jax.ShapeDtypeStruct((rows, width), BF16),
            jax.ShapeDtypeStruct((seqs, pairs, 2 * span, 2 * span), BF16),
            jax.ShapeDtypeStruct((seqs, HEADS * count, span), BF16),
        ],
        compiler_params=params(),
        name="attend",
    )(prefix, block, q, k, v, kp, vp, sums)


def feed_kernel(
    x_ref, mixed_ref, g_ref, wo_ref, wu_ref, wd_ref, gain_ref,
    out_ref, gm_ref, gr_ref, gout_ref, gup_ref, gdown_ref, ggain_ref,
    acc_out, acc_up, acc_down, acc_gain,
):
    step = pl.program_id(0)

    @pl.when(step == 0)
    def _():
        acc_out[...] = jnp.zeros_like(acc_out)
        acc_up[...] = jnp.zeros_like(acc_up)
        acc_down[...] = jnp.zeros_like(acc_down)
        acc_gain[...] = jnp.zeros_like(acc_gain)

    gain = gain_ref[gain_ref.shape[0] - 1 :, :]
    mixed = mixed_ref[...]
    w_out = rows_of(wo_ref)
    resid = x_ref[...].astype(F32) + dot_t(mixed, w_out)
    unit, inv = standardize(resid)
    normed = (unit * gain).astype(BF16)
    normed_t = normed.T
    grad = g_ref[...]
    grad_t = grad.T
    hidden_width = acc_up.shape[1]
    result = resid
    grad_norm = None
    for c in range(hidden_width // FF_CHUNK):
        cols = slice(c * FF_CHUNK, (c + 1) * FF_CHUNK)
        w_up = lanes_of(wu_ref, c, 1)
        w_down = lanes_of(wd_ref, c, 0)
        upper = dot(normed, w_up)
        grad_hidden = dot(grad, w_down)
        activated, slope = gelu_parts(upper)
        hidden = activated.astype(BF16)
        grad_upper = (grad_hidden * slope).astype(BF16)
        result = result + dot_t(hidden, w_down)
        back = dot_t(grad_upper, w_up)
        grad_norm = back if grad_norm is None else grad_norm + back
        acc_down[:, cols] += dot(grad_t, hidden)
        acc_up[:, cols] += dot(normed_t, grad_upper)
    out_ref[...] = result.astype(BF16)
    acc_gain[...] += fold_rows(grad_norm * unit)
    grad_resid = grad.astype(F32) + norm_back(grad_norm, unit, inv, gain)
    gr_ref[...] = grad_resid
    grad_branch = grad_resid.astype(BF16)
    acc_out[...] += dot(grad_branch.T, mixed)
    gm_ref[...] = dot(grad_branch, w_out).astype(BF16)

    @pl.when(step == pl.num_programs(0) - 1)
    def _():
        put_blocks(gout_ref, acc_out, 1)
        put_blocks(gup_ref, acc_up, 0)
        put_blocks(gdown_ref, acc_down, 1)
        ggain_ref[...] = acc_gain[...]


def feed(x, mixed, grad, w_out, w_up, w_down, gain, tile):
    rows, width = x.shape
    hidden = w_up.shape[1] * w_up.shape[3]
    wide = (width, hidden)
    square = (width, width)
    return pl.pallas_call(
        feed_kernel,
        grid=(rows // tile,),
        in_specs=[row_spec(tile, width)] * 3
        + [whole_spec(w_out.shape), whole_spec(w_up.shape), whole_spec(w_down.shape), whole_spec(gain.shape)],
        out_specs=[row_spec(tile, width)] * 3
        + [whole_spec(w_out.shape), whole_spec(w_up.shape), whole_spec(w_down.shape), whole_spec((8, width))],
        out_shape=[
            jax.ShapeDtypeStruct((rows, width), BF16),
            jax.ShapeDtypeStruct((rows, width), BF16),
            jax.ShapeDtypeStruct((rows, width), F32),
            jax.ShapeDtypeStruct(w_out.shape, BF16),
            jax.ShapeDtypeStruct(w_up.shape, BF16),
            jax.ShapeDtypeStruct(w_down.shape, BF16),
            jax.ShapeDtypeStruct((8, width), F32),
        ],
        scratch_shapes=[
            pltpu.VMEM(square, F32),
            pltpu.VMEM(wide, F32),
            pltpu.VMEM(wide, F32),
            pltpu.VMEM((8, width), F32),
        ],
        compiler_params=params(),
        name="feed",
    )(x, mixed, grad, w_out, w_up, w_down, gain)


def return_one(span, queries, keys, values, sums, grad_mixed, prob_at, sum_low):
    width = queries.shape[1]
    pair = 2 * width // HEADS
    half = pair // 2
    count = sums.shape[0]
    scale = half ** -0.5
    select = head_select(count, width)
    keys_t = keys.T
    sum_keys_t = per_head(sums[:, :width], select).T
    sum_values = per_head(sums[:, width : 2 * width], select)
    sum_prob = sum_low.astype(F32)
    sum_moved = sum_prob * dot_t(sum_values, grad_mixed)
    grad_q_parts = []
    grad_k_parts = []
    grad_v_parts = []
    sum_grads = []
    for p in range(HEADS // 2):
        lanes = slice(p * pair, (p + 1) * pair)
        grads2 = pair_halves(grad_mixed[:, lanes])
        grad_prob = dot_t(values[:, lanes], grads2)
        low = prob_at(p)
        prob = low.astype(F32)
        moved = prob * grad_prob
        deltas = jnp.sum(moved, axis=0, keepdims=True)
        sums_of = []
        for e in range(2):
            h = 2 * p + e
            part = slice(h * count, (h + 1) * count)
            delta = deltas[:, e * span : (e + 1) * span] + jnp.sum(sum_moved[part], axis=0, keepdims=True)
            sums_of.append(delta)
            sum_grads.append(sum_moved[part] - sum_prob[part] * delta)
        grad_scores = (moved - prob * jnp.concatenate(sums_of, axis=1)).astype(BF16)
        grad_k_parts.append(dot(grad_scores, pair_halves(queries[:, lanes])))
        grad_v_parts.append(dot(low, grads2))
        crossed = dot(keys_t[lanes, :], grad_scores)
        grad_q_parts.append(crossed[:half, :span])
        grad_q_parts.append(crossed[half:, span:])
    sum_scores_grad = jnp.concatenate(sum_grads, axis=0).astype(BF16)
    grad_q = jnp.concatenate(grad_q_parts, axis=0) + dot(sum_keys_t, sum_scores_grad)
    grad_q = (grad_q.T * scale).astype(BF16)
    grad_k = jnp.concatenate(grad_k_parts, axis=1).astype(BF16)
    grad_v = jnp.concatenate(grad_v_parts, axis=1).astype(BF16)
    wide_k = jnp.where(select, dot(sum_scores_grad, queries), 0.0)
    wide_v = jnp.where(select, dot(sum_low, grad_mixed), 0.0)
    folded_k = jnp.sum(wide_k.reshape(HEADS, count, width), axis=0)
    folded_v = jnp.sum(wide_v.reshape(HEADS, count, width), axis=0)
    return (
        jnp.concatenate([grad_q, grad_k[span:], grad_v[span:]], axis=1),
        jnp.concatenate([grad_k[:span], grad_v[:span]], axis=1),
        jnp.concatenate([folded_k, folded_v], axis=1) * (1.0 / span),
    )


def return_tile(weight, own, before, shared, normed, normed_prev, normed_sum, acc):
    width = normed.shape[1]
    grad_own = jnp.concatenate(own, axis=0)
    grad_before = jnp.concatenate(before, axis=0)
    grad_shared = jnp.concatenate(shared, axis=0).astype(BF16)
    normed_t = normed.T
    acc[:, :width] += dot(normed_t, grad_own[:, :width])
    acc[:, width:] += (
        dot(normed_t, grad_own[:, width:]) + dot(normed_prev.T, grad_before) + dot(normed_sum.T, grad_shared)
    )
    return grad_own, dot(grad_before, weight[width:]), dot(grad_shared, weight[width:])


def return_kernel(
    span, q_ref, k_ref, v_ref, kp_ref, vp_ref, sums_ref, gm_ref, prob_ref, psum_ref, n_ref, np_ref, nsum_ref, w_ref,
    gn_ref, gp_ref, gs_ref, gqkv_ref, acc,
):
    step = pl.program_id(0)

    @pl.when(step == 0)
    def _():
        acc[...] = jnp.zeros_like(acc)

    parts = []
    for s in range(TILE_SEQS):
        rows = slice(s * span, (s + 1) * span)
        parts.append(
            return_one(
                span,
                q_ref[rows, :],
                jnp.concatenate([kp_ref[rows, :], k_ref[rows, :]], axis=0),
                jnp.concatenate([vp_ref[rows, :], v_ref[rows, :]], axis=0),
                sums_ref[s],
                gm_ref[rows, :],
                lambda p, s=s: prob_ref[s, p],
                psum_ref[s],
            )
        )
    normed_sum = nsum_ref[...].reshape(-1, nsum_ref.shape[2])
    weight = rows_of(w_ref)
    grad_own, gp, gs = return_tile(weight, *zip(*parts), n_ref[...], np_ref[...], normed_sum, acc)
    gn_ref[...] = dot(grad_own, weight)
    gp_ref[...] = gp.astype(BF16)
    gs_ref[...] = gs.reshape(gs_ref.shape).astype(BF16)

    @pl.when(step == pl.num_programs(0) - 1)
    def _():
        put_blocks(gqkv_ref, acc[...].astype(BF16).T, 1)


def give_back(q, k, v, kp, vp, sums, gm, prob, psum, n, n_prev, n_sum, w_qkv, span):
    rows, width = q.shape
    tile = TILE_SEQS * span
    seqs, count = sums.shape[0], sums.shape[1]
    pairs = HEADS // 2
    return pl.pallas_call(
        functools.partial(return_kernel, span),
        grid=(rows // tile,),
        in_specs=[row_spec(tile, width)] * 5
        + [
            pl.BlockSpec((TILE_SEQS, count, 2 * width), lambda i: (i, 0, 0)),
            row_spec(tile, width),
            pl.BlockSpec((TILE_SEQS, pairs, 2 * span, 2 * span), lambda i: (i, 0, 0, 0)),
            pl.BlockSpec((TILE_SEQS, HEADS * count, span), lambda i: (i, 0, 0)),
            row_spec(tile, width),
            row_spec(tile, width),
            pl.BlockSpec((TILE_SEQS, count, width), lambda i: (i, 0, 0)),
            whole_spec(w_qkv.shape),
        ],
        out_specs=[
            row_spec(tile, width),
            row_spec(tile, width),
            pl.BlockSpec((TILE_SEQS, count, width), lambda i: (i, 0, 0)),
            whole_spec(w_qkv.shape),
        ],
        out_shape=[
            jax.ShapeDtypeStruct((rows, width), F32),
            jax.ShapeDtypeStruct((rows, width), BF16),
            jax.ShapeDtypeStruct((seqs, count, width), BF16),
            jax.ShapeDtypeStruct(w_qkv.shape, BF16),
        ],
        scratch_shapes=[pltpu.VMEM((width, 3 * width), F32)],
        compiler_params=params(),
        name="give_back",
    )(q, k, v, kp, vp, sums, gm, prob, psum, n, n_prev, n_sum, w_qkv)


def close_kernel(span, x_ref, gn_ref, gb_ref, gs_ref, gr_ref, gain_ref, out_ref, ggain_ref, acc):
    step = pl.program_id(0)
    width = x_ref.shape[1]

    @pl.when(step == 0)
    def _():
        acc[...] = jnp.zeros_like(acc)

    unit, inv = standardize(x_ref[...].astype(F32))
    grad_norm = gn_ref[...] + gb_ref[...].astype(F32)
    lifted = [
        grad_norm[s * span : (s + 1) * span] + gs_ref[s].astype(F32) for s in range(TILE_SEQS)
    ]
    grad_norm = jnp.concatenate(lifted, axis=0)
    acc[...] += fold_rows(grad_norm * unit)
    part = norm_back(grad_norm, unit, inv, gain_ref[...])
    out_ref[...] = (gr_ref[...] + part).astype(BF16)

    @pl.when(step == pl.num_programs(0) - 1)
    def _():
        ggain_ref[...] = acc[...]


def close(x, gn, gb, gs, gr, gain, span):
    rows, width = x.shape
    tile = TILE_SEQS * span
    return pl.pallas_call(
        functools.partial(close_kernel, span),
        grid=(rows // tile,),
        in_specs=[row_spec(tile, width)] * 3
        + [pl.BlockSpec((TILE_SEQS, 1, width), lambda i: (i, 0, 0)), row_spec(tile, width), whole_spec(gain.shape)],
        out_specs=[row_spec(tile, width), whole_spec((8, width))],
        out_shape=[jax.ShapeDtypeStruct((rows, width), BF16), jax.ShapeDtypeStruct((8, width), F32)],
        scratch_shapes=[pltpu.VMEM((8, width), F32)],
        compiler_params=params(),
        name="close",
    )(x, gn, gb, gs, gr, gain)


def in_order(count, seqs):
    row = lax.broadcasted_iota(jnp.int32, (count * seqs, count * seqs), 0)
    col = lax.broadcasted_iota(jnp.int32, (count * seqs, count * seqs), 1)
    return ((col % seqs == row // count) & (col // seqs == row % count)).astype(BF16)


def neighbour(by):
    depth, spot = lax.axis_index("dp"), lax.axis_index("ctx")
    return depth, lax.rem(spot + by + FLIPS, FLIPS)


ENTER_RELAYS = {
    1: ((1, "spread"), (2, "spread"), (3, "spread")),
    4: ((1, "cross"), (2, "cross")),
    5: ((3, "cross"),),
    7: ((1, "hand_over"), (2, "hand_over"), (3, "hand_over")),
}


def enter_kernel(
    depths, span,
    x_ref, prefix_ref, bq_ref, bo_ref, bu_ref, bd_ref, one_ref, two_ref,
    wq_out, wo_out, wu_out, wd_out, gain_out, q_out, k_out, v_out, kp_out, vp_out, n_out, np_out, mixed_out, prob_out,
    sums_out, psum_out,
    xp, wq, gains, q, k, v, kp, vp, n, n_prev, mixed, prob, slots,
    send, recv, keep, gain_send, gain_recv, sum_send, sum_recv, tok_send, tok_recv, out_sem, prob_sem, wq_sem,
):
    rows, width = x_ref.shape
    tile = TILE_SEQS * span
    tiles = rows // tile
    chunks = tiles // CHUNK_TILES
    seqs = rows // span
    spot = lax.axis_index("ctx")
    scale = (width // HEADS) ** -0.5
    gathers = [
        Gather(depths, own, full, send.at[a], recv.at[a], keep.at[a])
        for a, (own, full) in enumerate(((bq_ref, wq), (bo_ref, wo_out), (bu_ref, wu_out), (bd_ref, wd_out)))
    ]
    gain_share = Share(depths, gains, gain_send, gain_recv)
    sum_share = Share(depths, slots, sum_send, sum_recv)
    shard = jnp.concatenate([one_ref[...].reshape(1, -1), two_ref[...].reshape(1, -1)], axis=0).astype(F32)
    owner = lax.broadcasted_iota(jnp.int32, (2, width), 1) // shard.shape[1]
    gains[spot] = jnp.where(owner == spot, jnp.concatenate([shard] * FLIPS, axis=1), 0.0)

    @pl.when(spot == 0)
    def _():
        xp[...] = jnp.zeros_like(xp)

    def at(i):
        return pl.ds(pl.multiple_of(i * tile, tile), tile)

    def chunk_at(c):
        return pl.ds(pl.multiple_of(c * CHUNK_TILES * tile, CHUNK_TILES * tile), CHUNK_TILES * tile)

    def token_copy(i):
        return pltpu.make_async_remote_copy(
            src_ref=x_ref.at[at(i)],
            dst_ref=xp.at[at(i)],
            send_sem=tok_send.at[i],
            recv_sem=tok_recv.at[i],
            device_id=neighbour(1),
            device_id_type=MESH,
        )

    def out_copy(a, i):
        pairs = ((q, q_out), (k, k_out), (v, v_out), (n, n_out), (kp, kp_out), (vp, vp_out), (n_prev, np_out), (mixed, mixed_out))
        return pltpu.make_async_copy(pairs[a][0].at[at(i)], pairs[a][1].at[at(i)], out_sem.at[a, i])

    def prob_copy(i):
        part = pl.ds(i * TILE_SEQS, TILE_SEQS)
        return pltpu.make_async_copy(prob.at[part], prob_out.at[part], prob_sem.at[i])

    def send_tokens(first, last):
        @pl.when(spot < FLIPS - 1)
        def _():
            for i in range(first, last):
                token_copy(i).start()

    greet(depths)
    gathers[0].begin()
    gain_share.begin()
    send_tokens(0, 2)
    gain_share.forward()
    gain_share.complete()
    gain = gains[0]
    for c in range(1, FLIPS):
        gain = gain + gains[c]
    gain_out[...] = gain

    def normalize(c):
        n[chunk_at(c), :] = (standardize(x_ref[chunk_at(c), :].astype(F32))[0] * gain[0:1]).astype(BF16)

    def keep_mean(part, ref, weigh):
        means = [
            jnp.sum(ref[s * span : (s + 1) * span, :].astype(F32), axis=0, keepdims=True) * weigh for s in range(seqs)
        ]
        slots[spot, :, part * width : (part + 1) * width] = jnp.concatenate(means, axis=0).astype(BF16)

    pl.loop(0, chunks // 2)(normalize)
    gathers[0].spread()
    pl.loop(chunks // 2, chunks)(normalize)
    gathers[0].cross()
    keep_mean(2, n, 1.0)
    gathers[0].hand_over()
    send_tokens(2, 5)
    gathers[0].complete()
    wq_copy = pltpu.make_async_copy(wq, wq_out, wq_sem.at[0])
    wq_copy.start()

    def send_out(a, c):
        for t in range(CHUNK_TILES):
            out_copy(a, c * CHUNK_TILES + t).start()

    @pl.loop(0, chunks)
    def _(c):
        weight = rows_of(wq)
        normed = n[chunk_at(c), :]
        k[chunk_at(c), :] = dot_t(normed, weight[width : 2 * width]).astype(BF16)
        v[chunk_at(c), :] = dot_t(normed, weight[2 * width :]).astype(BF16)
        for a in (1, 2, 3):
            send_out(a, c)

    keep_mean(0, k, 1.0 / span)
    keep_mean(1, v, 1.0 / span)
    sum_share.begin()
    send_tokens(5, tiles)
    for gather in gathers[1:]:
        gather.begin()

    @pl.loop(0, chunks)
    def _(c):
        weight = rows_of(wq)
        rows_q = dot_t(n[chunk_at(c), :], weight[:width]).astype(BF16)
        q[chunk_at(c), :] = (rows_q.astype(F32) * scale).astype(BF16)
        send_out(0, c)

    sum_share.forward()

    def project_prev(c):
        @pl.when(spot > 0)
        def _():
            for t in range(CHUNK_TILES):
                token_copy(c * CHUNK_TILES + t).wait_recv()

        weight = rows_of(wq)
        normed = (standardize(xp[chunk_at(c), :].astype(F32))[0] * gain[0:1]).astype(BF16)
        n_prev[chunk_at(c), :] = normed
        kp[chunk_at(c), :] = dot_t(normed, weight[width : 2 * width]).astype(BF16)
        vp[chunk_at(c), :] = dot_t(normed, weight[2 * width :]).astype(BF16)
        for a in (4, 5, 6):
            send_out(a, c)

    pl.loop(0, 2)(project_prev)
    sum_share.complete()
    ordered = dot(in_order(FLIPS, seqs), slots[...].reshape(FLIPS * seqs, 3 * width)).astype(BF16)
    sums_out[...] = ordered.reshape(sums_out.shape)

    @pl.loop(0, tiles)
    def _(i):
        @pl.when((lax.rem(i, CHUNK_TILES) == 0) & (i >= 2 * CHUNK_TILES))
        def _():
            project_prev(i // CHUNK_TILES)

        for s in range(TILE_SEQS):
            here = pl.ds(pl.multiple_of(i * tile + s * span, span), span)
            seq = i * TILE_SEQS + s

            def keep_prob(p, both, seq=seq):
                prob[seq, p] = both

            rows_mixed, all_sums = attend_one(
                span,
                spot,
                prefix_ref[seq // prefix_ref.shape[1], lax.rem(seq, prefix_ref.shape[1])],
                q[here, :],
                jnp.concatenate([kp[here, :], k[here, :]], axis=0),
                jnp.concatenate([vp[here, :], v[here, :]], axis=0),
                sums_out[seq],
                keep_prob,
            )
            mixed[here, :] = rows_mixed
            psum_out[seq] = all_sums
        out_copy(7, i).start()
        prob_copy(i).start()
        for when, relays in ENTER_RELAYS.items():

            @pl.when(i == when)
            def _(relays=relays):
                for a, name in relays:
                    getattr(gathers[a], name)()

    for gather in gathers[1:]:
        gather.complete()
    for move in (*gathers, gain_share, sum_share):
        move.close()

    @pl.when(spot < FLIPS - 1)
    def _():
        for i in range(tiles):
            token_copy(i).wait_send()

    wq_copy.wait()

    @pl.loop(0, tiles)
    def _(i):
        for a in range(8):
            out_copy(a, i).wait()
        prob_copy(i).wait()


def enter(x, prefix, blocks, gain_one, gain_two, span, depths):
    rows, width = x.shape
    tile = TILE_SEQS * span
    tiles, seqs = rows // tile, rows // span
    low = jax.ShapeDtypeStruct((rows, width), BF16)
    fulls = [jax.ShapeDtypeStruct((depths, FLIPS) + b.shape, BF16) for b in blocks]
    prob_shape = (seqs, HEADS // 2, 2 * span, 2 * span)
    vmem = pl.BlockSpec(memory_space=pltpu.VMEM)
    far = pl.BlockSpec(memory_space=pl.ANY)
    sems = pltpu.SemaphoreType.DMA
    held = pltpu.VMEM((rows, width), BF16)
    return pl.pallas_call(
        functools.partial(enter_kernel, depths, span),
        in_specs=[vmem, pl.BlockSpec(memory_space=pltpu.SMEM)] + [vmem] * 6,
        out_specs=[far] * 4 + [vmem] + [far] * 9 + [vmem] * 2,
        out_shape=fulls
        + [jax.ShapeDtypeStruct((2, width), F32)]
        + [low] * 8
        + [
            jax.ShapeDtypeStruct(prob_shape, BF16),
            jax.ShapeDtypeStruct((seqs, FLIPS, 3 * width), BF16),
            jax.ShapeDtypeStruct((seqs, HEADS * FLIPS, span), BF16),
        ],
        scratch_shapes=[
            held,
            pltpu.VMEM(fulls[0].shape, BF16),
            pltpu.VMEM((FLIPS, 2, width), F32),
        ]
        + [held] * 8
        + [pltpu.VMEM(prob_shape, BF16), pltpu.VMEM((FLIPS, seqs, 3 * width), BF16)]
        + [
            sems((4, depths * FLIPS)), sems((4, depths * FLIPS)), sems((4,)),
            sems((FLIPS,)), sems((FLIPS,)), sems((FLIPS,)), sems((FLIPS,)),
            sems((tiles,)), sems((tiles,)), sems((8, tiles)), sems((tiles,)), sems((1,)),
        ],
        compiler_params=pltpu.CompilerParams(collective_id=0, has_side_effects=True, vmem_limit_bytes=VMEM_MOST),
        name="enter",
    )(x, prefix, *blocks, gain_one, gain_two)


LEAVE_RELAYS = {
    1: ((0, "cross"), (1, "cross")),
    2: ((2, "cross"),),
    3: ((0, "spread"), (1, "spread")),
    4: ((2, "spread"),),
    6: ((0, "climb"), (1, "climb")),
    7: ((2, "climb"),),
}


def leave_kernel(
    depths, span,
    q_in, k_in, v_in, kp_in, vp_in, gm_in, n_in, np_in, prob_in, gr_in, x_in,
    psum_ref, sums_ref, wq_ref, gout_ref, gup_ref, gdown_ref, gain_ref, ggain_ref,
    ig_out, dqkv_out, dout_out, dup_out, ddown_out, dgain_out,
    held, prob, kept, before, shared_rows, turned, turned_prev, turned_sum, one_sum, gp, gb, gr, x, ig, part, gs_send_buf, gs_slots, gain_slots, gain_deep,
    *rest,
):
    moves_refs, sems = rest[:16], rest[16:]
    send, recv, gs_send, gs_recv, gain_send, gain_recv, deep_send, deep_recv, gb_send, gb_recv, in_sem, late_sem, ig_sem = sems
    rows, width = gp.shape
    tile = TILE_SEQS * span
    tiles = rows // tile
    seqs = rows // span
    spot = lax.axis_index("ctx")
    parts = (gout_ref, gup_ref, gdown_ref, part)
    scatters = [
        Scatter(depths, parts[a], *moves_refs[4 * a : 4 * a + 4], send.at[a], recv.at[a]) for a in range(4)
    ]
    gain_share = Share(depths, gain_slots, gain_send, gain_recv)
    gs_moves = Moves(depths, gs_send, gs_recv)
    deep_moves = Moves(depths, deep_send, deep_recv)

    def at(i):
        return pl.ds(pl.multiple_of(i * tile, tile), tile)

    def at_sums(i):
        return pl.ds(pl.multiple_of(i * TILE_SEQS * FLIPS, TILE_SEQS * FLIPS), TILE_SEQS * FLIPS)

    def loads(i, slot):
        arrays = (q_in, k_in, v_in, kp_in, vp_in, gm_in, n_in, np_in)
        copies = [pltpu.make_async_copy(ref.at[at(i)], held.at[slot, a], in_sem.at[slot, a]) for a, ref in enumerate(arrays)]
        of_tile = pl.ds(i * TILE_SEQS, TILE_SEQS)
        return copies + [pltpu.make_async_copy(prob_in.at[of_tile], prob.at[slot], in_sem.at[slot, len(arrays)])]

    def gb_copy(i):
        return pltpu.make_async_remote_copy(
            src_ref=gp.at[at(i)],
            dst_ref=gb.at[at(i)],
            send_sem=gb_send.at[i],
            recv_sem=gb_recv.at[i],
            device_id=neighbour(-1),
            device_id_type=MESH,
        )

    for copy in loads(0, 0):
        copy.start()
    late = [pltpu.make_async_copy(gr_in, gr, late_sem.at[0]), pltpu.make_async_copy(x_in, x, late_sem.at[1])]

    @pl.when(spot == FLIPS - 1)
    def _():
        gb[...] = jnp.zeros_like(gb)

    greet(depths)
    turns = (*range(1, depths), 0)
    for scatter in scatters[:3]:
        scatter.begin(turns)

    @pl.loop(0, tiles)
    def _(i):
        slot = lax.rem(i, 2)
        for copy in loads(i, slot):
            copy.wait()

        @pl.when(i + 1 < tiles)
        def _():
            for copy in loads(i + 1, 1 - slot):
                copy.start()

        pieces = []
        for s in range(TILE_SEQS):
            here = slice(s * span, (s + 1) * span)
            seq = i * TILE_SEQS + s
            pieces.append(
                return_one(
                    span,
                    held[slot, 0, here],
                    jnp.concatenate([held[slot, 3, here], held[slot, 1, here]], axis=0),
                    jnp.concatenate([held[slot, 4, here], held[slot, 2, here]], axis=0),
                    sums_ref[seq],
                    held[slot, 5, here],
                    lambda p, s=s: prob[slot, s, p],
                    psum_ref[seq],
                )
            )
        own, back, shared = (jnp.concatenate(rows, axis=0) for rows in zip(*pieces))
        weight_kv = rows_of(wq_ref)[width:]
        kept[at(i), :] = own
        before[at(i), :] = back
        gp[at(i), :] = dot(back, weight_kv).astype(BF16)
        shared_rows[at_sums(i), :] = shared.astype(BF16)
        turned[:, at(i)] = held[slot, 6].T
        turned_prev[:, at(i)] = held[slot, 7].T

        @pl.when(spot > 0)
        def _():
            gb_copy(i).start()

        for when, relays in LEAVE_RELAYS.items():

            @pl.when(i == when)
            def _(relays=relays):
                for a, name in relays:
                    getattr(scatters[a], name)(turns)

        @pl.when(i == tiles - 3)
        def _():
            for copy in late:
                copy.start()

    to_sums = dot(shared_rows[...], rows_of(wq_ref)[width:]).astype(BF16)
    by_spot = lax.dot_general(
        in_order(FLIPS, seqs), to_sums, (((0,), (0,)), ((), ())), preferred_element_type=F32
    )
    gs_send_buf[...] = by_spot.astype(BF16).reshape(gs_send_buf.shape)
    for flip in (6, 7, 2, 4, 3, 5, 1):
        gs_moves.start(gs_send_buf.at[spot_of(depths, 0, flip)[1]], gs_slots.at[flip], flip, 0, flip)
    turned_sum[...] = sums_ref[:, :, 2 * width :].reshape(seqs * FLIPS, width).T
    lanes_in = width // depths

    def weigh(turns):
        owners = [spot_of(depths, turn, 0)[0] for turn in turns]
        tops = [pl.ds(pl.multiple_of(owner * lanes_in, lanes_in), lanes_in) for owner in owners]
        rows_own, rows_prev, rows_sum = (
            jnp.concatenate([ref[top, :] for top in tops], axis=0) for ref in (turned, turned_prev, turned_sum)
        )
        grad_q = dot(rows_own, kept[:, :width])
        grad_kv = dot(rows_own, kept[:, width:]) + dot(rows_prev, before[...]) + dot(rows_sum, shared_rows[...])
        low = jnp.concatenate([grad_q.astype(BF16), grad_kv.astype(BF16)], axis=1)
        for t, (owner, top) in enumerate(zip(owners, tops)):
            flat = low[t * lanes_in : (t + 1) * lanes_in].T
            part[owner] = flat.reshape(part.shape[1:])
            weighed = flat.astype(F32) * wq_ref[owner].reshape(flat.shape).astype(F32)
            one_sum[:, top] = jnp.sum(weighed, axis=0, keepdims=True)
        scatters[3].begin(turns)

    first, second = turns[: depths // 2], turns[depths // 2 :]
    weigh(first)
    weigh(second)
    scatters[3].cross(first)
    total_one = one_sum[...] / gain_ref[0:1]
    total_two = jnp.sum(ggain_ref[...], axis=0, keepdims=True)
    gain_slots[spot] = jnp.concatenate([total_one, total_two], axis=0)
    gain_share.begin()
    gain_share.forward()
    for copy in late:
        copy.wait()
    for flip in range(1, FLIPS):
        gs_moves.landed(gs_slots.at[flip], flip)
    shared = gs_send_buf[spot].astype(F32)
    for flip in range(1, FLIPS):
        shared = shared + gs_slots[flip].astype(F32)
    gain = gain_ref[0:1]

    def close_tile(i):
        @pl.when(spot < FLIPS - 1)
        def _():
            gb_copy(i).wait_recv()

        unit, inv = standardize(x[at(i), :].astype(F32))
        grad_norm = dot(kept[at(i), :], rows_of(wq_ref)) + gb[at(i), :].astype(F32)
        lifted = [
            grad_norm[s * span : (s + 1) * span] + shared[i * TILE_SEQS + s : i * TILE_SEQS + s + 1]
            for s in range(TILE_SEQS)
        ]
        grad_norm = jnp.concatenate(lifted, axis=0)
        ig[at(i), :] = (gr[at(i), :] + norm_back(grad_norm, unit, inv, gain)).astype(BF16)
        pltpu.make_async_copy(ig.at[at(i)], ig_out.at[at(i)], ig_sem.at[i]).start()

    def share_deep():
        gain_share.complete()
        over_ctx = gain_slots[0]
        for c in range(1, FLIPS):
            over_ctx = over_ctx + gain_slots[c]
        gain_deep[0] = over_ctx
        for turn in range(1, depths):
            deep_moves.start(gain_deep.at[0], gain_deep.at[depths - turn], depths - turn, turn, 0)

    after = {
        1: (functools.partial(scatters[3].cross, second), functools.partial(scatters[3].spread, first)),
        2: (share_deep, functools.partial(scatters[3].spread, second)),
        4: (functools.partial(scatters[3].climb, first),),
        6: (functools.partial(scatters[3].climb, second),),
    }
    for i in range(tiles):
        for relay in after.get(i, ()):
            relay()
        close_tile(i)
    for turn in range(1, depths):
        deep_moves.landed(gain_deep.at[turn], turn)
    over_all = gain_deep[0]
    for turn in range(1, depths):
        over_all = over_all + gain_deep[turn]
    lanes = width // FLIPS
    mine = jnp.zeros((2, lanes), F32)
    for c in range(FLIPS):
        mine = jnp.where(spot == c, over_all[:, c * lanes : (c + 1) * lanes], mine)
    dgain_out[...] = mine
    for out, scatter in zip((dout_out, dup_out, ddown_out, dqkv_out), scatters):
        out[...] = scatter.finish()
    for scatter in scatters:
        scatter.close()
    gain_share.close()
    gs_moves.drain(gs_slots.at[0])
    deep_moves.drain(gain_deep.at[0])

    @pl.when(spot > 0)
    def _():
        for i in range(tiles):
            gb_copy(i).wait_send()

    for i in range(tiles):
        pltpu.make_async_copy(ig.at[at(i)], ig_out.at[at(i)], ig_sem.at[i]).wait()


def leave(arrays, psum, sums, wq, partials, gains, ggain, span, depths):
    rows, width = arrays[0].shape
    tile = TILE_SEQS * span
    tiles, seqs = rows // tile, rows // span
    vmem = pl.BlockSpec(memory_space=pltpu.VMEM)
    far = pl.BlockSpec(memory_space=pl.ANY)
    sems = pltpu.SemaphoreType.DMA
    low = pltpu.VMEM((rows, width), BF16)
    high = pltpu.VMEM((rows, width), F32)
    shapes = [p.shape[2:] for p in (*partials, wq)]
    scratch = [
        pltpu.VMEM((2, 8, tile, width), BF16),
        pltpu.VMEM((2, TILE_SEQS, HEADS // 2, 2 * span, 2 * span), BF16),
        pltpu.VMEM((rows, 3 * width), BF16),
        pltpu.VMEM((rows, 2 * width), BF16),
        pltpu.VMEM((seqs * FLIPS, 2 * width), BF16),
        pltpu.VMEM((width, rows), BF16),
        pltpu.VMEM((width, rows), BF16),
        pltpu.VMEM((width, seqs * FLIPS), BF16),
        pltpu.VMEM((1, width), F32),
        low, low, high, low, low,
        pltpu.VMEM(wq.shape, BF16),
        pltpu.VMEM((FLIPS, seqs, width), BF16),
        pltpu.VMEM((FLIPS, seqs, width), BF16),
        pltpu.VMEM((FLIPS, 2, width), F32),
        pltpu.VMEM((depths, 2, width), F32),
    ]
    for shape in shapes:
        scratch += scatter_scratch(shape, depths)
    scratch += [
        sems((4, 8 * depths)), sems((4, 8 * depths)), sems((FLIPS,)), sems((FLIPS,)), sems((FLIPS,)), sems((FLIPS,)),
        sems((depths,)), sems((depths,)), sems((tiles,)), sems((tiles,)), sems((2, 9)), sems((2,)), sems((tiles,)),
    ]
    outs = [jax.ShapeDtypeStruct(shape, F32) for shape in (shapes[3], *shapes[:3])]
    return pl.pallas_call(
        functools.partial(leave_kernel, depths, span),
        in_specs=[far] * 11 + [vmem] * 8,
        out_specs=[far] + [vmem] * 5,
        out_shape=[jax.ShapeDtypeStruct((rows, width), BF16), *outs, jax.ShapeDtypeStruct((2, width // FLIPS), F32)],
        scratch_shapes=scratch,
        compiler_params=pltpu.CompilerParams(collective_id=1, has_side_effects=True, vmem_limit_bytes=VMEM_MOST),
        name="leave",
    )(*arrays, psum, sums, wq, *partials, gains, ggain)


def direct_shards(tokens, prefix, blocks, gain_one, gain_two, cotangent):
    span, width = tokens.shape[2], tokens.shape[3]
    depths = lax.axis_size("dp")
    x = tokens.reshape(-1, width)
    grad = cotangent.reshape(-1, width)
    (wq, wo, wu, wd, gains, q, k, v, kp, vp, n, n_prev, mixed, prob, sums, psum) = enter(
        x, prefix, blocks, gain_one, gain_two, span, depths
    )
    out, gm, gr, gout, gup, gdown, ggain = feed(x, mixed, grad, wo, wu, wd, gains, 2 * TILE_SEQS * span)
    arrays = (q, k, v, kp, vp, gm, n, n_prev, prob, gr, x)
    ig, dqkv, dout, dup, ddown, dgain = leave(arrays, psum, sums, wq, (gout, gup, gdown), gains, ggain, span, depths)
    return (
        out.reshape(tokens.shape),
        ig.reshape(tokens.shape),
        dqkv.T,
        dout.T,
        dup,
        ddown.T,
        dgain[0],
        dgain[1],
    )


def fetch(block, rows_along):
    spot, depth = (0, 1) if rows_along == 1 else (1, 0)
    whole = lax.all_gather(lax.all_gather(block, "ctx", axis=spot, tiled=True), "dp", axis=depth, tiled=True)
    return whole[None, None]


def reduce_weight(partial, rows_along):
    spot, depth = (0, 1) if rows_along == 1 else (1, 0)
    columns = lax.psum_scatter(partial[0, 0], "ctx", scatter_dimension=spot, tiled=True)
    return lax.psum_scatter(columns, "dp", scatter_dimension=depth, tiled=True).astype(F32)


def shards(tokens, prefix, w_qkv, w_out, w_up, w_down, gain_one, gain_two, cotangent):
    span, width = tokens.shape[2], tokens.shape[3]
    count = lax.axis_size("ctx")
    blocks = (w_qkv.T, w_out.T, w_up, w_down.T)
    if count == FLIPS and all(b.shape[0] % 16 == 0 and b.shape[1] % 128 == 0 for b in blocks):
        return direct_shards(tokens, prefix, blocks, gain_one, gain_two, cotangent)
    along = (1, 1, 0, 1)
    x = tokens.reshape(-1, width)
    grad = cotangent.reshape(-1, width)
    tile = TILE_SEQS * span
    block = lax.axis_index("ctx").reshape(1).astype(jnp.int32)
    x_prev = lax.ppermute(x, "ctx", [(i, i + 1) for i in range(count - 1)])
    gain1 = lax.all_gather(gain_one, "ctx", axis=0, tiled=True).astype(F32).reshape(1, width)
    gain2 = lax.all_gather(gain_two, "ctx", axis=0, tiled=True).astype(F32).reshape(1, width)
    wq, wo, wu, wd = (fetch(b, r) for b, r in zip(blocks, along))
    q, k, v, kp, vp, n, n_prev, own_sums = project(x, x_prev, wq, gain1, span)
    own_sums = own_sums.reshape(-1, 2 * width)
    n_sum = jnp.sum(n.reshape(-1, span, width).astype(F32), axis=1).astype(BF16)
    everything = lax.all_gather(jnp.concatenate([own_sums, n_sum], axis=1), "ctx", axis=0, tiled=False)
    everything = jnp.transpose(everything, (1, 0, 2))
    sums, n_sums = everything[:, :, : 2 * width], everything[:, :, 2 * width :]
    mixed, prob, psum = attend(prefix.reshape(-1), block, q, k, v, kp, vp, sums, span)
    out, gm, gr, gout, gup, gdown, ggain2 = feed(x, mixed, grad, wo, wu, wd, gain2, tile)
    gn, gp, gs, gqkv = give_back(q, k, v, kp, vp, sums, gm, prob, psum, n, n_prev, n_sums, wq, span)
    gb = lax.ppermute(gp, "ctx", [(i, i - 1) for i in range(1, count)])
    gs_own = lax.psum_scatter(gs, "ctx", scatter_dimension=1, tiled=True)
    input_grad, ggain1 = close(x, gn, gb, gs_own, gr, gain1, span)
    gains = jnp.concatenate([jnp.sum(ggain1, axis=0), jnp.sum(ggain2, axis=0)]).reshape(2, width)
    gains = lax.psum(gains, "dp")
    gains = lax.psum_scatter(gains, "ctx", scatter_dimension=1, tiled=True)
    sums_w = [reduce_weight(p, r) for p, r in zip((gqkv, gout, gup, gdown), along)]
    return (
        out.reshape(tokens.shape),
        input_grad.reshape(tokens.shape),
        sums_w[0].T,
        sums_w[1].T,
        sums_w[2],
        sums_w[3].T,
        gains[0],
        gains[1],
    )


def solution(mesh):
    rows = P(None, "dp", "ctx", None)
    both = P("dp", "ctx")
    return jax.shard_map(
        shards,
        mesh=mesh,
        in_specs=(rows, P(None, "dp"), both, both, both, both, P("ctx"), P("ctx"), rows),
        out_specs=(rows, rows, both, both, both, both, P("ctx"), P("ctx")),
        check_vma=False,
    )
```

```python
import functools
import math

import jax
import jax.numpy as jnp
from jax import lax
from jax.experimental import pallas as pl
from jax.experimental.pallas import tpu as pltpu
from jax.sharding import PartitionSpec as P

HEADS = 8
EPSILON = 1e-05
MASKED = -1e30
F32 = jnp.float32
BF16 = jnp.bfloat16
TILE_SEQS = 2
CHUNK_TILES = 2
FF_CHUNK = 1024
VMEM_MOST = 60 * 1024 * 1024

MESH = pl.DeviceIdType.MESH
FLIPS = 8


def place():
    depth, spot = lax.axis_index("dp"), lax.axis_index("ctx")
    return depth, spot, (spot % 2, (spot // 2) % 2, spot // 4)


def flipped(bits, flip):
    out = 0
    for i, bit in enumerate(bits):
        out = out + ((1 - bit) if (flip >> i) & 1 else bit) * (1 << i)
    return out


def spot_of(depths, turn, flip):
    depth, _, bits = place()
    return lax.rem(depth + turn, depths), flipped(bits, flip)


def greet(depths):
    barrier = pltpu.get_barrier_semaphore()
    peers = [(turn, 0) for turn in range(1, depths)] + [(0, flip) for flip in range(1, FLIPS)]
    for turn, flip in peers:
        pl.semaphore_signal(barrier, inc=1, device_id=spot_of(depths, turn, flip), device_id_type=MESH)
    pl.semaphore_wait(barrier, len(peers))


class Moves:
    def __init__(self, depths, send, recv):
        self.depths, self.send, self.recv, self.sent = depths, send, recv, 0

    def copy(self, source, target, number, slot, to_turn, to_flip):
        return pltpu.make_async_remote_copy(
            src_ref=source,
            dst_ref=target,
            send_sem=self.send.at[number],
            recv_sem=self.recv.at[slot],
            device_id=spot_of(self.depths, to_turn, to_flip),
            device_id_type=MESH,
        )

    def start(self, source, target, slot, to_turn, to_flip):
        self.copy(source, target, self.sent, slot, to_turn, to_flip).start()
        self.sent += 1

    def landed(self, target, slot):
        self.copy(target, target, 0, slot, 0, 1).wait_recv()

    def drain(self, like):
        for number in range(self.sent):
            self.copy(like, like, number, 0, 0, 1).wait_send()


class Gather(Moves):
    def __init__(self, depths, own, full, send, recv, keep):
        super().__init__(depths, send, recv)
        self.own, self.full, self.keep = own, full, keep

    def block(self, turn, flip):
        return self.full.at[spot_of(self.depths, turn, flip)]

    def push(self, turn, flip, to_turn, to_flip):
        there = ((turn - to_turn) % self.depths) * FLIPS + (flip ^ to_flip)
        source = self.own if (turn, flip) == (0, 0) else self.block(turn, flip)
        self.start(source, self.block(turn, flip), there, to_turn, to_flip)

    def arrive(self, turn, flip):
        self.landed(self.block(turn, flip), turn * FLIPS + flip)

    def begin(self):
        for turn in range(1, self.depths):
            self.push(0, 0, turn, 0)
        for flip in (2, 4, 1):
            self.push(0, 0, 0, flip)
        pltpu.make_async_copy(self.own, self.block(0, 0), self.keep).start()

    def spread(self):
        for turn in range(1, self.depths):
            self.arrive(turn, 0)
            for flip in (2, 4, 1):
                self.push(turn, 0, 0, flip)

    def cross(self, first_turn=0, last_turn=None):
        for turn in range(first_turn, self.depths if last_turn is None else last_turn):
            self.arrive(turn, 2)
            if turn < self.depths // 2:
                self.push(turn, 2, 0, 4)
            self.push(turn, 2, 0, 1)
            self.arrive(turn, 4)
            if turn >= self.depths // 2:
                self.push(turn, 4, 0, 2)
            self.push(turn, 4, 0, 1)

    def hand_over(self):
        for turn in range(self.depths):
            self.arrive(turn, 6)
            self.push(turn, 6, 0, 1)

    def complete(self):
        for turn in range(self.depths):
            for flip in (1, 3, 5, 7):
                self.arrive(turn, flip)
        pltpu.make_async_copy(self.own, self.block(0, 0), self.keep).wait()

    def close(self):
        self.drain(self.own)


class Share(Moves):
    def __init__(self, depths, slots, send, recv):
        super().__init__(depths, send, recv)
        self.slots = slots

    def block(self, flip):
        return self.slots.at[spot_of(self.depths, 0, flip)[1]]

    def begin(self):
        for flip in (2, 4, 6, 1):
            self.start(self.block(0), self.block(0), flip, 0, flip)

    def forward(self):
        for flip in (2, 4, 6):
            self.landed(self.block(flip), flip)
            self.start(self.block(flip), self.block(flip), flip ^ 1, 0, 1)

    def complete(self):
        for flip in (1, 3, 5, 7):
            self.landed(self.block(flip), flip)

    def close(self):
        self.drain(self.block(0))


class Scatter(Moves):
    def __init__(self, depths, part, mate, total, near, far, send, recv):
        super().__init__(depths, send, recv)
        self.part, self.mate, self.total, self.near, self.far = part, mate, total, near, far

    def block(self, turn, flip):
        return self.part.at[spot_of(self.depths, turn, flip)]

    push = Moves.start
    arrive = Moves.landed

    def begin(self, turns):
        for flip in (6, 2, 4, 0):
            for turn in turns:
                at = (flip // 2, turn)
                self.push(self.block(turn, flip ^ 1), self.mate.at[at], flip // 2 * self.depths + turn, 0, 1)

    def fold(self, turn, flip):
        self.arrive(self.mate.at[flip // 2, turn], flip // 2 * self.depths + turn)
        mine = self.block(turn, flip)[...].astype(F32)
        self.total[flip // 2, turn] = (mine + self.mate[flip // 2, turn].astype(F32)).astype(BF16)

    def cross(self, turns):
        base = 4 * self.depths
        for turn in turns:
            self.fold(turn, 6)
            by = 2 if turn < self.depths // 2 else 4
            self.push(self.total.at[3, turn], self.near.at[turn], base + turn, 0, by)

    def spread(self, turns):
        base = 4 * self.depths
        late = 5 * self.depths
        for turn in turns:
            self.fold(turn, 2)
            self.fold(turn, 4)
            via = 2 if turn < self.depths // 2 else 1
            self.arrive(self.near.at[turn], base + turn)
            self.total[via, turn] = (self.total[via, turn].astype(F32) + self.near[turn].astype(F32)).astype(BF16)
            self.push(self.total.at[1, turn], self.far.at[0, turn], late + turn, 0, 2)
            self.push(self.total.at[2, turn], self.far.at[1, turn], late + self.depths + turn, 0, 4)

    def climb(self, turns):
        late = 5 * self.depths
        last = 7 * self.depths
        for turn in turns:
            self.fold(turn, 0)
            self.arrive(self.far.at[0, turn], late + turn)
            self.arrive(self.far.at[1, turn], late + self.depths + turn)
            self.total[0, turn] = (
                self.total[0, turn].astype(F32) + self.far[0, turn].astype(F32) + self.far[1, turn].astype(F32)
            ).astype(BF16)
            if turn:
                back = self.depths - turn
                self.push(self.total.at[0, turn], self.far.at[2, back], last + back, turn, 0)

    def finish(self):
        last = 7 * self.depths
        out = self.total[0, 0].astype(F32)
        for turn in range(1, self.depths):
            self.arrive(self.far.at[2, turn], last + turn)
            out = out + self.far[2, turn].astype(F32)
        return out

    def close(self):
        self.drain(self.near.at[0])


def scatter_scratch(block, depths):
    return [
        pltpu.VMEM((4, depths) + block, BF16),
        pltpu.VMEM((4, depths) + block, BF16),
        pltpu.VMEM((depths,) + block, BF16),
        pltpu.VMEM((3, depths) + block, BF16),
    ]


def dot(a, b):
    return jnp.dot(a, b, preferred_element_type=F32)


def dot_t(a, b):
    return lax.dot_general(a, b, (((1,), (1,)), ((), ())), preferred_element_type=F32)


def standardize(values):
    row_mean = jnp.mean(values, axis=-1, keepdims=True)
    centred = values - row_mean
    variance = jnp.mean(centred * centred, axis=-1, keepdims=True)
    inv_std = lax.rsqrt(variance + EPSILON)
    return (centred * inv_std, inv_std)


def norm_back(grad_in, unit_rows, inv_std, gain):
    scaled = grad_in * gain
    row_mean = jnp.mean(scaled, axis=-1, keepdims=True)
    cross_mean = jnp.mean(scaled * unit_rows, axis=-1, keepdims=True)
    return inv_std * (scaled - row_mean - unit_rows * cross_mean)


def fold_rows(values):
    return jnp.sum(values.reshape(-1, 8, values.shape[-1]), axis=0)


def gelu_parts(upper):
    cdf = 0.5 * (1.0 + lax.erf(upper * 0.7071067811865476))
    slope = cdf + upper * jnp.exp(-0.5 * upper * upper) * 0.3989422804014327
    return (upper * cdf, slope)


def pair_halves(rows):
    lanes = lax.broadcasted_iota(jnp.int32, rows.shape, 1)
    half = rows.shape[1] // 2
    zero = jnp.zeros_like(rows)
    return jnp.concatenate(
        [jnp.where(lanes < half, rows, zero), jnp.where(lanes >= half, rows, zero)], axis=0
    )


def head_select(count, width):
    head_of_row = lax.broadcasted_iota(jnp.int32, (HEADS * count, width), 0) // count
    head_of_lane = lax.broadcasted_iota(jnp.int32, (HEADS * count, width), 1) // (width // HEADS)
    return head_of_row == head_of_lane


def per_head(rows, select):
    tiled = jnp.concatenate([rows.astype(F32)] * HEADS, axis=0)
    return jnp.where(select, tiled, 0.0).astype(BF16)


def rows_of(ref):
    depths, lanes = ref.shape[0], ref.shape[3]
    return jnp.concatenate([ref[d].reshape(-1, lanes) for d in range(depths)], axis=1)


def lanes_of(ref, chunk, along):
    lanes = ref.shape[3]
    take = (lambda i: ref[i]) if along == 0 else (lambda i: ref[:, i])
    if lanes >= FF_CHUNK:
        per = lanes // FF_CHUNK
        cut = slice(chunk % per * FF_CHUNK, (chunk % per + 1) * FF_CHUNK)
        return take(chunk // per).reshape(-1, lanes)[:, cut]
    per = FF_CHUNK // lanes
    return jnp.concatenate([take(i).reshape(-1, lanes) for i in range(chunk * per, (chunk + 1) * per)], axis=1)


def put_blocks(ref, values, rows_along):
    depths, spots, rows, lanes = ref.shape
    for d in range(depths):
        for c in range(spots):
            r, l = (c, d) if rows_along == 1 else (d, c)
            ref[d, c] = values[r * rows : (r + 1) * rows, l * lanes : (l + 1) * lanes].astype(ref.dtype)


def project_kernel(x_ref, xp_ref, w_ref, gain_ref, q_ref, k_ref, v_ref, kp_ref, vp_ref, n_ref, np_ref, sum_ref):
    width = x_ref.shape[1]
    gain = gain_ref[...]
    weight = rows_of(w_ref)
    normed = (standardize(x_ref[...].astype(F32))[0] * gain).astype(BF16)
    n_ref[...] = normed
    scale = (width // HEADS) ** -0.5
    q_ref[...] = (dot_t(normed, weight[:width]).astype(BF16).astype(F32) * scale).astype(BF16)
    for part, out in ((1, k_ref), (2, v_ref)):
        rows = dot_t(normed, weight[part * width : (part + 1) * width]).astype(BF16)
        out[...] = rows
        means = jnp.mean(rows.astype(F32).reshape(TILE_SEQS, -1, width), axis=1)
        sum_ref[0, :, (part - 1) * width : part * width] = means.astype(BF16)
    normed_prev = (standardize(xp_ref[...].astype(F32))[0] * gain).astype(BF16)
    np_ref[...] = normed_prev
    kp_ref[...] = dot_t(normed_prev, weight[width : 2 * width]).astype(BF16)
    vp_ref[...] = dot_t(normed_prev, weight[2 * width :]).astype(BF16)


def row_spec(rows, width):
    return pl.BlockSpec((rows, width), lambda i: (i, 0))


def whole_spec(shape):
    return pl.BlockSpec(shape, lambda i: (0,) * len(shape))


def params():
    return pltpu.CompilerParams(vmem_limit_bytes=VMEM_MOST)


def project(x, x_prev, w_qkv, gain, span):
    rows, width = x.shape
    tile = TILE_SEQS * span
    low = jax.ShapeDtypeStruct((rows, width), BF16)
    return pl.pallas_call(
        project_kernel,
        grid=(rows // tile,),
        in_specs=[row_spec(tile, width)] * 2 + [whole_spec(w_qkv.shape), whole_spec(gain.shape)],
        out_specs=[row_spec(tile, width)] * 7
        + [pl.BlockSpec((1, TILE_SEQS, 2 * width), lambda i: (i, 0, 0))],
        out_shape=[low] * 7 + [jax.ShapeDtypeStruct((rows // tile, TILE_SEQS, 2 * width), BF16)],
        compiler_params=params(),
        name="project",
    )(x, x_prev, w_qkv, gain)


def attend_one(span, block, prefix, queries, keys, values, sums, keep_prob):
    width = queries.shape[1]
    pair = 2 * width // HEADS
    half = pair // 2
    count = sums.shape[0]
    select = head_select(count, width)
    unit_pos = lax.broadcasted_iota(jnp.int32, (span, span), 0)
    query_pos = lax.broadcasted_iota(jnp.int32, (span, span), 1)
    sum_id = lax.broadcasted_iota(jnp.int32, (count, span), 0)
    sum_query = lax.broadcasted_iota(jnp.int32, (count, span), 1)
    bias_prev = jnp.where(block >= 1, 0.0, MASKED).astype(F32)
    start = block * span
    own_ok = (unit_pos <= query_pos) | (start + unit_pos < prefix)
    bias_own = jnp.where(own_ok, 0.0, MASKED)
    sum_ok = (sum_id <= block - 1) | (
        (start + sum_query < prefix) & (sum_id >= block + 1) & ((sum_id + 1) * span <= prefix)
    )
    bias_sum = jnp.where(sum_ok, math.log(span), MASKED)
    values_t = values.T
    sum_keys = per_head(sums[:, :width], select)
    sum_values_t = per_head(sums[:, width : 2 * width], select).T
    sum_scores = dot_t(sum_keys, queries)
    mixed_parts = []
    sum_probs = []
    for p in range(HEADS // 2):
        lanes = slice(p * pair, (p + 1) * pair)
        scores = dot_t(keys[:, lanes], pair_halves(queries[:, lanes]))
        probs = []
        for e in range(2):
            h = 2 * p + e
            cols = slice(e * span, (e + 1) * span)
            s_prev = scores[:span, cols]
            s_own = scores[span:, cols] + bias_own
            s_sum = sum_scores[h * count : (h + 1) * count] + bias_sum
            most = jnp.maximum(
                jnp.maximum(
                    jnp.max(s_prev, axis=0, keepdims=True) + bias_prev,
                    jnp.max(s_own, axis=0, keepdims=True),
                ),
                jnp.max(s_sum, axis=0, keepdims=True),
            )
            e_prev = jnp.exp(s_prev + (bias_prev - most))
            e_own = jnp.exp(s_own - most)
            e_sum = jnp.exp(s_sum - most)
            total = (
                jnp.sum(e_prev, axis=0, keepdims=True)
                + jnp.sum(e_own, axis=0, keepdims=True)
                + jnp.sum(e_sum, axis=0, keepdims=True)
            )
            inverse = 1.0 / total
            probs.append(jnp.concatenate([e_prev * inverse, e_own * inverse], axis=0).astype(BF16))
            sum_probs.append(e_sum * inverse)
        both = jnp.concatenate(probs, axis=1)
        keep_prob(p, both)
        crossed = dot(values_t[lanes, :], both)
        mixed_parts.append(crossed[:half, :span])
        mixed_parts.append(crossed[half:, span:])
    all_sums = jnp.concatenate(sum_probs, axis=0).astype(BF16)
    mixed_t = jnp.concatenate(mixed_parts, axis=0) + dot(sum_values_t, all_sums)
    return mixed_t.T.astype(BF16), all_sums


def attend_kernel(
    span, prefix_ref, block_ref, q_ref, k_ref, v_ref, kp_ref, vp_ref, sums_ref, mixed_ref, prob_ref, psum_ref
):
    for s in range(TILE_SEQS):
        rows = slice(s * span, (s + 1) * span)

        def keep_prob(p, both, s=s):
            prob_ref[s, p] = both

        mixed, all_sums = attend_one(
            span,
            block_ref[0],
            prefix_ref[pl.program_id(0) * TILE_SEQS + s],
            q_ref[rows, :],
            jnp.concatenate([kp_ref[rows, :], k_ref[rows, :]], axis=0),
            jnp.concatenate([vp_ref[rows, :], v_ref[rows, :]], axis=0),
            sums_ref[s],
            keep_prob,
        )
        mixed_ref[rows, :] = mixed
        psum_ref[s] = all_sums


def attend(prefix, block, q, k, v, kp, vp, sums, span):
    rows, width = q.shape
    tile = TILE_SEQS * span
    seqs, count = sums.shape[0], sums.shape[1]
    pairs = HEADS // 2
    return pl.pallas_call(
        functools.partial(attend_kernel, span),
        grid=(rows // tile,),
        in_specs=[pl.BlockSpec(memory_space=pltpu.SMEM)] * 2
        + [row_spec(tile, width)] * 5
        + [pl.BlockSpec((TILE_SEQS, count, 2 * width), lambda i: (i, 0, 0))],
        out_specs=[
            row_spec(tile, width),
            pl.BlockSpec((TILE_SEQS, pairs, 2 * span, 2 * span), lambda i: (i, 0, 0, 0)),
            pl.BlockSpec((TILE_SEQS, HEADS * count, span), lambda i: (i, 0, 0)),
        ],
        out_shape=[
            jax.ShapeDtypeStruct((rows, width), BF16),
            jax.ShapeDtypeStruct((seqs, pairs, 2 * span, 2 * span), BF16),
            jax.ShapeDtypeStruct((seqs, HEADS * count, span), BF16),
        ],
        compiler_params=params(),
        name="attend",
    )(prefix, block, q, k, v, kp, vp, sums)


def feed_kernel(
    x_ref, mixed_ref, g_ref, wo_ref, wu_ref, wd_ref, gain_ref,
    out_ref, gm_ref, gr_ref, gout_ref, gup_ref, gdown_ref, ggain_ref,
    acc_out, acc_up, acc_down, acc_gain,
):
    step = pl.program_id(0)

    @pl.when(step == 0)
    def _():
        acc_out[...] = jnp.zeros_like(acc_out)
        acc_up[...] = jnp.zeros_like(acc_up)
        acc_down[...] = jnp.zeros_like(acc_down)
        acc_gain[...] = jnp.zeros_like(acc_gain)

    gain = gain_ref[gain_ref.shape[0] - 1 :, :]
    mixed = mixed_ref[...]
    w_out = rows_of(wo_ref)
    resid = x_ref[...].astype(F32) + dot_t(mixed, w_out)
    unit, inv = standardize(resid)
    normed = (unit * gain).astype(BF16)
    normed_t = normed.T
    grad = g_ref[...]
    grad_t = grad.T
    hidden_width = acc_up.shape[1]
    result = resid
    grad_norm = None
    for c in range(hidden_width // FF_CHUNK):
        cols = slice(c * FF_CHUNK, (c + 1) * FF_CHUNK)
        w_up = lanes_of(wu_ref, c, 1)
        w_down = lanes_of(wd_ref, c, 0)
        upper = dot(normed, w_up)
        grad_hidden = dot(grad, w_down)
        activated, slope = gelu_parts(upper)
        hidden = activated.astype(BF16)
        grad_upper = (grad_hidden * slope).astype(BF16)
        result = result + dot_t(hidden, w_down)
        back = dot_t(grad_upper, w_up)
        grad_norm = back if grad_norm is None else grad_norm + back
        acc_down[:, cols] += dot(grad_t, hidden)
        acc_up[:, cols] += dot(normed_t, grad_upper)
    out_ref[...] = result.astype(BF16)
    acc_gain[...] += fold_rows(grad_norm * unit)
    grad_resid = grad.astype(F32) + norm_back(grad_norm, unit, inv, gain)
    gr_ref[...] = grad_resid
    grad_branch = grad_resid.astype(BF16)
    acc_out[...] += dot(grad_branch.T, mixed)
    gm_ref[...] = dot(grad_branch, w_out).astype(BF16)

    @pl.when(step == pl.num_programs(0) - 1)
    def _():
        put_blocks(gout_ref, acc_out, 1)
        put_blocks(gup_ref, acc_up, 0)
        put_blocks(gdown_ref, acc_down, 1)
        ggain_ref[...] = acc_gain[...]


def feed(x, mixed, grad, w_out, w_up, w_down, gain, tile):
    rows, width = x.shape
    hidden = w_up.shape[1] * w_up.shape[3]
    wide = (width, hidden)
    square = (width, width)
    return pl.pallas_call(
        feed_kernel,
        grid=(rows // tile,),
        in_specs=[row_spec(tile, width)] * 3
        + [whole_spec(w_out.shape), whole_spec(w_up.shape), whole_spec(w_down.shape), whole_spec(gain.shape)],
        out_specs=[row_spec(tile, width)] * 3
        + [whole_spec(w_out.shape), whole_spec(w_up.shape), whole_spec(w_down.shape), whole_spec((8, width))],
        out_shape=[
            jax.ShapeDtypeStruct((rows, width), BF16),
            jax.ShapeDtypeStruct((rows, width), BF16),
            jax.ShapeDtypeStruct((rows, width), F32),
            jax.ShapeDtypeStruct(w_out.shape, BF16),
            jax.ShapeDtypeStruct(w_up.shape, BF16),
            jax.ShapeDtypeStruct(w_down.shape, BF16),
            jax.ShapeDtypeStruct((8, width), F32),
        ],
        scratch_shapes=[
            pltpu.VMEM(square, F32),
            pltpu.VMEM(wide, F32),
            pltpu.VMEM(wide, F32),
            pltpu.VMEM((8, width), F32),
        ],
        compiler_params=params(),
        name="feed",
    )(x, mixed, grad, w_out, w_up, w_down, gain)


def return_one(span, queries, keys, values, sums, grad_mixed, prob_at, sum_low):
    width = queries.shape[1]
    pair = 2 * width // HEADS
    half = pair // 2
    count = sums.shape[0]
    scale = half ** -0.5
    select = head_select(count, width)
    keys_t = keys.T
    sum_keys_t = per_head(sums[:, :width], select).T
    sum_values = per_head(sums[:, width : 2 * width], select)
    sum_prob = sum_low.astype(F32)
    sum_moved = sum_prob * dot_t(sum_values, grad_mixed)
    grad_q_parts = []
    grad_k_parts = []
    grad_v_parts = []
    sum_grads = []
    for p in range(HEADS // 2):
        lanes = slice(p * pair, (p + 1) * pair)
        grads2 = pair_halves(grad_mixed[:, lanes])
        grad_prob = dot_t(values[:, lanes], grads2)
        low = prob_at(p)
        prob = low.astype(F32)
        moved = prob * grad_prob
        deltas = jnp.sum(moved, axis=0, keepdims=True)
        sums_of = []
        for e in range(2):
            h = 2 * p + e
            part = slice(h * count, (h + 1) * count)
            delta = deltas[:, e * span : (e + 1) * span] + jnp.sum(sum_moved[part], axis=0, keepdims=True)
            sums_of.append(delta)
            sum_grads.append(sum_moved[part] - sum_prob[part] * delta)
        grad_scores = (moved - prob * jnp.concatenate(sums_of, axis=1)).astype(BF16)
        grad_k_parts.append(dot(grad_scores, pair_halves(queries[:, lanes])))
        grad_v_parts.append(dot(low, grads2))
        crossed = dot(keys_t[lanes, :], grad_scores)
        grad_q_parts.append(crossed[:half, :span])
        grad_q_parts.append(crossed[half:, span:])
    sum_scores_grad = jnp.concatenate(sum_grads, axis=0).astype(BF16)
    grad_q = jnp.concatenate(grad_q_parts, axis=0) + dot(sum_keys_t, sum_scores_grad)
    grad_q = (grad_q.T * scale).astype(BF16)
    grad_k = jnp.concatenate(grad_k_parts, axis=1).astype(BF16)
    grad_v = jnp.concatenate(grad_v_parts, axis=1).astype(BF16)
    wide_k = jnp.where(select, dot(sum_scores_grad, queries), 0.0)
    wide_v = jnp.where(select, dot(sum_low, grad_mixed), 0.0)
    folded_k = jnp.sum(wide_k.reshape(HEADS, count, width), axis=0)
    folded_v = jnp.sum(wide_v.reshape(HEADS, count, width), axis=0)
    return (
        jnp.concatenate([grad_q, grad_k[span:], grad_v[span:]], axis=1),
        jnp.concatenate([grad_k[:span], grad_v[:span]], axis=1),
        jnp.concatenate([folded_k, folded_v], axis=1) * (1.0 / span),
    )


def return_tile(weight, own, before, shared, normed, normed_prev, normed_sum, acc):
    width = normed.shape[1]
    grad_own = jnp.concatenate(own, axis=0)
    grad_before = jnp.concatenate(before, axis=0)
    grad_shared = jnp.concatenate(shared, axis=0).astype(BF16)
    normed_t = normed.T
    acc[:, :width] += dot(normed_t, grad_own[:, :width])
    acc[:, width:] += (
        dot(normed_t, grad_own[:, width:]) + dot(normed_prev.T, grad_before) + dot(normed_sum.T, grad_shared)
    )
    return grad_own, dot(grad_before, weight[width:]), dot(grad_shared, weight[width:])


def return_kernel(
    span, q_ref, k_ref, v_ref, kp_ref, vp_ref, sums_ref, gm_ref, prob_ref, psum_ref, n_ref, np_ref, nsum_ref, w_ref,
    gn_ref, gp_ref, gs_ref, gqkv_ref, acc,
):
    step = pl.program_id(0)

    @pl.when(step == 0)
    def _():
        acc[...] = jnp.zeros_like(acc)

    parts = []
    for s in range(TILE_SEQS):
        rows = slice(s * span, (s + 1) * span)
        parts.append(
            return_one(
                span,
                q_ref[rows, :],
                jnp.concatenate([kp_ref[rows, :], k_ref[rows, :]], axis=0),
                jnp.concatenate([vp_ref[rows, :], v_ref[rows, :]], axis=0),
                sums_ref[s],
                gm_ref[rows, :],
                lambda p, s=s: prob_ref[s, p],
                psum_ref[s],
            )
        )
    normed_sum = nsum_ref[...].reshape(-1, nsum_ref.shape[2])
    weight = rows_of(w_ref)
    grad_own, gp, gs = return_tile(weight, *zip(*parts), n_ref[...], np_ref[...], normed_sum, acc)
    gn_ref[...] = dot(grad_own, weight)
    gp_ref[...] = gp.astype(BF16)
    gs_ref[...] = gs.reshape(gs_ref.shape).astype(BF16)

    @pl.when(step == pl.num_programs(0) - 1)
    def _():
        put_blocks(gqkv_ref, acc[...].astype(BF16).T, 1)


def give_back(q, k, v, kp, vp, sums, gm, prob, psum, n, n_prev, n_sum, w_qkv, span):
    rows, width = q.shape
    tile = TILE_SEQS * span
    seqs, count = sums.shape[0], sums.shape[1]
    pairs = HEADS // 2
    return pl.pallas_call(
        functools.partial(return_kernel, span),
        grid=(rows // tile,),
        in_specs=[row_spec(tile, width)] * 5
        + [
            pl.BlockSpec((TILE_SEQS, count, 2 * width), lambda i: (i, 0, 0)),
            row_spec(tile, width),
            pl.BlockSpec((TILE_SEQS, pairs, 2 * span, 2 * span), lambda i: (i, 0, 0, 0)),
            pl.BlockSpec((TILE_SEQS, HEADS * count, span), lambda i: (i, 0, 0)),
            row_spec(tile, width),
            row_spec(tile, width),
            pl.BlockSpec((TILE_SEQS, count, width), lambda i: (i, 0, 0)),
            whole_spec(w_qkv.shape),
        ],
        out_specs=[
            row_spec(tile, width),
            row_spec(tile, width),
            pl.BlockSpec((TILE_SEQS, count, width), lambda i: (i, 0, 0)),
            whole_spec(w_qkv.shape),
        ],
        out_shape=[
            jax.ShapeDtypeStruct((rows, width), F32),
            jax.ShapeDtypeStruct((rows, width), BF16),
            jax.ShapeDtypeStruct((seqs, count, width), BF16),
            jax.ShapeDtypeStruct(w_qkv.shape, BF16),
        ],
        scratch_shapes=[pltpu.VMEM((width, 3 * width), F32)],
        compiler_params=params(),
        name="give_back",
    )(q, k, v, kp, vp, sums, gm, prob, psum, n, n_prev, n_sum, w_qkv)


def close_kernel(span, x_ref, gn_ref, gb_ref, gs_ref, gr_ref, gain_ref, out_ref, ggain_ref, acc):
    step = pl.program_id(0)
    width = x_ref.shape[1]

    @pl.when(step == 0)
    def _():
        acc[...] = jnp.zeros_like(acc)

    unit, inv = standardize(x_ref[...].astype(F32))
    grad_norm = gn_ref[...] + gb_ref[...].astype(F32)
    lifted = [
        grad_norm[s * span : (s + 1) * span] + gs_ref[s].astype(F32) for s in range(TILE_SEQS)
    ]
    grad_norm = jnp.concatenate(lifted, axis=0)
    acc[...] += fold_rows(grad_norm * unit)
    part = norm_back(grad_norm, unit, inv, gain_ref[...])
    out_ref[...] = (gr_ref[...] + part).astype(BF16)

    @pl.when(step == pl.num_programs(0) - 1)
    def _():
        ggain_ref[...] = acc[...]


def close(x, gn, gb, gs, gr, gain, span):
    rows, width = x.shape
    tile = TILE_SEQS * span
    return pl.pallas_call(
        functools.partial(close_kernel, span),
        grid=(rows // tile,),
        in_specs=[row_spec(tile, width)] * 3
        + [pl.BlockSpec((TILE_SEQS, 1, width), lambda i: (i, 0, 0)), row_spec(tile, width), whole_spec(gain.shape)],
        out_specs=[row_spec(tile, width), whole_spec((8, width))],
        out_shape=[jax.ShapeDtypeStruct((rows, width), BF16), jax.ShapeDtypeStruct((8, width), F32)],
        scratch_shapes=[pltpu.VMEM((8, width), F32)],
        compiler_params=params(),
        name="close",
    )(x, gn, gb, gs, gr, gain)


def in_order(count, seqs):
    row = lax.broadcasted_iota(jnp.int32, (count * seqs, count * seqs), 0)
    col = lax.broadcasted_iota(jnp.int32, (count * seqs, count * seqs), 1)
    return ((col % seqs == row // count) & (col // seqs == row % count)).astype(BF16)


def neighbour(by):
    depth, spot = lax.axis_index("dp"), lax.axis_index("ctx")
    return depth, lax.rem(spot + by + FLIPS, FLIPS)


ENTER_RELAYS = {
    1: ((1, "spread"), (2, "spread"), (3, "spread")),
    4: ((1, "cross"), (2, "cross")),
    5: ((3, "cross"),),
    7: ((1, "hand_over"), (2, "hand_over"), (3, "hand_over")),
}


def enter_kernel(
    depths, span,
    x_in, prefix_ref, bq_ref, bo_ref, bu_ref, bd_ref, one_ref, two_ref,
    wq_out, wo_out, wu_out, wd_out, gain_out, q_out, k_out, v_out, kp_out, vp_out, n_out, np_out, mixed_out, prob_out,
    sums_out, psum_out,
    x_ref, xp, wq, gains, q, k, v, kp, vp, n, n_prev, mixed, prob, slots,
    send, recv, keep, gain_send, gain_recv, sum_send, sum_recv, tok_send, tok_recv, out_sem, prob_sem, wq_sem, x_sem,
):
    x_copy = pltpu.make_async_copy(x_in, x_ref, x_sem.at[0])
    x_copy.start()
    rows, width = x_ref.shape
    tile = TILE_SEQS * span
    tiles = rows // tile
    chunks = tiles // CHUNK_TILES
    seqs = rows // span
    spot = lax.axis_index("ctx")
    scale = (width // HEADS) ** -0.5
    gathers = [
        Gather(depths, own, full, send.at[a], recv.at[a], keep.at[a])
        for a, (own, full) in enumerate(((bq_ref, wq), (bo_ref, wo_out), (bu_ref, wu_out), (bd_ref, wd_out)))
    ]
    gain_share = Share(depths, gains, gain_send, gain_recv)
    sum_share = Share(depths, slots, sum_send, sum_recv)
    shard = jnp.concatenate([one_ref[...].reshape(1, -1), two_ref[...].reshape(1, -1)], axis=0).astype(F32)
    owner = lax.broadcasted_iota(jnp.int32, (2, width), 1) // shard.shape[1]
    gains[spot] = jnp.where(owner == spot, jnp.concatenate([shard] * FLIPS, axis=1), 0.0)

    @pl.when(spot == 0)
    def _():
        xp[...] = jnp.zeros_like(xp)

    def at(i):
        return pl.ds(pl.multiple_of(i * tile, tile), tile)

    def chunk_at(c):
        return pl.ds(pl.multiple_of(c * CHUNK_TILES * tile, CHUNK_TILES * tile), CHUNK_TILES * tile)

    def token_copy(i):
        return pltpu.make_async_remote_copy(
            src_ref=x_ref.at[at(i)],
            dst_ref=xp.at[at(i)],
            send_sem=tok_send.at[i],
            recv_sem=tok_recv.at[i],
            device_id=neighbour(1),
            device_id_type=MESH,
        )

    def out_copy(a, i):
        pairs = ((q, q_out), (k, k_out), (v, v_out), (n, n_out), (kp, kp_out), (vp, vp_out), (n_prev, np_out), (mixed, mixed_out))
        return pltpu.make_async_copy(pairs[a][0].at[at(i)], pairs[a][1].at[at(i)], out_sem.at[a, i])

    def prob_copy(i):
        part = pl.ds(i * TILE_SEQS, TILE_SEQS)
        return pltpu.make_async_copy(prob.at[part], prob_out.at[part], prob_sem.at[i])

    def send_tokens(first, last):
        @pl.when(spot < FLIPS - 1)
        def _():
            for i in range(first, last):
                token_copy(i).start()

    greet(depths)
    gathers[0].begin()
    gain_share.begin()
    x_copy.wait()
    send_tokens(0, 2)
    gain_share.forward()
    gain_share.complete()
    gain = gains[0]
    for c in range(1, FLIPS):
        gain = gain + gains[c]
    gain_out[...] = gain

    def normalize(c):
        n[chunk_at(c), :] = (standardize(x_ref[chunk_at(c), :].astype(F32))[0] * gain[0:1]).astype(BF16)

    def keep_mean(part, ref, weigh):
        means = [
            jnp.sum(ref[s * span : (s + 1) * span, :].astype(F32), axis=0, keepdims=True) * weigh for s in range(seqs)
        ]
        slots[spot, :, part * width : (part + 1) * width] = jnp.concatenate(means, axis=0).astype(BF16)

    pl.loop(0, chunks // 2)(normalize)
    gathers[0].cross(0, 1)
    gathers[0].spread()
    pl.loop(chunks // 2, chunks)(normalize)
    gathers[0].cross(1)
    keep_mean(2, n, 1.0)
    gathers[0].hand_over()
    send_tokens(2, 5)
    gathers[0].complete()
    wq_copy = pltpu.make_async_copy(wq, wq_out, wq_sem.at[0])
    wq_copy.start()

    def send_out(a, c):
        for t in range(CHUNK_TILES):
            out_copy(a, c * CHUNK_TILES + t).start()

    @pl.loop(0, chunks)
    def _(c):
        weight = rows_of(wq)
        normed = n[chunk_at(c), :]
        k[chunk_at(c), :] = dot_t(normed, weight[width : 2 * width]).astype(BF16)
        v[chunk_at(c), :] = dot_t(normed, weight[2 * width :]).astype(BF16)
        for a in (1, 2, 3):
            send_out(a, c)

    keep_mean(0, k, 1.0 / span)
    keep_mean(1, v, 1.0 / span)
    sum_share.begin()
    send_tokens(5, tiles)
    for gather in gathers[1:]:
        gather.begin()

    @pl.loop(0, chunks)
    def _(c):
        weight = rows_of(wq)
        rows_q = dot_t(n[chunk_at(c), :], weight[:width]).astype(BF16)
        q[chunk_at(c), :] = (rows_q.astype(F32) * scale).astype(BF16)
        send_out(0, c)

    def project_prev(c):
        @pl.when(spot > 0)
        def _():
            for t in range(CHUNK_TILES):
                token_copy(c * CHUNK_TILES + t).wait_recv()

        weight = rows_of(wq)
        normed = (standardize(xp[chunk_at(c), :].astype(F32))[0] * gain[0:1]).astype(BF16)
        n_prev[chunk_at(c), :] = normed
        kp[chunk_at(c), :] = dot_t(normed, weight[width : 2 * width]).astype(BF16)
        vp[chunk_at(c), :] = dot_t(normed, weight[2 * width :]).astype(BF16)
        for a in (4, 5, 6):
            send_out(a, c)

    project_prev(0)
    sum_share.forward()
    project_prev(1)
    sum_share.complete()
    ordered = dot(in_order(FLIPS, seqs), slots[...].reshape(FLIPS * seqs, 3 * width)).astype(BF16)
    sums_out[...] = ordered.reshape(sums_out.shape)
    @pl.loop(0, tiles)
    def _(i):
        @pl.when((lax.rem(i, CHUNK_TILES) == 0) & (i >= 2 * CHUNK_TILES))
        def _():
            project_prev(i // CHUNK_TILES)

        for s in range(TILE_SEQS):
            here = pl.ds(pl.multiple_of(i * tile + s * span, span), span)
            seq = i * TILE_SEQS + s

            def keep_prob(p, both, seq=seq):
                prob[seq, p] = both

            rows_mixed, all_sums = attend_one(
                span,
                spot,
                prefix_ref[seq // prefix_ref.shape[1], lax.rem(seq, prefix_ref.shape[1])],
                q[here, :],
                jnp.concatenate([kp[here, :], k[here, :]], axis=0),
                jnp.concatenate([vp[here, :], v[here, :]], axis=0),
                sums_out[seq],
                keep_prob,
            )
            mixed[here, :] = rows_mixed
            psum_out[seq] = all_sums
        out_copy(7, i).start()
        prob_copy(i).start()
        for when, relays in ENTER_RELAYS.items():

            @pl.when(i == when)
            def _(relays=relays):
                for a, name in relays:
                    getattr(gathers[a], name)()

    for gather in gathers[1:]:
        gather.complete()
    for move in (*gathers, gain_share, sum_share):
        move.close()

    @pl.when(spot < FLIPS - 1)
    def _():
        for i in range(tiles):
            token_copy(i).wait_send()

    wq_copy.wait()

    @pl.loop(0, tiles)
    def _(i):
        for a in range(8):
            out_copy(a, i).wait()
        prob_copy(i).wait()


def enter(x, prefix, blocks, gain_one, gain_two, span, depths):
    rows, width = x.shape
    tile = TILE_SEQS * span
    tiles, seqs = rows // tile, rows // span
    low = jax.ShapeDtypeStruct((rows, width), BF16)
    fulls = [jax.ShapeDtypeStruct((depths, FLIPS) + b.shape, BF16) for b in blocks]
    prob_shape = (seqs, HEADS // 2, 2 * span, 2 * span)
    vmem = pl.BlockSpec(memory_space=pltpu.VMEM)
    far = pl.BlockSpec(memory_space=pl.ANY)
    sems = pltpu.SemaphoreType.DMA
    held = pltpu.VMEM((rows, width), BF16)
    return pl.pallas_call(
        functools.partial(enter_kernel, depths, span),
        in_specs=[far, pl.BlockSpec(memory_space=pltpu.SMEM)] + [vmem] * 6,
        out_specs=[far] * 4 + [vmem] + [far] * 9 + [vmem] * 2,
        out_shape=fulls
        + [jax.ShapeDtypeStruct((2, width), F32)]
        + [low] * 8
        + [
            jax.ShapeDtypeStruct(prob_shape, BF16),
            jax.ShapeDtypeStruct((seqs, FLIPS, 3 * width), BF16),
            jax.ShapeDtypeStruct((seqs, HEADS * FLIPS, span), BF16),
        ],
        scratch_shapes=[
            held,
            held,
            pltpu.VMEM(fulls[0].shape, BF16),
            pltpu.VMEM((FLIPS, 2, width), F32),
        ]
        + [held] * 8
        + [pltpu.VMEM(prob_shape, BF16), pltpu.VMEM((FLIPS, seqs, 3 * width), BF16)]
        + [
            sems((4, depths * FLIPS)), sems((4, depths * FLIPS)), sems((4,)),
            sems((FLIPS,)), sems((FLIPS,)), sems((FLIPS,)), sems((FLIPS,)),
            sems((tiles,)), sems((tiles,)), sems((8, tiles)), sems((tiles,)), sems((1,)), sems((1,)),
        ],
        compiler_params=pltpu.CompilerParams(collective_id=0, has_side_effects=True, vmem_limit_bytes=VMEM_MOST),
        name="enter",
    )(x, prefix, *blocks, gain_one, gain_two)


LEAVE_RELAYS = {
    0: ((0, "cross"),),
    1: ((1, "cross"), (2, "cross")),
    3: ((0, "spread"), (1, "spread")),
    5: ((2, "spread"),),
    6: ((0, "climb"), (1, "climb")),
}


def leave_kernel(
    depths, span,
    q_in, k_in, v_in, kp_in, vp_in, gm_in, n_in, np_in, prob_in, gr_in, x_in,
    psum_in, sums_in, wq_in, gout_in, gup_in, gdown_in, gain_ref, ggain_ref,
    ig_out, dqkv_out, dout_out, dup_out, ddown_out, dgain_out,
    psum_ref, sums_ref, wq_ref, gout_ref, gup_ref, gdown_ref, held, prob, kept, before, shared_rows, turned, turned_prev, turned_sum, one_sum, gp, gb, gr, x, ig, part, gs_send_buf, gs_slots, gain_slots, gain_deep,
    *rest,
):
    moves_refs, sems = rest[:16], rest[16:]
    send, recv, gs_send, gs_recv, gain_send, gain_recv, deep_send, deep_recv, gb_send, gb_recv, in_sem, late_sem, ig_sem, whole_sem = sems
    inputs = (gout_in, gup_in, gdown_in, psum_in, sums_in, wq_in)
    landing = (gout_ref, gup_ref, gdown_ref, psum_ref, sums_ref, wq_ref)
    wholes = [pltpu.make_async_copy(a, b, whole_sem.at[n]) for n, (a, b) in enumerate(zip(inputs, landing))]
    for copy in wholes:
        copy.start()
    rows, width = gp.shape
    tile = TILE_SEQS * span
    tiles = rows // tile
    seqs = rows // span
    spot = lax.axis_index("ctx")
    parts = (gout_ref, gup_ref, gdown_ref, part)
    scatters = [
        Scatter(depths, parts[a], *moves_refs[4 * a : 4 * a + 4], send.at[a], recv.at[a]) for a in range(4)
    ]
    gain_share = Share(depths, gain_slots, gain_send, gain_recv)
    gs_moves = Moves(depths, gs_send, gs_recv)
    deep_moves = Moves(depths, deep_send, deep_recv)

    def at(i):
        return pl.ds(pl.multiple_of(i * tile, tile), tile)

    def at_sums(i):
        return pl.ds(pl.multiple_of(i * TILE_SEQS * FLIPS, TILE_SEQS * FLIPS), TILE_SEQS * FLIPS)

    def loads(i, slot):
        arrays = (q_in, k_in, v_in, kp_in, vp_in, gm_in, n_in, np_in)
        copies = [pltpu.make_async_copy(ref.at[at(i)], held.at[slot, a], in_sem.at[slot, a]) for a, ref in enumerate(arrays)]
        of_tile = pl.ds(i * TILE_SEQS, TILE_SEQS)
        return copies + [pltpu.make_async_copy(prob_in.at[of_tile], prob.at[slot], in_sem.at[slot, len(arrays)])]

    def gb_copy(i):
        return pltpu.make_async_remote_copy(
            src_ref=gp.at[at(i)],
            dst_ref=gb.at[at(i)],
            send_sem=gb_send.at[i],
            recv_sem=gb_recv.at[i],
            device_id=neighbour(-1),
            device_id_type=MESH,
        )

    for copy in loads(0, 0):
        copy.start()
    late = [pltpu.make_async_copy(gr_in, gr, late_sem.at[0]), pltpu.make_async_copy(x_in, x, late_sem.at[1])]

    @pl.when(spot == FLIPS - 1)
    def _():
        gb[...] = jnp.zeros_like(gb)

    greet(depths)
    turns = (*range(1, depths), 0)
    for copy, scatter in zip(wholes, scatters[:3]):
        copy.wait()
        scatter.begin(turns)
    for copy in wholes[3:]:
        copy.wait()

    @pl.loop(0, tiles)
    def _(i):
        slot = lax.rem(i, 2)
        for copy in loads(i, slot):
            copy.wait()

        @pl.when(i + 1 < tiles)
        def _():
            for copy in loads(i + 1, 1 - slot):
                copy.start()

        pieces = []
        for s in range(TILE_SEQS):
            here = slice(s * span, (s + 1) * span)
            seq = i * TILE_SEQS + s
            pieces.append(
                return_one(
                    span,
                    held[slot, 0, here],
                    jnp.concatenate([held[slot, 3, here], held[slot, 1, here]], axis=0),
                    jnp.concatenate([held[slot, 4, here], held[slot, 2, here]], axis=0),
                    sums_ref[seq],
                    held[slot, 5, here],
                    lambda p, s=s: prob[slot, s, p],
                    psum_ref[seq],
                )
            )
        own, back, shared = (jnp.concatenate(rows, axis=0) for rows in zip(*pieces))
        weight_kv = rows_of(wq_ref)[width:]
        kept[at(i), :] = own
        before[at(i), :] = back
        gp[at(i), :] = dot(back, weight_kv).astype(BF16)
        shared_rows[at_sums(i), :] = shared.astype(BF16)
        turned[:, at(i)] = held[slot, 6].T
        turned_prev[:, at(i)] = held[slot, 7].T

        @pl.when(spot > 0)
        def _():
            gb_copy(i).start()

        for when, relays in LEAVE_RELAYS.items():

            @pl.when(i == when)
            def _(relays=relays):
                for a, name in relays:
                    getattr(scatters[a], name)(turns)

        @pl.when(i == tiles - 3)
        def _():
            for copy in late:
                copy.start()

    to_sums = dot(shared_rows[...], rows_of(wq_ref)[width:]).astype(BF16)
    by_spot = lax.dot_general(
        in_order(FLIPS, seqs), to_sums, (((0,), (0,)), ((), ())), preferred_element_type=F32
    )
    gs_send_buf[...] = by_spot.astype(BF16).reshape(gs_send_buf.shape)
    for flip in (6, 7, 2, 4, 3, 5, 1):
        gs_moves.start(gs_send_buf.at[spot_of(depths, 0, flip)[1]], gs_slots.at[flip], flip, 0, flip)
    turned_sum[...] = sums_ref[:, :, 2 * width :].reshape(seqs * FLIPS, width).T
    lanes_in = width // depths

    def weigh(turns):
        owners = [spot_of(depths, turn, 0)[0] for turn in turns]
        tops = [pl.ds(pl.multiple_of(owner * lanes_in, lanes_in), lanes_in) for owner in owners]
        rows_own, rows_prev, rows_sum = (
            jnp.concatenate([ref[top, :] for top in tops], axis=0) for ref in (turned, turned_prev, turned_sum)
        )
        grad_q = dot(rows_own, kept[:, :width])
        grad_kv = dot(rows_own, kept[:, width:]) + dot(rows_prev, before[...]) + dot(rows_sum, shared_rows[...])
        low = jnp.concatenate([grad_q.astype(BF16), grad_kv.astype(BF16)], axis=1)
        for t, (owner, top) in enumerate(zip(owners, tops)):
            flat = low[t * lanes_in : (t + 1) * lanes_in].T
            part[owner] = flat.reshape(part.shape[1:])
            weighed = flat.astype(F32) * wq_ref[owner].reshape(flat.shape).astype(F32)
            one_sum[:, top] = jnp.sum(weighed, axis=0, keepdims=True)
        scatters[3].begin(turns)

    first, second = turns[: depths // 2], turns[depths // 2 :]
    weigh(first)
    weigh(second)
    scatters[3].cross(first)
    total_one = one_sum[...] / gain_ref[0:1]
    total_two = jnp.sum(ggain_ref[...], axis=0, keepdims=True)
    gain_slots[spot] = jnp.concatenate([total_one, total_two], axis=0)
    gain_share.begin()
    gain_share.forward()
    for copy in late:
        copy.wait()
    for flip in range(1, FLIPS):
        gs_moves.landed(gs_slots.at[flip], flip)
    shared = gs_send_buf[spot].astype(F32)
    for flip in range(1, FLIPS):
        shared = shared + gs_slots[flip].astype(F32)
    gain = gain_ref[0:1]

    def close_tile(i):
        @pl.when(spot < FLIPS - 1)
        def _():
            gb_copy(i).wait_recv()

        unit, inv = standardize(x[at(i), :].astype(F32))
        grad_norm = dot(kept[at(i), :], rows_of(wq_ref)) + gb[at(i), :].astype(F32)
        lifted = [
            grad_norm[s * span : (s + 1) * span] + shared[i * TILE_SEQS + s : i * TILE_SEQS + s + 1]
            for s in range(TILE_SEQS)
        ]
        grad_norm = jnp.concatenate(lifted, axis=0)
        ig[at(i), :] = (gr[at(i), :] + norm_back(grad_norm, unit, inv, gain)).astype(BF16)
        pltpu.make_async_copy(ig.at[at(i)], ig_out.at[at(i)], ig_sem.at[i]).start()

    def share_deep():
        gain_share.complete()
        over_ctx = gain_slots[0]
        for c in range(1, FLIPS):
            over_ctx = over_ctx + gain_slots[c]
        gain_deep[0] = over_ctx
        for turn in range(1, depths):
            deep_moves.start(gain_deep.at[0], gain_deep.at[depths - turn], depths - turn, turn, 0)

    after = {
        1: (functools.partial(scatters[3].cross, second), functools.partial(scatters[3].spread, first)),
        2: (share_deep, functools.partial(scatters[3].spread, second)),
        0: (functools.partial(scatters[2].climb, turns),),
        4: (functools.partial(scatters[3].climb, first),),
        6: (functools.partial(scatters[3].climb, second),),
    }
    for i in range(tiles):
        for relay in after.get(i, ()):
            relay()
        close_tile(i)
    for turn in range(1, depths):
        deep_moves.landed(gain_deep.at[turn], turn)
    over_all = gain_deep[0]
    for turn in range(1, depths):
        over_all = over_all + gain_deep[turn]
    lanes = width // FLIPS
    mine = jnp.zeros((2, lanes), F32)
    for c in range(FLIPS):
        mine = jnp.where(spot == c, over_all[:, c * lanes : (c + 1) * lanes], mine)
    dgain_out[...] = mine
    for out, scatter in zip((dout_out, dup_out, ddown_out, dqkv_out), scatters):
        out[...] = scatter.finish()
    for scatter in scatters:
        scatter.close()
    gain_share.close()
    gs_moves.drain(gs_slots.at[0])
    deep_moves.drain(gain_deep.at[0])

    @pl.when(spot > 0)
    def _():
        for i in range(tiles):
            gb_copy(i).wait_send()

    for i in range(tiles):
        pltpu.make_async_copy(ig.at[at(i)], ig_out.at[at(i)], ig_sem.at[i]).wait()


def leave(arrays, psum, sums, wq, partials, gains, ggain, span, depths):
    rows, width = arrays[0].shape
    tile = TILE_SEQS * span
    tiles, seqs = rows // tile, rows // span
    vmem = pl.BlockSpec(memory_space=pltpu.VMEM)
    far = pl.BlockSpec(memory_space=pl.ANY)
    sems = pltpu.SemaphoreType.DMA
    low = pltpu.VMEM((rows, width), BF16)
    high = pltpu.VMEM((rows, width), F32)
    shapes = [p.shape[2:] for p in (*partials, wq)]
    scratch = [pltpu.VMEM(a.shape, BF16) for a in (psum, sums, wq, *partials)]
    scratch += [
        pltpu.VMEM((2, 8, tile, width), BF16),
        pltpu.VMEM((2, TILE_SEQS, HEADS // 2, 2 * span, 2 * span), BF16),
        pltpu.VMEM((rows, 3 * width), BF16),
        pltpu.VMEM((rows, 2 * width), BF16),
        pltpu.VMEM((seqs * FLIPS, 2 * width), BF16),
        pltpu.VMEM((width, rows), BF16),
        pltpu.VMEM((width, rows), BF16),
        pltpu.VMEM((width, seqs * FLIPS), BF16),
        pltpu.VMEM((1, width), F32),
        low, low, high, low, low,
        pltpu.VMEM(wq.shape, BF16),
        pltpu.VMEM((FLIPS, seqs, width), BF16),
        pltpu.VMEM((FLIPS, seqs, width), BF16),
        pltpu.VMEM((FLIPS, 2, width), F32),
        pltpu.VMEM((depths, 2, width), F32),
    ]
    for shape in shapes:
        scratch += scatter_scratch(shape, depths)
    scratch += [
        sems((4, 8 * depths)), sems((4, 8 * depths)), sems((FLIPS,)), sems((FLIPS,)), sems((FLIPS,)), sems((FLIPS,)),
        sems((depths,)), sems((depths,)), sems((tiles,)), sems((tiles,)), sems((2, 9)), sems((2,)), sems((tiles,)), sems((6,)),
    ]
    outs = [jax.ShapeDtypeStruct(shape, F32) for shape in (shapes[3], *shapes[:3])]
    return pl.pallas_call(
        functools.partial(leave_kernel, depths, span),
        in_specs=[far] * 17 + [vmem] * 2,
        out_specs=[far] + [vmem] * 5,
        out_shape=[jax.ShapeDtypeStruct((rows, width), BF16), *outs, jax.ShapeDtypeStruct((2, width // FLIPS), F32)],
        scratch_shapes=scratch,
        compiler_params=pltpu.CompilerParams(collective_id=1, has_side_effects=True, vmem_limit_bytes=VMEM_MOST),
        name="leave",
    )(*arrays, psum, sums, wq, *partials, gains, ggain)


def direct_shards(tokens, prefix, blocks, gain_one, gain_two, cotangent):
    span, width = tokens.shape[2], tokens.shape[3]
    depths = lax.axis_size("dp")
    x = tokens.reshape(-1, width)
    grad = cotangent.reshape(-1, width)
    (wq, wo, wu, wd, gains, q, k, v, kp, vp, n, n_prev, mixed, prob, sums, psum) = enter(
        x, prefix, blocks, gain_one, gain_two, span, depths
    )
    out, gm, gr, gout, gup, gdown, ggain = feed(x, mixed, grad, wo, wu, wd, gains, 2 * TILE_SEQS * span)
    arrays = (q, k, v, kp, vp, gm, n, n_prev, prob, gr, x)
    ig, dqkv, dout, dup, ddown, dgain = leave(arrays, psum, sums, wq, (gout, gup, gdown), gains, ggain, span, depths)
    return (
        out.reshape(tokens.shape),
        ig.reshape(tokens.shape),
        dqkv.T,
        dout.T,
        dup,
        ddown.T,
        dgain[0],
        dgain[1],
    )


def fetch(block, rows_along):
    spot, depth = (0, 1) if rows_along == 1 else (1, 0)
    whole = lax.all_gather(lax.all_gather(block, "ctx", axis=spot, tiled=True), "dp", axis=depth, tiled=True)
    return whole[None, None]


def reduce_weight(partial, rows_along):
    spot, depth = (0, 1) if rows_along == 1 else (1, 0)
    columns = lax.psum_scatter(partial[0, 0], "ctx", scatter_dimension=spot, tiled=True)
    return lax.psum_scatter(columns, "dp", scatter_dimension=depth, tiled=True).astype(F32)


def shards(tokens, prefix, w_qkv, w_out, w_up, w_down, gain_one, gain_two, cotangent):
    span, width = tokens.shape[2], tokens.shape[3]
    count = lax.axis_size("ctx")
    blocks = (w_qkv.T, w_out.T, w_up, w_down.T)
    if count == FLIPS and all(b.shape[0] % 16 == 0 and b.shape[1] % 128 == 0 for b in blocks):
        return direct_shards(tokens, prefix, blocks, gain_one, gain_two, cotangent)
    along = (1, 1, 0, 1)
    x = tokens.reshape(-1, width)
    grad = cotangent.reshape(-1, width)
    tile = TILE_SEQS * span
    block = lax.axis_index("ctx").reshape(1).astype(jnp.int32)
    x_prev = lax.ppermute(x, "ctx", [(i, i + 1) for i in range(count - 1)])
    gain1 = lax.all_gather(gain_one, "ctx", axis=0, tiled=True).astype(F32).reshape(1, width)
    gain2 = lax.all_gather(gain_two, "ctx", axis=0, tiled=True).astype(F32).reshape(1, width)
    wq, wo, wu, wd = (fetch(b, r) for b, r in zip(blocks, along))
    q, k, v, kp, vp, n, n_prev, own_sums = project(x, x_prev, wq, gain1, span)
    own_sums = own_sums.reshape(-1, 2 * width)
    n_sum = jnp.sum(n.reshape(-1, span, width).astype(F32), axis=1).astype(BF16)
    everything = lax.all_gather(jnp.concatenate([own_sums, n_sum], axis=1), "ctx", axis=0, tiled=False)
    everything = jnp.transpose(everything, (1, 0, 2))
    sums, n_sums = everything[:, :, : 2 * width], everything[:, :, 2 * width :]
    mixed, prob, psum = attend(prefix.reshape(-1), block, q, k, v, kp, vp, sums, span)
    out, gm, gr, gout, gup, gdown, ggain2 = feed(x, mixed, grad, wo, wu, wd, gain2, tile)
    gn, gp, gs, gqkv = give_back(q, k, v, kp, vp, sums, gm, prob, psum, n, n_prev, n_sums, wq, span)
    gb = lax.ppermute(gp, "ctx", [(i, i - 1) for i in range(1, count)])
    gs_own = lax.psum_scatter(gs, "ctx", scatter_dimension=1, tiled=True)
    input_grad, ggain1 = close(x, gn, gb, gs_own, gr, gain1, span)
    gains = jnp.concatenate([jnp.sum(ggain1, axis=0), jnp.sum(ggain2, axis=0)]).reshape(2, width)
    gains = lax.psum(gains, "dp")
    gains = lax.psum_scatter(gains, "ctx", scatter_dimension=1, tiled=True)
    sums_w = [reduce_weight(p, r) for p, r in zip((gqkv, gout, gup, gdown), along)]
    return (
        out.reshape(tokens.shape),
        input_grad.reshape(tokens.shape),
        sums_w[0].T,
        sums_w[1].T,
        sums_w[2],
        sums_w[3].T,
        gains[0],
        gains[1],
    )


def solution(mesh):
    rows = P(None, "dp", "ctx", None)
    both = P("dp", "ctx")
    return jax.shard_map(
        shards,
        mesh=mesh,
        in_specs=(rows, P(None, "dp"), both, both, both, both, P("ctx"), P("ctx"), rows),
        out_specs=(rows, rows, both, both, both, both, P("ctx"), P("ctx")),
        check_vma=False,
    )
```

```python
import functools
import math

import jax
import jax.numpy as jnp
from jax import lax
from jax.experimental import pallas as pl
from jax.experimental.pallas import tpu as pltpu
from jax.sharding import PartitionSpec as P

HEADS = 8
EPSILON = 1e-05
MASKED = -1e30
F32 = jnp.float32
BF16 = jnp.bfloat16
TILE_SEQS = 2
CHUNK_TILES = 2
FF_CHUNK = 1024
VMEM_MOST = 60 * 1024 * 1024

MESH = pl.DeviceIdType.MESH
FLIPS = 8


def place():
    depth, spot = lax.axis_index("dp"), lax.axis_index("ctx")
    return depth, spot, (spot % 2, (spot // 2) % 2, spot // 4)


def flipped(bits, flip):
    out = 0
    for i, bit in enumerate(bits):
        out = out + ((1 - bit) if (flip >> i) & 1 else bit) * (1 << i)
    return out


def spot_of(depths, turn, flip):
    depth, _, bits = place()
    return lax.rem(depth + turn, depths), flipped(bits, flip)


def greet(depths):
    barrier = pltpu.get_barrier_semaphore()
    peers = [(turn, 0) for turn in range(1, depths)] + [(0, flip) for flip in range(1, FLIPS)]
    for turn, flip in peers:
        pl.semaphore_signal(barrier, inc=1, device_id=spot_of(depths, turn, flip), device_id_type=MESH)
    pl.semaphore_wait(barrier, len(peers))


class Moves:
    def __init__(self, depths, send, recv):
        self.depths, self.send, self.recv, self.sent = depths, send, recv, 0

    def copy(self, source, target, number, slot, to_turn, to_flip):
        return pltpu.make_async_remote_copy(
            src_ref=source,
            dst_ref=target,
            send_sem=self.send.at[number],
            recv_sem=self.recv.at[slot],
            device_id=spot_of(self.depths, to_turn, to_flip),
            device_id_type=MESH,
        )

    def start(self, source, target, slot, to_turn, to_flip):
        self.copy(source, target, self.sent, slot, to_turn, to_flip).start()
        self.sent += 1

    def landed(self, target, slot):
        self.copy(target, target, 0, slot, 0, 1).wait_recv()

    def drain(self, like):
        for number in range(self.sent):
            self.copy(like, like, number, 0, 0, 1).wait_send()


class Gather(Moves):
    def __init__(self, depths, own, full, send, recv, keep):
        super().__init__(depths, send, recv)
        self.own, self.full, self.keep = own, full, keep

    def block(self, turn, flip):
        return self.full.at[spot_of(self.depths, turn, flip)]

    def push(self, turn, flip, to_turn, to_flip):
        there = ((turn - to_turn) % self.depths) * FLIPS + (flip ^ to_flip)
        source = self.own if (turn, flip) == (0, 0) else self.block(turn, flip)
        self.start(source, self.block(turn, flip), there, to_turn, to_flip)

    def arrive(self, turn, flip):
        self.landed(self.block(turn, flip), turn * FLIPS + flip)

    def begin(self):
        for turn in range(1, self.depths):
            self.push(0, 0, turn, 0)
        for flip in (2, 4, 1):
            self.push(0, 0, 0, flip)
        pltpu.make_async_copy(self.own, self.block(0, 0), self.keep).start()

    def spread(self):
        for turn in range(1, self.depths):
            self.arrive(turn, 0)
            for flip in (2, 4, 1):
                self.push(turn, 0, 0, flip)

    def cross(self, first_turn=0, last_turn=None):
        for turn in range(first_turn, self.depths if last_turn is None else last_turn):
            self.arrive(turn, 2)
            if turn < self.depths // 2:
                self.push(turn, 2, 0, 4)
            self.push(turn, 2, 0, 1)
            self.arrive(turn, 4)
            if turn >= self.depths // 2:
                self.push(turn, 4, 0, 2)
            self.push(turn, 4, 0, 1)

    def hand_over(self):
        for turn in range(self.depths):
            self.arrive(turn, 6)
            self.push(turn, 6, 0, 1)

    def complete(self):
        for turn in range(self.depths):
            for flip in (1, 3, 5, 7):
                self.arrive(turn, flip)
        pltpu.make_async_copy(self.own, self.block(0, 0), self.keep).wait()

    def close(self):
        self.drain(self.own)


class Share(Moves):
    def __init__(self, depths, slots, send, recv):
        super().__init__(depths, send, recv)
        self.slots = slots

    def block(self, flip):
        return self.slots.at[spot_of(self.depths, 0, flip)[1]]

    def begin(self):
        for flip in (2, 4, 6, 1):
            self.start(self.block(0), self.block(0), flip, 0, flip)

    def forward(self):
        for flip in (2, 4, 6):
            self.landed(self.block(flip), flip)
            self.start(self.block(flip), self.block(flip), flip ^ 1, 0, 1)

    def complete(self):
        for flip in (1, 3, 5, 7):
            self.landed(self.block(flip), flip)

    def close(self):
        self.drain(self.block(0))


class Scatter(Moves):
    def __init__(self, depths, part, mate, total, near, far, send, recv):
        super().__init__(depths, send, recv)
        self.part, self.mate, self.total, self.near, self.far = part, mate, total, near, far

    def block(self, turn, flip):
        return self.part.at[spot_of(self.depths, turn, flip)]

    push = Moves.start
    arrive = Moves.landed

    def begin(self, turns):
        for flip in (6, 2, 4, 0):
            for turn in turns:
                at = (flip // 2, turn)
                self.push(self.block(turn, flip ^ 1), self.mate.at[at], flip // 2 * self.depths + turn, 0, 1)

    def fold(self, turn, flip):
        self.arrive(self.mate.at[flip // 2, turn], flip // 2 * self.depths + turn)
        mine = self.block(turn, flip)[...].astype(F32)
        self.total[flip // 2, turn] = (mine + self.mate[flip // 2, turn].astype(F32)).astype(BF16)

    def cross(self, turns):
        base = 4 * self.depths
        for turn in turns:
            self.fold(turn, 6)
            by = 2 if turn < self.depths // 2 else 4
            self.push(self.total.at[3, turn], self.near.at[turn], base + turn, 0, by)

    def spread(self, turns):
        base = 4 * self.depths
        late = 5 * self.depths
        for turn in turns:
            self.fold(turn, 2)
            self.fold(turn, 4)
            via = 2 if turn < self.depths // 2 else 1
            self.arrive(self.near.at[turn], base + turn)
            self.total[via, turn] = (self.total[via, turn].astype(F32) + self.near[turn].astype(F32)).astype(BF16)
            self.push(self.total.at[1, turn], self.far.at[0, turn], late + turn, 0, 2)
            self.push(self.total.at[2, turn], self.far.at[1, turn], late + self.depths + turn, 0, 4)

    def climb(self, turns):
        late = 5 * self.depths
        last = 7 * self.depths
        for turn in turns:
            self.fold(turn, 0)
            self.arrive(self.far.at[0, turn], late + turn)
            self.arrive(self.far.at[1, turn], late + self.depths + turn)
            self.total[0, turn] = (
                self.total[0, turn].astype(F32) + self.far[0, turn].astype(F32) + self.far[1, turn].astype(F32)
            ).astype(BF16)
            if turn:
                back = self.depths - turn
                self.push(self.total.at[0, turn], self.far.at[2, back], last + back, turn, 0)

    def finish(self):
        last = 7 * self.depths
        out = self.total[0, 0].astype(F32)
        for turn in range(1, self.depths):
            self.arrive(self.far.at[2, turn], last + turn)
            out = out + self.far[2, turn].astype(F32)
        return out

    def close(self):
        self.drain(self.near.at[0])


def scatter_scratch(block, depths):
    return [
        pltpu.VMEM((4, depths) + block, BF16),
        pltpu.VMEM((4, depths) + block, BF16),
        pltpu.VMEM((depths,) + block, BF16),
        pltpu.VMEM((3, depths) + block, BF16),
    ]


def dot(a, b):
    return jnp.dot(a, b, preferred_element_type=F32)


def dot_t(a, b):
    return lax.dot_general(a, b, (((1,), (1,)), ((), ())), preferred_element_type=F32)


def standardize(values):
    row_mean = jnp.mean(values, axis=-1, keepdims=True)
    centred = values - row_mean
    variance = jnp.mean(centred * centred, axis=-1, keepdims=True)
    inv_std = lax.rsqrt(variance + EPSILON)
    return (centred * inv_std, inv_std)


def norm_back(grad_in, unit_rows, inv_std, gain):
    scaled = grad_in * gain
    row_mean = jnp.mean(scaled, axis=-1, keepdims=True)
    cross_mean = jnp.mean(scaled * unit_rows, axis=-1, keepdims=True)
    return inv_std * (scaled - row_mean - unit_rows * cross_mean)


def fold_rows(values):
    return jnp.sum(values.reshape(-1, 8, values.shape[-1]), axis=0)


def gelu_parts(upper):
    cdf = 0.5 * (1.0 + lax.erf(upper * 0.7071067811865476))
    slope = cdf + upper * jnp.exp(-0.5 * upper * upper) * 0.3989422804014327
    return (upper * cdf, slope)


def pair_halves(rows):
    lanes = lax.broadcasted_iota(jnp.int32, rows.shape, 1)
    half = rows.shape[1] // 2
    zero = jnp.zeros_like(rows)
    return jnp.concatenate(
        [jnp.where(lanes < half, rows, zero), jnp.where(lanes >= half, rows, zero)], axis=0
    )


def head_select(count, width):
    head_of_row = lax.broadcasted_iota(jnp.int32, (HEADS * count, width), 0) // count
    head_of_lane = lax.broadcasted_iota(jnp.int32, (HEADS * count, width), 1) // (width // HEADS)
    return head_of_row == head_of_lane


def per_head(rows, select):
    tiled = jnp.concatenate([rows.astype(F32)] * HEADS, axis=0)
    return jnp.where(select, tiled, 0.0).astype(BF16)


def rows_of(ref):
    depths, lanes = ref.shape[0], ref.shape[3]
    return jnp.concatenate([ref[d].reshape(-1, lanes) for d in range(depths)], axis=1)


def lanes_of(ref, chunk, along):
    lanes = ref.shape[3]
    take = (lambda i: ref[i]) if along == 0 else (lambda i: ref[:, i])
    if lanes >= FF_CHUNK:
        per = lanes // FF_CHUNK
        cut = slice(chunk % per * FF_CHUNK, (chunk % per + 1) * FF_CHUNK)
        return take(chunk // per).reshape(-1, lanes)[:, cut]
    per = FF_CHUNK // lanes
    return jnp.concatenate([take(i).reshape(-1, lanes) for i in range(chunk * per, (chunk + 1) * per)], axis=1)


def put_blocks(ref, values, rows_along):
    depths, spots, rows, lanes = ref.shape
    for d in range(depths):
        for c in range(spots):
            r, l = (c, d) if rows_along == 1 else (d, c)
            ref[d, c] = values[r * rows : (r + 1) * rows, l * lanes : (l + 1) * lanes].astype(ref.dtype)


def project_kernel(x_ref, xp_ref, w_ref, gain_ref, q_ref, k_ref, v_ref, kp_ref, vp_ref, n_ref, np_ref, sum_ref):
    width = x_ref.shape[1]
    gain = gain_ref[...]
    weight = rows_of(w_ref)
    normed = (standardize(x_ref[...].astype(F32))[0] * gain).astype(BF16)
    n_ref[...] = normed
    scale = (width // HEADS) ** -0.5
    q_ref[...] = (dot_t(normed, weight[:width]).astype(BF16).astype(F32) * scale).astype(BF16)
    for part, out in ((1, k_ref), (2, v_ref)):
        rows = dot_t(normed, weight[part * width : (part + 1) * width]).astype(BF16)
        out[...] = rows
        means = jnp.mean(rows.astype(F32).reshape(TILE_SEQS, -1, width), axis=1)
        sum_ref[0, :, (part - 1) * width : part * width] = means.astype(BF16)
    normed_prev = (standardize(xp_ref[...].astype(F32))[0] * gain).astype(BF16)
    np_ref[...] = normed_prev
    kp_ref[...] = dot_t(normed_prev, weight[width : 2 * width]).astype(BF16)
    vp_ref[...] = dot_t(normed_prev, weight[2 * width :]).astype(BF16)


def row_spec(rows, width):
    return pl.BlockSpec((rows, width), lambda i: (i, 0))


def whole_spec(shape):
    return pl.BlockSpec(shape, lambda i: (0,) * len(shape))


def params():
    return pltpu.CompilerParams(vmem_limit_bytes=VMEM_MOST)


def project(x, x_prev, w_qkv, gain, span):
    rows, width = x.shape
    tile = TILE_SEQS * span
    low = jax.ShapeDtypeStruct((rows, width), BF16)
    return pl.pallas_call(
        project_kernel,
        grid=(rows // tile,),
        in_specs=[row_spec(tile, width)] * 2 + [whole_spec(w_qkv.shape), whole_spec(gain.shape)],
        out_specs=[row_spec(tile, width)] * 7
        + [pl.BlockSpec((1, TILE_SEQS, 2 * width), lambda i: (i, 0, 0))],
        out_shape=[low] * 7 + [jax.ShapeDtypeStruct((rows // tile, TILE_SEQS, 2 * width), BF16)],
        compiler_params=params(),
        name="project",
    )(x, x_prev, w_qkv, gain)


def attend_one(span, block, prefix, queries, keys, values, sums, keep_prob):
    width = queries.shape[1]
    pair = 2 * width // HEADS
    half = pair // 2
    count = sums.shape[0]
    select = head_select(count, width)
    unit_pos = lax.broadcasted_iota(jnp.int32, (span, span), 0)
    query_pos = lax.broadcasted_iota(jnp.int32, (span, span), 1)
    sum_id = lax.broadcasted_iota(jnp.int32, (count, span), 0)
    sum_query = lax.broadcasted_iota(jnp.int32, (count, span), 1)
    bias_prev = jnp.where(block >= 1, 0.0, MASKED).astype(F32)
    start = block * span
    own_ok = (unit_pos <= query_pos) | (start + unit_pos < prefix)
    bias_own = jnp.where(own_ok, 0.0, MASKED)
    sum_ok = (sum_id <= block - 1) | (
        (start + sum_query < prefix) & (sum_id >= block + 1) & ((sum_id + 1) * span <= prefix)
    )
    bias_sum = jnp.where(sum_ok, math.log(span), MASKED)
    values_t = values.T
    sum_keys = per_head(sums[:, :width], select)
    sum_values_t = per_head(sums[:, width : 2 * width], select).T
    sum_scores = dot_t(sum_keys, queries)
    mixed_parts = []
    sum_probs = []
    for p in range(HEADS // 2):
        lanes = slice(p * pair, (p + 1) * pair)
        scores = dot_t(keys[:, lanes], pair_halves(queries[:, lanes]))
        probs = []
        for e in range(2):
            h = 2 * p + e
            cols = slice(e * span, (e + 1) * span)
            s_prev = scores[:span, cols]
            s_own = scores[span:, cols] + bias_own
            s_sum = sum_scores[h * count : (h + 1) * count] + bias_sum
            most = jnp.maximum(
                jnp.maximum(
                    jnp.max(s_prev, axis=0, keepdims=True) + bias_prev,
                    jnp.max(s_own, axis=0, keepdims=True),
                ),
                jnp.max(s_sum, axis=0, keepdims=True),
            )
            e_prev = jnp.exp(s_prev + (bias_prev - most))
            e_own = jnp.exp(s_own - most)
            e_sum = jnp.exp(s_sum - most)
            total = (
                jnp.sum(e_prev, axis=0, keepdims=True)
                + jnp.sum(e_own, axis=0, keepdims=True)
                + jnp.sum(e_sum, axis=0, keepdims=True)
            )
            inverse = 1.0 / total
            probs.append(jnp.concatenate([e_prev * inverse, e_own * inverse], axis=0).astype(BF16))
            sum_probs.append(e_sum * inverse)
        both = jnp.concatenate(probs, axis=1)
        keep_prob(p, both)
        crossed = dot(values_t[lanes, :], both)
        mixed_parts.append(crossed[:half, :span])
        mixed_parts.append(crossed[half:, span:])
    all_sums = jnp.concatenate(sum_probs, axis=0).astype(BF16)
    mixed_t = jnp.concatenate(mixed_parts, axis=0) + dot(sum_values_t, all_sums)
    return mixed_t.T.astype(BF16), all_sums


def attend_kernel(
    span, prefix_ref, block_ref, q_ref, k_ref, v_ref, kp_ref, vp_ref, sums_ref, mixed_ref, prob_ref, psum_ref
):
    for s in range(TILE_SEQS):
        rows = slice(s * span, (s + 1) * span)

        def keep_prob(p, both, s=s):
            prob_ref[s, p] = both

        mixed, all_sums = attend_one(
            span,
            block_ref[0],
            prefix_ref[pl.program_id(0) * TILE_SEQS + s],
            q_ref[rows, :],
            jnp.concatenate([kp_ref[rows, :], k_ref[rows, :]], axis=0),
            jnp.concatenate([vp_ref[rows, :], v_ref[rows, :]], axis=0),
            sums_ref[s],
            keep_prob,
        )
        mixed_ref[rows, :] = mixed
        psum_ref[s] = all_sums


def attend(prefix, block, q, k, v, kp, vp, sums, span):
    rows, width = q.shape
    tile = TILE_SEQS * span
    seqs, count = sums.shape[0], sums.shape[1]
    pairs = HEADS // 2
    return pl.pallas_call(
        functools.partial(attend_kernel, span),
        grid=(rows // tile,),
        in_specs=[pl.BlockSpec(memory_space=pltpu.SMEM)] * 2
        + [row_spec(tile, width)] * 5
        + [pl.BlockSpec((TILE_SEQS, count, 2 * width), lambda i: (i, 0, 0))],
        out_specs=[
            row_spec(tile, width),
            pl.BlockSpec((TILE_SEQS, pairs, 2 * span, 2 * span), lambda i: (i, 0, 0, 0)),
            pl.BlockSpec((TILE_SEQS, HEADS * count, span), lambda i: (i, 0, 0)),
        ],
        out_shape=[
            jax.ShapeDtypeStruct((rows, width), BF16),
            jax.ShapeDtypeStruct((seqs, pairs, 2 * span, 2 * span), BF16),
            jax.ShapeDtypeStruct((seqs, HEADS * count, span), BF16),
        ],
        compiler_params=params(),
        name="attend",
    )(prefix, block, q, k, v, kp, vp, sums)


def feed_kernel(
    x_ref, mixed_ref, g_ref, wo_ref, wu_ref, wd_ref, gain_ref,
    out_ref, gm_ref, gr_ref, gout_ref, gup_ref, gdown_ref, ggain_ref,
    acc_out, acc_up, acc_down, acc_gain,
):
    step = pl.program_id(0)

    @pl.when(step == 0)
    def _():
        acc_out[...] = jnp.zeros_like(acc_out)
        acc_up[...] = jnp.zeros_like(acc_up)
        acc_down[...] = jnp.zeros_like(acc_down)
        acc_gain[...] = jnp.zeros_like(acc_gain)

    gain = gain_ref[gain_ref.shape[0] - 1 :, :]
    mixed = mixed_ref[...]
    w_out = rows_of(wo_ref)
    resid = x_ref[...].astype(F32) + dot_t(mixed, w_out)
    unit, inv = standardize(resid)
    normed = (unit * gain).astype(BF16)
    normed_t = normed.T
    grad = g_ref[...]
    grad_t = grad.T
    hidden_width = acc_up.shape[1]
    result = resid
    grad_norm = None
    for c in range(hidden_width // FF_CHUNK):
        cols = slice(c * FF_CHUNK, (c + 1) * FF_CHUNK)
        w_up = lanes_of(wu_ref, c, 1)
        w_down = lanes_of(wd_ref, c, 0)
        upper = dot(normed, w_up)
        grad_hidden = dot(grad, w_down)
        activated, slope = gelu_parts(upper)
        hidden = activated.astype(BF16)
        grad_upper = (grad_hidden * slope).astype(BF16)
        result = result + dot_t(hidden, w_down)
        back = dot_t(grad_upper, w_up)
        grad_norm = back if grad_norm is None else grad_norm + back
        acc_down[:, cols] += dot(grad_t, hidden)
        acc_up[:, cols] += dot(normed_t, grad_upper)
    out_ref[...] = result.astype(BF16)
    acc_gain[...] += fold_rows(grad_norm * unit)
    grad_resid = grad.astype(F32) + norm_back(grad_norm, unit, inv, gain)
    gr_ref[...] = grad_resid
    grad_branch = grad_resid.astype(BF16)
    acc_out[...] += dot(grad_branch.T, mixed)
    gm_ref[...] = dot(grad_branch, w_out).astype(BF16)

    @pl.when(step == pl.num_programs(0) - 1)
    def _():
        put_blocks(gout_ref, acc_out, 1)
        put_blocks(gup_ref, acc_up, 0)
        put_blocks(gdown_ref, acc_down, 1)
        ggain_ref[...] = acc_gain[...]


def feed(x, mixed, grad, w_out, w_up, w_down, gain, tile):
    rows, width = x.shape
    hidden = w_up.shape[1] * w_up.shape[3]
    wide = (width, hidden)
    square = (width, width)
    return pl.pallas_call(
        feed_kernel,
        grid=(rows // tile,),
        in_specs=[row_spec(tile, width)] * 3
        + [whole_spec(w_out.shape), whole_spec(w_up.shape), whole_spec(w_down.shape), whole_spec(gain.shape)],
        out_specs=[row_spec(tile, width)] * 3
        + [whole_spec(w_out.shape), whole_spec(w_up.shape), whole_spec(w_down.shape), whole_spec((8, width))],
        out_shape=[
            jax.ShapeDtypeStruct((rows, width), BF16),
            jax.ShapeDtypeStruct((rows, width), BF16),
            jax.ShapeDtypeStruct((rows, width), F32),
            jax.ShapeDtypeStruct(w_out.shape, BF16),
            jax.ShapeDtypeStruct(w_up.shape, BF16),
            jax.ShapeDtypeStruct(w_down.shape, BF16),
            jax.ShapeDtypeStruct((8, width), F32),
        ],
        scratch_shapes=[
            pltpu.VMEM(square, F32),
            pltpu.VMEM(wide, F32),
            pltpu.VMEM(wide, F32),
            pltpu.VMEM((8, width), F32),
        ],
        compiler_params=params(),
        name="feed",
    )(x, mixed, grad, w_out, w_up, w_down, gain)


def return_one(span, queries, keys, values, sums, grad_mixed, prob_at, sum_low):
    width = queries.shape[1]
    pair = 2 * width // HEADS
    half = pair // 2
    count = sums.shape[0]
    scale = half ** -0.5
    select = head_select(count, width)
    keys_t = keys.T
    sum_keys_t = per_head(sums[:, :width], select).T
    sum_values = per_head(sums[:, width : 2 * width], select)
    sum_prob = sum_low.astype(F32)
    sum_moved = sum_prob * dot_t(sum_values, grad_mixed)
    grad_q_parts = []
    grad_k_parts = []
    grad_v_parts = []
    sum_grads = []
    for p in range(HEADS // 2):
        lanes = slice(p * pair, (p + 1) * pair)
        grads2 = pair_halves(grad_mixed[:, lanes])
        grad_prob = dot_t(values[:, lanes], grads2)
        low = prob_at(p)
        prob = low.astype(F32)
        moved = prob * grad_prob
        deltas = jnp.sum(moved, axis=0, keepdims=True)
        sums_of = []
        for e in range(2):
            h = 2 * p + e
            part = slice(h * count, (h + 1) * count)
            delta = deltas[:, e * span : (e + 1) * span] + jnp.sum(sum_moved[part], axis=0, keepdims=True)
            sums_of.append(delta)
            sum_grads.append(sum_moved[part] - sum_prob[part] * delta)
        grad_scores = (moved - prob * jnp.concatenate(sums_of, axis=1)).astype(BF16)
        grad_k_parts.append(dot(grad_scores, pair_halves(queries[:, lanes])))
        grad_v_parts.append(dot(low, grads2))
        crossed = dot(keys_t[lanes, :], grad_scores)
        grad_q_parts.append(crossed[:half, :span])
        grad_q_parts.append(crossed[half:, span:])
    sum_scores_grad = jnp.concatenate(sum_grads, axis=0).astype(BF16)
    grad_q = jnp.concatenate(grad_q_parts, axis=0) + dot(sum_keys_t, sum_scores_grad)
    grad_q = (grad_q.T * scale).astype(BF16)
    grad_k = jnp.concatenate(grad_k_parts, axis=1).astype(BF16)
    grad_v = jnp.concatenate(grad_v_parts, axis=1).astype(BF16)
    wide_k = jnp.where(select, dot(sum_scores_grad, queries), 0.0)
    wide_v = jnp.where(select, dot(sum_low, grad_mixed), 0.0)
    folded_k = jnp.sum(wide_k.reshape(HEADS, count, width), axis=0)
    folded_v = jnp.sum(wide_v.reshape(HEADS, count, width), axis=0)
    return (
        jnp.concatenate([grad_q, grad_k[span:], grad_v[span:]], axis=1),
        jnp.concatenate([grad_k[:span], grad_v[:span]], axis=1),
        jnp.concatenate([folded_k, folded_v], axis=1) * (1.0 / span),
    )


def return_tile(weight, own, before, shared, normed, normed_prev, normed_sum, acc):
    width = normed.shape[1]
    grad_own = jnp.concatenate(own, axis=0)
    grad_before = jnp.concatenate(before, axis=0)
    grad_shared = jnp.concatenate(shared, axis=0).astype(BF16)
    normed_t = normed.T
    acc[:, :width] += dot(normed_t, grad_own[:, :width])
    acc[:, width:] += (
        dot(normed_t, grad_own[:, width:]) + dot(normed_prev.T, grad_before) + dot(normed_sum.T, grad_shared)
    )
    return grad_own, dot(grad_before, weight[width:]), dot(grad_shared, weight[width:])


def return_kernel(
    span, q_ref, k_ref, v_ref, kp_ref, vp_ref, sums_ref, gm_ref, prob_ref, psum_ref, n_ref, np_ref, nsum_ref, w_ref,
    gn_ref, gp_ref, gs_ref, gqkv_ref, acc,
):
    step = pl.program_id(0)

    @pl.when(step == 0)
    def _():
        acc[...] = jnp.zeros_like(acc)

    parts = []
    for s in range(TILE_SEQS):
        rows = slice(s * span, (s + 1) * span)
        parts.append(
            return_one(
                span,
                q_ref[rows, :],
                jnp.concatenate([kp_ref[rows, :], k_ref[rows, :]], axis=0),
                jnp.concatenate([vp_ref[rows, :], v_ref[rows, :]], axis=0),
                sums_ref[s],
                gm_ref[rows, :],
                lambda p, s=s: prob_ref[s, p],
                psum_ref[s],
            )
        )
    normed_sum = nsum_ref[...].reshape(-1, nsum_ref.shape[2])
    weight = rows_of(w_ref)
    grad_own, gp, gs = return_tile(weight, *zip(*parts), n_ref[...], np_ref[...], normed_sum, acc)
    gn_ref[...] = dot(grad_own, weight)
    gp_ref[...] = gp.astype(BF16)
    gs_ref[...] = gs.reshape(gs_ref.shape).astype(BF16)

    @pl.when(step == pl.num_programs(0) - 1)
    def _():
        put_blocks(gqkv_ref, acc[...].astype(BF16).T, 1)


def give_back(q, k, v, kp, vp, sums, gm, prob, psum, n, n_prev, n_sum, w_qkv, span):
    rows, width = q.shape
    tile = TILE_SEQS * span
    seqs, count = sums.shape[0], sums.shape[1]
    pairs = HEADS // 2
    return pl.pallas_call(
        functools.partial(return_kernel, span),
        grid=(rows // tile,),
        in_specs=[row_spec(tile, width)] * 5
        + [
            pl.BlockSpec((TILE_SEQS, count, 2 * width), lambda i: (i, 0, 0)),
            row_spec(tile, width),
            pl.BlockSpec((TILE_SEQS, pairs, 2 * span, 2 * span), lambda i: (i, 0, 0, 0)),
            pl.BlockSpec((TILE_SEQS, HEADS * count, span), lambda i: (i, 0, 0)),
            row_spec(tile, width),
            row_spec(tile, width),
            pl.BlockSpec((TILE_SEQS, count, width), lambda i: (i, 0, 0)),
            whole_spec(w_qkv.shape),
        ],
        out_specs=[
            row_spec(tile, width),
            row_spec(tile, width),
            pl.BlockSpec((TILE_SEQS, count, width), lambda i: (i, 0, 0)),
            whole_spec(w_qkv.shape),
        ],
        out_shape=[
            jax.ShapeDtypeStruct((rows, width), F32),
            jax.ShapeDtypeStruct((rows, width), BF16),
            jax.ShapeDtypeStruct((seqs, count, width), BF16),
            jax.ShapeDtypeStruct(w_qkv.shape, BF16),
        ],
        scratch_shapes=[pltpu.VMEM((width, 3 * width), F32)],
        compiler_params=params(),
        name="give_back",
    )(q, k, v, kp, vp, sums, gm, prob, psum, n, n_prev, n_sum, w_qkv)


def close_kernel(span, x_ref, gn_ref, gb_ref, gs_ref, gr_ref, gain_ref, out_ref, ggain_ref, acc):
    step = pl.program_id(0)
    width = x_ref.shape[1]

    @pl.when(step == 0)
    def _():
        acc[...] = jnp.zeros_like(acc)

    unit, inv = standardize(x_ref[...].astype(F32))
    grad_norm = gn_ref[...] + gb_ref[...].astype(F32)
    lifted = [
        grad_norm[s * span : (s + 1) * span] + gs_ref[s].astype(F32) for s in range(TILE_SEQS)
    ]
    grad_norm = jnp.concatenate(lifted, axis=0)
    acc[...] += fold_rows(grad_norm * unit)
    part = norm_back(grad_norm, unit, inv, gain_ref[...])
    out_ref[...] = (gr_ref[...] + part).astype(BF16)

    @pl.when(step == pl.num_programs(0) - 1)
    def _():
        ggain_ref[...] = acc[...]


def close(x, gn, gb, gs, gr, gain, span):
    rows, width = x.shape
    tile = TILE_SEQS * span
    return pl.pallas_call(
        functools.partial(close_kernel, span),
        grid=(rows // tile,),
        in_specs=[row_spec(tile, width)] * 3
        + [pl.BlockSpec((TILE_SEQS, 1, width), lambda i: (i, 0, 0)), row_spec(tile, width), whole_spec(gain.shape)],
        out_specs=[row_spec(tile, width), whole_spec((8, width))],
        out_shape=[jax.ShapeDtypeStruct((rows, width), BF16), jax.ShapeDtypeStruct((8, width), F32)],
        scratch_shapes=[pltpu.VMEM((8, width), F32)],
        compiler_params=params(),
        name="close",
    )(x, gn, gb, gs, gr, gain)


def in_order(count, seqs):
    row = lax.broadcasted_iota(jnp.int32, (count * seqs, count * seqs), 0)
    col = lax.broadcasted_iota(jnp.int32, (count * seqs, count * seqs), 1)
    return ((col % seqs == row // count) & (col // seqs == row % count)).astype(BF16)


def neighbour(by):
    depth, spot = lax.axis_index("dp"), lax.axis_index("ctx")
    return depth, lax.rem(spot + by + FLIPS, FLIPS)


ENTER_RELAYS = {
    1: ((1, "spread"), (2, "spread"), (3, "spread")),
    4: ((1, "cross"), (2, "cross")),
    5: ((3, "cross"),),
    7: ((1, "hand_over"), (2, "hand_over"), (3, "hand_over")),
}


def enter_kernel(
    depths, span,
    x_in, prefix_ref, bq_ref, bo_ref, bu_ref, bd_ref, one_ref, two_ref,
    wq_out, wo_out, wu_out, wd_out, gain_out, q_out, k_out, v_out, kp_out, vp_out, n_out, np_out, mixed_out, prob_out,
    sums_out, psum_out,
    x_ref, xp, wq, gains, q, k, v, kp, vp, n, n_prev, mixed, prob, slots,
    send, recv, keep, gain_send, gain_recv, sum_send, sum_recv, tok_send, tok_recv, out_sem, prob_sem, wq_sem, x_sem,
):
    x_copy = pltpu.make_async_copy(x_in, x_ref, x_sem.at[0])
    x_copy.start()
    rows, width = x_ref.shape
    tile = TILE_SEQS * span
    tiles = rows // tile
    chunks = tiles // CHUNK_TILES
    seqs = rows // span
    spot = lax.axis_index("ctx")
    scale = (width // HEADS) ** -0.5
    gathers = [
        Gather(depths, own, full, send.at[a], recv.at[a], keep.at[a])
        for a, (own, full) in enumerate(((bq_ref, wq), (bo_ref, wo_out), (bu_ref, wu_out), (bd_ref, wd_out)))
    ]
    gain_share = Share(depths, gains, gain_send, gain_recv)
    sum_share = Share(depths, slots, sum_send, sum_recv)
    shard = jnp.concatenate([one_ref[...].reshape(1, -1), two_ref[...].reshape(1, -1)], axis=0).astype(F32)
    owner = lax.broadcasted_iota(jnp.int32, (2, width), 1) // shard.shape[1]
    gains[spot] = jnp.where(owner == spot, jnp.concatenate([shard] * FLIPS, axis=1), 0.0)

    @pl.when(spot == 0)
    def _():
        xp[...] = jnp.zeros_like(xp)

    def at(i):
        return pl.ds(pl.multiple_of(i * tile, tile), tile)

    def chunk_at(c):
        return pl.ds(pl.multiple_of(c * CHUNK_TILES * tile, CHUNK_TILES * tile), CHUNK_TILES * tile)

    def token_copy(i):
        return pltpu.make_async_remote_copy(
            src_ref=x_ref.at[at(i)],
            dst_ref=xp.at[at(i)],
            send_sem=tok_send.at[i],
            recv_sem=tok_recv.at[i],
            device_id=neighbour(1),
            device_id_type=MESH,
        )

    def out_copy(a, i):
        pairs = ((q, q_out), (k, k_out), (v, v_out), (n, n_out), (kp, kp_out), (vp, vp_out), (n_prev, np_out), (mixed, mixed_out))
        return pltpu.make_async_copy(pairs[a][0].at[at(i)], pairs[a][1].at[at(i)], out_sem.at[a, i])

    def prob_copy(i):
        part = pl.ds(i * TILE_SEQS, TILE_SEQS)
        return pltpu.make_async_copy(prob.at[part], prob_out.at[part], prob_sem.at[i])

    def send_tokens(first, last):
        @pl.when(spot < FLIPS - 1)
        def _():
            for i in range(first, last):
                token_copy(i).start()

    greet(depths)
    gathers[0].begin()
    gain_share.begin()
    x_copy.wait()
    send_tokens(0, 2)
    gain_share.forward()
    gain_share.complete()
    gain = gains[0]
    for c in range(1, FLIPS):
        gain = gain + gains[c]
    gain_out[...] = gain

    def normalize(c):
        n[chunk_at(c), :] = (standardize(x_ref[chunk_at(c), :].astype(F32))[0] * gain[0:1]).astype(BF16)

    def keep_mean(part, ref, weigh):
        means = [
            jnp.sum(ref[s * span : (s + 1) * span, :].astype(F32), axis=0, keepdims=True) * weigh for s in range(seqs)
        ]
        slots[spot, :, part * width : (part + 1) * width] = jnp.concatenate(means, axis=0).astype(BF16)

    pl.loop(0, chunks // 2)(normalize)
    gathers[0].cross(0, 1)
    gathers[0].spread()
    pl.loop(chunks // 2, chunks)(normalize)
    gathers[0].cross(1)
    keep_mean(2, n, 1.0)
    gathers[0].hand_over()
    send_tokens(2, 5)
    gathers[0].complete()
    wq_copy = pltpu.make_async_copy(wq, wq_out, wq_sem.at[0])
    wq_copy.start()

    def send_out(a, c):
        for t in range(CHUNK_TILES):
            out_copy(a, c * CHUNK_TILES + t).start()

    @pl.loop(0, chunks)
    def _(c):
        weight = rows_of(wq)
        normed = n[chunk_at(c), :]
        k[chunk_at(c), :] = dot_t(normed, weight[width : 2 * width]).astype(BF16)
        v[chunk_at(c), :] = dot_t(normed, weight[2 * width :]).astype(BF16)
        for a in (1, 2, 3):
            send_out(a, c)

    keep_mean(0, k, 1.0 / span)
    keep_mean(1, v, 1.0 / span)
    sum_share.begin()
    send_tokens(5, tiles)
    for gather in gathers[1:]:
        gather.begin()

    @pl.loop(0, chunks)
    def _(c):
        weight = rows_of(wq)
        rows_q = dot_t(n[chunk_at(c), :], weight[:width]).astype(BF16)
        q[chunk_at(c), :] = (rows_q.astype(F32) * scale).astype(BF16)
        send_out(0, c)

    def project_prev(c):
        @pl.when(spot > 0)
        def _():
            for t in range(CHUNK_TILES):
                token_copy(c * CHUNK_TILES + t).wait_recv()

        weight = rows_of(wq)
        normed = (standardize(xp[chunk_at(c), :].astype(F32))[0] * gain[0:1]).astype(BF16)
        n_prev[chunk_at(c), :] = normed
        kp[chunk_at(c), :] = dot_t(normed, weight[width : 2 * width]).astype(BF16)
        vp[chunk_at(c), :] = dot_t(normed, weight[2 * width :]).astype(BF16)
        for a in (4, 5, 6):
            send_out(a, c)

    project_prev(0)
    sum_share.forward()
    project_prev(1)
    sum_share.complete()
    ordered = dot(in_order(FLIPS, seqs), slots[...].reshape(FLIPS * seqs, 3 * width)).astype(BF16)
    sums_out[...] = ordered.reshape(sums_out.shape)
    @pl.loop(0, tiles)
    def _(i):
        @pl.when((lax.rem(i, CHUNK_TILES) == 0) & (i >= 2 * CHUNK_TILES))
        def _():
            project_prev(i // CHUNK_TILES)

        for s in range(TILE_SEQS):
            here = pl.ds(pl.multiple_of(i * tile + s * span, span), span)
            seq = i * TILE_SEQS + s

            def keep_prob(p, both, seq=seq):
                prob[seq, p] = both

            rows_mixed, all_sums = attend_one(
                span,
                spot,
                prefix_ref[seq // prefix_ref.shape[1], lax.rem(seq, prefix_ref.shape[1])],
                q[here, :],
                jnp.concatenate([kp[here, :], k[here, :]], axis=0),
                jnp.concatenate([vp[here, :], v[here, :]], axis=0),
                sums_out[seq],
                keep_prob,
            )
            mixed[here, :] = rows_mixed
            psum_out[seq] = all_sums
        out_copy(7, i).start()
        prob_copy(i).start()
        for when, relays in ENTER_RELAYS.items():

            @pl.when(i == when)
            def _(relays=relays):
                for a, name in relays:
                    getattr(gathers[a], name)()

    for gather in gathers[1:]:
        gather.complete()
    for move in (*gathers, gain_share, sum_share):
        move.close()

    @pl.when(spot < FLIPS - 1)
    def _():
        for i in range(tiles):
            token_copy(i).wait_send()

    wq_copy.wait()

    @pl.loop(0, tiles)
    def _(i):
        for a in range(8):
            out_copy(a, i).wait()
        prob_copy(i).wait()


def enter(x, prefix, blocks, gain_one, gain_two, span, depths):
    rows, width = x.shape
    tile = TILE_SEQS * span
    tiles, seqs = rows // tile, rows // span
    low = jax.ShapeDtypeStruct((rows, width), BF16)
    fulls = [jax.ShapeDtypeStruct((depths, FLIPS) + b.shape, BF16) for b in blocks]
    prob_shape = (seqs, HEADS // 2, 2 * span, 2 * span)
    vmem = pl.BlockSpec(memory_space=pltpu.VMEM)
    far = pl.BlockSpec(memory_space=pl.ANY)
    sems = pltpu.SemaphoreType.DMA
    held = pltpu.VMEM((rows, width), BF16)
    return pl.pallas_call(
        functools.partial(enter_kernel, depths, span),
        in_specs=[far, pl.BlockSpec(memory_space=pltpu.SMEM)] + [vmem] * 6,
        out_specs=[far] * 4 + [vmem] + [far] * 9 + [vmem] * 2,
        out_shape=fulls
        + [jax.ShapeDtypeStruct((2, width), F32)]
        + [low] * 8
        + [
            jax.ShapeDtypeStruct(prob_shape, BF16),
            jax.ShapeDtypeStruct((seqs, FLIPS, 3 * width), BF16),
            jax.ShapeDtypeStruct((seqs, HEADS * FLIPS, span), BF16),
        ],
        scratch_shapes=[
            held,
            held,
            pltpu.VMEM(fulls[0].shape, BF16),
            pltpu.VMEM((FLIPS, 2, width), F32),
        ]
        + [held] * 8
        + [pltpu.VMEM(prob_shape, BF16), pltpu.VMEM((FLIPS, seqs, 3 * width), BF16)]
        + [
            sems((4, depths * FLIPS)), sems((4, depths * FLIPS)), sems((4,)),
            sems((FLIPS,)), sems((FLIPS,)), sems((FLIPS,)), sems((FLIPS,)),
            sems((tiles,)), sems((tiles,)), sems((8, tiles)), sems((tiles,)), sems((1,)), sems((1,)),
        ],
        compiler_params=pltpu.CompilerParams(collective_id=0, has_side_effects=True, vmem_limit_bytes=VMEM_MOST),
        name="enter",
    )(x, prefix, *blocks, gain_one, gain_two)


LEAVE_RELAYS = {
    0: ((0, "cross"),),
    1: ((1, "cross"), (2, "cross")),
    3: ((0, "spread"), (1, "spread")),
    5: ((2, "spread"),),
    6: ((0, "climb"), (1, "climb")),
}


def leave_kernel(
    depths, span,
    q_in, k_in, v_in, kp_in, vp_in, gm_in, n_in, np_in, prob_in, gr_in, x_in,
    psum_in, sums_in, wq_in, gout_in, gup_in, gdown_in, gain_ref, ggain_ref,
    ig_out, dqkv_out, dout_out, dup_out, ddown_out, dgain_out,
    psum_ref, sums_ref, wq_ref, gout_ref, gup_ref, gdown_ref, held, prob, kept, before, shared_rows, turned, turned_prev, turned_sum, one_sum, gp, gb, gr, x, ig, part, gs_send_buf, gs_slots, gain_slots, gain_deep,
    *rest,
):
    moves_refs, sems = rest[:16], rest[16:]
    send, recv, gs_send, gs_recv, gain_send, gain_recv, deep_send, deep_recv, gb_send, gb_recv, in_sem, late_sem, ig_sem, whole_sem = sems
    inputs = (gout_in, gup_in, gdown_in, psum_in, sums_in, wq_in)
    landing = (gout_ref, gup_ref, gdown_ref, psum_ref, sums_ref, wq_ref)
    wholes = [pltpu.make_async_copy(a, b, whole_sem.at[n]) for n, (a, b) in enumerate(zip(inputs, landing))]
    for copy in wholes:
        copy.start()
    rows, width = gp.shape
    tile = TILE_SEQS * span
    tiles = rows // tile
    seqs = rows // span
    spot = lax.axis_index("ctx")
    parts = (gout_ref, gup_ref, gdown_ref, part)
    scatters = [
        Scatter(depths, parts[a], *moves_refs[4 * a : 4 * a + 4], send.at[a], recv.at[a]) for a in range(4)
    ]
    gain_share = Share(depths, gain_slots, gain_send, gain_recv)
    gs_moves = Moves(depths, gs_send, gs_recv)
    deep_moves = Moves(depths, deep_send, deep_recv)

    def at(i):
        return pl.ds(pl.multiple_of(i * tile, tile), tile)

    def at_sums(i):
        return pl.ds(pl.multiple_of(i * TILE_SEQS * FLIPS, TILE_SEQS * FLIPS), TILE_SEQS * FLIPS)

    def loads(i, slot):
        arrays = (q_in, k_in, v_in, kp_in, vp_in, gm_in, n_in, np_in)
        copies = [pltpu.make_async_copy(ref.at[at(i)], held.at[slot, a], in_sem.at[slot, a]) for a, ref in enumerate(arrays)]
        of_tile = pl.ds(i * TILE_SEQS, TILE_SEQS)
        return copies + [pltpu.make_async_copy(prob_in.at[of_tile], prob.at[slot], in_sem.at[slot, len(arrays)])]

    def gb_copy(i):
        return pltpu.make_async_remote_copy(
            src_ref=gp.at[at(i)],
            dst_ref=gb.at[at(i)],
            send_sem=gb_send.at[i],
            recv_sem=gb_recv.at[i],
            device_id=neighbour(-1),
            device_id_type=MESH,
        )

    for copy in loads(0, 0):
        copy.start()
    late = [pltpu.make_async_copy(gr_in, gr, late_sem.at[0]), pltpu.make_async_copy(x_in, x, late_sem.at[1])]

    @pl.when(spot == FLIPS - 1)
    def _():
        gb[...] = jnp.zeros_like(gb)

    greet(depths)
    turns = (*range(1, depths), 0)
    for copy, scatter in zip(wholes, scatters[:3]):
        copy.wait()
        scatter.begin(turns)
    for copy in wholes[3:]:
        copy.wait()

    @pl.loop(0, tiles)
    def _(i):
        slot = lax.rem(i, 2)
        for copy in loads(i, slot):
            copy.wait()

        @pl.when(i + 1 < tiles)
        def _():
            for copy in loads(i + 1, 1 - slot):
                copy.start()

        pieces = []
        for s in range(TILE_SEQS):
            here = slice(s * span, (s + 1) * span)
            seq = i * TILE_SEQS + s
            pieces.append(
                return_one(
                    span,
                    held[slot, 0, here],
                    jnp.concatenate([held[slot, 3, here], held[slot, 1, here]], axis=0),
                    jnp.concatenate([held[slot, 4, here], held[slot, 2, here]], axis=0),
                    sums_ref[seq],
                    held[slot, 5, here],
                    lambda p, s=s: prob[slot, s, p],
                    psum_ref[seq],
                )
            )
        own, back, shared = (jnp.concatenate(rows, axis=0) for rows in zip(*pieces))
        weight_kv = rows_of(wq_ref)[width:]
        kept[at(i), :] = own
        before[at(i), :] = back
        gp[at(i), :] = dot(back, weight_kv).astype(BF16)
        shared_rows[at_sums(i), :] = shared.astype(BF16)
        turned[:, at(i)] = held[slot, 6].T
        turned_prev[:, at(i)] = held[slot, 7].T

        @pl.when(spot > 0)
        def _():
            gb_copy(i).start()

        for when, relays in LEAVE_RELAYS.items():

            @pl.when(i == when)
            def _(relays=relays):
                for a, name in relays:
                    getattr(scatters[a], name)(turns)

        @pl.when(i == tiles - 3)
        def _():
            for copy in late:
                copy.start()

    to_sums = dot(shared_rows[...], rows_of(wq_ref)[width:]).astype(BF16)
    by_spot = lax.dot_general(
        in_order(FLIPS, seqs), to_sums, (((0,), (0,)), ((), ())), preferred_element_type=F32
    )
    gs_send_buf[...] = by_spot.astype(BF16).reshape(gs_send_buf.shape)
    for flip in (6, 7, 2, 4, 3, 5, 1):
        gs_moves.start(gs_send_buf.at[spot_of(depths, 0, flip)[1]], gs_slots.at[flip], flip, 0, flip)
    turned_sum[...] = sums_ref[:, :, 2 * width :].reshape(seqs * FLIPS, width).T
    lanes_in = width // depths

    def weigh(turns):
        owners = [spot_of(depths, turn, 0)[0] for turn in turns]
        tops = [pl.ds(pl.multiple_of(owner * lanes_in, lanes_in), lanes_in) for owner in owners]
        rows_own, rows_prev, rows_sum = (
            jnp.concatenate([ref[top, :] for top in tops], axis=0) for ref in (turned, turned_prev, turned_sum)
        )
        grad_q = dot(rows_own, kept[:, :width])
        grad_kv = dot(rows_own, kept[:, width:]) + dot(rows_prev, before[...]) + dot(rows_sum, shared_rows[...])
        low = jnp.concatenate([grad_q.astype(BF16), grad_kv.astype(BF16)], axis=1)
        for t, (owner, top) in enumerate(zip(owners, tops)):
            flat = low[t * lanes_in : (t + 1) * lanes_in].T
            part[owner] = flat.reshape(part.shape[1:])
            weighed = flat.astype(F32) * wq_ref[owner].reshape(flat.shape).astype(F32)
            one_sum[:, top] = jnp.sum(weighed, axis=0, keepdims=True)
        scatters[3].begin(turns)

    first, second = turns[: depths // 2], turns[depths // 2 :]
    weigh(first)
    weigh(second)
    scatters[3].cross(first)
    total_one = one_sum[...] / gain_ref[0:1]
    total_two = jnp.sum(ggain_ref[...], axis=0, keepdims=True)
    gain_slots[spot] = jnp.concatenate([total_one, total_two], axis=0)
    gain_share.begin()
    gain_share.forward()
    for copy in late:
        copy.wait()
    for flip in range(1, FLIPS):
        gs_moves.landed(gs_slots.at[flip], flip)
    shared = gs_send_buf[spot].astype(F32)
    for flip in range(1, FLIPS):
        shared = shared + gs_slots[flip].astype(F32)
    gain = gain_ref[0:1]

    def close_tile(i):
        @pl.when(spot < FLIPS - 1)
        def _():
            gb_copy(i).wait_recv()

        unit, inv = standardize(x[at(i), :].astype(F32))
        grad_norm = dot(kept[at(i), :], rows_of(wq_ref)) + gb[at(i), :].astype(F32)
        lifted = [
            grad_norm[s * span : (s + 1) * span] + shared[i * TILE_SEQS + s : i * TILE_SEQS + s + 1]
            for s in range(TILE_SEQS)
        ]
        grad_norm = jnp.concatenate(lifted, axis=0)
        ig[at(i), :] = (gr[at(i), :] + norm_back(grad_norm, unit, inv, gain)).astype(BF16)
        pltpu.make_async_copy(ig.at[at(i)], ig_out.at[at(i)], ig_sem.at[i]).start()

    def share_deep():
        gain_share.complete()
        over_ctx = gain_slots[0]
        for c in range(1, FLIPS):
            over_ctx = over_ctx + gain_slots[c]
        gain_deep[0] = over_ctx
        for turn in range(1, depths):
            deep_moves.start(gain_deep.at[0], gain_deep.at[depths - turn], depths - turn, turn, 0)

    after = {
        1: (functools.partial(scatters[3].cross, second), functools.partial(scatters[3].spread, first)),
        2: (share_deep, functools.partial(scatters[3].spread, second)),
        0: (functools.partial(scatters[2].climb, turns),),
        4: (functools.partial(scatters[3].climb, first),),
        6: (functools.partial(scatters[3].climb, second),),
    }
    for i in range(tiles):
        for relay in after.get(i, ()):
            relay()
        close_tile(i)
    for turn in range(1, depths):
        deep_moves.landed(gain_deep.at[turn], turn)
    over_all = gain_deep[0]
    for turn in range(1, depths):
        over_all = over_all + gain_deep[turn]
    lanes = width // FLIPS
    mine = jnp.zeros((2, lanes), F32)
    for c in range(FLIPS):
        mine = jnp.where(spot == c, over_all[:, c * lanes : (c + 1) * lanes], mine)
    dgain_out[...] = mine
    for out, scatter in zip((dout_out, dup_out, ddown_out, dqkv_out), scatters):
        out[...] = scatter.finish()
    for scatter in scatters:
        scatter.close()
    gain_share.close()
    gs_moves.drain(gs_slots.at[0])
    deep_moves.drain(gain_deep.at[0])

    @pl.when(spot > 0)
    def _():
        for i in range(tiles):
            gb_copy(i).wait_send()

    for i in range(tiles):
        pltpu.make_async_copy(ig.at[at(i)], ig_out.at[at(i)], ig_sem.at[i]).wait()


def leave(arrays, psum, sums, wq, partials, gains, ggain, span, depths):
    rows, width = arrays[0].shape
    tile = TILE_SEQS * span
    tiles, seqs = rows // tile, rows // span
    vmem = pl.BlockSpec(memory_space=pltpu.VMEM)
    far = pl.BlockSpec(memory_space=pl.ANY)
    sems = pltpu.SemaphoreType.DMA
    low = pltpu.VMEM((rows, width), BF16)
    high = pltpu.VMEM((rows, width), F32)
    shapes = [p.shape[2:] for p in (*partials, wq)]
    scratch = [pltpu.VMEM(a.shape, BF16) for a in (psum, sums, wq, *partials)]
    scratch += [
        pltpu.VMEM((2, 8, tile, width), BF16),
        pltpu.VMEM((2, TILE_SEQS, HEADS // 2, 2 * span, 2 * span), BF16),
        pltpu.VMEM((rows, 3 * width), BF16),
        pltpu.VMEM((rows, 2 * width), BF16),
        pltpu.VMEM((seqs * FLIPS, 2 * width), BF16),
        pltpu.VMEM((width, rows), BF16),
        pltpu.VMEM((width, rows), BF16),
        pltpu.VMEM((width, seqs * FLIPS), BF16),
        pltpu.VMEM((1, width), F32),
        low, low, high, low, low,
        pltpu.VMEM(wq.shape, BF16),
        pltpu.VMEM((FLIPS, seqs, width), BF16),
        pltpu.VMEM((FLIPS, seqs, width), BF16),
        pltpu.VMEM((FLIPS, 2, width), F32),
        pltpu.VMEM((depths, 2, width), F32),
    ]
    for shape in shapes:
        scratch += scatter_scratch(shape, depths)
    scratch += [
        sems((4, 8 * depths)), sems((4, 8 * depths)), sems((FLIPS,)), sems((FLIPS,)), sems((FLIPS,)), sems((FLIPS,)),
        sems((depths,)), sems((depths,)), sems((tiles,)), sems((tiles,)), sems((2, 9)), sems((2,)), sems((tiles,)), sems((6,)),
    ]
    outs = [jax.ShapeDtypeStruct(shape, F32) for shape in (shapes[3], *shapes[:3])]
    return pl.pallas_call(
        functools.partial(leave_kernel, depths, span),
        in_specs=[far] * 17 + [vmem] * 2,
        out_specs=[far] + [vmem] * 5,
        out_shape=[jax.ShapeDtypeStruct((rows, width), BF16), *outs, jax.ShapeDtypeStruct((2, width // FLIPS), F32)],
        scratch_shapes=scratch,
        compiler_params=pltpu.CompilerParams(collective_id=1, has_side_effects=True, vmem_limit_bytes=VMEM_MOST),
        name="leave",
    )(*arrays, psum, sums, wq, *partials, gains, ggain)


FINISH_PIECES = 8


def finish_kernel(ig_in, *refs):
    turned, (gains, ig_out), flat = refs[:4], refs[4:6], refs[6:10]
    one_out, two_out, held, load_sem, store_sem = refs[10:]
    rows = ig_in.shape[0] // FINISH_PIECES
    pieces = [pl.ds(i * rows, rows) for i in range(FINISH_PIECES)]
    loads = [pltpu.make_async_copy(ig_in.at[p], held.at[p], load_sem.at[i]) for i, p in enumerate(pieces)]
    stores = [pltpu.make_async_copy(held.at[p], ig_out.at[p], store_sem.at[i]) for i, p in enumerate(pieces)]
    for copy in loads:
        copy.start()
    for given, out in zip(turned, flat):
        out[...] = given[...] if given.shape == out.shape else given[...].T
    one_out[...] = gains[0:1, :].reshape(one_out.shape)
    two_out[...] = gains[1:2, :].reshape(two_out.shape)
    for load, store in zip(loads, stores):
        load.wait()
        store.start()
    for copy in stores:
        copy.wait()


def finish(ig, grads, dgain, shapes):
    vmem = pl.BlockSpec(memory_space=pltpu.VMEM)
    far = pl.BlockSpec(memory_space=pl.ANY)
    outs = [jax.ShapeDtypeStruct(shape, F32) for shape in (*shapes, dgain.shape[1:], dgain.shape[1:])]
    sems = pltpu.SemaphoreType.DMA((FINISH_PIECES,))
    return pl.pallas_call(
        finish_kernel,
        in_specs=[far] + [vmem] * 5,
        out_specs=[far] + [vmem] * 6,
        out_shape=[jax.ShapeDtypeStruct(ig.shape, ig.dtype), *outs],
        scratch_shapes=[pltpu.VMEM(ig.shape, ig.dtype), sems, sems],
        compiler_params=params(),
        name="finish",
    )(ig, *grads, dgain)


def direct_shards(tokens, prefix, blocks, gain_one, gain_two, cotangent):
    span, width = tokens.shape[2], tokens.shape[3]
    depths = lax.axis_size("dp")
    x = tokens.reshape(-1, width)
    grad = cotangent.reshape(-1, width)
    (wq, wo, wu, wd, gains, q, k, v, kp, vp, n, n_prev, mixed, prob, sums, psum) = enter(
        x, prefix, blocks, gain_one, gain_two, span, depths
    )
    out, gm, gr, gout, gup, gdown, ggain = feed(x, mixed, grad, wo, wu, wd, gains, 2 * TILE_SEQS * span)
    arrays = (q, k, v, kp, vp, gm, n, n_prev, prob, gr, x)
    ig, dqkv, dout, dup, ddown, dgain = leave(arrays, psum, sums, wq, (gout, gup, gdown), gains, ggain, span, depths)
    shapes = [blocks[0].shape[::-1], blocks[1].shape[::-1], blocks[2].shape, blocks[3].shape[::-1]]
    ig, *rest = finish(ig, (dqkv, dout, dup, ddown), dgain, shapes)
    return out.reshape(tokens.shape), ig.reshape(tokens.shape), *rest


def fetch(block, rows_along):
    spot, depth = (0, 1) if rows_along == 1 else (1, 0)
    whole = lax.all_gather(lax.all_gather(block, "ctx", axis=spot, tiled=True), "dp", axis=depth, tiled=True)
    return whole[None, None]


def reduce_weight(partial, rows_along):
    spot, depth = (0, 1) if rows_along == 1 else (1, 0)
    columns = lax.psum_scatter(partial[0, 0], "ctx", scatter_dimension=spot, tiled=True)
    return lax.psum_scatter(columns, "dp", scatter_dimension=depth, tiled=True).astype(F32)


def shards(tokens, prefix, w_qkv, w_out, w_up, w_down, gain_one, gain_two, cotangent):
    span, width = tokens.shape[2], tokens.shape[3]
    count = lax.axis_size("ctx")
    blocks = (w_qkv.T, w_out.T, w_up, w_down.T)
    if count == FLIPS and all(b.shape[0] % 16 == 0 and b.shape[1] % 128 == 0 for b in blocks):
        return direct_shards(tokens, prefix, blocks, gain_one, gain_two, cotangent)
    along = (1, 1, 0, 1)
    x = tokens.reshape(-1, width)
    grad = cotangent.reshape(-1, width)
    tile = TILE_SEQS * span
    block = lax.axis_index("ctx").reshape(1).astype(jnp.int32)
    x_prev = lax.ppermute(x, "ctx", [(i, i + 1) for i in range(count - 1)])
    gain1 = lax.all_gather(gain_one, "ctx", axis=0, tiled=True).astype(F32).reshape(1, width)
    gain2 = lax.all_gather(gain_two, "ctx", axis=0, tiled=True).astype(F32).reshape(1, width)
    wq, wo, wu, wd = (fetch(b, r) for b, r in zip(blocks, along))
    q, k, v, kp, vp, n, n_prev, own_sums = project(x, x_prev, wq, gain1, span)
    own_sums = own_sums.reshape(-1, 2 * width)
    n_sum = jnp.sum(n.reshape(-1, span, width).astype(F32), axis=1).astype(BF16)
    everything = lax.all_gather(jnp.concatenate([own_sums, n_sum], axis=1), "ctx", axis=0, tiled=False)
    everything = jnp.transpose(everything, (1, 0, 2))
    sums, n_sums = everything[:, :, : 2 * width], everything[:, :, 2 * width :]
    mixed, prob, psum = attend(prefix.reshape(-1), block, q, k, v, kp, vp, sums, span)
    out, gm, gr, gout, gup, gdown, ggain2 = feed(x, mixed, grad, wo, wu, wd, gain2, tile)
    gn, gp, gs, gqkv = give_back(q, k, v, kp, vp, sums, gm, prob, psum, n, n_prev, n_sums, wq, span)
    gb = lax.ppermute(gp, "ctx", [(i, i - 1) for i in range(1, count)])
    gs_own = lax.psum_scatter(gs, "ctx", scatter_dimension=1, tiled=True)
    input_grad, ggain1 = close(x, gn, gb, gs_own, gr, gain1, span)
    gains = jnp.concatenate([jnp.sum(ggain1, axis=0), jnp.sum(ggain2, axis=0)]).reshape(2, width)
    gains = lax.psum(gains, "dp")
    gains = lax.psum_scatter(gains, "ctx", scatter_dimension=1, tiled=True)
    sums_w = [reduce_weight(p, r) for p, r in zip((gqkv, gout, gup, gdown), along)]
    return (
        out.reshape(tokens.shape),
        input_grad.reshape(tokens.shape),
        sums_w[0].T,
        sums_w[1].T,
        sums_w[2],
        sums_w[3].T,
        gains[0],
        gains[1],
    )


def solution(mesh):
    rows = P(None, "dp", "ctx", None)
    both = P("dp", "ctx")
    return jax.shard_map(
        shards,
        mesh=mesh,
        in_specs=(rows, P(None, "dp"), both, both, both, both, P("ctx"), P("ctx"), rows),
        out_specs=(rows, rows, both, both, both, both, P("ctx"), P("ctx")),
        check_vma=False,
    )
```

```python
import functools
import math

import jax
import jax.numpy as jnp
from jax import lax
from jax.experimental import pallas as pl
from jax.experimental.pallas import tpu as pltpu
from jax.sharding import PartitionSpec as P

HEADS = 8
EPSILON = 1e-05
MASKED = -1e30
F32 = jnp.float32
BF16 = jnp.bfloat16
TILE_SEQS = 2
CHUNK_TILES = 2
FF_CHUNK = 1024
VMEM_MOST = 60 * 1024 * 1024

MESH = pl.DeviceIdType.MESH
FLIPS = 8


def place():
    depth, spot = lax.axis_index("dp"), lax.axis_index("ctx")
    return depth, spot, (spot % 2, (spot // 2) % 2, spot // 4)


def flipped(bits, flip):
    out = 0
    for i, bit in enumerate(bits):
        out = out + ((1 - bit) if (flip >> i) & 1 else bit) * (1 << i)
    return out


def spot_of(depths, turn, flip):
    depth, _, bits = place()
    return lax.rem(depth + turn, depths), flipped(bits, flip)


def greet(depths):
    barrier = pltpu.get_barrier_semaphore()
    peers = [(turn, 0) for turn in range(1, depths)] + [(0, flip) for flip in range(1, FLIPS)]
    for turn, flip in peers:
        pl.semaphore_signal(barrier, inc=1, device_id=spot_of(depths, turn, flip), device_id_type=MESH)
    pl.semaphore_wait(barrier, len(peers))


class Moves:
    def __init__(self, depths, send, recv):
        self.depths, self.send, self.recv, self.sent = depths, send, recv, 0

    def copy(self, source, target, number, slot, to_turn, to_flip):
        return pltpu.make_async_remote_copy(
            src_ref=source,
            dst_ref=target,
            send_sem=self.send.at[number],
            recv_sem=self.recv.at[slot],
            device_id=spot_of(self.depths, to_turn, to_flip),
            device_id_type=MESH,
        )

    def start(self, source, target, slot, to_turn, to_flip):
        self.copy(source, target, self.sent, slot, to_turn, to_flip).start()
        self.sent += 1

    def landed(self, target, slot):
        self.copy(target, target, 0, slot, 0, 1).wait_recv()

    def drain(self, like):
        for number in range(self.sent):
            self.copy(like, like, number, 0, 0, 1).wait_send()


class Gather(Moves):
    def __init__(self, depths, own, full, send, recv, keep):
        super().__init__(depths, send, recv)
        self.own, self.full, self.keep = own, full, keep

    def block(self, turn, flip):
        return self.full.at[spot_of(self.depths, turn, flip)]

    def push(self, turn, flip, to_turn, to_flip):
        there = ((turn - to_turn) % self.depths) * FLIPS + (flip ^ to_flip)
        source = self.own if (turn, flip) == (0, 0) else self.block(turn, flip)
        self.start(source, self.block(turn, flip), there, to_turn, to_flip)

    def arrive(self, turn, flip):
        self.landed(self.block(turn, flip), turn * FLIPS + flip)

    def begin(self):
        for turn in range(1, self.depths):
            self.push(0, 0, turn, 0)
        for flip in (2, 4, 1):
            self.push(0, 0, 0, flip)
        pltpu.make_async_copy(self.own, self.block(0, 0), self.keep).start()

    def spread(self):
        for turn in range(1, self.depths):
            self.arrive(turn, 0)
            for flip in (2, 4, 1):
                self.push(turn, 0, 0, flip)

    def cross(self, first_turn=0, last_turn=None):
        for turn in range(first_turn, self.depths if last_turn is None else last_turn):
            self.arrive(turn, 2)
            if turn < self.depths // 2:
                self.push(turn, 2, 0, 4)
            self.push(turn, 2, 0, 1)
            self.arrive(turn, 4)
            if turn >= self.depths // 2:
                self.push(turn, 4, 0, 2)
            self.push(turn, 4, 0, 1)

    def hand_over(self):
        for turn in range(self.depths):
            self.arrive(turn, 6)
            self.push(turn, 6, 0, 1)

    def complete(self):
        for turn in range(self.depths):
            for flip in (1, 3, 5, 7):
                self.arrive(turn, flip)
        pltpu.make_async_copy(self.own, self.block(0, 0), self.keep).wait()

    def close(self):
        self.drain(self.own)


class Share(Moves):
    def __init__(self, depths, slots, send, recv):
        super().__init__(depths, send, recv)
        self.slots = slots

    def block(self, flip):
        return self.slots.at[spot_of(self.depths, 0, flip)[1]]

    def begin(self):
        for flip in (2, 4, 6, 1):
            self.start(self.block(0), self.block(0), flip, 0, flip)

    def forward(self):
        for flip in (2, 4, 6):
            self.landed(self.block(flip), flip)
            self.start(self.block(flip), self.block(flip), flip ^ 1, 0, 1)

    def complete(self):
        for flip in (1, 3, 5, 7):
            self.landed(self.block(flip), flip)

    def close(self):
        self.drain(self.block(0))


class Scatter(Moves):
    def __init__(self, depths, part, mate, total, near, far, send, recv):
        super().__init__(depths, send, recv)
        self.part, self.mate, self.total, self.near, self.far = part, mate, total, near, far

    def block(self, turn, flip):
        return self.part.at[spot_of(self.depths, turn, flip)]

    push = Moves.start
    arrive = Moves.landed

    def begin(self, turns):
        for flip in (6, 2, 4, 0):
            for turn in turns:
                at = (flip // 2, turn)
                self.push(self.block(turn, flip ^ 1), self.mate.at[at], flip // 2 * self.depths + turn, 0, 1)

    def fold(self, turn, flip):
        self.arrive(self.mate.at[flip // 2, turn], flip // 2 * self.depths + turn)
        mine = self.block(turn, flip)[...].astype(F32)
        self.total[flip // 2, turn] = (mine + self.mate[flip // 2, turn].astype(F32)).astype(BF16)

    def cross(self, turns):
        base = 4 * self.depths
        for turn in turns:
            self.fold(turn, 6)
            by = 2 if turn < self.depths // 2 else 4
            self.push(self.total.at[3, turn], self.near.at[turn], base + turn, 0, by)

    def spread(self, turns):
        base = 4 * self.depths
        late = 5 * self.depths
        for turn in turns:
            self.fold(turn, 2)
            self.fold(turn, 4)
            via = 2 if turn < self.depths // 2 else 1
            self.arrive(self.near.at[turn], base + turn)
            self.total[via, turn] = (self.total[via, turn].astype(F32) + self.near[turn].astype(F32)).astype(BF16)
            self.push(self.total.at[1, turn], self.far.at[0, turn], late + turn, 0, 2)
            self.push(self.total.at[2, turn], self.far.at[1, turn], late + self.depths + turn, 0, 4)

    def climb(self, turns):
        late = 5 * self.depths
        last = 7 * self.depths
        for turn in turns:
            self.fold(turn, 0)
            self.arrive(self.far.at[0, turn], late + turn)
            self.arrive(self.far.at[1, turn], late + self.depths + turn)
            self.total[0, turn] = (
                self.total[0, turn].astype(F32) + self.far[0, turn].astype(F32) + self.far[1, turn].astype(F32)
            ).astype(BF16)
            if turn:
                back = self.depths - turn
                self.push(self.total.at[0, turn], self.far.at[2, back], last + back, turn, 0)

    def finish(self):
        last = 7 * self.depths
        out = self.total[0, 0].astype(F32)
        for turn in range(1, self.depths):
            self.arrive(self.far.at[2, turn], last + turn)
            out = out + self.far[2, turn].astype(F32)
        return out

    def close(self):
        self.drain(self.near.at[0])


def scatter_scratch(block, depths):
    return [
        pltpu.VMEM((4, depths) + block, BF16),
        pltpu.VMEM((4, depths) + block, BF16),
        pltpu.VMEM((depths,) + block, BF16),
        pltpu.VMEM((3, depths) + block, BF16),
    ]


def dot(a, b):
    return jnp.dot(a, b, preferred_element_type=F32)


def dot_t(a, b):
    return lax.dot_general(a, b, (((1,), (1,)), ((), ())), preferred_element_type=F32)


def standardize(values):
    row_mean = jnp.mean(values, axis=-1, keepdims=True)
    centred = values - row_mean
    variance = jnp.mean(centred * centred, axis=-1, keepdims=True)
    inv_std = lax.rsqrt(variance + EPSILON)
    return (centred * inv_std, inv_std)


def norm_back(grad_in, unit_rows, inv_std, gain):
    scaled = grad_in * gain
    row_mean = jnp.mean(scaled, axis=-1, keepdims=True)
    cross_mean = jnp.mean(scaled * unit_rows, axis=-1, keepdims=True)
    return inv_std * (scaled - row_mean - unit_rows * cross_mean)


def fold_rows(values):
    return jnp.sum(values.reshape(-1, 8, values.shape[-1]), axis=0)


def gelu_parts(upper):
    cdf = 0.5 * (1.0 + lax.erf(upper * 0.7071067811865476))
    slope = cdf + upper * jnp.exp(-0.5 * upper * upper) * 0.3989422804014327
    return (upper * cdf, slope)


def pair_halves(rows):
    lanes = lax.broadcasted_iota(jnp.int32, rows.shape, 1)
    half = rows.shape[1] // 2
    zero = jnp.zeros_like(rows)
    return jnp.concatenate(
        [jnp.where(lanes < half, rows, zero), jnp.where(lanes >= half, rows, zero)], axis=0
    )


def head_select(count, width):
    head_of_row = lax.broadcasted_iota(jnp.int32, (HEADS * count, width), 0) // count
    head_of_lane = lax.broadcasted_iota(jnp.int32, (HEADS * count, width), 1) // (width // HEADS)
    return head_of_row == head_of_lane


def per_head(rows, select):
    tiled = jnp.concatenate([rows.astype(F32)] * HEADS, axis=0)
    return jnp.where(select, tiled, 0.0).astype(BF16)


def rows_of(ref):
    depths, lanes = ref.shape[0], ref.shape[3]
    return jnp.concatenate([ref[d].reshape(-1, lanes) for d in range(depths)], axis=1)


def lanes_of(ref, chunk, along):
    lanes = ref.shape[3]
    take = (lambda i: ref[i]) if along == 0 else (lambda i: ref[:, i])
    if lanes >= FF_CHUNK:
        per = lanes // FF_CHUNK
        cut = slice(chunk % per * FF_CHUNK, (chunk % per + 1) * FF_CHUNK)
        return take(chunk // per).reshape(-1, lanes)[:, cut]
    per = FF_CHUNK // lanes
    return jnp.concatenate([take(i).reshape(-1, lanes) for i in range(chunk * per, (chunk + 1) * per)], axis=1)


def put_blocks(ref, values, rows_along):
    depths, spots, rows, lanes = ref.shape
    for d in range(depths):
        for c in range(spots):
            r, l = (c, d) if rows_along == 1 else (d, c)
            ref[d, c] = values[r * rows : (r + 1) * rows, l * lanes : (l + 1) * lanes].astype(ref.dtype)


def project_kernel(x_ref, xp_ref, w_ref, gain_ref, q_ref, k_ref, v_ref, kp_ref, vp_ref, n_ref, np_ref, sum_ref):
    width = x_ref.shape[1]
    gain = gain_ref[...]
    weight = rows_of(w_ref)
    normed = (standardize(x_ref[...].astype(F32))[0] * gain).astype(BF16)
    n_ref[...] = normed
    scale = (width // HEADS) ** -0.5
    q_ref[...] = (dot_t(normed, weight[:width]).astype(BF16).astype(F32) * scale).astype(BF16)
    for part, out in ((1, k_ref), (2, v_ref)):
        rows = dot_t(normed, weight[part * width : (part + 1) * width]).astype(BF16)
        out[...] = rows
        means = jnp.mean(rows.astype(F32).reshape(TILE_SEQS, -1, width), axis=1)
        sum_ref[0, :, (part - 1) * width : part * width] = means.astype(BF16)
    normed_prev = (standardize(xp_ref[...].astype(F32))[0] * gain).astype(BF16)
    np_ref[...] = normed_prev
    kp_ref[...] = dot_t(normed_prev, weight[width : 2 * width]).astype(BF16)
    vp_ref[...] = dot_t(normed_prev, weight[2 * width :]).astype(BF16)


def row_spec(rows, width):
    return pl.BlockSpec((rows, width), lambda i: (i, 0))


def whole_spec(shape):
    return pl.BlockSpec(shape, lambda i: (0,) * len(shape))


def params():
    return pltpu.CompilerParams(vmem_limit_bytes=VMEM_MOST)


def project(x, x_prev, w_qkv, gain, span):
    rows, width = x.shape
    tile = TILE_SEQS * span
    low = jax.ShapeDtypeStruct((rows, width), BF16)
    return pl.pallas_call(
        project_kernel,
        grid=(rows // tile,),
        in_specs=[row_spec(tile, width)] * 2 + [whole_spec(w_qkv.shape), whole_spec(gain.shape)],
        out_specs=[row_spec(tile, width)] * 7
        + [pl.BlockSpec((1, TILE_SEQS, 2 * width), lambda i: (i, 0, 0))],
        out_shape=[low] * 7 + [jax.ShapeDtypeStruct((rows // tile, TILE_SEQS, 2 * width), BF16)],
        compiler_params=params(),
        name="project",
    )(x, x_prev, w_qkv, gain)


def attend_one(span, block, prefix, queries, keys, values, sums, keep_prob):
    width = queries.shape[1]
    pair = 2 * width // HEADS
    half = pair // 2
    count = sums.shape[0]
    select = head_select(count, width)
    unit_pos = lax.broadcasted_iota(jnp.int32, (span, span), 0)
    query_pos = lax.broadcasted_iota(jnp.int32, (span, span), 1)
    sum_id = lax.broadcasted_iota(jnp.int32, (count, span), 0)
    sum_query = lax.broadcasted_iota(jnp.int32, (count, span), 1)
    bias_prev = jnp.where(block >= 1, 0.0, MASKED).astype(F32)
    start = block * span
    own_ok = (unit_pos <= query_pos) | (start + unit_pos < prefix)
    bias_own = jnp.where(own_ok, 0.0, MASKED)
    sum_ok = (sum_id <= block - 1) | (
        (start + sum_query < prefix) & (sum_id >= block + 1) & ((sum_id + 1) * span <= prefix)
    )
    bias_sum = jnp.where(sum_ok, math.log(span), MASKED)
    values_t = values.T
    sum_keys = per_head(sums[:, :width], select)
    sum_values_t = per_head(sums[:, width : 2 * width], select).T
    sum_scores = dot_t(sum_keys, queries)
    mixed_parts = []
    sum_probs = []
    for p in range(HEADS // 2):
        lanes = slice(p * pair, (p + 1) * pair)
        scores = dot_t(keys[:, lanes], pair_halves(queries[:, lanes]))
        probs = []
        for e in range(2):
            h = 2 * p + e
            cols = slice(e * span, (e + 1) * span)
            s_prev = scores[:span, cols]
            s_own = scores[span:, cols] + bias_own
            s_sum = sum_scores[h * count : (h + 1) * count] + bias_sum
            most = jnp.maximum(
                jnp.maximum(
                    jnp.max(s_prev, axis=0, keepdims=True) + bias_prev,
                    jnp.max(s_own, axis=0, keepdims=True),
                ),
                jnp.max(s_sum, axis=0, keepdims=True),
            )
            e_prev = jnp.exp(s_prev + (bias_prev - most))
            e_own = jnp.exp(s_own - most)
            e_sum = jnp.exp(s_sum - most)
            total = (
                jnp.sum(e_prev, axis=0, keepdims=True)
                + jnp.sum(e_own, axis=0, keepdims=True)
                + jnp.sum(e_sum, axis=0, keepdims=True)
            )
            inverse = 1.0 / total
            probs.append(jnp.concatenate([e_prev * inverse, e_own * inverse], axis=0).astype(BF16))
            sum_probs.append(e_sum * inverse)
        both = jnp.concatenate(probs, axis=1)
        keep_prob(p, both)
        crossed = dot(values_t[lanes, :], both)
        mixed_parts.append(crossed[:half, :span])
        mixed_parts.append(crossed[half:, span:])
    all_sums = jnp.concatenate(sum_probs, axis=0).astype(BF16)
    mixed_t = jnp.concatenate(mixed_parts, axis=0) + dot(sum_values_t, all_sums)
    return mixed_t.T.astype(BF16), all_sums


def attend_kernel(
    span, prefix_ref, block_ref, q_ref, k_ref, v_ref, kp_ref, vp_ref, sums_ref, mixed_ref, prob_ref, psum_ref
):
    for s in range(TILE_SEQS):
        rows = slice(s * span, (s + 1) * span)

        def keep_prob(p, both, s=s):
            prob_ref[s, p] = both

        mixed, all_sums = attend_one(
            span,
            block_ref[0],
            prefix_ref[pl.program_id(0) * TILE_SEQS + s],
            q_ref[rows, :],
            jnp.concatenate([kp_ref[rows, :], k_ref[rows, :]], axis=0),
            jnp.concatenate([vp_ref[rows, :], v_ref[rows, :]], axis=0),
            sums_ref[s],
            keep_prob,
        )
        mixed_ref[rows, :] = mixed
        psum_ref[s] = all_sums


def attend(prefix, block, q, k, v, kp, vp, sums, span):
    rows, width = q.shape
    tile = TILE_SEQS * span
    seqs, count = sums.shape[0], sums.shape[1]
    pairs = HEADS // 2
    return pl.pallas_call(
        functools.partial(attend_kernel, span),
        grid=(rows // tile,),
        in_specs=[pl.BlockSpec(memory_space=pltpu.SMEM)] * 2
        + [row_spec(tile, width)] * 5
        + [pl.BlockSpec((TILE_SEQS, count, 2 * width), lambda i: (i, 0, 0))],
        out_specs=[
            row_spec(tile, width),
            pl.BlockSpec((TILE_SEQS, pairs, 2 * span, 2 * span), lambda i: (i, 0, 0, 0)),
            pl.BlockSpec((TILE_SEQS, HEADS * count, span), lambda i: (i, 0, 0)),
        ],
        out_shape=[
            jax.ShapeDtypeStruct((rows, width), BF16),
            jax.ShapeDtypeStruct((seqs, pairs, 2 * span, 2 * span), BF16),
            jax.ShapeDtypeStruct((seqs, HEADS * count, span), BF16),
        ],
        compiler_params=params(),
        name="attend",
    )(prefix, block, q, k, v, kp, vp, sums)


def feed_kernel(
    x_ref, mixed_ref, g_ref, wo_ref, wu_ref, wd_ref, gain_ref,
    out_ref, gm_ref, gr_ref, gout_ref, gup_ref, gdown_ref, ggain_ref,
    acc_out, acc_up, acc_down, acc_gain,
):
    step = pl.program_id(0)

    @pl.when(step == 0)
    def _():
        acc_out[...] = jnp.zeros_like(acc_out)
        acc_up[...] = jnp.zeros_like(acc_up)
        acc_down[...] = jnp.zeros_like(acc_down)
        acc_gain[...] = jnp.zeros_like(acc_gain)

    gain = gain_ref[gain_ref.shape[0] - 1 :, :]
    mixed = mixed_ref[...]
    w_out = rows_of(wo_ref)
    resid = x_ref[...].astype(F32) + dot_t(mixed, w_out)
    unit, inv = standardize(resid)
    normed = (unit * gain).astype(BF16)
    normed_t = normed.T
    grad = g_ref[...]
    grad_t = grad.T
    hidden_width = acc_up.shape[1]
    result = resid
    grad_norm = None
    for c in range(hidden_width // FF_CHUNK):
        cols = slice(c * FF_CHUNK, (c + 1) * FF_CHUNK)
        w_up = lanes_of(wu_ref, c, 1)
        w_down = lanes_of(wd_ref, c, 0)
        upper = dot(normed, w_up)
        grad_hidden = dot(grad, w_down)
        activated, slope = gelu_parts(upper)
        hidden = activated.astype(BF16)
        grad_upper = (grad_hidden * slope).astype(BF16)
        result = result + dot_t(hidden, w_down)
        back = dot_t(grad_upper, w_up)
        grad_norm = back if grad_norm is None else grad_norm + back
        acc_down[:, cols] += dot(grad_t, hidden)
        acc_up[:, cols] += dot(normed_t, grad_upper)
    out_ref[...] = result.astype(BF16)
    acc_gain[...] += fold_rows(grad_norm * unit)
    grad_resid = grad.astype(F32) + norm_back(grad_norm, unit, inv, gain)
    gr_ref[...] = grad_resid
    grad_branch = grad_resid.astype(BF16)
    acc_out[...] += dot(grad_branch.T, mixed)
    gm_ref[...] = dot(grad_branch, w_out).astype(BF16)

    @pl.when(step == pl.num_programs(0) - 1)
    def _():
        put_blocks(gout_ref, acc_out, 1)
        put_blocks(gup_ref, acc_up, 0)
        put_blocks(gdown_ref, acc_down, 1)
        ggain_ref[...] = acc_gain[...]


def feed(x, mixed, grad, w_out, w_up, w_down, gain, tile):
    rows, width = x.shape
    hidden = w_up.shape[1] * w_up.shape[3]
    wide = (width, hidden)
    square = (width, width)
    return pl.pallas_call(
        feed_kernel,
        grid=(rows // tile,),
        in_specs=[row_spec(tile, width)] * 3
        + [whole_spec(w_out.shape), whole_spec(w_up.shape), whole_spec(w_down.shape), whole_spec(gain.shape)],
        out_specs=[row_spec(tile, width)] * 3
        + [whole_spec(w_out.shape), whole_spec(w_up.shape), whole_spec(w_down.shape), whole_spec((8, width))],
        out_shape=[
            jax.ShapeDtypeStruct((rows, width), BF16),
            jax.ShapeDtypeStruct((rows, width), BF16),
            jax.ShapeDtypeStruct((rows, width), F32),
            jax.ShapeDtypeStruct(w_out.shape, BF16),
            jax.ShapeDtypeStruct(w_up.shape, BF16),
            jax.ShapeDtypeStruct(w_down.shape, BF16),
            jax.ShapeDtypeStruct((8, width), F32),
        ],
        scratch_shapes=[
            pltpu.VMEM(square, F32),
            pltpu.VMEM(wide, F32),
            pltpu.VMEM(wide, F32),
            pltpu.VMEM((8, width), F32),
        ],
        compiler_params=params(),
        name="feed",
    )(x, mixed, grad, w_out, w_up, w_down, gain)


def return_one(span, queries, keys, values, sums, grad_mixed, prob_at, sum_low):
    width = queries.shape[1]
    pair = 2 * width // HEADS
    half = pair // 2
    count = sums.shape[0]
    scale = half ** -0.5
    select = head_select(count, width)
    keys_t = keys.T
    sum_keys_t = per_head(sums[:, :width], select).T
    sum_values = per_head(sums[:, width : 2 * width], select)
    sum_prob = sum_low.astype(F32)
    sum_moved = sum_prob * dot_t(sum_values, grad_mixed)
    grad_q_parts = []
    grad_k_parts = []
    grad_v_parts = []
    sum_grads = []
    for p in range(HEADS // 2):
        lanes = slice(p * pair, (p + 1) * pair)
        grads2 = pair_halves(grad_mixed[:, lanes])
        grad_prob = dot_t(values[:, lanes], grads2)
        low = prob_at(p)
        prob = low.astype(F32)
        moved = prob * grad_prob
        deltas = jnp.sum(moved, axis=0, keepdims=True)
        sums_of = []
        for e in range(2):
            h = 2 * p + e
            part = slice(h * count, (h + 1) * count)
            delta = deltas[:, e * span : (e + 1) * span] + jnp.sum(sum_moved[part], axis=0, keepdims=True)
            sums_of.append(delta)
            sum_grads.append(sum_moved[part] - sum_prob[part] * delta)
        grad_scores = (moved - prob * jnp.concatenate(sums_of, axis=1)).astype(BF16)
        grad_k_parts.append(dot(grad_scores, pair_halves(queries[:, lanes])))
        grad_v_parts.append(dot(low, grads2))
        crossed = dot(keys_t[lanes, :], grad_scores)
        grad_q_parts.append(crossed[:half, :span])
        grad_q_parts.append(crossed[half:, span:])
    sum_scores_grad = jnp.concatenate(sum_grads, axis=0).astype(BF16)
    grad_q = jnp.concatenate(grad_q_parts, axis=0) + dot(sum_keys_t, sum_scores_grad)
    grad_q = (grad_q.T * scale).astype(BF16)
    grad_k = jnp.concatenate(grad_k_parts, axis=1).astype(BF16)
    grad_v = jnp.concatenate(grad_v_parts, axis=1).astype(BF16)
    wide_k = jnp.where(select, dot(sum_scores_grad, queries), 0.0)
    wide_v = jnp.where(select, dot(sum_low, grad_mixed), 0.0)
    folded_k = jnp.sum(wide_k.reshape(HEADS, count, width), axis=0)
    folded_v = jnp.sum(wide_v.reshape(HEADS, count, width), axis=0)
    return (
        jnp.concatenate([grad_q, grad_k[span:], grad_v[span:]], axis=1),
        jnp.concatenate([grad_k[:span], grad_v[:span]], axis=1),
        jnp.concatenate([folded_k, folded_v], axis=1) * (1.0 / span),
    )


def return_tile(weight, own, before, shared, normed, normed_prev, normed_sum, acc):
    width = normed.shape[1]
    grad_own = jnp.concatenate(own, axis=0)
    grad_before = jnp.concatenate(before, axis=0)
    grad_shared = jnp.concatenate(shared, axis=0).astype(BF16)
    normed_t = normed.T
    acc[:, :width] += dot(normed_t, grad_own[:, :width])
    acc[:, width:] += (
        dot(normed_t, grad_own[:, width:]) + dot(normed_prev.T, grad_before) + dot(normed_sum.T, grad_shared)
    )
    return grad_own, dot(grad_before, weight[width:]), dot(grad_shared, weight[width:])


def return_kernel(
    span, q_ref, k_ref, v_ref, kp_ref, vp_ref, sums_ref, gm_ref, prob_ref, psum_ref, n_ref, np_ref, nsum_ref, w_ref,
    gn_ref, gp_ref, gs_ref, gqkv_ref, acc,
):
    step = pl.program_id(0)

    @pl.when(step == 0)
    def _():
        acc[...] = jnp.zeros_like(acc)

    parts = []
    for s in range(TILE_SEQS):
        rows = slice(s * span, (s + 1) * span)
        parts.append(
            return_one(
                span,
                q_ref[rows, :],
                jnp.concatenate([kp_ref[rows, :], k_ref[rows, :]], axis=0),
                jnp.concatenate([vp_ref[rows, :], v_ref[rows, :]], axis=0),
                sums_ref[s],
                gm_ref[rows, :],
                lambda p, s=s: prob_ref[s, p],
                psum_ref[s],
            )
        )
    normed_sum = nsum_ref[...].reshape(-1, nsum_ref.shape[2])
    weight = rows_of(w_ref)
    grad_own, gp, gs = return_tile(weight, *zip(*parts), n_ref[...], np_ref[...], normed_sum, acc)
    gn_ref[...] = dot(grad_own, weight)
    gp_ref[...] = gp.astype(BF16)
    gs_ref[...] = gs.reshape(gs_ref.shape).astype(BF16)

    @pl.when(step == pl.num_programs(0) - 1)
    def _():
        put_blocks(gqkv_ref, acc[...].astype(BF16).T, 1)


def give_back(q, k, v, kp, vp, sums, gm, prob, psum, n, n_prev, n_sum, w_qkv, span):
    rows, width = q.shape
    tile = TILE_SEQS * span
    seqs, count = sums.shape[0], sums.shape[1]
    pairs = HEADS // 2
    return pl.pallas_call(
        functools.partial(return_kernel, span),
        grid=(rows // tile,),
        in_specs=[row_spec(tile, width)] * 5
        + [
            pl.BlockSpec((TILE_SEQS, count, 2 * width), lambda i: (i, 0, 0)),
            row_spec(tile, width),
            pl.BlockSpec((TILE_SEQS, pairs, 2 * span, 2 * span), lambda i: (i, 0, 0, 0)),
            pl.BlockSpec((TILE_SEQS, HEADS * count, span), lambda i: (i, 0, 0)),
            row_spec(tile, width),
            row_spec(tile, width),
            pl.BlockSpec((TILE_SEQS, count, width), lambda i: (i, 0, 0)),
            whole_spec(w_qkv.shape),
        ],
        out_specs=[
            row_spec(tile, width),
            row_spec(tile, width),
            pl.BlockSpec((TILE_SEQS, count, width), lambda i: (i, 0, 0)),
            whole_spec(w_qkv.shape),
        ],
        out_shape=[
            jax.ShapeDtypeStruct((rows, width), F32),
            jax.ShapeDtypeStruct((rows, width), BF16),
            jax.ShapeDtypeStruct((seqs, count, width), BF16),
            jax.ShapeDtypeStruct(w_qkv.shape, BF16),
        ],
        scratch_shapes=[pltpu.VMEM((width, 3 * width), F32)],
        compiler_params=params(),
        name="give_back",
    )(q, k, v, kp, vp, sums, gm, prob, psum, n, n_prev, n_sum, w_qkv)


def close_kernel(span, x_ref, gn_ref, gb_ref, gs_ref, gr_ref, gain_ref, out_ref, ggain_ref, acc):
    step = pl.program_id(0)
    width = x_ref.shape[1]

    @pl.when(step == 0)
    def _():
        acc[...] = jnp.zeros_like(acc)

    unit, inv = standardize(x_ref[...].astype(F32))
    grad_norm = gn_ref[...] + gb_ref[...].astype(F32)
    lifted = [
        grad_norm[s * span : (s + 1) * span] + gs_ref[s].astype(F32) for s in range(TILE_SEQS)
    ]
    grad_norm = jnp.concatenate(lifted, axis=0)
    acc[...] += fold_rows(grad_norm * unit)
    part = norm_back(grad_norm, unit, inv, gain_ref[...])
    out_ref[...] = (gr_ref[...] + part).astype(BF16)

    @pl.when(step == pl.num_programs(0) - 1)
    def _():
        ggain_ref[...] = acc[...]


def close(x, gn, gb, gs, gr, gain, span):
    rows, width = x.shape
    tile = TILE_SEQS * span
    return pl.pallas_call(
        functools.partial(close_kernel, span),
        grid=(rows // tile,),
        in_specs=[row_spec(tile, width)] * 3
        + [pl.BlockSpec((TILE_SEQS, 1, width), lambda i: (i, 0, 0)), row_spec(tile, width), whole_spec(gain.shape)],
        out_specs=[row_spec(tile, width), whole_spec((8, width))],
        out_shape=[jax.ShapeDtypeStruct((rows, width), BF16), jax.ShapeDtypeStruct((8, width), F32)],
        scratch_shapes=[pltpu.VMEM((8, width), F32)],
        compiler_params=params(),
        name="close",
    )(x, gn, gb, gs, gr, gain)


def in_order(count, seqs):
    row = lax.broadcasted_iota(jnp.int32, (count * seqs, count * seqs), 0)
    col = lax.broadcasted_iota(jnp.int32, (count * seqs, count * seqs), 1)
    return ((col % seqs == row // count) & (col // seqs == row % count)).astype(BF16)


def neighbour(by):
    depth, spot = lax.axis_index("dp"), lax.axis_index("ctx")
    return depth, lax.rem(spot + by + FLIPS, FLIPS)


ENTER_RELAYS = {
    1: ((1, "spread"), (2, "spread"), (3, "spread")),
    4: ((1, "cross"), (2, "cross")),
    5: ((3, "cross"),),
    7: ((1, "hand_over"), (2, "hand_over"), (3, "hand_over")),
}


def enter_kernel(
    depths, span,
    x_in, prefix_ref, bq_ref, bo_ref, bu_ref, bd_ref, one_ref, two_ref,
    wq_out, wo_out, wu_out, wd_out, gain_out, q_out, k_out, v_out, kp_out, vp_out, n_out, np_out, mixed_out, prob_out,
    sums_out, psum_out,
    x_ref, xp, wq, gains, q, k, v, kp, vp, n, n_prev, mixed, prob, slots,
    send, recv, keep, gain_send, gain_recv, sum_send, sum_recv, tok_send, tok_recv, out_sem, prob_sem, wq_sem, x_sem,
):
    x_copy = pltpu.make_async_copy(x_in, x_ref, x_sem.at[0])
    x_copy.start()
    rows, width = x_ref.shape
    tile = TILE_SEQS * span
    tiles = rows // tile
    chunks = tiles // CHUNK_TILES
    seqs = rows // span
    spot = lax.axis_index("ctx")
    scale = (width // HEADS) ** -0.5
    gathers = [
        Gather(depths, own, full, send.at[a], recv.at[a], keep.at[a])
        for a, (own, full) in enumerate(((bq_ref, wq), (bo_ref, wo_out), (bu_ref, wu_out), (bd_ref, wd_out)))
    ]
    gain_share = Share(depths, gains, gain_send, gain_recv)
    sum_share = Share(depths, slots, sum_send, sum_recv)
    shard = jnp.concatenate([one_ref[...].reshape(1, -1), two_ref[...].reshape(1, -1)], axis=0).astype(F32)
    owner = lax.broadcasted_iota(jnp.int32, (2, width), 1) // shard.shape[1]
    gains[spot] = jnp.where(owner == spot, jnp.concatenate([shard] * FLIPS, axis=1), 0.0)

    @pl.when(spot == 0)
    def _():
        xp[...] = jnp.zeros_like(xp)

    def at(i):
        return pl.ds(pl.multiple_of(i * tile, tile), tile)

    def chunk_at(c):
        return pl.ds(pl.multiple_of(c * CHUNK_TILES * tile, CHUNK_TILES * tile), CHUNK_TILES * tile)

    def token_copy(i):
        return pltpu.make_async_remote_copy(
            src_ref=x_ref.at[at(i)],
            dst_ref=xp.at[at(i)],
            send_sem=tok_send.at[i],
            recv_sem=tok_recv.at[i],
            device_id=neighbour(1),
            device_id_type=MESH,
        )

    def out_copy(a, i):
        pairs = ((q, q_out), (k, k_out), (v, v_out), (n, n_out), (kp, kp_out), (vp, vp_out), (n_prev, np_out), (mixed, mixed_out))
        return pltpu.make_async_copy(pairs[a][0].at[at(i)], pairs[a][1].at[at(i)], out_sem.at[a, i])

    def prob_copy(i):
        part = pl.ds(i * TILE_SEQS, TILE_SEQS)
        return pltpu.make_async_copy(prob.at[part], prob_out.at[part], prob_sem.at[i])

    def send_tokens(first, last):
        @pl.when(spot < FLIPS - 1)
        def _():
            for i in range(first, last):
                token_copy(i).start()

    greet(depths)
    gathers[0].begin()
    gain_share.begin()
    x_copy.wait()
    send_tokens(0, 2)
    gain_share.forward()
    gain_share.complete()
    gain = gains[0]
    for c in range(1, FLIPS):
        gain = gain + gains[c]
    gain_out[...] = gain

    def normalize(c):
        n[chunk_at(c), :] = (standardize(x_ref[chunk_at(c), :].astype(F32))[0] * gain[0:1]).astype(BF16)

    def keep_mean(part, ref, weigh):
        means = [
            jnp.sum(ref[s * span : (s + 1) * span, :].astype(F32), axis=0, keepdims=True) * weigh for s in range(seqs)
        ]
        slots[spot, :, part * width : (part + 1) * width] = jnp.concatenate(means, axis=0).astype(BF16)

    pl.loop(0, chunks // 2)(normalize)
    gathers[0].cross(0, 1)
    gathers[0].spread()
    pl.loop(chunks // 2, chunks)(normalize)
    gathers[0].cross(1)
    keep_mean(2, n, 1.0)
    gathers[0].hand_over()
    send_tokens(2, 5)
    gathers[0].complete()
    wq_copy = pltpu.make_async_copy(wq, wq_out, wq_sem.at[0])
    wq_copy.start()

    def send_out(a, c):
        for t in range(CHUNK_TILES):
            out_copy(a, c * CHUNK_TILES + t).start()

    @pl.loop(0, chunks)
    def _(c):
        weight = rows_of(wq)
        normed = n[chunk_at(c), :]
        k[chunk_at(c), :] = dot_t(normed, weight[width : 2 * width]).astype(BF16)
        v[chunk_at(c), :] = dot_t(normed, weight[2 * width :]).astype(BF16)
        for a in (1, 2, 3):
            send_out(a, c)

    keep_mean(0, k, 1.0 / span)
    keep_mean(1, v, 1.0 / span)
    sum_share.begin()
    send_tokens(5, tiles)
    for gather in gathers[1:]:
        gather.begin()

    @pl.loop(0, chunks)
    def _(c):
        weight = rows_of(wq)
        rows_q = dot_t(n[chunk_at(c), :], weight[:width]).astype(BF16)
        q[chunk_at(c), :] = (rows_q.astype(F32) * scale).astype(BF16)
        send_out(0, c)

    def project_prev(c):
        @pl.when(spot > 0)
        def _():
            for t in range(CHUNK_TILES):
                token_copy(c * CHUNK_TILES + t).wait_recv()

        weight = rows_of(wq)
        normed = (standardize(xp[chunk_at(c), :].astype(F32))[0] * gain[0:1]).astype(BF16)
        n_prev[chunk_at(c), :] = normed
        kp[chunk_at(c), :] = dot_t(normed, weight[width : 2 * width]).astype(BF16)
        vp[chunk_at(c), :] = dot_t(normed, weight[2 * width :]).astype(BF16)
        for a in (4, 5, 6):
            send_out(a, c)

    project_prev(0)
    sum_share.forward()
    project_prev(1)
    sum_share.complete()
    ordered = dot(in_order(FLIPS, seqs), slots[...].reshape(FLIPS * seqs, 3 * width)).astype(BF16)
    sums_out[...] = ordered.reshape(sums_out.shape)
    @pl.loop(0, tiles)
    def _(i):
        @pl.when((lax.rem(i, CHUNK_TILES) == 0) & (i >= 2 * CHUNK_TILES))
        def _():
            project_prev(i // CHUNK_TILES)

        for s in range(TILE_SEQS):
            here = pl.ds(pl.multiple_of(i * tile + s * span, span), span)
            seq = i * TILE_SEQS + s

            def keep_prob(p, both, seq=seq):
                prob[seq, p] = both

            rows_mixed, all_sums = attend_one(
                span,
                spot,
                prefix_ref[seq // prefix_ref.shape[1], lax.rem(seq, prefix_ref.shape[1])],
                q[here, :],
                jnp.concatenate([kp[here, :], k[here, :]], axis=0),
                jnp.concatenate([vp[here, :], v[here, :]], axis=0),
                sums_out[seq],
                keep_prob,
            )
            mixed[here, :] = rows_mixed
            psum_out[seq] = all_sums
        out_copy(7, i).start()
        prob_copy(i).start()
        for when, relays in ENTER_RELAYS.items():

            @pl.when(i == when)
            def _(relays=relays):
                for a, name in relays:
                    getattr(gathers[a], name)()

    for gather in gathers[1:]:
        gather.complete()
    for move in (*gathers, gain_share, sum_share):
        move.close()

    @pl.when(spot < FLIPS - 1)
    def _():
        for i in range(tiles):
            token_copy(i).wait_send()

    wq_copy.wait()

    @pl.loop(0, tiles)
    def _(i):
        for a in range(8):
            out_copy(a, i).wait()
        prob_copy(i).wait()


def enter(x, prefix, blocks, gain_one, gain_two, span, depths):
    rows, width = x.shape
    tile = TILE_SEQS * span
    tiles, seqs = rows // tile, rows // span
    low = jax.ShapeDtypeStruct((rows, width), BF16)
    fulls = [jax.ShapeDtypeStruct((depths, FLIPS) + b.shape, BF16) for b in blocks]
    prob_shape = (seqs, HEADS // 2, 2 * span, 2 * span)
    vmem = pl.BlockSpec(memory_space=pltpu.VMEM)
    far = pl.BlockSpec(memory_space=pl.ANY)
    sems = pltpu.SemaphoreType.DMA
    held = pltpu.VMEM((rows, width), BF16)
    return pl.pallas_call(
        functools.partial(enter_kernel, depths, span),
        in_specs=[far, pl.BlockSpec(memory_space=pltpu.SMEM)] + [vmem] * 6,
        out_specs=[far] * 4 + [vmem] + [far] * 9 + [vmem] * 2,
        out_shape=fulls
        + [jax.ShapeDtypeStruct((2, width), F32)]
        + [low] * 8
        + [
            jax.ShapeDtypeStruct(prob_shape, BF16),
            jax.ShapeDtypeStruct((seqs, FLIPS, 3 * width), BF16),
            jax.ShapeDtypeStruct((seqs, HEADS * FLIPS, span), BF16),
        ],
        scratch_shapes=[
            held,
            held,
            pltpu.VMEM(fulls[0].shape, BF16),
            pltpu.VMEM((FLIPS, 2, width), F32),
        ]
        + [held] * 8
        + [pltpu.VMEM(prob_shape, BF16), pltpu.VMEM((FLIPS, seqs, 3 * width), BF16)]
        + [
            sems((4, depths * FLIPS)), sems((4, depths * FLIPS)), sems((4,)),
            sems((FLIPS,)), sems((FLIPS,)), sems((FLIPS,)), sems((FLIPS,)),
            sems((tiles,)), sems((tiles,)), sems((8, tiles)), sems((tiles,)), sems((1,)), sems((1,)),
        ],
        compiler_params=pltpu.CompilerParams(collective_id=0, has_side_effects=True, vmem_limit_bytes=VMEM_MOST),
        name="enter",
    )(x, prefix, *blocks, gain_one, gain_two)


LEAVE_RELAYS = {
    0: ((0, "cross"),),
    1: ((1, "cross"), (2, "cross")),
    3: ((0, "spread"), (1, "spread")),
    5: ((2, "spread"),),
    6: ((0, "climb"), (1, "climb")),
}


def leave_kernel(
    depths, span,
    q_in, k_in, v_in, kp_in, vp_in, gm_in, n_in, np_in, prob_in, gr_in, x_in,
    psum_in, sums_in, wq_in, gout_in, gup_in, gdown_in, gain_ref, ggain_ref,
    ig_out, dqkv_out, dout_out, dup_out, ddown_out, dgain_out,
    psum_ref, sums_ref, wq_ref, gout_ref, gup_ref, gdown_ref, held, prob, kept, before, shared_rows, turned, turned_prev, turned_sum, one_sum, gp, gb, gr, x, ig, part, gs_send_buf, gs_slots, gain_slots, gain_deep,
    *rest,
):
    moves_refs, sems = rest[:16], rest[16:]
    send, recv, gs_send, gs_recv, gain_send, gain_recv, deep_send, deep_recv, gb_send, gb_recv, in_sem, late_sem, ig_sem, whole_sem = sems
    inputs = (gout_in, gup_in, gdown_in, psum_in, sums_in, wq_in)
    landing = (gout_ref, gup_ref, gdown_ref, psum_ref, sums_ref, wq_ref)
    wholes = [pltpu.make_async_copy(a, b, whole_sem.at[n]) for n, (a, b) in enumerate(zip(inputs, landing))]
    for copy in wholes:
        copy.start()
    rows, width = gp.shape
    tile = TILE_SEQS * span
    tiles = rows // tile
    seqs = rows // span
    spot = lax.axis_index("ctx")
    parts = (gout_ref, gup_ref, gdown_ref, part)
    scatters = [
        Scatter(depths, parts[a], *moves_refs[4 * a : 4 * a + 4], send.at[a], recv.at[a]) for a in range(4)
    ]
    gain_share = Share(depths, gain_slots, gain_send, gain_recv)
    gs_moves = Moves(depths, gs_send, gs_recv)
    deep_moves = Moves(depths, deep_send, deep_recv)

    def at(i):
        return pl.ds(pl.multiple_of(i * tile, tile), tile)

    def at_sums(i):
        return pl.ds(pl.multiple_of(i * TILE_SEQS * FLIPS, TILE_SEQS * FLIPS), TILE_SEQS * FLIPS)

    def loads(i, slot):
        arrays = (q_in, k_in, v_in, kp_in, vp_in, gm_in, n_in, np_in)
        copies = [pltpu.make_async_copy(ref.at[at(i)], held.at[slot, a], in_sem.at[slot, a]) for a, ref in enumerate(arrays)]
        of_tile = pl.ds(i * TILE_SEQS, TILE_SEQS)
        return copies + [pltpu.make_async_copy(prob_in.at[of_tile], prob.at[slot], in_sem.at[slot, len(arrays)])]

    def gb_copy(i):
        return pltpu.make_async_remote_copy(
            src_ref=gp.at[at(i)],
            dst_ref=gb.at[at(i)],
            send_sem=gb_send.at[i],
            recv_sem=gb_recv.at[i],
            device_id=neighbour(-1),
            device_id_type=MESH,
        )

    for copy in loads(0, 0):
        copy.start()
    late = [pltpu.make_async_copy(gr_in, gr, late_sem.at[0]), pltpu.make_async_copy(x_in, x, late_sem.at[1])]

    @pl.when(spot == FLIPS - 1)
    def _():
        gb[...] = jnp.zeros_like(gb)

    greet(depths)
    turns = (*range(1, depths), 0)
    for copy, scatter in zip(wholes, scatters[:3]):
        copy.wait()
        scatter.begin(turns)
    for copy in wholes[3:]:
        copy.wait()

    @pl.loop(0, tiles)
    def _(i):
        slot = lax.rem(i, 2)
        for copy in loads(i, slot):
            copy.wait()

        @pl.when(i + 1 < tiles)
        def _():
            for copy in loads(i + 1, 1 - slot):
                copy.start()

        pieces = []
        for s in range(TILE_SEQS):
            here = slice(s * span, (s + 1) * span)
            seq = i * TILE_SEQS + s
            pieces.append(
                return_one(
                    span,
                    held[slot, 0, here],
                    jnp.concatenate([held[slot, 3, here], held[slot, 1, here]], axis=0),
                    jnp.concatenate([held[slot, 4, here], held[slot, 2, here]], axis=0),
                    sums_ref[seq],
                    held[slot, 5, here],
                    lambda p, s=s: prob[slot, s, p],
                    psum_ref[seq],
                )
            )
        own, back, shared = (jnp.concatenate(rows, axis=0) for rows in zip(*pieces))
        weight_kv = rows_of(wq_ref)[width:]
        kept[at(i), :] = own
        before[at(i), :] = back
        gp[at(i), :] = dot(back, weight_kv).astype(BF16)
        shared_rows[at_sums(i), :] = shared.astype(BF16)
        turned[:, at(i)] = held[slot, 6].T
        turned_prev[:, at(i)] = held[slot, 7].T

        @pl.when(spot > 0)
        def _():
            gb_copy(i).start()

        for when, relays in LEAVE_RELAYS.items():

            @pl.when(i == when)
            def _(relays=relays):
                for a, name in relays:
                    getattr(scatters[a], name)(turns)

        @pl.when(i == tiles - 3)
        def _():
            for copy in late:
                copy.start()

    to_sums = dot(shared_rows[...], rows_of(wq_ref)[width:]).astype(BF16)
    by_spot = lax.dot_general(
        in_order(FLIPS, seqs), to_sums, (((0,), (0,)), ((), ())), preferred_element_type=F32
    )
    gs_send_buf[...] = by_spot.astype(BF16).reshape(gs_send_buf.shape)
    for flip in (6, 7, 2, 4, 3, 5, 1):
        gs_moves.start(gs_send_buf.at[spot_of(depths, 0, flip)[1]], gs_slots.at[flip], flip, 0, flip)
    turned_sum[...] = sums_ref[:, :, 2 * width :].reshape(seqs * FLIPS, width).T
    lanes_in = width // depths

    def weigh(turns):
        owners = [spot_of(depths, turn, 0)[0] for turn in turns]
        tops = [pl.ds(pl.multiple_of(owner * lanes_in, lanes_in), lanes_in) for owner in owners]
        rows_own, rows_prev, rows_sum = (
            jnp.concatenate([ref[top, :] for top in tops], axis=0) for ref in (turned, turned_prev, turned_sum)
        )
        grad_q = dot(rows_own, kept[:, :width])
        grad_kv = dot(rows_own, kept[:, width:]) + dot(rows_prev, before[...]) + dot(rows_sum, shared_rows[...])
        low = jnp.concatenate([grad_q.astype(BF16), grad_kv.astype(BF16)], axis=1)
        for t, (owner, top) in enumerate(zip(owners, tops)):
            flat = low[t * lanes_in : (t + 1) * lanes_in].T
            part[owner] = flat.reshape(part.shape[1:])
            weighed = flat.astype(F32) * wq_ref[owner].reshape(flat.shape).astype(F32)
            one_sum[:, top] = jnp.sum(weighed, axis=0, keepdims=True)
        scatters[3].begin(turns)

    first, second = turns[: depths // 2], turns[depths // 2 :]
    weigh(first)
    weigh(second)
    scatters[3].cross(first)
    total_one = one_sum[...] / gain_ref[0:1]
    total_two = jnp.sum(ggain_ref[...], axis=0, keepdims=True)
    gain_slots[spot] = jnp.concatenate([total_one, total_two], axis=0)
    gain_share.begin()
    gain_share.forward()
    for copy in late:
        copy.wait()
    for flip in range(1, FLIPS):
        gs_moves.landed(gs_slots.at[flip], flip)
    shared = gs_send_buf[spot].astype(F32)
    for flip in range(1, FLIPS):
        shared = shared + gs_slots[flip].astype(F32)
    gain = gain_ref[0:1]

    def close_tile(i):
        @pl.when(spot < FLIPS - 1)
        def _():
            gb_copy(i).wait_recv()

        unit, inv = standardize(x[at(i), :].astype(F32))
        grad_norm = dot(kept[at(i), :], rows_of(wq_ref)) + gb[at(i), :].astype(F32)
        lifted = [
            grad_norm[s * span : (s + 1) * span] + shared[i * TILE_SEQS + s : i * TILE_SEQS + s + 1]
            for s in range(TILE_SEQS)
        ]
        grad_norm = jnp.concatenate(lifted, axis=0)
        ig[at(i), :] = (gr[at(i), :] + norm_back(grad_norm, unit, inv, gain)).astype(BF16)
        pltpu.make_async_copy(ig.at[at(i)], ig_out.at[at(i)], ig_sem.at[i]).start()

    def share_deep():
        gain_share.complete()
        over_ctx = gain_slots[0]
        for c in range(1, FLIPS):
            over_ctx = over_ctx + gain_slots[c]
        gain_deep[0] = over_ctx
        for turn in range(1, depths):
            deep_moves.start(gain_deep.at[0], gain_deep.at[depths - turn], depths - turn, turn, 0)

    after = {
        1: (functools.partial(scatters[3].cross, second), functools.partial(scatters[3].spread, first)),
        2: (share_deep, functools.partial(scatters[3].spread, second)),
        0: (functools.partial(scatters[2].climb, turns),),
        4: (functools.partial(scatters[3].climb, first),),
        6: (functools.partial(scatters[3].climb, second),),
    }
    for i in range(tiles):
        for relay in after.get(i, ()):
            relay()
        close_tile(i)
    for turn in range(1, depths):
        deep_moves.landed(gain_deep.at[turn], turn)
    over_all = gain_deep[0]
    for turn in range(1, depths):
        over_all = over_all + gain_deep[turn]
    lanes = width // FLIPS
    mine = jnp.zeros((2, lanes), F32)
    for c in range(FLIPS):
        mine = jnp.where(spot == c, over_all[:, c * lanes : (c + 1) * lanes], mine)
    dgain_out[...] = mine
    for out, scatter in zip((dout_out, dup_out, ddown_out, dqkv_out), scatters):
        out[...] = scatter.finish()
    for scatter in scatters:
        scatter.close()
    gain_share.close()
    gs_moves.drain(gs_slots.at[0])
    deep_moves.drain(gain_deep.at[0])

    @pl.when(spot > 0)
    def _():
        for i in range(tiles):
            gb_copy(i).wait_send()

    for i in range(tiles):
        pltpu.make_async_copy(ig.at[at(i)], ig_out.at[at(i)], ig_sem.at[i]).wait()


def leave(arrays, psum, sums, wq, partials, gains, ggain, span, depths):
    rows, width = arrays[0].shape
    tile = TILE_SEQS * span
    tiles, seqs = rows // tile, rows // span
    vmem = pl.BlockSpec(memory_space=pltpu.VMEM)
    far = pl.BlockSpec(memory_space=pl.ANY)
    sems = pltpu.SemaphoreType.DMA
    low = pltpu.VMEM((rows, width), BF16)
    high = pltpu.VMEM((rows, width), F32)
    shapes = [p.shape[2:] for p in (*partials, wq)]
    scratch = [pltpu.VMEM(a.shape, BF16) for a in (psum, sums, wq, *partials)]
    scratch += [
        pltpu.VMEM((2, 8, tile, width), BF16),
        pltpu.VMEM((2, TILE_SEQS, HEADS // 2, 2 * span, 2 * span), BF16),
        pltpu.VMEM((rows, 3 * width), BF16),
        pltpu.VMEM((rows, 2 * width), BF16),
        pltpu.VMEM((seqs * FLIPS, 2 * width), BF16),
        pltpu.VMEM((width, rows), BF16),
        pltpu.VMEM((width, rows), BF16),
        pltpu.VMEM((width, seqs * FLIPS), BF16),
        pltpu.VMEM((1, width), F32),
        low, low, high, low, low,
        pltpu.VMEM(wq.shape, BF16),
        pltpu.VMEM((FLIPS, seqs, width), BF16),
        pltpu.VMEM((FLIPS, seqs, width), BF16),
        pltpu.VMEM((FLIPS, 2, width), F32),
        pltpu.VMEM((depths, 2, width), F32),
    ]
    for shape in shapes:
        scratch += scatter_scratch(shape, depths)
    scratch += [
        sems((4, 8 * depths)), sems((4, 8 * depths)), sems((FLIPS,)), sems((FLIPS,)), sems((FLIPS,)), sems((FLIPS,)),
        sems((depths,)), sems((depths,)), sems((tiles,)), sems((tiles,)), sems((2, 9)), sems((2,)), sems((tiles,)), sems((6,)),
    ]
    outs = [jax.ShapeDtypeStruct(shape, F32) for shape in (shapes[3], *shapes[:3])]
    return pl.pallas_call(
        functools.partial(leave_kernel, depths, span),
        in_specs=[far] * 17 + [vmem] * 2,
        out_specs=[far] + [vmem] * 5,
        out_shape=[jax.ShapeDtypeStruct((rows, width), BF16), *outs, jax.ShapeDtypeStruct((2, width // FLIPS), F32)],
        scratch_shapes=scratch,
        compiler_params=pltpu.CompilerParams(collective_id=1, has_side_effects=True, vmem_limit_bytes=VMEM_MOST),
        name="leave",
    )(*arrays, psum, sums, wq, *partials, gains, ggain)


FINISH_PIECES = 8


def finish_kernel(ig_in, *refs):
    turned, (gains, ig_out), flat = refs[:4], refs[4:6], refs[6:10]
    one_out, two_out, held, load_sem, store_sem = refs[10:]
    rows = ig_in.shape[0] // FINISH_PIECES
    pieces = [pl.ds(i * rows, rows) for i in range(FINISH_PIECES)]
    loads = [pltpu.make_async_copy(ig_in.at[p], held.at[p], load_sem.at[i]) for i, p in enumerate(pieces)]
    stores = [pltpu.make_async_copy(held.at[p], ig_out.at[p], store_sem.at[i]) for i, p in enumerate(pieces)]
    for copy in loads:
        copy.start()
    for given, out in zip(turned, flat):
        out[...] = given[...]
    one_out[...] = gains[0:1, :].reshape(one_out.shape)
    two_out[...] = gains[1:2, :].reshape(two_out.shape)
    for load, store in zip(loads, stores):
        load.wait()
        store.start()
    for copy in stores:
        copy.wait()


def finish(ig, grads, dgain, shapes):
    vmem = pl.BlockSpec(memory_space=pltpu.VMEM)
    far = pl.BlockSpec(memory_space=pl.ANY)
    outs = [jax.ShapeDtypeStruct(shape, F32) for shape in (*shapes, dgain.shape[1:], dgain.shape[1:])]
    sems = pltpu.SemaphoreType.DMA((FINISH_PIECES,))
    return pl.pallas_call(
        finish_kernel,
        in_specs=[far] + [vmem] * 5,
        out_specs=[far] + [vmem] * 6,
        out_shape=[jax.ShapeDtypeStruct(ig.shape, ig.dtype), *outs],
        scratch_shapes=[pltpu.VMEM(ig.shape, ig.dtype), sems, sems],
        compiler_params=params(),
        name="finish",
    )(ig, *grads, dgain)


def direct_shards(tokens, prefix, blocks, gain_one, gain_two, cotangent):
    span, width = tokens.shape[2], tokens.shape[3]
    depths = lax.axis_size("dp")
    x = tokens.reshape(-1, width)
    grad = cotangent.reshape(-1, width)
    (wq, wo, wu, wd, gains, q, k, v, kp, vp, n, n_prev, mixed, prob, sums, psum) = enter(
        x, prefix, blocks, gain_one, gain_two, span, depths
    )
    out, gm, gr, gout, gup, gdown, ggain = feed(x, mixed, grad, wo, wu, wd, gains, 2 * TILE_SEQS * span)
    arrays = (q, k, v, kp, vp, gm, n, n_prev, prob, gr, x)
    ig, dqkv, dout, dup, ddown, dgain = leave(arrays, psum, sums, wq, (gout, gup, gdown), gains, ggain, span, depths)
    ig, dqkv, dout, dup, ddown, one, two = finish(ig, (dqkv, dout, dup, ddown), dgain, [b.shape for b in blocks])
    return out.reshape(tokens.shape), ig.reshape(tokens.shape), dqkv.T, dout.T, dup, ddown.T, one, two


def fetch(block, rows_along):
    spot, depth = (0, 1) if rows_along == 1 else (1, 0)
    whole = lax.all_gather(lax.all_gather(block, "ctx", axis=spot, tiled=True), "dp", axis=depth, tiled=True)
    return whole[None, None]


def reduce_weight(partial, rows_along):
    spot, depth = (0, 1) if rows_along == 1 else (1, 0)
    columns = lax.psum_scatter(partial[0, 0], "ctx", scatter_dimension=spot, tiled=True)
    return lax.psum_scatter(columns, "dp", scatter_dimension=depth, tiled=True).astype(F32)


def shards(tokens, prefix, w_qkv, w_out, w_up, w_down, gain_one, gain_two, cotangent):
    span, width = tokens.shape[2], tokens.shape[3]
    count = lax.axis_size("ctx")
    blocks = (w_qkv.T, w_out.T, w_up, w_down.T)
    if count == FLIPS and all(b.shape[0] % 16 == 0 and b.shape[1] % 128 == 0 for b in blocks):
        return direct_shards(tokens, prefix, blocks, gain_one, gain_two, cotangent)
    along = (1, 1, 0, 1)
    x = tokens.reshape(-1, width)
    grad = cotangent.reshape(-1, width)
    tile = TILE_SEQS * span
    block = lax.axis_index("ctx").reshape(1).astype(jnp.int32)
    x_prev = lax.ppermute(x, "ctx", [(i, i + 1) for i in range(count - 1)])
    gain1 = lax.all_gather(gain_one, "ctx", axis=0, tiled=True).astype(F32).reshape(1, width)
    gain2 = lax.all_gather(gain_two, "ctx", axis=0, tiled=True).astype(F32).reshape(1, width)
    wq, wo, wu, wd = (fetch(b, r) for b, r in zip(blocks, along))
    q, k, v, kp, vp, n, n_prev, own_sums = project(x, x_prev, wq, gain1, span)
    own_sums = own_sums.reshape(-1, 2 * width)
    n_sum = jnp.sum(n.reshape(-1, span, width).astype(F32), axis=1).astype(BF16)
    everything = lax.all_gather(jnp.concatenate([own_sums, n_sum], axis=1), "ctx", axis=0, tiled=False)
    everything = jnp.transpose(everything, (1, 0, 2))
    sums, n_sums = everything[:, :, : 2 * width], everything[:, :, 2 * width :]
    mixed, prob, psum = attend(prefix.reshape(-1), block, q, k, v, kp, vp, sums, span)
    out, gm, gr, gout, gup, gdown, ggain2 = feed(x, mixed, grad, wo, wu, wd, gain2, tile)
    gn, gp, gs, gqkv = give_back(q, k, v, kp, vp, sums, gm, prob, psum, n, n_prev, n_sums, wq, span)
    gb = lax.ppermute(gp, "ctx", [(i, i - 1) for i in range(1, count)])
    gs_own = lax.psum_scatter(gs, "ctx", scatter_dimension=1, tiled=True)
    input_grad, ggain1 = close(x, gn, gb, gs_own, gr, gain1, span)
    gains = jnp.concatenate([jnp.sum(ggain1, axis=0), jnp.sum(ggain2, axis=0)]).reshape(2, width)
    gains = lax.psum(gains, "dp")
    gains = lax.psum_scatter(gains, "ctx", scatter_dimension=1, tiled=True)
    sums_w = [reduce_weight(p, r) for p, r in zip((gqkv, gout, gup, gdown), along)]
    return (
        out.reshape(tokens.shape),
        input_grad.reshape(tokens.shape),
        sums_w[0].T,
        sums_w[1].T,
        sums_w[2],
        sums_w[3].T,
        gains[0],
        gains[1],
    )


def solution(mesh):
    rows = P(None, "dp", "ctx", None)
    both = P("dp", "ctx")
    return jax.shard_map(
        shards,
        mesh=mesh,
        in_specs=(rows, P(None, "dp"), both, both, both, both, P("ctx"), P("ctx"), rows),
        out_specs=(rows, rows, both, both, both, both, P("ctx"), P("ctx")),
        check_vma=False,
    )
```
